32 devices in a mesh: dp: 8 (over z, x), row: 2 (over core), col: 2 (over y).
Axes of the slice: x: 2, y: 2, z: 4, core: 2. Of those that a mesh axis runs over, the one named last changes fastest.
Arguments:
- tokens: bfloat16 [2, 8, 256, 2048], P(None, None, 'dp', ('row', 'col')), may hold values from -57 to 57
- lengths: int32 [2, 8], replicated, may hold values from 64 to 256, as said below
- deal_order: int32 [2, 8], replicated, may hold values from 0 to 7, each once within a row
- attention_gain: float32 [2048], P(('row', 'col')), may hold values from 0.25 to 1.75
- query_weight: bfloat16 [2048, 2048], P('row', 'col'), may hold values from -0.1875 to 0.1875
- key_weight: bfloat16 [2048, 2048], P('row', 'col'), may hold values from -0.1875 to 0.1875
- value_weight: bfloat16 [2048, 2048], P('row', 'col'), may hold values from -0.125 to 0.125
- output_weight: bfloat16 [2048, 2048], P('col', 'row'), may hold values from -0.25 to 0.25
- feed_gain: float32 [2048], P(('row', 'col')), may hold values from 0.25 to 1.75
- gate_weight: bfloat16 [2048, 8192], P('row', 'col'), may hold values from -0.125 to 0.125
- up_weight: bfloat16 [2048, 8192], P('row', 'col'), may hold values from -0.125 to 0.125
- down_weight: bfloat16 [8192, 2048], P('col', 'row'), may hold values from -0.09375 to 0.09375
- cotangent: bfloat16 [2, 8, 256, 2048], P(None, 'dp', None, ('row', 'col')), may hold values from -6 to 6
Outputs:
- layer_output: bfloat16 [2, 8, 256, 2048], P(None, None, 'dp', ('row', 'col'))
- tokens_grad: bfloat16 [2, 8, 256, 2048], P(None, None, 'dp', ('row', 'col'))
- attention_gain_grad: float32 [2048], P(('row', 'col', 'dp'))
- query_grad: float32 [2048, 2048], P(('row', 'dp'), 'col')
- key_grad: float32 [2048, 2048], P(('row', 'dp'), 'col')
- value_grad: float32 [2048, 2048], P(('row', 'dp'), 'col')
- output_grad: float32 [2048, 2048], P(('col', 'dp'), 'row')
- feed_gain_grad: float32 [2048], P(('row', 'col', 'dp'))
- gate_grad: float32 [2048, 8192], P(('row', 'dp'), 'col')
- up_grad: float32 [2048, 8192], P(('row', 'dp'), 'col')
- down_grad: float32 [8192, 2048], P(('col', 'dp'), 'row')
The draws below stay inside these ranges and needn't reach their ends.
Inputs may be any that keep to these rules, and one draw needn't show every extreme that they name: `lengths`: in each micro-batch one sequence has exactly 256 tokens. `deal_order`: each row holds every number of 0 to 7 once.
All inputs are finite; a program needn't handle non-finite values.
Results may differ from the reference program's by a relative error of at most 0.023.
Values may be sent and summed in bfloat16 or wider, within the bound.
A program may use at most 256 MiB of HBM per device.

```python
import math
import jax
import jax.numpy as jnp
from jax import lax

D = 2048
HEADS = 32
HEAD_DIM = 64
FF = 8192
SL = 256
MICRO = 2
NSEQ = 8


def draw_tokens(key, part):
    base_key, column_key, row_key = jax.random.split(key, 3)
    full_shape = (MICRO, NSEQ, SL, D)
    base_values = jnp.clip(jax.random.normal(base_key, full_shape, jnp.float32), -6.0, 6.0)
    column_ramp = jnp.exp(2.3 * (jnp.arange(D, dtype=jnp.float32) / D - 0.5))
    jitter = jnp.exp(jax.random.uniform(column_key, (D,), jnp.float32, -0.4, 0.4))
    row_scale = jnp.exp(jax.random.uniform(row_key, (MICRO, NSEQ, SL, 1), jnp.float32, -0.7, 0.7))
    return (base_values * column_ramp * jitter * row_scale).astype(jnp.bfloat16)


def draw_lengths(key, part):
    first_key, second_key = jax.random.split(key, 2)
    drawn_lengths = jax.random.randint(first_key, (MICRO, NSEQ), SL // 4, SL + 1)
    chosen = jax.random.randint(second_key, (MICRO, 1), 0, NSEQ)
    columns = jnp.arange(NSEQ)[None, :]
    return jnp.where(columns == chosen, SL, drawn_lengths).astype(jnp.int32)


def block_scale(own_key, extent, shards, smallest, high):
    loudness = 1.0
    for axis_at, parts in shards:
        draws = jax.random.uniform(jax.random.fold_in(jax.random.fold_in(own_key, 6), axis_at), (parts,), jnp.float32, smallest / len(shards), high / len(shards))
        loudness = loudness * jnp.repeat(jnp.exp(draws), extent[axis_at] // parts).reshape((-1,) + (1,) * (len(extent) - 1 - axis_at))
    return loudness


def gaussian(stream_key, extent, spread, most, pieces=(), held_as=jnp.bfloat16):
    entries = spread * jax.random.normal(stream_key, extent, jnp.float32)
    if pieces:
        entries = entries * block_scale(stream_key, extent, pieces, -0.22, 0.18)
    return jnp.clip(entries, -most, most).astype(held_as)


def setup_inputs(seed: int = 0) -> dict:
    keys = jax.random.split(jax.random.key(seed), 14)
    return {
        "tokens": draw_tokens(jax.random.fold_in(keys[13], 71), 0),
        "lengths": draw_lengths(jax.random.fold_in(keys[13], 71), 0),
        "deal_order": jax.vmap(lambda own: jax.random.permutation(own, NSEQ))(jax.random.split(keys[2], MICRO)).reshape((MICRO, NSEQ)).astype(jnp.int32),
        "attention_gain": jnp.clip(1.0 + 0.15 * jax.random.normal(keys[3], (D,), jnp.float32), 0.25, 1.75),
        "query_weight": gaussian(keys[4], (D, D), (D // 2) ** -0.5, 0.1875, ((0, 2), (1, 2))),
        "key_weight": gaussian(keys[5], (D, D), (D // 2) ** -0.5, 0.1875, ((0, 2), (1, 2))),
        "value_weight": gaussian(keys[6], (D, D), D ** -0.5, 0.125, ((0, 2), (1, 2))),
        "output_weight": gaussian(keys[7], (D, D), (D // 4) ** -0.5, 0.25, ((0, 2), (1, 2))),
        "feed_gain": jnp.clip(1.0 + 0.15 * jax.random.normal(keys[8], (D,), jnp.float32), 0.25, 1.75),
        "gate_weight": gaussian(keys[9], (D, FF), D ** -0.5, 0.125, ((0, 2), (1, 2))),
        "up_weight": gaussian(keys[10], (D, FF), D ** -0.5, 0.125, ((0, 2), (1, 2))),
        "down_weight": gaussian(keys[11], (FF, D), (FF // 2) ** -0.5, 0.09375, ((0, 2), (1, 2))),
        "cotangent": gaussian(keys[12], (MICRO, NSEQ, SL, D), 1.0, 6.0, ((1, 8), (3, 4))),
    }


EPSILON = 1e-05
ROPE_THETA = 130000.0
MASKED_SCORE = -1000000000.0
PRECISE = lax.Precision.HIGHEST

@jax.custom_vjp
def low(v):
    return lax.optimization_barrier(v.astype(jnp.bfloat16)).astype(jnp.float32)

@jax.custom_vjp
def low_back(v):
    return v

def low_keep(v):
    return (low(v), None)

def low_pass(kept, grad):
    return (grad,)

def back_keep(v):
    return (v, None)

def back_low(kept, grad):
    return (low(grad),)
low.defvjp(low_keep, low_pass)
low_back.defvjp(back_keep, back_low)

def rope_tables(slot_count, head_width):
    half_width = head_width // 2
    frequency = jnp.exp(jnp.arange(half_width, dtype=jnp.float32) * (-2.0 * math.log(ROPE_THETA) / head_width))
    angles = jnp.arange(slot_count, dtype=jnp.float32)[:, None] * frequency[None, :]
    return (jnp.cos(angles)[:, None, :], jnp.sin(angles)[:, None, :])

def rotate(values, cosine_table, sine_table):
    half_width = values.shape[-1] // 2
    first_half = values[..., :half_width]
    second_half = values[..., half_width:]
    return jnp.concatenate([first_half * cosine_table - second_half * sine_table, second_half * cosine_table + first_half * sine_table], axis=-1)

def rms_norm(values, gain_vector):
    inverse_rms = lax.rsqrt(lax.optimization_barrier(jnp.mean(values * values, axis=-1, keepdims=True)) + EPSILON)
    return values * inverse_rms * gain_vector

def project(values, weight):
    return jnp.einsum('bsd,de->bse', values, weight, precision=PRECISE)

def attend(block_item):
    queries, key_rows, values, length = block_item
    scores = jnp.einsum('qhd,khd->hqk', queries, key_rows, precision=PRECISE) * HEAD_DIM ** (-0.5)
    scores = low_back(scores)
    positions = jnp.arange(SL, dtype=jnp.int32)
    allowed = (positions[None, :] <= positions[:, None]) & (positions[None, :] < length)
    scores = jnp.where(allowed[None], scores, MASKED_SCORE)
    row_top = lax.optimization_barrier(jnp.max(scores, axis=-1, keepdims=True))
    exp_scores = jnp.exp(scores - row_top)
    softmax_out = exp_scores / lax.optimization_barrier(jnp.sum(exp_scores, axis=-1, keepdims=True))
    return jnp.einsum('hqk,khd->qhd', low(softmax_out), values, precision=PRECISE)

def layer(token_rows, row_lengths, attention_gain, query_weight, key_weight, value_weight, output_weight, feed_gain, gate_weight, up_weight, down_weight):
    cosine_table, sine_table = rope_tables(SL, HEAD_DIM)
    head_shape = token_rows.shape[:2] + (HEADS, HEAD_DIM)
    normed_first = low(rms_norm(token_rows, attention_gain))
    queries = low_back(project(normed_first, query_weight))
    key_rows = low_back(project(normed_first, key_weight))
    values = low_back(project(normed_first, value_weight))
    queries = low(rotate(queries.reshape(head_shape), cosine_table, sine_table))
    key_rows = low(rotate(key_rows.reshape(head_shape), cosine_table, sine_table))
    values = low(values.reshape(head_shape))
    mixed_heads = lax.map(jax.checkpoint(attend), (queries, key_rows, values, row_lengths))
    mixed_heads = low(low_back(mixed_heads.reshape(token_rows.shape)))
    middle = token_rows + low_back(project(mixed_heads, output_weight))
    normed_second = low(rms_norm(middle, feed_gain))
    gate_sum = low_back(project(normed_second, gate_weight))
    up_sum = low_back(project(normed_second, up_weight))
    hidden = low(gate_sum / (1.0 + jnp.exp(-gate_sum)) * up_sum)
    return middle + low_back(project(hidden, down_weight))

def reference(tokens, lengths, deal_order, attention_gain, query_weight, key_weight, value_weight, output_weight, feed_gain, gate_weight, up_weight, down_weight, cotangent):
    slot_of = jnp.argsort(deal_order, axis=1).astype(jnp.int32)
    sequence_grad = jnp.take_along_axis(cotangent, slot_of[:, :, None, None], axis=1).astype(jnp.float32)
    positions = jnp.arange(SL, dtype=jnp.int32)
    live_rows = (positions[None, None, :] < lengths[:, :, None]).astype(jnp.float32)
    sequence_grad = sequence_grad * live_rows[..., None]
    sequence_total = MICRO * NSEQ
    group_size = math.gcd(sequence_total, max(1, 4096 // SL))
    step_count = sequence_total // group_size
    inputs_by_step = tokens.astype(jnp.float32).reshape(step_count, group_size, SL, D)
    grads_by_step = sequence_grad.reshape(step_count, group_size, SL, D)
    lengths_by_step = lengths.reshape(step_count, group_size)
    weights = (attention_gain.astype(jnp.float32), query_weight.astype(jnp.float32), key_weight.astype(jnp.float32), value_weight.astype(jnp.float32), output_weight.astype(jnp.float32), feed_gain.astype(jnp.float32), gate_weight.astype(jnp.float32), up_weight.astype(jnp.float32), down_weight.astype(jnp.float32))

    def one_step(running_sums, block_item):
        block_tokens, block_grad, block_lengths = block_item

        def forward(token_values, *weight_values):
            return layer(token_values, block_lengths, *weight_values)
        block_out, pullback = jax.vjp(forward, block_tokens, *weights)
        pulled = pullback(block_grad)
        summed = tuple((old_value + new_value for old_value, new_value in zip(running_sums, pulled[1:])))
        return (summed, (block_out.astype(jnp.bfloat16), pulled[0].astype(jnp.bfloat16)))
    zeros_init = tuple((jnp.zeros_like(weight_item) for weight_item in weights))
    grad_sums, outputs_pair = lax.scan(one_step, zeros_init, (inputs_by_step, grads_by_step, lengths_by_step))
    layer_output = outputs_pair[0].reshape(MICRO, NSEQ, SL, D)
    tokens_grad = outputs_pair[1].reshape(MICRO, NSEQ, SL, D)
    return (layer_output, tokens_grad, grad_sums[0], grad_sums[1], grad_sums[2], grad_sums[3], grad_sums[4], grad_sums[5], grad_sums[6], grad_sums[7], grad_sums[8])
```

```python
import math

import jax
import jax.numpy as jnp
from jax import lax
from jax.experimental import pallas as pl
from jax.experimental.pallas import tpu as pltpu
from jax.sharding import PartitionSpec as P

D = 2048
HEADS = 32
HEAD_DIM = 64
SL = 256
MICRO = 2
ROWS = MICRO * SL

EPSILON = 1e-05
ROPE_THETA = 130000.0
MASKED_SCORE = -1000000000.0
F32 = jnp.float32
BF16 = jnp.bfloat16
SWAP = [(0, 1), (1, 0)]


def mm(a, b):
    return jnp.dot(a, b, preferred_element_type=F32)


def mm_nt(a, b):
    return lax.dot_general(a, b, (((1,), (1,)), ((), ())), preferred_element_type=F32)


def mm_tn(a, b):
    return lax.dot_general(a, b, (((0,), (0,)), ((), ())), preferred_element_type=F32)


def rope_tables():
    half = HEAD_DIM // 2
    frequency = jnp.exp(
        jnp.arange(half, dtype=F32) * (-2.0 * math.log(ROPE_THETA) / HEAD_DIM)
    )
    angles = jnp.arange(SL, dtype=F32)[:, None] * frequency[None, :]
    cosine = jnp.cos(angles)
    sine = jnp.sin(angles)
    zero = jnp.zeros_like(sine)
    table_cos = jnp.concatenate([cosine] * 4, axis=1)
    table_first = jnp.concatenate([sine, zero] * 2, axis=1)
    table_second = jnp.concatenate([zero, sine] * 2, axis=1)
    return table_cos, table_first, table_second


def turn(v, cos, first, second):
    ahead = pltpu.roll(v, 128 - HEAD_DIM // 2, 1)
    behind = pltpu.roll(v, HEAD_DIM // 2, 1)
    return v * cos - ahead * first + behind * second


def turn_back(v, cos, first, second):
    ahead = pltpu.roll(v, 128 - HEAD_DIM // 2, 1)
    behind = pltpu.roll(v, HEAD_DIM // 2, 1)
    return v * cos + ahead * first - behind * second


def head_mask(head):
    lane = lax.broadcasted_iota(jnp.int32, (SL, 128), 1)
    return (lane // HEAD_DIM) == head


def softmax_of(q, k, allowed):
    scores = mm_nt(q, k) * HEAD_DIM ** (-0.5)
    scores = jnp.where(allowed, scores, MASKED_SCORE)
    exps = jnp.exp(scores - jnp.max(scores, axis=1, keepdims=True))
    return exps / jnp.sum(exps, axis=1, keepdims=True)


def allowed_of(length):
    query = lax.broadcasted_iota(jnp.int32, (SL, SL), 0)
    key = lax.broadcasted_iota(jnp.int32, (SL, SL), 1)
    return (key <= query) & (key < length)


def attend_kernel(len_ref, q_ref, k_ref, v_ref, cos_ref, first_ref, second_ref, o_ref, qr_ref, kr_ref, vr_ref):
    cos, first, second = cos_ref[...], first_ref[...], second_ref[...]
    qr = turn(q_ref[...], cos, first, second).astype(BF16)
    kr = turn(k_ref[...], cos, first, second).astype(BF16)
    vr = v_ref[...].astype(BF16)
    qr_ref[...] = qr
    kr_ref[...] = kr
    vr_ref[...] = vr
    allowed = allowed_of(len_ref[pl.program_id(0)])
    out = jnp.zeros((SL, 128), F32)
    for head in range(2):
        mask = head_mask(head)
        probs = softmax_of(jnp.where(mask, qr, jnp.zeros_like(qr)), kr, allowed).astype(BF16)
        out = out + mm(probs, jnp.where(mask, vr, jnp.zeros_like(vr)))
    o_ref[...] = out.astype(BF16)


def attend_grad_kernel(
    len_ref, qr_ref, kr_ref, vr_ref, od_ref, cos_ref, first_ref, second_ref, dq_ref, dk_ref, dv_ref
):
    cos, first, second = cos_ref[...], first_ref[...], second_ref[...]
    qr, kr, vr, od = qr_ref[...], kr_ref[...], vr_ref[...], od_ref[...]
    allowed = allowed_of(len_ref[pl.program_id(0)])
    dq = jnp.zeros((SL, 128), F32)
    dk = jnp.zeros((SL, 128), F32)
    dv = jnp.zeros((SL, 128), F32)
    zero = jnp.zeros_like(qr)
    for head in range(2):
        mask = head_mask(head)
        q_own = jnp.where(mask, qr, zero)
        k_own = jnp.where(mask, kr, zero)
        od_own = jnp.where(mask, od, zero)
        probs = softmax_of(q_own, kr, allowed)
        d_probs = mm_nt(od_own, vr)
        dv = dv + mm_tn(probs.astype(BF16), od_own)
        inner = jnp.sum(probs * d_probs, axis=1, keepdims=True)
        d_scores = (probs * (d_probs - inner)).astype(BF16)
        dq = dq + mm(d_scores, k_own)
        dk = dk + mm_tn(d_scores, q_own)
    scale = HEAD_DIM ** (-0.5)
    dq_ref[...] = turn_back(dq * scale, cos, first, second).astype(BF16)
    dk_ref[...] = turn_back(dk * scale, cos, first, second).astype(BF16)
    dv_ref[...] = dv.astype(BF16)


def attention_specs(width):
    pairs = width // 128

    def part(index):
        return pl.BlockSpec((SL, 128), lambda m, h, lens: (m, index * pairs + h))

    table = pl.BlockSpec((SL, 128), lambda m, h, lens: (0, 0))
    return pairs, part, table


def attend_forward(lengths, qkv, tables):
    width = qkv.shape[1] // 3
    pairs, part, table = attention_specs(width)
    shape = jax.ShapeDtypeStruct((ROWS, width), BF16)
    return pl.pallas_call(
        attend_kernel,
        out_shape=(shape,) * 4,
        grid_spec=pltpu.PrefetchScalarGridSpec(
            num_scalar_prefetch=1,
            grid=(MICRO, pairs),
            in_specs=[part(0), part(1), part(2), table, table, table],
            out_specs=[part(0)] * 4,
        ),
        cost_estimate=pl.CostEstimate(
            flops=ROWS * SL * width * 4, bytes_accessed=ROWS * width * 20, transcendentals=0
        ),
    )(lengths, qkv, qkv, qkv, *tables)


def attend_backward(lengths, qr, kr, vr, od, tables):
    width = qr.shape[1]
    pairs, part, table = attention_specs(width)
    shape = jax.ShapeDtypeStruct((ROWS, width), BF16)
    return pl.pallas_call(
        attend_grad_kernel,
        out_shape=(shape,) * 3,
        grid_spec=pltpu.PrefetchScalarGridSpec(
            num_scalar_prefetch=1,
            grid=(MICRO, pairs),
            in_specs=[part(0)] * 4 + [table] * 3,
            out_specs=[part(0)] * 3,
        ),
        cost_estimate=pl.CostEstimate(
            flops=ROWS * SL * width * 10, bytes_accessed=ROWS * width * 14, transcendentals=0
        ),
    )(lengths, qr, kr, vr, od, *tables)


def per_device(
    tokens,
    lengths,
    deal_order,
    attention_gain,
    query_weight,
    key_weight,
    value_weight,
    output_weight,
    feed_gain,
    gate_weight,
    up_weight,
    down_weight,
    cotangent,
):
    groups = lax.axis_size("dp")
    line = groups // 2
    dp = lax.axis_index("dp")
    row = lax.axis_index("row")
    col = lax.axis_index("col")
    z, x = dp // 2, dp % 2
    half = D // 2
    block = D // 4

    def over_row(v):
        return lax.ppermute(v, "row", SWAP)

    def over_col(v):
        return lax.ppermute(v, "col", SWAP)

    def over_x(v):
        return lax.ppermute(v, "dp", [(i, i ^ 1) for i in range(groups)])

    def ordered(own, other, index, axis=-1):
        return jnp.where(
            index == 0,
            jnp.concatenate([own, other], axis=axis),
            jnp.concatenate([other, own], axis=axis),
        )

    def halves(v, axis):
        size = v.shape[axis] // 2
        own = lax.dynamic_slice_in_dim(v, row * size, size, axis)
        other = lax.dynamic_slice_in_dim(v, (1 - row) * size, size, axis)
        return own, other

    def x_parts(v, width):
        even = jnp.concatenate(
            [v[:, s : s + width] for s in range(0, v.shape[1], 2 * width)], axis=1
        )
        odd = jnp.concatenate(
            [v[:, s : s + width] for s in range(width, v.shape[1], 2 * width)], axis=1
        )
        return jnp.where(x == 0, even, odd), jnp.where(x == 0, odd, even)

    def line_sum(grads, index_of):
        size = grads.shape[0] // line

        def chunk(dest):
            at = index_of(jnp.clip(dest, 0, line - 1))
            return lax.dynamic_slice_in_dim(grads, at * size, size, 0)

        right = left = None
        for step in range(line - 1):
            send_right = chunk(line - 1 - step + z)
            send_left = chunk(step - (line - 1 - z))
            if step:
                send_right = (send_right.astype(F32) + right.astype(F32)).astype(BF16)
                send_left = (send_left.astype(F32) + left.astype(F32)).astype(BF16)
            rights = [
                (2 * i + k, 2 * i + 2 + k) for i in range(min(step, line - 2) + 1) for k in range(2)
            ]
            lefts = [(2 * (line - 1) + 1 - a, 2 * (line - 1) + 1 - b) for a, b in rights]
            right = lax.ppermute(send_right, "dp", rights)
            left = lax.ppermute(send_left, "dp", lefts)
        return chunk(z).astype(F32) + right.astype(F32) + left.astype(F32)

    def plain_index(dest):
        return dest

    def row_index(dest):
        return lax.rem(dest + line - row * (line // 2), line)

    dealt = lax.all_to_all(
        jnp.take_along_axis(tokens, deal_order[:, :, None, None], axis=1),
        "dp",
        split_axis=1,
        concat_axis=2,
        tiled=True,
    )
    own_order = lax.dynamic_slice_in_dim(deal_order, dp, 1, 1)
    own_lengths = jnp.take_along_axis(lengths, own_order, axis=1)[:, 0]
    tables = rope_tables()
    live = (jnp.arange(SL, dtype=jnp.int32)[None, :] < own_lengths[:, None]).reshape(ROWS, 1)
    top_block = jnp.where(live, cotangent.reshape(ROWS, block), 0.0).astype(BF16)

    gains = jnp.stack([attention_gain, feed_gain])
    gains_half = ordered(gains, over_col(gains), col)
    gains_other = over_row(gains_half)
    gains_full = jnp.concatenate([gains_half, gains_other], axis=1)

    x_block = dealt.reshape(ROWS, block)
    x_half = ordered(x_block, over_col(x_block), col)
    x_other = over_row(x_half)

    own, other = [], []
    for w in (query_weight, key_weight, value_weight):
        a, b = halves(w, 1)
        own.append(a)
        other.append(b)
    qkv_w = jnp.concatenate(
        [jnp.concatenate(own, axis=1), over_row(jnp.concatenate(other, axis=1))], axis=0
    )
    a, b = halves(output_weight, 0)
    out_w = jnp.concatenate([a, over_row(b)], axis=1)
    gate_own, gate_other = halves(gate_weight, 1)
    up_own, up_other = halves(up_weight, 1)
    pair_w = jnp.concatenate(
        [
            jnp.concatenate([gate_own, up_own], axis=1),
            over_row(jnp.concatenate([gate_other, up_other], axis=1)),
        ],
        axis=0,
    )
    a, b = halves(down_weight, 0)
    down_w = jnp.concatenate([a, over_row(b)], axis=1)

    top_half = ordered(top_block, over_col(top_block), col)
    top_full = jnp.concatenate([top_half, over_row(top_half)], axis=1)
    top_pair = jnp.concatenate([top_half, over_x(top_half)], axis=0)
    hidden_grad = mm_nt(top_full, down_w)

    x_full = jnp.concatenate([x_half, x_other], axis=1).astype(F32)
    inverse_first = lax.rsqrt(jnp.mean(x_full * x_full, axis=1, keepdims=True) + EPSILON)
    normed_first = (x_full * inverse_first * gains_full[0][None, :]).astype(BF16)
    qkv = mm(normed_first, qkv_w)
    mixed, qr, kr, vr = attend_forward(own_lengths, qkv, tables)
    partial = mm(mixed, out_w)
    summed = (partial[:, :half] + over_row(partial[:, half:].astype(BF16)).astype(F32)).astype(BF16)
    middle = x_half.astype(F32) + (summed.astype(F32) + over_col(summed).astype(F32))

    middle_low = middle.astype(BF16)
    middle_full = jnp.concatenate([middle_low, over_row(middle_low)], axis=1).astype(F32)
    inverse_second = lax.rsqrt(
        jnp.mean(middle_full * middle_full, axis=1, keepdims=True) + EPSILON
    )
    normed_second = (middle_full * inverse_second * gains_full[1][None, :]).astype(BF16)
    gate_up = mm(normed_second, pair_w)
    quarter = gate_up.shape[1] // 2
    gate, up = gate_up[:, :quarter], gate_up[:, quarter:]
    sigmoid = 1.0 / (1.0 + jnp.exp(-gate))
    swish = gate * sigmoid
    hidden = (swish * up).astype(BF16)
    gate_grad = (hidden_grad * up * sigmoid * (1.0 + gate * (1.0 - sigmoid))).astype(BF16)
    up_grad = (hidden_grad * swish).astype(BF16)

    def side_grad(values, others):
        width = 2 * values.shape[1] // groups
        mine, theirs = x_parts(values, width)
        pair = jnp.concatenate([mine, over_x(theirs)], axis=0)
        both = jnp.concatenate([pair, over_row(pair)], axis=1)
        return line_sum(mm_tn(both, others).astype(BF16), row_index)

    down_sum = side_grad(hidden, top_pair)

    def width_pair(values):
        mine, theirs = x_parts(values, values.shape[1] // groups)
        return jnp.concatenate([mine, over_x(theirs)], axis=0)

    def inner_grad(left_pair, values):
        pair = jnp.concatenate([values, over_x(values)], axis=0)
        both = jnp.concatenate([pair, over_row(pair)], axis=1)
        return line_sum(mm_tn(left_pair, both).astype(BF16), plain_index)

    def columns_in_order(v):
        size = v.shape[1] // 2
        return ordered(v[:, :size], v[:, size:], row)

    second_pair = width_pair(normed_second[:, :half])
    gate_sum = columns_in_order(inner_grad(second_pair, gate_grad))
    up_sum = columns_in_order(inner_grad(second_pair, up_grad))

    partial = mm_nt(jnp.concatenate([gate_grad, up_grad], axis=1), pair_w)
    summed = (partial[:, :half] + over_row(partial[:, half:].astype(BF16)).astype(F32)).astype(BF16)
    second_grad = summed.astype(F32) + over_col(summed).astype(F32)
    feed_piece = jnp.sum(second_grad * middle * inverse_second, axis=0)
    scaled = second_grad * gains_half[1][None, :]
    dot = jnp.sum(scaled * middle, axis=1, keepdims=True)
    dot = dot + over_row(dot)
    middle_grad = (
        top_half.astype(F32) + scaled * inverse_second - middle * (inverse_second**3 * dot / D)
    )
    branch = middle_grad.astype(BF16)
    branch_full = jnp.concatenate([branch, over_row(branch)], axis=1)
    mixed_grad = mm_nt(branch_full, out_w).astype(BF16)
    dq, dk, dv = attend_backward(own_lengths, qr, kr, vr, mixed_grad, tables)
    dqkv = jnp.concatenate([dq, dk, dv], axis=1)

    branch_pair = jnp.concatenate([branch, over_x(branch)], axis=0)
    output_sum = side_grad(mixed, branch_pair)

    def own_block(v):
        return lax.dynamic_slice_in_dim(v, col * block, block, 1)

    def block_sum(partial):
        summed = partial[:, :half] + over_row(partial[:, half:].astype(BF16)).astype(F32)
        theirs = lax.dynamic_slice_in_dim(summed, (1 - col) * block, block, 1)
        return own_block(summed) + over_col(theirs.astype(BF16)).astype(F32)

    first_grad = block_sum(mm_nt(dqkv, qkv_w))
    x_own = x_block.astype(F32)
    gain_own = own_block(gains_half)
    attention_piece = jnp.sum(first_grad * x_own * inverse_first, axis=0)
    scaled = first_grad * gain_own[0][None, :]
    dot = jnp.sum(scaled * x_own, axis=1, keepdims=True)
    dot = dot + over_row(dot)
    dot = dot + over_col(dot)
    input_grad = (
        own_block(middle_grad) + scaled * inverse_first - x_own * (inverse_first**3 * dot / D)
    )

    first_pair = width_pair(normed_first[:, :half])
    pieces = inner_grad(first_pair, dqkv)
    size = dq.shape[1]
    mine, theirs = pieces[:, : 3 * size], pieces[:, 3 * size :]
    qkv_sums = [
        ordered(mine[:, k * size : (k + 1) * size], theirs[:, k * size : (k + 1) * size], row)
        for k in range(3)
    ]

    layer_block = own_block(middle) + block_sum(mm(hidden, down_w))

    gain_sums = lax.psum(
        jnp.stack([attention_piece, own_block(feed_piece[None])[0]]), "dp"
    )
    gain_size = block // groups
    gain_sums = lax.dynamic_slice_in_dim(gain_sums, dp * gain_size, gain_size, 1)

    slot_of = jnp.argsort(deal_order, axis=1)[:, :, None, None]

    def returned(v):
        back = lax.all_to_all(
            v.astype(BF16).reshape(MICRO, 1, SL, block), "dp", split_axis=2, concat_axis=1, tiled=True
        )
        return jnp.take_along_axis(back, slot_of, axis=1)

    return (
        returned(layer_block),
        returned(input_grad),
        gain_sums[0],
        qkv_sums[0],
        qkv_sums[1],
        qkv_sums[2],
        output_sum,
        gain_sums[1],
        gate_sum,
        up_sum,
        down_sum,
    )


def solution(mesh):
    in_specs = (
        P(None, None, "dp", ("row", "col")),
        P(),
        P(),
        P(("row", "col")),
        P("row", "col"),
        P("row", "col"),
        P("row", "col"),
        P("col", "row"),
        P(("row", "col")),
        P("row", "col"),
        P("row", "col"),
        P("col", "row"),
        P(None, "dp", None, ("row", "col")),
    )
    out_specs = (
        P(None, None, "dp", ("row", "col")),
        P(None, None, "dp", ("row", "col")),
        P(("row", "col", "dp")),
        P(("row", "dp"), "col"),
        P(("row", "dp"), "col"),
        P(("row", "dp"), "col"),
        P(("col", "dp"), "row"),
        P(("row", "col", "dp")),
        P(("row", "dp"), "col"),
        P(("row", "dp"), "col"),
        P(("col", "dp"), "row"),
    )
    return jax.shard_map(
        per_device, mesh=mesh, in_specs=in_specs, out_specs=out_specs, check_vma=False
    )
```

```python
import math

import jax
import jax.numpy as jnp
from jax import lax
from jax.experimental import pallas as pl
from jax.experimental.pallas import tpu as pltpu
from jax.sharding import PartitionSpec as P

D = 2048
HEADS = 32
HEAD_DIM = 64
SL = 256
MICRO = 2
ROWS = MICRO * SL

EPSILON = 1e-05
ROPE_THETA = 130000.0
MASKED_SCORE = -1000000000.0
F32 = jnp.float32
BF16 = jnp.bfloat16
SWAP = [(0, 1), (1, 0)]


def mm(a, b):
    return jnp.dot(a, b, preferred_element_type=F32)


def mm_nt(a, b):
    return lax.dot_general(a, b, (((1,), (1,)), ((), ())), preferred_element_type=F32)


def mm_tn(a, b):
    return lax.dot_general(a, b, (((0,), (0,)), ((), ())), preferred_element_type=F32)


def rope_tables():
    half = HEAD_DIM // 2
    frequency = jnp.exp(
        jnp.arange(half, dtype=F32) * (-2.0 * math.log(ROPE_THETA) / HEAD_DIM)
    )
    angles = jnp.arange(SL, dtype=F32)[:, None] * frequency[None, :]
    cosine = jnp.cos(angles)
    sine = jnp.sin(angles)
    zero = jnp.zeros_like(sine)
    table_cos = jnp.concatenate([cosine] * 4, axis=1)
    table_first = jnp.concatenate([sine, zero] * 2, axis=1)
    table_second = jnp.concatenate([zero, sine] * 2, axis=1)
    return table_cos, table_first, table_second


def turn(v, cos, first, second):
    ahead = pltpu.roll(v, 128 - HEAD_DIM // 2, 1)
    behind = pltpu.roll(v, HEAD_DIM // 2, 1)
    return v * cos - ahead * first + behind * second


def turn_back(v, cos, first, second):
    ahead = pltpu.roll(v, 128 - HEAD_DIM // 2, 1)
    behind = pltpu.roll(v, HEAD_DIM // 2, 1)
    return v * cos + ahead * first - behind * second


def head_mask(head):
    lane = lax.broadcasted_iota(jnp.int32, (SL, 128), 1)
    return (lane // HEAD_DIM) == head


def softmax_of(q, k, allowed):
    scores = mm_nt(q, k) * HEAD_DIM ** (-0.5)
    scores = jnp.where(allowed, scores, MASKED_SCORE)
    exps = jnp.exp(scores - jnp.max(scores, axis=1, keepdims=True))
    return exps / jnp.sum(exps, axis=1, keepdims=True)


def allowed_of(length):
    query = lax.broadcasted_iota(jnp.int32, (SL, SL), 0)
    key = lax.broadcasted_iota(jnp.int32, (SL, SL), 1)
    return (key <= query) & (key < length)


FREE = pl.CostEstimate(flops=0, bytes_accessed=0, transcendentals=0)
BUSY = pl.CostEstimate(flops=20 * 10**9, bytes_accessed=60 * 10**6, transcendentals=0)


def whole(shape):
    return pl.BlockSpec(shape, lambda *at: (0,) * len(shape), pipeline_mode=pl.Buffered(1))


def attend_kernel(len_ref, qkv_ref, cos_ref, first_ref, second_ref, o_ref, turned_ref):
    cos, first, second = cos_ref[...], first_ref[...], second_ref[...]
    qr = turn(qkv_ref[:, :128], cos, first, second).astype(BF16)
    kr = turn(qkv_ref[:, 128:256], cos, first, second).astype(BF16)
    vr = qkv_ref[:, 256:].astype(BF16)
    turned_ref[:, :128] = qr
    turned_ref[:, 128:256] = kr
    turned_ref[:, 256:] = vr
    allowed = allowed_of(len_ref[pl.program_id(0)])
    out = jnp.zeros((SL, 128), F32)
    for head in range(2):
        mask = head_mask(head)
        probs = softmax_of(jnp.where(mask, qr, jnp.zeros_like(qr)), kr, allowed).astype(BF16)
        out = out + mm(probs, jnp.where(mask, vr, jnp.zeros_like(vr)))
    o_ref[...] = out.astype(BF16)


def attend_grad_kernel(len_ref, turned_ref, od_ref, cos_ref, first_ref, second_ref, grad_ref):
    cos, first, second = cos_ref[...], first_ref[...], second_ref[...]
    qr, kr, vr = turned_ref[:, :128], turned_ref[:, 128:256], turned_ref[:, 256:]
    od = od_ref[...]
    allowed = allowed_of(len_ref[pl.program_id(0)])
    dq = jnp.zeros((SL, 128), F32)
    dk = jnp.zeros((SL, 128), F32)
    dv = jnp.zeros((SL, 128), F32)
    zero = jnp.zeros_like(qr)
    for head in range(2):
        mask = head_mask(head)
        q_own = jnp.where(mask, qr, zero)
        k_own = jnp.where(mask, kr, zero)
        od_own = jnp.where(mask, od, zero)
        probs = softmax_of(q_own, kr, allowed)
        d_probs = mm_nt(od_own, vr)
        dv = dv + mm_tn(probs.astype(BF16), od_own)
        inner = jnp.sum(probs * d_probs, axis=1, keepdims=True)
        d_scores = (probs * (d_probs - inner)).astype(BF16)
        dq = dq + mm(d_scores, k_own)
        dk = dk + mm_tn(d_scores, q_own)
    scale = HEAD_DIM ** (-0.5)
    grad_ref[:, :128] = turn_back(dq * scale, cos, first, second).astype(BF16)
    grad_ref[:, 128:256] = turn_back(dk * scale, cos, first, second).astype(BF16)
    grad_ref[:, 256:] = dv.astype(BF16)


def pair_block(width):
    return pl.BlockSpec((SL, width), lambda m, h, lens: (m, h))


TABLE = pl.BlockSpec((SL, 128), lambda m, h, lens: (0, 0))


def attend_forward(lengths, qkv, tables):
    width = qkv.shape[1]
    return pl.pallas_call(
        attend_kernel,
        out_shape=(
            jax.ShapeDtypeStruct((ROWS, width // 3), BF16),
            jax.ShapeDtypeStruct((ROWS, width), BF16),
        ),
        grid_spec=pltpu.PrefetchScalarGridSpec(
            num_scalar_prefetch=1,
            grid=(MICRO, width // 384),
            in_specs=[pair_block(384)] + [TABLE] * 3,
            out_specs=[pair_block(128), pair_block(384)],
        ),
        cost_estimate=FREE,
    )(lengths, qkv, *tables)


def attend_backward(lengths, turned, od, tables):
    width = turned.shape[1]
    return pl.pallas_call(
        attend_grad_kernel,
        out_shape=jax.ShapeDtypeStruct((ROWS, width), BF16),
        grid_spec=pltpu.PrefetchScalarGridSpec(
            num_scalar_prefetch=1,
            grid=(MICRO, width // 384),
            in_specs=[pair_block(384), pair_block(128)] + [TABLE] * 3,
            out_specs=pair_block(384),
        ),
        cost_estimate=FREE,
    )(lengths, turned, od, *tables)


def multiply(a, w, transposed, tile, dtype):
    height, depth = a.shape
    width = w.shape[0] if transposed else w.shape[1]

    def kernel(a_ref, w_ref, o_ref):
        form = mm_nt if transposed else mm
        o_ref[...] = form(a_ref[...], w_ref[...]).astype(dtype)

    if transposed:
        w_spec = pl.BlockSpec((tile, depth), lambda j: (j, 0))
    else:
        w_spec = pl.BlockSpec((depth, tile), lambda j: (0, j))
    return pl.pallas_call(
        kernel,
        out_shape=jax.ShapeDtypeStruct((height, width), dtype),
        grid=(width // tile,),
        in_specs=[whole(a.shape), w_spec],
        out_specs=pl.BlockSpec((height, tile), lambda j: (0, j)),
        cost_estimate=FREE,
    )(a, w)


def split_product(parts, w, transposed, tile, cost=FREE):
    count = len(parts)
    height = parts[0].shape[0]
    width = w.shape[0] if transposed else w.shape[1]
    steps = width // tile
    half = steps // 2

    def kernel(*refs):
        form = mm_nt if transposed else mm
        total = form(refs[0][...], refs[count][...])
        for at in range(1, count):
            total = total + form(refs[at][...], refs[count + at][...])
        kept_ref, sent_ref = refs[2 * count :]
        step = pl.program_id(0)

        @pl.when(step < half)
        def _():
            sent_ref[...] = total.astype(BF16)

        @pl.when(step >= half)
        def _():
            kept_ref[...] = total

    def w_spec(at, depth):
        if transposed:
            return pl.BlockSpec((tile, depth), lambda j: (lax.rem(j + half, steps), at))
        return pl.BlockSpec((depth, tile), lambda j: (at, lax.rem(j + half, steps)))

    return pl.pallas_call(
        kernel,
        out_shape=(
            jax.ShapeDtypeStruct((height, width // 2), F32),
            jax.ShapeDtypeStruct((height, width // 2), BF16),
        ),
        grid=(steps,),
        in_specs=[whole(part.shape) for part in parts]
        + [w_spec(at, part.shape[1]) for at, part in enumerate(parts)],
        out_specs=(
            pl.BlockSpec((height, tile), lambda j: (0, jnp.maximum(j - half, 0))),
            pl.BlockSpec((height, tile), lambda j: (0, jnp.minimum(j, half - 1))),
        ),
        cost_estimate=cost,
    )(*parts, *([w] * count))


def feed_kernel(x_ref, gate_ref, up_ref, da_ref, hidden_ref, dg_ref, du_ref):
    x = x_ref[...]
    gate = mm(x, gate_ref[...])
    up = mm(x, up_ref[...])
    da = da_ref[...]
    sigmoid = 1.0 / (1.0 + jnp.exp(-gate))
    swish = gate * sigmoid
    hidden_ref[...] = (swish * up).astype(BF16)
    dg_ref[...] = (da * up * sigmoid * (1.0 + gate * (1.0 - sigmoid))).astype(BF16)
    du_ref[...] = (da * swish).astype(BF16)


def feed_forward(x, pair_w, hidden_grad, tile=256):
    height, depth = x.shape
    width = hidden_grad.shape[1]
    steps = width // tile
    tall = pl.BlockSpec((height, tile), lambda j: (0, j))
    return pl.pallas_call(
        feed_kernel,
        out_shape=(jax.ShapeDtypeStruct((height, width), BF16),) * 3,
        grid=(steps,),
        in_specs=[
            whole(x.shape),
            pl.BlockSpec((depth, tile), lambda j: (0, j)),
            pl.BlockSpec((depth, tile), lambda j: (0, j + steps)),
            tall,
        ],
        out_specs=(tall,) * 3,
        cost_estimate=FREE,
    )(x, pair_w, pair_w, hidden_grad)


def side_grads(left, left_across, right):
    depth, height = left[0].shape
    width = right[0].shape[1]
    tile = width // 2

    def kernel(lo, lr, xo, xr, ro, rr, o_ref):
        @pl.when(pl.program_id(0) == 0)
        def _():
            o_ref[...] = (mm_tn(lo[...], ro[...]) + mm_tn(lr[...], rr[...])).astype(BF16)

        @pl.when(pl.program_id(0) == 1)
        def _():
            o_ref[...] = (mm_tn(xo[...], ro[...]) + mm_tn(xr[...], rr[...])).astype(BF16)

    wide = pl.BlockSpec((depth, tile), lambda p, j: (0, j))
    return pl.pallas_call(
        kernel,
        out_shape=jax.ShapeDtypeStruct((2 * height, width), BF16),
        grid=(2, 2),
        in_specs=[whole(left[0].shape)] * 4 + [wide] * 2,
        out_specs=pl.BlockSpec((height, tile), lambda p, j: (p, j)),
        cost_estimate=FREE,
    )(*left, *left_across, *right)


def wide_grads(left, right, right_across):
    depth, height = left[0].shape
    width = right[0].shape[1]
    tile = width // 2

    def kernel(lo, lr, ro, rr, xo, xr, o_ref):
        @pl.when(pl.program_id(0) == 0)
        def _():
            o_ref[...] = (mm_tn(lo[...], ro[...]) + mm_tn(lr[...], rr[...])).astype(BF16)

        @pl.when(pl.program_id(0) == 1)
        def _():
            o_ref[...] = (mm_tn(lo[...], xo[...]) + mm_tn(lr[...], xr[...])).astype(BF16)

    own = pl.BlockSpec((depth, tile), lambda p, j: (0, jnp.where(p == 0, j, 1)))
    across = pl.BlockSpec((depth, tile), lambda p, j: (0, jnp.where(p == 0, 0, j)))
    return pl.pallas_call(
        kernel,
        out_shape=jax.ShapeDtypeStruct((height, 2 * width), BF16),
        grid=(2, 2),
        in_specs=[whole(left[0].shape)] * 2 + [own] * 2 + [across] * 2,
        out_specs=pl.BlockSpec((height, tile), lambda p, j: (0, 2 * p + j)),
        cost_estimate=FREE,
    )(*left, *right, *right_across)


def line_add_kernel(at_ref, gr_ref, gl_ref, r_ref, l_ref, right_ref, left_ref):
    right_ref[...] = (gr_ref[...].astype(F32) + r_ref[...].astype(F32)).astype(BF16)
    left_ref[...] = (gl_ref[...].astype(F32) + l_ref[...].astype(F32)).astype(BF16)


def line_add(at, grads, right, left):
    height, width = right.shape
    tile = width // 4
    plain = pl.BlockSpec((height, tile), lambda j, at: (0, j))
    shape = jax.ShapeDtypeStruct(right.shape, BF16)
    return pl.pallas_call(
        line_add_kernel,
        out_shape=(shape, shape),
        grid_spec=pltpu.PrefetchScalarGridSpec(
            num_scalar_prefetch=1,
            grid=(4,),
            in_specs=[
                pl.BlockSpec((height, tile), lambda j, at: (at[0], j)),
                pl.BlockSpec((height, tile), lambda j, at: (at[1], j)),
                plain,
                plain,
            ],
            out_specs=[plain, plain],
        ),
        cost_estimate=FREE,
    )(at, grads, grads, right, left)


def line_end_kernel(pieces, at_ref, g_ref, r_ref, l_ref, *out_refs):
    total = g_ref[...].astype(F32) + r_ref[...].astype(F32) + l_ref[...].astype(F32)
    size = total.shape[1] // pieces
    for k in range(pieces):
        out_refs[k][...] = total[:, k * size : (k + 1) * size]


def line_end(at, grads, right, left, pieces, parts, tiles):
    height, width = right.shape
    tile = width // (parts * tiles)

    def came(p, j, at):
        return (0, p * tiles + j)

    def out(p, j, at):
        return (0, jnp.where(at[1] == 0, p, parts - 1 - p) * tiles + j)

    return pl.pallas_call(
        lambda *refs: line_end_kernel(pieces, *refs),
        out_shape=(jax.ShapeDtypeStruct((height, width // pieces), F32),) * pieces,
        grid_spec=pltpu.PrefetchScalarGridSpec(
            num_scalar_prefetch=1,
            grid=(parts, tiles),
            in_specs=[
                pl.BlockSpec((height, tile), lambda p, j, at: (at[0], p * tiles + j)),
                pl.BlockSpec((height, tile), came),
                pl.BlockSpec((height, tile), came),
            ],
            out_specs=[pl.BlockSpec((height, tile // pieces), out)] * pieces,
        ),
        cost_estimate=FREE,
    )(at, grads, right, left)


def swap_kernel(plan, given, count, *refs):
    weights, outs = refs[:given], refs[given : given + count]
    rest = refs[given + count :]
    held, (send_sem, recv_sem, in_sem, out_sem) = rest[: len(plan)], rest[len(plan) :]
    row = lax.axis_index("row")
    barrier = pltpu.get_barrier_semaphore()
    pl.semaphore_signal(
        barrier, inc=1, device_id={"row": 1 - row}, device_id_type=pl.DeviceIdType.MESH
    )
    remote, local = [], []
    for at, (source, by_rows, out, start, offset, size) in enumerate(plan):
        weight = weights[source]
        height, width = weight.shape

        def part(index):
            if by_rows:
                return weight.at[pl.ds(pl.multiple_of(index * size, size), size), :]
            first = pl.multiple_of(index * (width // 2) + start, 128)
            return weight.at[:, pl.ds(first, size)]

        def place(second):
            if by_rows:
                return outs[out].at[:, pl.ds(second * width, width)]
            return outs[out].at[pl.ds(second * height, height), pl.ds(offset, size)]

        remote.append(
            pltpu.make_async_remote_copy(
                src_ref=part(1 - row),
                dst_ref=place(1),
                send_sem=send_sem.at[at],
                recv_sem=recv_sem.at[at],
                device_id={"row": 1 - row},
                device_id_type=pl.DeviceIdType.MESH,
            )
        )
        local.append(
            (
                pltpu.make_async_copy(part(row), held[at], in_sem.at[at]),
                pltpu.make_async_copy(held[at], place(0), out_sem.at[at]),
            )
        )
    for fetch, _ in local:
        fetch.start()
    pl.semaphore_wait(barrier, 1)
    for copy in remote:
        copy.start()
    for fetch, store in local:
        fetch.wait()
        store.start()
    for _, store in local:
        store.wait()
    for copy in remote:
        copy.wait()


def swap_weights(weights, plan, shapes, identity):
    held = []
    for source, by_rows, _, _, _, size in plan:
        height, width = weights[source].shape
        held.append((size, width) if by_rows else (height, size))
    sems = pltpu.SemaphoreType.DMA((len(plan),))
    return pl.pallas_call(
        lambda *refs: swap_kernel(plan, len(weights), len(shapes), *refs),
        out_shape=[jax.ShapeDtypeStruct(shape, BF16) for shape in shapes],
        in_specs=[pl.BlockSpec(memory_space=pl.ANY)] * len(weights),
        out_specs=[pl.BlockSpec(memory_space=pl.ANY)] * len(shapes),
        scratch_shapes=[pltpu.VMEM(shape, BF16) for shape in held] + [sems] * 4,
        compiler_params=pltpu.CompilerParams(collective_id=identity, has_side_effects=True),
        cost_estimate=FREE,
    )(*weights)


MESH = pl.DeviceIdType.MESH


def greet(*moves):
    barrier = pltpu.get_barrier_semaphore()
    total = 0
    for count, target in moves:
        total = total + count

        @pl.when(count > 0)
        def _():
            pl.semaphore_signal(barrier, inc=1, device_id=target, device_id_type=MESH)

    pl.semaphore_wait(barrier, total)


class ZLine:
    def __init__(self, line, grads, out, stage, came, sems, count, sided):
        self.line, self.grads, self.out, self.stage = line, grads, out, stage
        self.came, self.sems, self.sided = came, sems, sided
        width = grads.shape[1] // count
        self.pieces = [(k, pl.ds(k * width, width)) for k in range(count)]
        self.dp, self.row = lax.axis_index("dp"), lax.axis_index("row")
        self.z = self.dp // 2
        self.last = line - 1
        self.ways = ((0, self.z, 2), (1, self.last - self.z, -2))

    def rows_of(self, dest):
        size = self.grads.shape[0] // self.line
        if self.sided:
            dest = lax.rem(dest + self.line - self.row * (self.line // 2), self.line)
        return pl.ds(pl.multiple_of(dest * size, size), size)

    def copy(self, source, way, step, slot, piece, columns):
        return pltpu.make_async_remote_copy(
            src_ref=source,
            dst_ref=self.came.at[way, slot, :, columns],
            send_sem=self.sems.at[0, way, slot, piece],
            recv_sem=self.sems.at[1, way, slot, piece],
            device_id={"dp": self.dp + step},
            device_id_type=MESH,
        )

    def arrived(self, way, step, slot, piece, columns):
        held = self.came.at[way, slot, :, columns]
        self.copy(held, way, step, slot, piece, columns).wait_recv()
        return held

    def run(self, start, stop):
        def one_step(slot, _):
            for piece, columns in self.pieces:
                for way, place, step in self.ways:
                    far = self.last - slot + place
                    dest = far if step > 0 else self.last - far

                    @pl.when((place == 0) & (place < self.last))
                    def _():
                        source = self.grads.at[self.rows_of(dest), columns]
                        self.copy(source, way, step, slot, piece, columns).start()

                    @pl.when((place > 0) & (place <= slot))
                    def _():
                        held = self.arrived(way, step, slot - 1, piece, columns)

                        @pl.when(place < self.last)
                        def _():
                            held[...] = (
                                held[...].astype(F32)
                                + self.grads[self.rows_of(dest), columns].astype(F32)
                            ).astype(BF16)
                            self.copy(held, way, step, slot, piece, columns).start()

            return 0

        lax.fori_loop(start, stop, one_step, 0)

    def finish(self):
        own = self.rows_of(self.z)
        for piece, columns in self.pieces:
            self.stage[:, columns] = self.grads[own, columns].astype(F32)
            for way, place, step in self.ways:

                @pl.when(place > 0)
                def _():
                    held = self.arrived(way, step, self.last - 1, piece, columns)
                    self.stage[:, columns] += held[...].astype(F32)

        def settle(slot, _):
            for piece, columns in self.pieces:
                for way, place, step in self.ways:

                    @pl.when((place <= slot) & (place < self.last))
                    def _():
                        held = self.came.at[way, slot, :, columns]
                        self.copy(held, way, step, slot, piece, columns).wait_send()

            return 0

        lax.fori_loop(0, self.last, settle, 0)

    def moves(self):
        return (
            (jnp.minimum(self.z, 1), {"dp": self.dp - 2}),
            (jnp.minimum(self.last - self.z, 1), {"dp": self.dp + 2}),
        )


def tiles_loop(width, tile, body):
    def one(j, _):
        body(pl.ds(pl.multiple_of(j * tile, tile), tile), j * tile)
        return 0

    lax.fori_loop(0, width // tile, one, 0)


def tail_kernel(
    line,
    gate_grads,
    up,
    up_row,
    second_mine,
    second_came,
    dqkv,
    dqkv_row,
    first_mine,
    first_came,
    branch,
    mixed_mine,
    mixed_came,
    mixed_row,
    mixed_came_row,
    gate_out,
    up_out,
    qkv_out,
    output_out,
    gate_z,
    up_z,
    qkv_z,
    output_z,
    up_grads,
    qkv_grads,
    output_grads,
    up_came,
    up_came_row,
    dqkv_came,
    dqkv_came_row,
    branch_came,
    turned_left,
    gate_stage,
    up_stage,
    qkv_stage,
    output_stage,
    gate_sems,
    up_sems,
    qkv_sems,
    output_sems,
    swap_sems,
    out_sems,
):
    dp, row = lax.axis_index("dp"), lax.axis_index("row")
    partner = dp + 1 - 2 * lax.rem(dp, 2)
    gate_line = ZLine(line, gate_grads, gate_out, gate_stage, gate_z, gate_sems, 4, False)
    up_line = ZLine(line, up_grads, up_out, up_stage, up_z, up_sems, 4, False)
    qkv_line = ZLine(line, qkv_grads, qkv_out, qkv_stage, qkv_z, qkv_sems, 3, False)
    output_line = ZLine(line, output_grads, output_out, output_stage, output_z, output_sems, 1, True)

    def swap(source, target, at, device):
        return pltpu.make_async_remote_copy(
            src_ref=source,
            dst_ref=target,
            send_sem=swap_sems.at[0, at],
            recv_sem=swap_sems.at[1, at],
            device_id=device,
            device_id_type=MESH,
        )

    up_x = swap(up, up_came, 0, {"dp": partner})
    branch_x = swap(branch, branch_came, 1, {"dp": partner})
    dqkv_x = swap(dqkv, dqkv_came, 2, {"dp": partner})
    up_across = swap(up_came, up_came_row, 3, {"row": 1 - row})
    dqkv_across = swap(dqkv_came, dqkv_came_row, 4, {"row": 1 - row})

    def store(line_of, at):
        copy = pltpu.make_async_copy(line_of.stage, line_of.out, out_sems.at[at])
        copy.start()
        return copy

    greet(*gate_line.moves(), (jnp.int32(1), {"dp": partner}), (jnp.int32(1), {"row": 1 - row}))
    gate_line.run(0, 1)
    up_x.start()
    branch_x.start()
    dqkv_x.start()

    depth = second_mine.shape[0]
    turned_left[:, :depth] = second_mine[...].T
    turned_left[:, depth:] = second_came[...].T
    gate_line.run(1, 2)

    def wide(target, shift, mine, came):
        def body(columns, start):
            total = mm(turned_left[:, :depth], mine[:, columns])
            total = total + mm(turned_left[:, depth:], came[:, columns])
            tile = total.shape[1]
            target[:, pl.ds(pl.multiple_of(shift + start, tile), tile)] = total.astype(BF16)

        tiles_loop(mine.shape[1], 512, body)

    up_x.wait_recv()
    up_across.start()
    gate_line.run(2, line - 1)
    wide(up_grads, 0, up, up_came)
    up_across.wait_recv()
    wide(up_grads, up.shape[1], up_row, up_came_row)
    up_line.run(0, 1)
    gate_line.finish()
    gate_store = store(gate_line, 0)

    turned_left[:, :depth] = first_mine[...].T
    turned_left[:, depth:] = first_came[...].T
    branch_x.wait_recv()

    def side(start, mine, came):
        def body(columns, _):
            total = mm_tn(mine[...], branch[:, columns]) + mm_tn(came[...], branch_came[:, columns])
            output_grads[pl.ds(start, mine.shape[1]), columns] = total.astype(BF16)

        tiles_loop(branch.shape[1], 512, body)

    side(0, mixed_mine, mixed_came)
    side(mixed_mine.shape[1], mixed_row, mixed_came_row)
    output_line.run(0, 1)
    up_line.run(1, 2)
    dqkv_x.wait_recv()
    dqkv_across.start()
    wide(qkv_grads, 0, dqkv, dqkv_came)
    dqkv_across.wait_recv()
    wide(qkv_grads, dqkv.shape[1], dqkv_row, dqkv_came_row)
    qkv_line.run(0, 1)
    output_line.run(1, 2)
    up_line.run(2, line - 1)
    qkv_line.run(1, 2)
    output_line.run(2, line - 1)
    up_line.finish()
    up_store = store(up_line, 1)
    qkv_line.run(2, line - 1)
    output_line.finish()
    output_store = store(output_line, 2)
    qkv_line.finish()
    qkv_store = store(qkv_line, 3)
    for copy in (up_x, branch_x, dqkv_x, up_across, dqkv_across):
        copy.wait_send()
    for copy in (gate_store, up_store, output_store, qkv_store):
        copy.wait()


def tail_sums(line, identity, *values):
    (gate_grads, up, _, _, _, dqkv, _, _, _, branch) = values[:10]
    rows = gate_grads.shape[0]
    side_rows = 2 * values[10].shape[1]
    tokens = up.shape[0]
    widths = (gate_grads.shape[1], gate_grads.shape[1], 2 * dqkv.shape[1], branch.shape[1])
    heights = (rows, rows, rows, side_rows)
    pieces = (4, 4, 3, 1)
    sizes = [(h // line, w) for h, w in zip(heights, widths)]
    vmem = pl.BlockSpec(memory_space=pltpu.VMEM)

    def buffer(*shape):
        return pltpu.VMEM(shape, BF16)

    return pl.pallas_call(
        lambda *refs: tail_kernel(line, *refs),
        out_shape=[jax.ShapeDtypeStruct(size, F32) for size in sizes],
        in_specs=[vmem] * len(values),
        out_specs=[pl.BlockSpec(memory_space=pl.ANY)] * 4,
        scratch_shapes=[buffer(2, line - 1, *size) for size in sizes]
        + [buffer(h, w) for h, w in zip(heights[1:], widths[1:])]
        + [buffer(*up.shape)] * 2
        + [buffer(*dqkv.shape)] * 2
        + [buffer(*branch.shape)]
        + [buffer(rows, 2 * tokens)]
        + [pltpu.VMEM(size, F32) for size in sizes]
        + [pltpu.SemaphoreType.DMA((2, 2, line - 1, count)) for count in pieces]
        + [pltpu.SemaphoreType.DMA((2, 5)), pltpu.SemaphoreType.DMA((4,))],
        compiler_params=pltpu.CompilerParams(
            collective_id=identity, has_side_effects=True, vmem_limit_bytes=67043328
        ),
        cost_estimate=FREE,
    )(*values)


def per_device(
    tokens,
    lengths,
    deal_order,
    attention_gain,
    query_weight,
    key_weight,
    value_weight,
    output_weight,
    feed_gain,
    gate_weight,
    up_weight,
    down_weight,
    cotangent,
):
    groups = lax.axis_size("dp")
    line = groups // 2
    dp = lax.axis_index("dp")
    row = lax.axis_index("row")
    col = lax.axis_index("col")
    z, x = dp // 2, dp % 2
    half = D // 2
    block = D // 4

    def over_row(v):
        return lax.ppermute(v, "row", SWAP)

    def over_col(v):
        return lax.ppermute(v, "col", SWAP)

    def over_x(v):
        return lax.ppermute(v, "dp", [(i, i ^ 1) for i in range(groups)])

    def ordered(own, other, index, axis=-1):
        return jnp.where(
            index == 0,
            jnp.concatenate([own, other], axis=axis),
            jnp.concatenate([other, own], axis=axis),
        )

    def x_parts(v, width):
        even = jnp.concatenate(
            [v[:, s : s + width] for s in range(0, v.shape[1], 2 * width)], axis=1
        )
        odd = jnp.concatenate(
            [v[:, s : s + width] for s in range(width, v.shape[1], 2 * width)], axis=1
        )
        return jnp.where(x == 0, even, odd), jnp.where(x == 0, odd, even)

    token = []

    def ordered_after(*values):
        out = lax.optimization_barrier(tuple(values) + tuple(token))
        return out[: len(values)] if len(values) > 1 else out[0]

    def mark(value):
        token[:] = [value]
        return value

    def arrive(*values):
        out = ordered_after(*values)
        mark(out[0] if len(values) > 1 else out)
        return out

    class Line:
        def __init__(self, grads, index_of):
            self.grads = grads
            self.size = grads.shape[0] // line
            self.index_of = index_of
            self.step = 0
            self.right = self.left = None

        def chunk(self, at):
            return lax.dynamic_slice_in_dim(self.grads, at * self.size, self.size, 0)

        def advance(self):
            step = self.step
            if step >= line - 1:
                return
            self.step += 1
            at_right = self.index_of(jnp.clip(line - 1 - step + z, 0, line - 1))
            at_left = self.index_of(jnp.clip(step - (line - 1 - z), 0, line - 1))
            if step:
                right, left = arrive(self.right, self.left)
                send_right, send_left = line_add(
                    jnp.stack([at_right, at_left]), self.grads, right, left
                )
                mark(send_left)
            else:
                send_right, send_left = self.chunk(at_right), self.chunk(at_left)
            rights = [
                (2 * i + k, 2 * i + 2 + k) for i in range(min(step, line - 2) + 1) for k in range(2)
            ]
            lefts = [(2 * (line - 1) + 1 - a, 2 * (line - 1) + 1 - b) for a, b in rights]
            self.right = lax.ppermute(send_right, "dp", rights)
            self.left = lax.ppermute(send_left, "dp", lefts)

        def total(self, pieces, parts, tiles):
            while self.step < line - 1:
                self.advance()
            right, left = arrive(self.right, self.left)
            at = jnp.stack([self.index_of(z), row])
            out = line_end(at, self.grads, right, left, pieces, parts, tiles)
            mark(out[0])
            return out

    def plain_index(dest):
        return dest

    def side_index(dest):
        return lax.rem(dest + line - row * (line // 2), line)

    def all_sum(v):
        if groups & (groups - 1):
            return lax.psum(v, "dp")
        reach = 1
        while reach < groups:
            v = v + lax.ppermute(v, "dp", [(i, i ^ reach) for i in range(groups)])
            reach *= 2
        return v

    gathered = jnp.take_along_axis(tokens, deal_order[:, :, None, None], axis=1)
    gathered = mark(lax.optimization_barrier(gathered))
    dealt = lax.all_to_all(gathered, "dp", split_axis=1, concat_axis=2, tiled=True)
    own_order = lax.dynamic_slice_in_dim(deal_order, dp, 1, 1)
    own_lengths = jnp.take_along_axis(lengths, own_order, axis=1)[:, 0]
    tables = rope_tables()
    live = (jnp.arange(SL, dtype=jnp.int32)[None, :] < own_lengths[:, None]).reshape(ROWS, 1)
    top_block = jnp.where(live, cotangent.reshape(ROWS, block), 0.0).astype(BF16)

    gains = jnp.stack([attention_gain, feed_gain])
    gains_half = ordered(gains, over_col(gains), col)
    gains_other = over_row(gains_half)
    gains_full = jnp.concatenate([gains_half, gains_other], axis=1)

    top_col = over_col(top_block)
    quarter = gate_weight.shape[1] // 2
    gate_weight, up_weight = ordered_after(gate_weight, up_weight)
    (pair_w,) = swap_weights(
        (gate_weight, up_weight),
        ((0, False, 0, 0, 0, quarter), (1, False, 0, 0, quarter, quarter)),
        ((D, 2 * quarter),),
        0,
    )
    mark(pair_w)
    x_block = arrive(dealt).reshape(ROWS, block)
    x_came = over_col(x_block)
    heads = query_weight.shape[1] // 2
    query_weight, key_weight, value_weight, output_weight = ordered_after(
        query_weight, key_weight, value_weight, output_weight
    )
    plan = [
        (kind, False, 0, at, 3 * at + 128 * kind, 128)
        for kind in range(3)
        for at in range(0, heads, 128)
    ]
    qkv_w, out_w = swap_weights(
        (query_weight, key_weight, value_weight, output_weight),
        tuple(plan) + ((3, True, 1, 0, 0, heads),),
        ((D, 3 * heads), (heads, D)),
        1,
    )
    mark(qkv_w)
    top_half = ordered(top_block, arrive(top_col), col)
    top_half = mark(lax.optimization_barrier(top_half))
    x_half = ordered(x_block, arrive(x_came), col)
    x_half = mark(lax.optimization_barrier(x_half))
    top_came = over_x(top_half)
    top_row = over_row(top_half)

    x_other = arrive(over_row(x_half))
    x_full = jnp.concatenate([x_half, x_other], axis=1).astype(F32)
    inverse_first = lax.rsqrt(jnp.mean(x_full * x_full, axis=1, keepdims=True) + EPSILON)
    normed_first = (x_full * inverse_first * gains_full[0][None, :]).astype(BF16)
    normed_first = mark(lax.optimization_barrier(normed_first))
    qkv = multiply(normed_first, qkv_w, False, 384, F32)
    mixed, turned = attend_forward(own_lengths, qkv, tables)
    kept, sent = split_product([mixed], out_w, False, 512)
    mark(sent)
    came = arrive(over_row(sent))
    summed = (kept + came.astype(F32)).astype(BF16)
    summed = mark(lax.optimization_barrier(summed))
    summed_other = over_col(summed)
    top_row = arrive(top_row)
    narrow = half // groups
    first_mine, first_theirs = x_parts(normed_first[:, :half], narrow)
    top_full = jnp.concatenate([top_half, top_row], axis=1)
    (down_w,) = swap_weights(
        (ordered_after(down_weight),),
        ((0, True, 0, 0, 0, down_weight.shape[0] // 2),),
        ((down_weight.shape[0] // 2, D),),
        2,
    )
    hidden_grad = mark(multiply(top_full, down_w, True, 512, F32))
    mixed_mine, mixed_theirs = x_parts(mixed, 2 * mixed.shape[1] // groups)
    top_came = arrive(top_came)
    first_came = over_x(ordered_after(first_theirs))
    summed_other = arrive(summed_other)
    middle = x_half.astype(F32) + (summed.astype(F32) + summed_other.astype(F32))

    middle_low = middle.astype(BF16)
    middle_low, middle = lax.optimization_barrier((middle_low, middle))
    mark(middle_low)
    middle_other = arrive(over_row(middle_low))
    middle_full = jnp.concatenate([middle_low, middle_other], axis=1).astype(F32)
    inverse_second = lax.rsqrt(
        jnp.mean(middle_full * middle_full, axis=1, keepdims=True) + EPSILON
    )
    normed_second = (middle_full * inverse_second * gains_full[1][None, :]).astype(BF16)
    normed_second = mark(lax.optimization_barrier(normed_second))
    hidden, gate_grad, up_grad = feed_forward(normed_second, pair_w, hidden_grad)
    mark(hidden)
    first_came = arrive(first_came)

    def own_block(v):
        return lax.dynamic_slice_in_dim(v, col * block, block, 1)

    def joined(kept, came):
        return mark(lax.optimization_barrier(kept + arrive(came).astype(F32)))

    def to_col(summed):
        theirs = lax.dynamic_slice_in_dim(summed, (1 - col) * block, block, 1)
        return over_col(theirs.astype(BF16))

    second_mine, second_theirs = x_parts(normed_second[:, :half], narrow)
    hidden_mine, hidden_theirs = x_parts(hidden, 2 * quarter // groups)
    hidden_mine, hidden_theirs = lax.optimization_barrier((hidden_mine, hidden_theirs))
    mark(hidden_theirs)

    hidden_came = over_x(hidden_theirs)
    hidden_row = over_row(hidden_mine)
    gate_first, up_first = ordered_after(gate_grad, up_grad)
    kept, sent = split_product([gate_first, up_first], pair_w, True, 512, BUSY)
    mark(sent)
    summed = joined(kept, over_row(sent)).astype(BF16)
    summed_other = over_col(summed)
    gate_row, up_row = over_row(gate_first), over_row(up_first)
    layer_kept, sent = split_product([ordered_after(hidden)], down_w, False, 512)
    mark(sent)
    layer_came = over_row(sent)

    hidden_came, hidden_row = arrive(hidden_came, hidden_row)
    gate_came = over_x(ordered_after(gate_grad))
    hidden_came_row = arrive(over_row(hidden_came))
    down_grads = mark(
        side_grads(
            (hidden_mine, hidden_came), (hidden_row, hidden_came_row), (top_half, top_came)
        )
    )
    down_line = Line(down_grads, side_index)
    down_line.advance()
    mixed_mine, mixed_theirs = x_parts(mixed, 2 * mixed.shape[1] // groups)
    second_came = over_x(ordered_after(second_theirs))
    mixed_came = over_x(ordered_after(mixed_theirs))
    mixed_row = over_row(mixed_mine)

    summed_other = arrive(summed_other)
    second_grad = summed.astype(F32) + summed_other.astype(F32)
    feed_piece = jnp.sum(second_grad * middle * inverse_second, axis=0)
    scaled = second_grad * gains_half[1][None, :]
    dot = jnp.sum(scaled * middle, axis=1, keepdims=True)
    dot = dot + over_row(dot)
    middle_grad = (
        top_half.astype(F32) + scaled * inverse_second - middle * (inverse_second**3 * dot / D)
    )
    branch = middle_grad.astype(BF16)
    middle_grad, branch = lax.optimization_barrier((middle_grad, branch))
    mark(branch)
    branch_row = over_row(branch)
    branch_row = arrive(branch_row)
    branch_full = jnp.concatenate([branch, branch_row], axis=1)
    mixed_grad = mark(multiply(branch_full, out_w, True, 256, BF16))
    down_line.advance()
    dqkv = mark(attend_backward(own_lengths, turned, ordered_after(mixed_grad), tables))
    dqkv_row = over_row(dqkv)
    gate_came, second_came = arrive(gate_came, second_came)
    gate_came_row = over_row(gate_came)
    kept, sent = split_product([ordered_after(dqkv)], qkv_w, True, 512)
    mark(sent)
    came = over_row(sent)
    down_line.advance()
    gate_row, up_row = arrive(gate_row, up_row)
    gate_came_row = arrive(gate_came_row)
    gate_grads = mark(
        wide_grads(
            (second_mine, second_came), (gate_grad, gate_came), (gate_row, gate_came_row)
        )
    )
    mixed_row, mixed_came = arrive(mixed_row, mixed_came)
    mixed_came_row = over_row(mixed_came)
    summed = joined(kept, came)
    first_kept, first_sent = own_block(summed), to_col(summed)
    summed = joined(layer_kept, layer_came)
    layer_kept, layer_sent = own_block(summed), to_col(summed)
    mixed_came_row, dqkv_row = arrive(mixed_came_row, dqkv_row)
    (down_sum,) = down_line.total(1, 1, 4)

    gate_sum, up_sum, qkv_sum, output_sum = tail_sums(
        line,
        3,
        *ordered_after(
            gate_grads,
            up_grad,
            up_row,
            second_mine,
            second_came,
            dqkv,
            dqkv_row,
            first_mine,
            first_came,
            branch,
            mixed_mine,
            mixed_came,
            mixed_row,
            mixed_came_row,
        ),
    )
    mark(output_sum)
    gate_sum = ordered(gate_sum[:, :quarter], gate_sum[:, quarter:], row)
    up_sum = ordered(up_sum[:, :quarter], up_sum[:, quarter:], row)
    qkv_sum = ordered(qkv_sum[:, : 3 * heads], qkv_sum[:, 3 * heads :], row)
    qkv_sums = [
        jnp.concatenate(
            [qkv_sum[:, s : s + 128] for s in range(128 * kind, 6 * heads, 384)], axis=1
        )
        for kind in range(3)
    ]

    first_grad = first_kept + arrive(first_sent).astype(F32)
    x_own = x_block.astype(F32)
    gain_own = own_block(gains_half)
    attention_piece = jnp.sum(first_grad * x_own * inverse_first, axis=0)
    scaled = first_grad * gain_own[0][None, :]
    dot = jnp.sum(scaled * x_own, axis=1, keepdims=True)
    dot = dot + over_row(dot)
    dot = dot + over_col(dot)
    input_grad = (
        own_block(middle_grad) + scaled * inverse_first - x_own * (inverse_first**3 * dot / D)
    ).astype(BF16)
    input_grad = mark(lax.optimization_barrier(input_grad))
    layer_block = own_block(middle) + layer_kept + arrive(layer_sent).astype(F32)
    layer_block = mark(lax.optimization_barrier(layer_block.astype(BF16)))

    gain_sums = all_sum(jnp.stack([attention_piece, own_block(feed_piece[None])[0]]))
    gain_size = block // groups
    gain_sums = lax.dynamic_slice_in_dim(gain_sums, dp * gain_size, gain_size, 1)

    slot_of = jnp.argsort(deal_order, axis=1)[:, :, None, None]

    def returned(v):
        back = lax.all_to_all(
            v.reshape(MICRO, 1, SL, block), "dp", split_axis=2, concat_axis=1, tiled=True
        )
        return jnp.take_along_axis(back, slot_of, axis=1)

    return (
        returned(layer_block),
        returned(input_grad),
        gain_sums[0],
        qkv_sums[0],
        qkv_sums[1],
        qkv_sums[2],
        output_sum,
        gain_sums[1],
        gate_sum,
        up_sum,
        down_sum,
    )


def solution(mesh):
    in_specs = (
        P(None, None, "dp", ("row", "col")),
        P(),
        P(),
        P(("row", "col")),
        P("row", "col"),
        P("row", "col"),
        P("row", "col"),
        P("col", "row"),
        P(("row", "col")),
        P("row", "col"),
        P("row", "col"),
        P("col", "row"),
        P(None, "dp", None, ("row", "col")),
    )
    out_specs = (
        P(None, None, "dp", ("row", "col")),
        P(None, None, "dp", ("row", "col")),
        P(("row", "col", "dp")),
        P(("row", "dp"), "col"),
        P(("row", "dp"), "col"),
        P(("row", "dp"), "col"),
        P(("col", "dp"), "row"),
        P(("row", "col", "dp")),
        P(("row", "dp"), "col"),
        P(("row", "dp"), "col"),
        P(("col", "dp"), "row"),
    )
    return jax.shard_map(
        per_device, mesh=mesh, in_specs=in_specs, out_specs=out_specs, check_vma=False
    )
```

```python
import math

import jax
import jax.numpy as jnp
from jax import lax
from jax.experimental import pallas as pl
from jax.experimental.pallas import tpu as pltpu
from jax.sharding import PartitionSpec as P

D = 2048
HEADS = 32
HEAD_DIM = 64
SL = 256
MICRO = 2
ROWS = MICRO * SL

EPSILON = 1e-05
ROPE_THETA = 130000.0
MASKED_SCORE = -1000000000.0
F32 = jnp.float32
BF16 = jnp.bfloat16
SWAP = [(0, 1), (1, 0)]


def mm(a, b):
    return jnp.dot(a, b, preferred_element_type=F32)


def mm_nt(a, b):
    return lax.dot_general(a, b, (((1,), (1,)), ((), ())), preferred_element_type=F32)


def mm_tn(a, b):
    return lax.dot_general(a, b, (((0,), (0,)), ((), ())), preferred_element_type=F32)


def rope_tables():
    half = HEAD_DIM // 2
    frequency = jnp.exp(
        jnp.arange(half, dtype=F32) * (-2.0 * math.log(ROPE_THETA) / HEAD_DIM)
    )
    angles = jnp.arange(SL, dtype=F32)[:, None] * frequency[None, :]
    cosine = jnp.cos(angles)
    sine = jnp.sin(angles)
    zero = jnp.zeros_like(sine)
    table_cos = jnp.concatenate([cosine] * 4, axis=1)
    table_first = jnp.concatenate([sine, zero] * 2, axis=1)
    table_second = jnp.concatenate([zero, sine] * 2, axis=1)
    return table_cos, table_first, table_second


def turn(v, cos, first, second):
    ahead = pltpu.roll(v, 128 - HEAD_DIM // 2, 1)
    behind = pltpu.roll(v, HEAD_DIM // 2, 1)
    return v * cos - ahead * first + behind * second


def turn_back(v, cos, first, second):
    ahead = pltpu.roll(v, 128 - HEAD_DIM // 2, 1)
    behind = pltpu.roll(v, HEAD_DIM // 2, 1)
    return v * cos + ahead * first - behind * second


def head_mask(head):
    lane = lax.broadcasted_iota(jnp.int32, (SL, 128), 1)
    return (lane // HEAD_DIM) == head


def softmax_of(q, k, allowed):
    scores = mm_nt(q, k) * HEAD_DIM ** (-0.5)
    scores = jnp.where(allowed, scores, MASKED_SCORE)
    exps = jnp.exp(scores - jnp.max(scores, axis=1, keepdims=True))
    return exps / jnp.sum(exps, axis=1, keepdims=True)


def allowed_of(length):
    query = lax.broadcasted_iota(jnp.int32, (SL, SL), 0)
    key = lax.broadcasted_iota(jnp.int32, (SL, SL), 1)
    return (key <= query) & (key < length)


FREE = pl.CostEstimate(flops=0, bytes_accessed=0, transcendentals=0)
BUSY = pl.CostEstimate(flops=20 * 10**9, bytes_accessed=60 * 10**6, transcendentals=0)


def whole(shape):
    return pl.BlockSpec(shape, lambda *at: (0,) * len(shape), pipeline_mode=pl.Buffered(1))


def attend_kernel(len_ref, qkv_ref, cos_ref, first_ref, second_ref, o_ref, turned_ref):
    cos, first, second = cos_ref[...], first_ref[...], second_ref[...]
    qr = turn(qkv_ref[:, :128], cos, first, second).astype(BF16)
    kr = turn(qkv_ref[:, 128:256], cos, first, second).astype(BF16)
    vr = qkv_ref[:, 256:].astype(BF16)
    turned_ref[:, :128] = qr
    turned_ref[:, 128:256] = kr
    turned_ref[:, 256:] = vr
    allowed = allowed_of(len_ref[pl.program_id(0)])
    out = jnp.zeros((SL, 128), F32)
    for head in range(2):
        mask = head_mask(head)
        probs = softmax_of(jnp.where(mask, qr, jnp.zeros_like(qr)), kr, allowed).astype(BF16)
        out = out + mm(probs, jnp.where(mask, vr, jnp.zeros_like(vr)))
    o_ref[...] = out.astype(BF16)


def head_grads(qr, kr, vr, od, allowed, cos, first, second):
    dq = jnp.zeros((SL, 128), F32)
    dk = jnp.zeros((SL, 128), F32)
    dv = jnp.zeros((SL, 128), F32)
    zero = jnp.zeros_like(qr)
    for head in range(2):
        mask = head_mask(head)
        q_own = jnp.where(mask, qr, zero)
        k_own = jnp.where(mask, kr, zero)
        od_own = jnp.where(mask, od, zero)
        probs = softmax_of(q_own, kr, allowed)
        d_probs = mm_nt(od_own, vr)
        dv = dv + mm_tn(probs.astype(BF16), od_own)
        inner = jnp.sum(probs * d_probs, axis=1, keepdims=True)
        d_scores = (probs * (d_probs - inner)).astype(BF16)
        dq = dq + mm(d_scores, k_own)
        dk = dk + mm_tn(d_scores, q_own)
    scale = HEAD_DIM ** (-0.5)
    return (
        turn_back(dq * scale, cos, first, second).astype(BF16),
        turn_back(dk * scale, cos, first, second).astype(BF16),
        dv.astype(BF16),
    )


def pair_block(width):
    return pl.BlockSpec((SL, width), lambda m, h, lens: (m, h))


TABLE = pl.BlockSpec((SL, 128), lambda m, h, lens: (0, 0))


def attend_forward(lengths, qkv, tables):
    width = qkv.shape[1]
    return pl.pallas_call(
        attend_kernel,
        out_shape=(
            jax.ShapeDtypeStruct((ROWS, width // 3), BF16),
            jax.ShapeDtypeStruct((ROWS, width), BF16),
        ),
        grid_spec=pltpu.PrefetchScalarGridSpec(
            num_scalar_prefetch=1,
            grid=(MICRO, width // 384),
            in_specs=[pair_block(384)] + [TABLE] * 3,
            out_specs=[pair_block(128), pair_block(384)],
        ),
        cost_estimate=FREE,
    )(lengths, qkv, *tables)


def multiply(a, w, transposed, tile, dtype):
    height, depth = a.shape
    width = w.shape[0] if transposed else w.shape[1]

    def kernel(a_ref, w_ref, o_ref):
        form = mm_nt if transposed else mm
        o_ref[...] = form(a_ref[...], w_ref[...]).astype(dtype)

    if transposed:
        w_spec = pl.BlockSpec((tile, depth), lambda j: (j, 0))
    else:
        w_spec = pl.BlockSpec((depth, tile), lambda j: (0, j))
    return pl.pallas_call(
        kernel,
        out_shape=jax.ShapeDtypeStruct((height, width), dtype),
        grid=(width // tile,),
        in_specs=[whole(a.shape), w_spec],
        out_specs=pl.BlockSpec((height, tile), lambda j: (0, j)),
        cost_estimate=FREE,
    )(a, w)


def split_product(parts, w, transposed, tile, cost=FREE):
    count = len(parts)
    height = parts[0].shape[0]
    width = w.shape[0] if transposed else w.shape[1]
    steps = width // tile
    half = steps // 2

    def kernel(*refs):
        form = mm_nt if transposed else mm
        total = form(refs[0][...], refs[count][...])
        for at in range(1, count):
            total = total + form(refs[at][...], refs[count + at][...])
        kept_ref, sent_ref = refs[2 * count :]
        step = pl.program_id(0)

        @pl.when(step < half)
        def _():
            sent_ref[...] = total.astype(BF16)

        @pl.when(step >= half)
        def _():
            kept_ref[...] = total

    def w_spec(at, depth):
        if transposed:
            return pl.BlockSpec((tile, depth), lambda j: (lax.rem(j + half, steps), at))
        return pl.BlockSpec((depth, tile), lambda j: (at, lax.rem(j + half, steps)))

    return pl.pallas_call(
        kernel,
        out_shape=(
            jax.ShapeDtypeStruct((height, width // 2), F32),
            jax.ShapeDtypeStruct((height, width // 2), BF16),
        ),
        grid=(steps,),
        in_specs=[whole(part.shape) for part in parts]
        + [w_spec(at, part.shape[1]) for at, part in enumerate(parts)],
        out_specs=(
            pl.BlockSpec((height, tile), lambda j: (0, jnp.maximum(j - half, 0))),
            pl.BlockSpec((height, tile), lambda j: (0, jnp.minimum(j, half - 1))),
        ),
        cost_estimate=cost,
    )(*parts, *([w] * count))


def feed_kernel(x_ref, gate_ref, up_ref, da_ref, hidden_ref, dg_ref, du_ref):
    x = x_ref[...]
    gate = mm(x, gate_ref[...])
    up = mm(x, up_ref[...])
    da = da_ref[...]
    sigmoid = 1.0 / (1.0 + jnp.exp(-gate))
    swish = gate * sigmoid
    hidden_ref[...] = (swish * up).astype(BF16)
    dg_ref[...] = (da * up * sigmoid * (1.0 + gate * (1.0 - sigmoid))).astype(BF16)
    du_ref[...] = (da * swish).astype(BF16)


def feed_forward(x, pair_w, hidden_grad, tile=256):
    height, depth = x.shape
    width = hidden_grad.shape[1]
    steps = width // tile
    tall = pl.BlockSpec((height, tile), lambda j: (0, j))
    return pl.pallas_call(
        feed_kernel,
        out_shape=(jax.ShapeDtypeStruct((height, width), BF16),) * 3,
        grid=(steps,),
        in_specs=[
            whole(x.shape),
            pl.BlockSpec((depth, tile), lambda j: (0, j)),
            pl.BlockSpec((depth, tile), lambda j: (0, j + steps)),
            tall,
        ],
        out_specs=(tall,) * 3,
        cost_estimate=FREE,
    )(x, pair_w, pair_w, hidden_grad)


def swap_kernel(plan, given, count, *refs):
    weights, outs = refs[:given], refs[given : given + count]
    rest = refs[given + count :]
    held, (send_sem, recv_sem, in_sem, out_sem) = rest[: len(plan)], rest[len(plan) :]
    row = lax.axis_index("row")
    barrier = pltpu.get_barrier_semaphore()
    pl.semaphore_signal(
        barrier, inc=1, device_id={"row": 1 - row}, device_id_type=pl.DeviceIdType.MESH
    )
    remote, local = [], []
    for at, (source, by_rows, out, start, offset, size) in enumerate(plan):
        weight = weights[source]
        height, width = weight.shape

        def part(index):
            if by_rows:
                return weight.at[pl.ds(pl.multiple_of(index * size, size), size), :]
            first = pl.multiple_of(index * (width // 2) + start, 128)
            return weight.at[:, pl.ds(first, size)]

        def place(second):
            if by_rows:
                return outs[out].at[:, pl.ds(second * width, width)]
            return outs[out].at[pl.ds(second * height, height), pl.ds(offset, size)]

        remote.append(
            pltpu.make_async_remote_copy(
                src_ref=part(1 - row),
                dst_ref=place(1),
                send_sem=send_sem.at[at],
                recv_sem=recv_sem.at[at],
                device_id={"row": 1 - row},
                device_id_type=pl.DeviceIdType.MESH,
            )
        )
        local.append(
            (
                pltpu.make_async_copy(part(row), held[at], in_sem.at[at]),
                pltpu.make_async_copy(held[at], place(0), out_sem.at[at]),
            )
        )
    for fetch, _ in local:
        fetch.start()
    pl.semaphore_wait(barrier, 1)
    for copy in remote:
        copy.start()
    for fetch, store in local:
        fetch.wait()
        store.start()
    for _, store in local:
        store.wait()
    for copy in remote:
        copy.wait()


def swap_weights(weights, plan, shapes, identity):
    held = []
    for source, by_rows, _, _, _, size in plan:
        height, width = weights[source].shape
        held.append((size, width) if by_rows else (height, size))
    sems = pltpu.SemaphoreType.DMA((len(plan),))
    return pl.pallas_call(
        lambda *refs: swap_kernel(plan, len(weights), len(shapes), *refs),
        out_shape=[jax.ShapeDtypeStruct(shape, BF16) for shape in shapes],
        in_specs=[pl.BlockSpec(memory_space=pl.ANY)] * len(weights),
        out_specs=[pl.BlockSpec(memory_space=pl.ANY)] * len(shapes),
        scratch_shapes=[pltpu.VMEM(shape, BF16) for shape in held] + [sems] * 4,
        compiler_params=pltpu.CompilerParams(collective_id=identity, has_side_effects=True),
        cost_estimate=FREE,
    )(*weights)


MESH = pl.DeviceIdType.MESH


def greet(*moves):
    barrier = pltpu.get_barrier_semaphore()
    total = 0
    for count, target in moves:
        total = total + count

        @pl.when(count > 0)
        def _():
            pl.semaphore_signal(barrier, inc=1, device_id=target, device_id_type=MESH)

    pl.semaphore_wait(barrier, total)


class ZLine:
    def __init__(self, line, grads, out, stage, came, sems, count, sided):
        self.line, self.grads, self.out, self.stage = line, grads, out, stage
        self.came, self.sems, self.sided = came, sems, sided
        width = grads.shape[1] // count
        self.pieces = [(k, pl.ds(k * width, width)) for k in range(count)]
        self.dp, self.row = lax.axis_index("dp"), lax.axis_index("row")
        self.z = self.dp // 2
        self.last = line - 1
        self.ways = ((0, self.z, 2), (1, self.last - self.z, -2))

    def rows_of(self, dest):
        size = self.grads.shape[0] // self.line
        if self.sided:
            dest = lax.rem(dest + self.line - self.row * (self.line // 2), self.line)
        return pl.ds(pl.multiple_of(dest * size, size), size)

    def copy(self, source, way, step, slot, piece, columns):
        return pltpu.make_async_remote_copy(
            src_ref=source,
            dst_ref=self.came.at[way, slot, :, columns],
            send_sem=self.sems.at[0, way, slot, piece],
            recv_sem=self.sems.at[1, way, slot, piece],
            device_id={"dp": self.dp + step},
            device_id_type=MESH,
        )

    def arrived(self, way, step, slot, piece, columns):
        held = self.came.at[way, slot, :, columns]
        self.copy(held, way, step, slot, piece, columns).wait_recv()
        return held

    def run(self, start, stop):
        def one_step(slot, _):
            for piece, columns in self.pieces:
                for way, place, step in self.ways:
                    far = self.last - slot + place
                    dest = far if step > 0 else self.last - far

                    @pl.when((place == 0) & (place < self.last))
                    def _():
                        source = self.grads.at[self.rows_of(dest), columns]
                        self.copy(source, way, step, slot, piece, columns).start()

                    @pl.when((place > 0) & (place <= slot))
                    def _():
                        held = self.arrived(way, step, slot - 1, piece, columns)

                        @pl.when(place < self.last)
                        def _():
                            held[...] = (
                                held[...].astype(F32)
                                + self.grads[self.rows_of(dest), columns].astype(F32)
                            ).astype(BF16)
                            self.copy(held, way, step, slot, piece, columns).start()

            return 0

        lax.fori_loop(start, stop, one_step, 0)

    def finish(self):
        own = self.rows_of(self.z)
        for piece, columns in self.pieces:
            self.stage[:, columns] = self.grads[own, columns].astype(F32)
            for way, place, step in self.ways:

                @pl.when(place > 0)
                def _():
                    held = self.arrived(way, step, self.last - 1, piece, columns)
                    self.stage[:, columns] += held[...].astype(F32)

        def settle(slot, _):
            for piece, columns in self.pieces:
                for way, place, step in self.ways:

                    @pl.when((place <= slot) & (place < self.last))
                    def _():
                        held = self.came.at[way, slot, :, columns]
                        self.copy(held, way, step, slot, piece, columns).wait_send()

            return 0

        lax.fori_loop(0, self.last, settle, 0)

    def moves(self):
        return (
            (jnp.minimum(self.z, 1), {"dp": self.dp - 2}),
            (jnp.minimum(self.last - self.z, 1), {"dp": self.dp + 2}),
        )


def tiles_loop(width, tile, body):
    def one(j, _):
        body(pl.ds(pl.multiple_of(j * tile, tile), tile), j * tile)
        return 0

    lax.fori_loop(0, width // tile, one, 0)


def tail_kernel(
    line,
    gate_grads,
    up,
    up_row,
    second_mine,
    second_came,
    dqkv,
    dqkv_row,
    first_mine,
    first_came,
    branch,
    mixed_mine,
    mixed_came,
    mixed_row,
    mixed_came_row,
    gate_out,
    up_out,
    qkv_out,
    output_out,
    gate_z,
    up_z,
    qkv_z,
    output_z,
    up_grads,
    qkv_grads,
    output_grads,
    up_came,
    up_came_row,
    dqkv_came,
    dqkv_came_row,
    branch_came,
    turned_left,
    gate_stage,
    up_stage,
    qkv_stage,
    output_stage,
    gate_sems,
    up_sems,
    qkv_sems,
    output_sems,
    swap_sems,
    out_sems,
):
    dp, row = lax.axis_index("dp"), lax.axis_index("row")
    partner = dp + 1 - 2 * lax.rem(dp, 2)
    gate_line = ZLine(line, gate_grads, gate_out, gate_stage, gate_z, gate_sems, 4, False)
    up_line = ZLine(line, up_grads, up_out, up_stage, up_z, up_sems, 4, False)
    qkv_line = ZLine(line, qkv_grads, qkv_out, qkv_stage, qkv_z, qkv_sems, 3, False)
    output_line = ZLine(line, output_grads, output_out, output_stage, output_z, output_sems, 1, True)

    def swap(source, target, at, device):
        return pltpu.make_async_remote_copy(
            src_ref=source,
            dst_ref=target,
            send_sem=swap_sems.at[0, at],
            recv_sem=swap_sems.at[1, at],
            device_id=device,
            device_id_type=MESH,
        )

    up_x = swap(up, up_came, 0, {"dp": partner})
    branch_x = swap(branch, branch_came, 1, {"dp": partner})
    dqkv_x = swap(dqkv, dqkv_came, 2, {"dp": partner})
    up_across = swap(up_came, up_came_row, 3, {"row": 1 - row})
    dqkv_across = swap(dqkv_came, dqkv_came_row, 4, {"row": 1 - row})

    def store(line_of, at):
        copy = pltpu.make_async_copy(line_of.stage, line_of.out, out_sems.at[at])
        copy.start()
        return copy

    greet(*gate_line.moves(), (jnp.int32(1), {"dp": partner}), (jnp.int32(1), {"row": 1 - row}))
    gate_line.run(0, 1)
    up_x.start()
    branch_x.start()
    dqkv_x.start()

    depth = second_mine.shape[0]
    turned_left[:, :depth] = second_mine[...].T
    turned_left[:, depth:] = second_came[...].T
    gate_line.run(1, 2)

    def wide(target, shift, mine, came):
        def body(columns, start):
            total = mm(turned_left[:, :depth], mine[:, columns])
            total = total + mm(turned_left[:, depth:], came[:, columns])
            tile = total.shape[1]
            target[:, pl.ds(pl.multiple_of(shift + start, tile), tile)] = total.astype(BF16)

        tiles_loop(mine.shape[1], 512, body)

    up_x.wait_recv()
    up_across.start()
    gate_line.run(2, line - 1)
    wide(up_grads, 0, up, up_came)
    up_across.wait_recv()
    wide(up_grads, up.shape[1], up_row, up_came_row)
    up_line.run(0, 1)
    gate_line.finish()
    gate_store = store(gate_line, 0)

    turned_left[:, :depth] = first_mine[...].T
    turned_left[:, depth:] = first_came[...].T
    branch_x.wait_recv()

    def side(start, mine, came):
        def body(columns, _):
            total = mm_tn(mine[...], branch[:, columns]) + mm_tn(came[...], branch_came[:, columns])
            output_grads[pl.ds(start, mine.shape[1]), columns] = total.astype(BF16)

        tiles_loop(branch.shape[1], 512, body)

    side(0, mixed_mine, mixed_came)
    side(mixed_mine.shape[1], mixed_row, mixed_came_row)
    output_line.run(0, 1)
    up_line.run(1, 2)
    dqkv_x.wait_recv()
    dqkv_across.start()
    wide(qkv_grads, 0, dqkv, dqkv_came)
    dqkv_across.wait_recv()
    wide(qkv_grads, dqkv.shape[1], dqkv_row, dqkv_came_row)
    qkv_line.run(0, 1)
    output_line.run(1, 2)
    up_line.run(2, line - 1)
    qkv_line.run(1, 2)
    output_line.run(2, line - 1)
    up_line.finish()
    up_store = store(up_line, 1)
    qkv_line.run(2, line - 1)
    output_line.finish()
    output_store = store(output_line, 2)
    qkv_line.finish()
    qkv_store = store(qkv_line, 3)
    for copy in (up_x, branch_x, dqkv_x, up_across, dqkv_across):
        copy.wait_send()
    for copy in (gate_store, up_store, output_store, qkv_store):
        copy.wait()


def stream(source_of, slots_of, sems, count, body):
    def fetch(j, slot):
        return [
            pltpu.make_async_copy(source, target, sems.at[slot, k])
            for k, (source, target) in enumerate(zip(source_of(j), slots_of(slot)))
        ]

    for copy in fetch(0, 0):
        copy.start()

    def one(j, _):
        slot = lax.rem(j, 2)

        @pl.when(j + 1 < count)
        def _():
            for copy in fetch(j + 1, 1 - slot):
                copy.start()

        for copy in fetch(j, slot):
            copy.wait()
        body(j, slot)
        return 0

    lax.fori_loop(0, count, one, 0)


def rows_loop(body, size=64):
    def one(j, _):
        body(pl.ds(pl.multiple_of(j * size, size), size))
        return 0

    lax.fori_loop(0, ROWS // size, one, 0)


def chain_kernel(
    line,
    hidden,
    gate_grad,
    up_grad,
    second_mine,
    second_theirs,
    top_half,
    top_came,
    mixed_came,
    pair_w,
    down_w,
    qkv_w,
    out_w,
    turned,
    middle,
    inverse_first,
    inverse_second,
    gain_second,
    gain_first,
    x_own,
    key_live,
    cos,
    first,
    second,
    down_out,
    gate_grads,
    second_came,
    up_row,
    dqkv,
    dqkv_row,
    branch,
    mixed_came_row,
    both_out,
    pieces_out,
    gate_row,
    gate_came,
    gate_came_row,
    tiles,
    tall_tiles,
    pair_tiles,
    kept,
    sent,
    row_came,
    summed,
    col_came,
    block_sent,
    block_came,
    hidden_row,
    hidden_came,
    hidden_came_row,
    branch_row,
    dots,
    down_grads,
    down_z,
    middle_own,
    layer_own,
    first_own,
    mixed_grad,
    turned_left,
    feed_sum,
    attention_sum,
    swap_sems,
    piece_sems,
    tile_sems,
    down_sems,
    copy_sems,
):
    dp, row, col = lax.axis_index("dp"), lax.axis_index("row"), lax.axis_index("col")
    x = lax.rem(dp, 2)
    partner = {"dp": dp + 1 - 2 * x}
    across = {"row": 1 - row}
    beside = {"col": 1 - col}
    down_line = ZLine(line, down_grads, down_out, None, down_z, down_sems, 4, True)
    half = D // 2
    block = D // 4
    quarter = hidden.shape[1]
    pending = []

    def swap(source, target, at, device, sems=swap_sems):
        copy = pltpu.make_async_remote_copy(
            src_ref=source,
            dst_ref=target,
            send_sem=sems.at[0, at],
            recv_sem=sems.at[1, at],
            device_id=device,
            device_id_type=MESH,
        )
        return copy

    def begin(copy):
        copy.start()
        pending.append(copy)
        return copy

    greet(
        *down_line.moves(),
        (jnp.int32(1), partner),
        (jnp.int32(1), across),
        (jnp.int32(1), beside),
    )

    per = line // 2
    width = quarter // line

    def hidden_part(index, at):
        return hidden.at[:, pl.ds(pl.multiple_of((2 * at + index) * width, width), width)]

    to_x, to_row, on_row = [], [], []
    for at in range(per):
        there = pl.ds(at * width, width)
        to_x.append(
            begin(swap(hidden_part(1 - x, at), hidden_came.at[:, there], at, partner, piece_sems))
        )
    for at in range(per):
        there = pl.ds(at * width, width)
        to_row.append(
            begin(swap(hidden_part(x, at), hidden_row.at[:, there], per + at, across, piece_sems))
        )
    second_x = begin(swap(second_theirs, second_came, 0, partner))
    gate_x = begin(swap(gate_grad, gate_came, 1, partner))

    def nt_product(w, depth, start, body):
        stream(
            lambda j: [w.at[pl.ds(pl.multiple_of(start + j * 256, 256), 256), :]],
            lambda slot: [tiles.at[slot, :, pl.ds(0, depth)]],
            tile_sems,
            half // 256,
            body,
        )

    def columns_at(j, size=256):
        return pl.ds(pl.multiple_of(j * size, size), size)

    def pair_body(target, dtype):
        def body(j, slot):
            total = mm_nt(gate_grad[...], tiles[slot, :, :quarter])
            total = total + mm_nt(up_grad[...], tiles[slot, :, quarter:])
            target[:, columns_at(j)] = total.astype(dtype)

        return body

    nt_product(pair_w, 2 * quarter, half, pair_body(sent, BF16))
    pair_r = begin(swap(sent, row_came.at[0], 2, across))
    nt_product(pair_w, 2 * quarter, 0, pair_body(kept, F32))
    pair_r.wait_recv()

    def join_pair(rows):
        summed[rows, :] = (kept[rows, :] + row_came[0, rows, :].astype(F32)).astype(BF16)

    rows_loop(join_pair)
    pair_c = begin(swap(summed, col_came, 3, beside))
    gate_r = begin(swap(gate_grad, gate_row, 4, across))
    up_r = begin(swap(up_grad, up_row, 5, across))
    mixed_r = begin(swap(mixed_came, mixed_came_row, 6, across))

    def down_product(start, target, dtype):
        def body(j, slot):
            target[:, columns_at(j)] = mm(hidden[...], tall_tiles[slot]).astype(dtype)

        stream(
            lambda j: [down_w.at[:, pl.ds(pl.multiple_of(start + j * 256, 256), 256)]],
            lambda slot: [tall_tiles.at[slot]],
            tile_sems,
            half // 256,
            body,
        )

    pair_r.wait_send()
    pending[:] = [copy for copy in pending if copy is not pair_r]
    down_product(half, sent, BF16)
    layer_r = begin(swap(sent, row_came.at[1], 7, across))
    down_product(0, kept, F32)
    layer_r.wait_recv()

    def mine_of(value):
        return jnp.where(col == 0, value[:, :block], value[:, block:])

    def theirs_of(value):
        return jnp.where(col == 0, value[:, block:], value[:, :block])

    def join_layer(rows):
        total = kept[rows, :] + row_came[1, rows, :].astype(F32)
        layer_own[rows, :] = mine_of(total)
        block_sent[0, rows, :] = theirs_of(total).astype(BF16)

    rows_loop(join_layer)
    layer_c = begin(swap(block_sent.at[0], block_came.at[0], 8, beside))
    middle_in = pltpu.make_async_copy(middle, kept, copy_sems.at[0])
    middle_in.start()

    for copy in to_x:
        copy.wait_recv()
    for at in range(per):
        there = pl.ds(at * width, width)
        on_row.append(
            begin(
                swap(
                    hidden_came.at[:, there],
                    hidden_came_row.at[:, there],
                    2 * per + at,
                    across,
                    piece_sems,
                )
            )
        )

    def down_grad(part, left_of, came):
        def body(columns, _):
            for at in range(per):
                there = pl.ds(at * width, width)
                total = mm_tn(left_of(at)[...], top_half[:, columns])
                total = total + mm_tn(came[:, there], top_came[:, columns])
                down_grads[pl.ds((part * per + at) * width, width), columns] = total.astype(BF16)

        tiles_loop(half, 512, body)

    down_grad(0, lambda at: hidden_part(x, at), hidden_came)
    for copy in to_row + on_row:
        copy.wait_recv()
    down_grad(1, lambda at: hidden_row.at[:, pl.ds(at * width, width)], hidden_came_row)
    down_line.run(0, 1)

    middle_in.wait()
    pair_c.wait_recv()
    feed_sum[...] = jnp.zeros_like(feed_sum)

    def second_grads(rows):
        grad = summed[rows, :].astype(F32) + col_came[rows, :].astype(F32)
        return grad, grad * gain_second[...]

    def norm_first_pass(rows):
        grad, scaled = second_grads(rows)
        held = kept[rows, :]
        feed_sum[...] += jnp.sum(grad * held * inverse_second[rows, :], axis=0, keepdims=True)
        total = jnp.sum(scaled * held, axis=1, keepdims=True)
        dots[0, rows, :] = jnp.broadcast_to(total, (total.shape[0], 128))

    rows_loop(norm_first_pass)
    dot_r = begin(swap(dots.at[0], dots.at[1], 9, across))
    dot_r.wait_recv()

    def norm_second_pass(rows):
        _, scaled = second_grads(rows)
        held = kept[rows, :]
        inverse = inverse_second[rows, :]
        dot = dots[0, rows, :1] + dots[1, rows, :1]
        grad = (
            top_half[rows, :].astype(F32) + scaled * inverse - held * (inverse**3 * dot / D)
        )
        branch[rows, :] = grad.astype(BF16)
        middle_own[rows, :] = mine_of(grad)
        layer_own[rows, :] += mine_of(held)

    rows_loop(norm_second_pass)
    branch_r = begin(swap(branch, branch_row, 10, across))
    branch_r.wait_recv()

    def mixed_body(j, slot):
        total = mm_nt(branch[...], tiles[slot, :, :half])
        total = total + mm_nt(branch_row[...], tiles[slot, :, half:D])
        mixed_grad[:, columns_at(j)] = total.astype(BF16)

    stream(
        lambda j: [out_w.at[pl.ds(pl.multiple_of(j * 256, 256), 256), :]],
        lambda slot: [tiles.at[slot, :, pl.ds(0, D)]],
        tile_sems,
        out_w.shape[0] // 256,
        mixed_body,
    )
    down_line.run(1, 2)
    pairs = turned.shape[1] // 384
    lower = lax.broadcasted_iota(jnp.int32, (SL, SL), 1) <= lax.broadcasted_iota(
        jnp.int32, (SL, SL), 0
    )

    def attend(at, _):
        micro, pair = at // pairs, lax.rem(at, pairs)
        rows = pl.ds(pl.multiple_of(micro * SL, SL), SL)

        def part(kind):
            return pl.ds(pl.multiple_of(pair * 384 + kind * 128, 128), 128)

        allowed = lower & (key_live[pl.ds(micro, 1), :] > 0.5)
        dq, dk, dv = head_grads(
            turned[rows, part(0)],
            turned[rows, part(1)],
            turned[rows, part(2)],
            mixed_grad[rows, pl.ds(pl.multiple_of(pair * 128, 128), 128)],
            allowed,
            cos[...],
            first[...],
            second[...],
        )
        dqkv[rows, part(0)] = dq
        dqkv[rows, part(1)] = dk
        dqkv[rows, part(2)] = dv
        return 0

    lax.fori_loop(0, MICRO * pairs, attend, 0)

    def first_body(target, dtype):
        def body(j, slot):
            total = mm_nt(dqkv[...], tiles[slot, :, : dqkv.shape[1]])
            target[:, columns_at(j)] = total.astype(dtype)

        return body

    layer_r.wait_send()
    pending[:] = [copy for copy in pending if copy is not layer_r]
    nt_product(qkv_w, dqkv.shape[1], half, first_body(sent, BF16))
    first_r = begin(swap(sent, row_came.at[2], 11, across))
    dqkv_r = begin(swap(dqkv, dqkv_row, 12, across))
    nt_product(qkv_w, dqkv.shape[1], 0, first_body(kept, F32))
    first_r.wait_recv()

    def join_first(rows):
        total = kept[rows, :] + row_came[2, rows, :].astype(F32)
        first_own[rows, :] = mine_of(total)
        block_sent[1, rows, :] = theirs_of(total).astype(BF16)

    rows_loop(join_first)
    first_c = begin(swap(block_sent.at[1], block_came.at[1], 13, beside))
    down_line.run(2, line - 1)

    second_x.wait_recv()
    depth = second_mine.shape[0]
    turned_left[:, :depth] = second_mine[...].T
    turned_left[:, depth:] = second_came[...].T
    gate_x.wait_recv()
    gate_on = begin(swap(gate_came, gate_came_row, 14, across))

    def gate_part(shift, sources, values):
        def body(j, slot):
            mine, came = values(j, slot)
            total = mm(turned_left[:, :depth], mine) + mm(turned_left[:, depth:], came)
            there = pl.ds(pl.multiple_of(shift + j * 512, 512), 512)
            gate_grads[:, there] = total.astype(BF16)

        stream(
            lambda j: [source.at[:, columns_at(j, 512)] for source in sources],
            lambda slot: [pair_tiles.at[slot, k] for k in range(len(sources))],
            tile_sems,
            quarter // 512,
            body,
        )

    gate_part(
        0,
        [gate_came],
        lambda j, slot: (gate_grad[:, columns_at(j, 512)], pair_tiles[slot, 0]),
    )
    gate_r.wait_recv()
    gate_on.wait_recv()
    gate_part(
        quarter,
        [gate_row, gate_came_row],
        lambda j, slot: (pair_tiles[slot, 0], pair_tiles[slot, 1]),
    )

    layer_c.wait_recv()
    first_c.wait_recv()
    attention_sum[...] = jnp.zeros_like(attention_sum)

    def last_first_pass(rows):
        layer = layer_own[rows, :] + block_came[0, rows, :].astype(F32)
        both_out[rows, :] = layer.astype(BF16)
        grad = first_own[rows, :] + block_came[1, rows, :].astype(F32)
        first_own[rows, :] = grad
        held = x_own[rows, :].astype(F32)
        attention_sum[...] += jnp.sum(grad * held * inverse_first[rows, :], axis=0, keepdims=True)
        total = jnp.sum(grad * gain_first[...] * held, axis=1, keepdims=True)
        dots[2, rows, :] = jnp.broadcast_to(total, (total.shape[0], 128))

    rows_loop(last_first_pass)
    dot_r = begin(swap(dots.at[2], dots.at[3], 15, across))
    dot_r.wait_recv()

    def add_dots(rows):
        dots[4, rows, :] = dots[2, rows, :] + dots[3, rows, :]

    rows_loop(add_dots)
    dot_c = begin(swap(dots.at[4], dots.at[5], 16, beside))
    dot_c.wait_recv()

    def last_second_pass(rows):
        inverse = inverse_first[rows, :]
        dot = dots[4, rows, :1] + dots[5, rows, :1]
        scaled = first_own[rows, :] * gain_first[...]
        held = x_own[rows, :].astype(F32)
        grad = middle_own[rows, :] + scaled * inverse - held * (inverse**3 * dot / D)
        below = pl.ds(pl.multiple_of(rows.start + ROWS, rows.size), rows.size)
        both_out[below, :] = grad.astype(BF16)

    rows_loop(last_second_pass)
    pieces_out[0:1, :] = attention_sum[...]
    pieces_out[1:2, :] = mine_of(feed_sum[...])

    down_line.stage = kept.at[pl.ds(0, down_grads.shape[0] // line), :]
    down_line.finish()
    down_store = pltpu.make_async_copy(down_line.stage, down_out, copy_sems.at[1])
    down_store.start()
    for copy in (up_r, mixed_r, dqkv_r):
        copy.wait_recv()
    for copy in pending:
        copy.wait_send()
    down_store.wait()


def chain(line, identity, *values):
    hidden, gate_grad = values[:2]
    quarter = hidden.shape[1]
    narrow = values[3].shape[1]
    mixed_width = values[7].shape[1]
    qkv_width = values[12].shape[1]
    half, block = D // 2, D // 4
    rows = quarter // 2
    vmem = pl.BlockSpec(memory_space=pltpu.VMEM)
    anywhere = pl.BlockSpec(memory_space=pl.ANY)
    outside = {8, 9, 10, 11, 13}

    def array(*shape, dtype=BF16):
        return jax.ShapeDtypeStruct(shape, dtype)

    def buffer(*shape, dtype=BF16):
        return pltpu.VMEM(shape, dtype)

    outs = [
        (array(2 * rows // line, half, dtype=F32), anywhere),
        (array(narrow, 2 * quarter), vmem),
        (array(ROWS, narrow), vmem),
        (array(ROWS, quarter), anywhere),
        (array(ROWS, qkv_width), vmem),
        (array(ROWS, qkv_width), anywhere),
        (array(ROWS, half), vmem),
        (array(ROWS, mixed_width), anywhere),
        (array(2 * ROWS, block), vmem),
        (array(2, block, dtype=F32), vmem),
        (array(ROWS, quarter), anywhere),
        (array(ROWS, quarter), anywhere),
        (array(ROWS, quarter), anywhere),
    ]
    sem = pltpu.SemaphoreType.DMA
    return pl.pallas_call(
        lambda *refs: chain_kernel(line, *refs),
        out_shape=[shape for shape, _ in outs],
        in_specs=[anywhere if k in outside else vmem for k in range(len(values))],
        out_specs=[place for _, place in outs],
        scratch_shapes=[
            buffer(2, 256, 2 * quarter),
            buffer(2, quarter, 256),
            buffer(2, 2, ROWS, 512),
            buffer(ROWS, half, dtype=F32),
            buffer(ROWS, half),
            buffer(3, ROWS, half),
            buffer(ROWS, half),
            buffer(ROWS, half),
            buffer(2, ROWS, block),
            buffer(2, ROWS, block),
            buffer(ROWS, rows),
            buffer(ROWS, rows),
            buffer(ROWS, rows),
            buffer(ROWS, half),
            buffer(6, ROWS, 128, dtype=F32),
            buffer(2 * rows, half),
            buffer(2, line - 1, 2 * rows // line, half),
            buffer(ROWS, block, dtype=F32),
            buffer(ROWS, block, dtype=F32),
            buffer(ROWS, block, dtype=F32),
            buffer(ROWS, qkv_width // 3),
            buffer(narrow, 2 * ROWS),
            buffer(1, half, dtype=F32),
            buffer(1, block, dtype=F32),
            sem((2, 17)),
            sem((2, 3 * (line // 2))),
            sem((2, 2)),
            sem((2, 2, line - 1, 4)),
            sem((2,)),
        ],
        compiler_params=pltpu.CompilerParams(
            collective_id=identity, has_side_effects=True, vmem_limit_bytes=67043328
        ),
        cost_estimate=FREE,
    )(*values)


def tail_sums(line, identity, *values):
    (gate_grads, up, _, _, _, dqkv, _, _, _, branch) = values[:10]
    rows = gate_grads.shape[0]
    side_rows = 2 * values[10].shape[1]
    tokens = up.shape[0]
    widths = (gate_grads.shape[1], gate_grads.shape[1], 2 * dqkv.shape[1], branch.shape[1])
    heights = (rows, rows, rows, side_rows)
    pieces = (4, 4, 3, 1)
    sizes = [(h // line, w) for h, w in zip(heights, widths)]
    vmem = pl.BlockSpec(memory_space=pltpu.VMEM)

    def buffer(*shape):
        return pltpu.VMEM(shape, BF16)

    return pl.pallas_call(
        lambda *refs: tail_kernel(line, *refs),
        out_shape=[jax.ShapeDtypeStruct(size, F32) for size in sizes],
        in_specs=[vmem] * len(values),
        out_specs=[pl.BlockSpec(memory_space=pl.ANY)] * 4,
        scratch_shapes=[buffer(2, line - 1, *size) for size in sizes]
        + [buffer(h, w) for h, w in zip(heights[1:], widths[1:])]
        + [buffer(*up.shape)] * 2
        + [buffer(*dqkv.shape)] * 2
        + [buffer(*branch.shape)]
        + [buffer(rows, 2 * tokens)]
        + [pltpu.VMEM(size, F32) for size in sizes]
        + [pltpu.SemaphoreType.DMA((2, 2, line - 1, count)) for count in pieces]
        + [pltpu.SemaphoreType.DMA((2, 5)), pltpu.SemaphoreType.DMA((4,))],
        compiler_params=pltpu.CompilerParams(
            collective_id=identity, has_side_effects=True, vmem_limit_bytes=67043328
        ),
        cost_estimate=FREE,
    )(*values)


def per_device(
    tokens,
    lengths,
    deal_order,
    attention_gain,
    query_weight,
    key_weight,
    value_weight,
    output_weight,
    feed_gain,
    gate_weight,
    up_weight,
    down_weight,
    cotangent,
):
    groups = lax.axis_size("dp")
    line = groups // 2
    dp = lax.axis_index("dp")
    row = lax.axis_index("row")
    col = lax.axis_index("col")
    z, x = dp // 2, dp % 2
    half = D // 2
    block = D // 4

    def over_row(v):
        return lax.ppermute(v, "row", SWAP)

    def over_col(v):
        return lax.ppermute(v, "col", SWAP)

    def over_x(v):
        return lax.ppermute(v, "dp", [(i, i ^ 1) for i in range(groups)])

    def ordered(own, other, index, axis=-1):
        return jnp.where(
            index == 0,
            jnp.concatenate([own, other], axis=axis),
            jnp.concatenate([other, own], axis=axis),
        )

    def x_parts(v, width):
        even = jnp.concatenate(
            [v[:, s : s + width] for s in range(0, v.shape[1], 2 * width)], axis=1
        )
        odd = jnp.concatenate(
            [v[:, s : s + width] for s in range(width, v.shape[1], 2 * width)], axis=1
        )
        return jnp.where(x == 0, even, odd), jnp.where(x == 0, odd, even)

    token = []

    def ordered_after(*values):
        out = lax.optimization_barrier(tuple(values) + tuple(token))
        return out[: len(values)] if len(values) > 1 else out[0]

    def mark(value):
        token[:] = [value]
        return value

    def arrive(*values):
        out = ordered_after(*values)
        mark(out[0] if len(values) > 1 else out)
        return out

    def all_sum(v):
        if groups & (groups - 1):
            return lax.psum(v, "dp")
        reach = 1
        while reach < groups:
            v = v + lax.ppermute(v, "dp", [(i, i ^ reach) for i in range(groups)])
            reach *= 2
        return v

    gathered = jnp.take_along_axis(tokens, deal_order[:, :, None, None], axis=1)
    gathered = mark(lax.optimization_barrier(gathered))
    dealt = lax.all_to_all(gathered, "dp", split_axis=1, concat_axis=2, tiled=True)
    own_order = lax.dynamic_slice_in_dim(deal_order, dp, 1, 1)
    own_lengths = jnp.take_along_axis(lengths, own_order, axis=1)[:, 0]
    tables = rope_tables()
    live = (jnp.arange(SL, dtype=jnp.int32)[None, :] < own_lengths[:, None]).reshape(ROWS, 1)
    key_live = live.reshape(MICRO, SL).astype(F32)
    top_block = jnp.where(live, cotangent.reshape(ROWS, block), 0.0).astype(BF16)

    gains = jnp.stack([attention_gain, feed_gain])
    gains_half = ordered(gains, over_col(gains), col)
    gains_other = over_row(gains_half)
    gains_full = jnp.concatenate([gains_half, gains_other], axis=1)

    top_col = over_col(top_block)
    quarter = gate_weight.shape[1] // 2
    gate_weight, up_weight = ordered_after(gate_weight, up_weight)
    (pair_w,) = swap_weights(
        (gate_weight, up_weight),
        ((0, False, 0, 0, 0, quarter), (1, False, 0, 0, quarter, quarter)),
        ((D, 2 * quarter),),
        0,
    )
    mark(pair_w)
    x_block = arrive(dealt).reshape(ROWS, block)
    x_came = over_col(x_block)
    heads = query_weight.shape[1] // 2
    query_weight, key_weight, value_weight, output_weight = ordered_after(
        query_weight, key_weight, value_weight, output_weight
    )
    plan = [
        (kind, False, 0, at, 3 * at + 128 * kind, 128)
        for kind in range(3)
        for at in range(0, heads, 128)
    ]
    qkv_w, out_w = swap_weights(
        (query_weight, key_weight, value_weight, output_weight),
        tuple(plan) + ((3, True, 1, 0, 0, heads),),
        ((D, 3 * heads), (heads, D)),
        1,
    )
    mark(qkv_w)
    top_half = ordered(top_block, arrive(top_col), col)
    top_half = mark(lax.optimization_barrier(top_half))
    x_half = ordered(x_block, arrive(x_came), col)
    x_half = mark(lax.optimization_barrier(x_half))
    top_came = over_x(top_half)
    top_row = over_row(top_half)

    x_other = arrive(over_row(x_half))
    x_full = jnp.concatenate([x_half, x_other], axis=1).astype(F32)
    inverse_first = lax.rsqrt(jnp.mean(x_full * x_full, axis=1, keepdims=True) + EPSILON)
    normed_first = (x_full * inverse_first * gains_full[0][None, :]).astype(BF16)
    normed_first = mark(lax.optimization_barrier(normed_first))
    qkv = multiply(normed_first, qkv_w, False, 384, F32)
    mixed, turned = attend_forward(own_lengths, qkv, tables)
    kept, sent = split_product([mixed], out_w, False, 512)
    mark(sent)
    came = arrive(over_row(sent))
    summed = (kept + came.astype(F32)).astype(BF16)
    summed = mark(lax.optimization_barrier(summed))
    summed_other = over_col(summed)
    top_row = arrive(top_row)
    narrow = half // groups
    first_mine, first_theirs = x_parts(normed_first[:, :half], narrow)
    top_full = jnp.concatenate([top_half, top_row], axis=1)
    (down_w,) = swap_weights(
        (ordered_after(down_weight),),
        ((0, True, 0, 0, 0, down_weight.shape[0] // 2),),
        ((down_weight.shape[0] // 2, D),),
        2,
    )
    hidden_grad = mark(multiply(top_full, down_w, True, 512, F32))
    top_came = arrive(top_came)
    mixed_mine, mixed_theirs = x_parts(mixed, 2 * mixed.shape[1] // groups)
    first_came = over_x(ordered_after(first_theirs))
    mixed_came = over_x(ordered_after(mixed_theirs))
    mixed_row = over_row(mixed_mine)
    summed_other = arrive(summed_other)
    middle = x_half.astype(F32) + (summed.astype(F32) + summed_other.astype(F32))

    middle_low = middle.astype(BF16)
    middle_low, middle = lax.optimization_barrier((middle_low, middle))
    mark(middle_low)
    middle_other = arrive(over_row(middle_low))
    middle_full = jnp.concatenate([middle_low, middle_other], axis=1).astype(F32)
    inverse_second = lax.rsqrt(
        jnp.mean(middle_full * middle_full, axis=1, keepdims=True) + EPSILON
    )
    normed_second = (middle_full * inverse_second * gains_full[1][None, :]).astype(BF16)
    normed_second = mark(lax.optimization_barrier(normed_second))
    hidden, gate_grad, up_grad = feed_forward(normed_second, pair_w, hidden_grad)
    mark(hidden)
    first_came, mixed_came, mixed_row = arrive(first_came, mixed_came, mixed_row)

    def own_block(v):
        return lax.dynamic_slice_in_dim(v, col * block, block, 1)

    second_mine, second_theirs = x_parts(normed_second[:, :half], narrow)
    (
        down_sum,
        gate_grads,
        second_came,
        up_row,
        dqkv,
        dqkv_row,
        branch,
        mixed_came_row,
        both,
        pieces,
        _,
        _,
        _,
    ) = chain(
        line,
        4,
        *ordered_after(
            hidden,
            gate_grad,
            up_grad,
            second_mine,
            second_theirs,
            top_half,
            top_came,
            mixed_came,
            pair_w,
            down_w,
            qkv_w,
            out_w,
            turned,
            middle,
            inverse_first,
            inverse_second,
            gains_half[1:],
            own_block(gains_half)[:1],
            x_block,
            key_live,
            *tables,
        ),
    )
    mark(both)

    gate_sum, up_sum, qkv_sum, output_sum = tail_sums(
        line,
        3,
        *ordered_after(
            gate_grads,
            up_grad,
            up_row,
            second_mine,
            second_came,
            dqkv,
            dqkv_row,
            first_mine,
            first_came,
            branch,
            mixed_mine,
            mixed_came,
            mixed_row,
            mixed_came_row,
        ),
    )
    mark(output_sum)
    gate_sum = ordered(gate_sum[:, :quarter], gate_sum[:, quarter:], row)
    up_sum = ordered(up_sum[:, :quarter], up_sum[:, quarter:], row)
    qkv_sum = ordered(qkv_sum[:, : 3 * heads], qkv_sum[:, 3 * heads :], row)
    qkv_sums = [
        jnp.concatenate(
            [qkv_sum[:, s : s + 128] for s in range(128 * kind, 6 * heads, 384)], axis=1
        )
        for kind in range(3)
    ]

    gain_sums = all_sum(pieces)
    gain_size = block // groups
    gain_sums = lax.dynamic_slice_in_dim(gain_sums, dp * gain_size, gain_size, 1)

    slot_of = jnp.argsort(deal_order, axis=1)[:, :, None, None]
    back = lax.all_to_all(
        both.reshape(2 * MICRO, 1, SL, block), "dp", split_axis=2, concat_axis=1, tiled=True
    )
    back = ordered_after(back)
    layer_output = jnp.take_along_axis(back[:MICRO], slot_of, axis=1)
    tokens_grad = jnp.take_along_axis(back[MICRO:], slot_of, axis=1)

    return (
        layer_output,
        tokens_grad,
        gain_sums[0],
        qkv_sums[0],
        qkv_sums[1],
        qkv_sums[2],
        output_sum,
        gain_sums[1],
        gate_sum,
        up_sum,
        down_sum,
    )


def solution(mesh):
    in_specs = (
        P(None, None, "dp", ("row", "col")),
        P(),
        P(),
        P(("row", "col")),
        P("row", "col"),
        P("row", "col"),
        P("row", "col"),
        P("col", "row"),
        P(("row", "col")),
        P("row", "col"),
        P("row", "col"),
        P("col", "row"),
        P(None, "dp", None, ("row", "col")),
    )
    out_specs = (
        P(None, None, "dp", ("row", "col")),
        P(None, None, "dp", ("row", "col")),
        P(("row", "col", "dp")),
        P(("row", "dp"), "col"),
        P(("row", "dp"), "col"),
        P(("row", "dp"), "col"),
        P(("col", "dp"), "row"),
        P(("row", "col", "dp")),
        P(("row", "dp"), "col"),
        P(("row", "dp"), "col"),
        P(("col", "dp"), "row"),
    )
    return jax.shard_map(
        per_device, mesh=mesh, in_specs=in_specs, out_specs=out_specs, check_vma=False
    )
```

```python
import math

import jax
import jax.numpy as jnp
from jax import lax
from jax.experimental import pallas as pl
from jax.experimental.pallas import tpu as pltpu
from jax.sharding import PartitionSpec as P

D = 2048
HEADS = 32
HEAD_DIM = 64
SL = 256
MICRO = 2
ROWS = MICRO * SL

EPSILON = 1e-05
ROPE_THETA = 130000.0
MASKED_SCORE = -1000000000.0
F32 = jnp.float32
BF16 = jnp.bfloat16
SWAP = [(0, 1), (1, 0)]


def mm(a, b):
    return jnp.dot(a, b, preferred_element_type=F32)


def mm_nt(a, b):
    return lax.dot_general(a, b, (((1,), (1,)), ((), ())), preferred_element_type=F32)


def mm_tn(a, b):
    return lax.dot_general(a, b, (((0,), (0,)), ((), ())), preferred_element_type=F32)


def rope_tables():
    half = HEAD_DIM // 2
    frequency = jnp.exp(
        jnp.arange(half, dtype=F32) * (-2.0 * math.log(ROPE_THETA) / HEAD_DIM)
    )
    angles = jnp.arange(SL, dtype=F32)[:, None] * frequency[None, :]
    cosine = jnp.cos(angles)
    sine = jnp.sin(angles)
    zero = jnp.zeros_like(sine)
    table_cos = jnp.concatenate([cosine] * 4, axis=1)
    table_first = jnp.concatenate([sine, zero] * 2, axis=1)
    table_second = jnp.concatenate([zero, sine] * 2, axis=1)
    return table_cos, table_first, table_second


def turn(v, cos, first, second):
    ahead = pltpu.roll(v, 128 - HEAD_DIM // 2, 1)
    behind = pltpu.roll(v, HEAD_DIM // 2, 1)
    return v * cos - ahead * first + behind * second


def turn_back(v, cos, first, second):
    ahead = pltpu.roll(v, 128 - HEAD_DIM // 2, 1)
    behind = pltpu.roll(v, HEAD_DIM // 2, 1)
    return v * cos + ahead * first - behind * second


def head_mask(head):
    lane = lax.broadcasted_iota(jnp.int32, (SL, 128), 1)
    return (lane // HEAD_DIM) == head


def softmax_of(q, k, allowed):
    scores = mm_nt(q, k) * HEAD_DIM ** (-0.5)
    scores = jnp.where(allowed, scores, MASKED_SCORE)
    exps = jnp.exp(scores - jnp.max(scores, axis=1, keepdims=True))
    return exps / jnp.sum(exps, axis=1, keepdims=True)


def allowed_of(length):
    query = lax.broadcasted_iota(jnp.int32, (SL, SL), 0)
    key = lax.broadcasted_iota(jnp.int32, (SL, SL), 1)
    return (key <= query) & (key < length)


FREE = pl.CostEstimate(flops=0, bytes_accessed=0, transcendentals=0)
BUSY = pl.CostEstimate(flops=20 * 10**9, bytes_accessed=60 * 10**6, transcendentals=0)


def whole(shape):
    return pl.BlockSpec(shape, lambda *at: (0,) * len(shape), pipeline_mode=pl.Buffered(1))


def attend_kernel(len_ref, qkv_ref, cos_ref, first_ref, second_ref, o_ref, turned_ref):
    cos, first, second = cos_ref[...], first_ref[...], second_ref[...]
    qr = turn(qkv_ref[:, :128], cos, first, second).astype(BF16)
    kr = turn(qkv_ref[:, 128:256], cos, first, second).astype(BF16)
    vr = qkv_ref[:, 256:].astype(BF16)
    turned_ref[:, :128] = qr
    turned_ref[:, 128:256] = kr
    turned_ref[:, 256:] = vr
    allowed = allowed_of(len_ref[pl.program_id(0)])
    out = jnp.zeros((SL, 128), F32)
    for head in range(2):
        mask = head_mask(head)
        probs = softmax_of(jnp.where(mask, qr, jnp.zeros_like(qr)), kr, allowed).astype(BF16)
        out = out + mm(probs, jnp.where(mask, vr, jnp.zeros_like(vr)))
    o_ref[...] = out.astype(BF16)


def head_grads(qr, kr, vr, od, allowed, cos, first, second):
    dq = jnp.zeros((SL, 128), F32)
    dk = jnp.zeros((SL, 128), F32)
    dv = jnp.zeros((SL, 128), F32)
    zero = jnp.zeros_like(qr)
    for head in range(2):
        mask = head_mask(head)
        q_own = jnp.where(mask, qr, zero)
        k_own = jnp.where(mask, kr, zero)
        od_own = jnp.where(mask, od, zero)
        probs = softmax_of(q_own, kr, allowed)
        d_probs = mm_nt(od_own, vr)
        dv = dv + mm_tn(probs.astype(BF16), od_own)
        inner = jnp.sum(probs * d_probs, axis=1, keepdims=True)
        d_scores = (probs * (d_probs - inner)).astype(BF16)
        dq = dq + mm(d_scores, k_own)
        dk = dk + mm_tn(d_scores, q_own)
    scale = HEAD_DIM ** (-0.5)
    return (
        turn_back(dq * scale, cos, first, second).astype(BF16),
        turn_back(dk * scale, cos, first, second).astype(BF16),
        dv.astype(BF16),
    )


def pair_block(width):
    return pl.BlockSpec((SL, width), lambda m, h, lens: (m, h))


TABLE = pl.BlockSpec((SL, 128), lambda m, h, lens: (0, 0))


def attend_forward(lengths, qkv, tables):
    width = qkv.shape[1]
    return pl.pallas_call(
        attend_kernel,
        out_shape=(
            jax.ShapeDtypeStruct((ROWS, width // 3), BF16),
            jax.ShapeDtypeStruct((ROWS, width), BF16),
        ),
        grid_spec=pltpu.PrefetchScalarGridSpec(
            num_scalar_prefetch=1,
            grid=(MICRO, width // 384),
            in_specs=[pair_block(384)] + [TABLE] * 3,
            out_specs=[pair_block(128), pair_block(384)],
        ),
        cost_estimate=FREE,
    )(lengths, qkv, *tables)


def multiply(a, w, transposed, tile, dtype):
    height, depth = a.shape
    width = w.shape[0] if transposed else w.shape[1]

    def kernel(a_ref, w_ref, o_ref):
        form = mm_nt if transposed else mm
        o_ref[...] = form(a_ref[...], w_ref[...]).astype(dtype)

    if transposed:
        w_spec = pl.BlockSpec((tile, depth), lambda j: (j, 0))
    else:
        w_spec = pl.BlockSpec((depth, tile), lambda j: (0, j))
    return pl.pallas_call(
        kernel,
        out_shape=jax.ShapeDtypeStruct((height, width), dtype),
        grid=(width // tile,),
        in_specs=[whole(a.shape), w_spec],
        out_specs=pl.BlockSpec((height, tile), lambda j: (0, j)),
        cost_estimate=FREE,
    )(a, w)


def split_product(parts, w, transposed, tile, cost=FREE):
    count = len(parts)
    height = parts[0].shape[0]
    width = w.shape[0] if transposed else w.shape[1]
    steps = width // tile
    half = steps // 2

    def kernel(*refs):
        form = mm_nt if transposed else mm
        total = form(refs[0][...], refs[count][...])
        for at in range(1, count):
            total = total + form(refs[at][...], refs[count + at][...])
        kept_ref, sent_ref = refs[2 * count :]
        step = pl.program_id(0)

        @pl.when(step < half)
        def _():
            sent_ref[...] = total.astype(BF16)

        @pl.when(step >= half)
        def _():
            kept_ref[...] = total

    def w_spec(at, depth):
        if transposed:
            return pl.BlockSpec((tile, depth), lambda j: (lax.rem(j + half, steps), at))
        return pl.BlockSpec((depth, tile), lambda j: (at, lax.rem(j + half, steps)))

    return pl.pallas_call(
        kernel,
        out_shape=(
            jax.ShapeDtypeStruct((height, width // 2), F32),
            jax.ShapeDtypeStruct((height, width // 2), BF16),
        ),
        grid=(steps,),
        in_specs=[whole(part.shape) for part in parts]
        + [w_spec(at, part.shape[1]) for at, part in enumerate(parts)],
        out_specs=(
            pl.BlockSpec((height, tile), lambda j: (0, jnp.maximum(j - half, 0))),
            pl.BlockSpec((height, tile), lambda j: (0, jnp.minimum(j, half - 1))),
        ),
        cost_estimate=cost,
    )(*parts, *([w] * count))


def feed_kernel(x_ref, gate_ref, up_ref, da_ref, hidden_ref, dg_ref, du_ref):
    x = x_ref[...]
    gate = mm(x, gate_ref[...])
    up = mm(x, up_ref[...])
    da = da_ref[...]
    sigmoid = 1.0 / (1.0 + jnp.exp(-gate))
    swish = gate * sigmoid
    hidden_ref[...] = (swish * up).astype(BF16)
    dg_ref[...] = (da * up * sigmoid * (1.0 + gate * (1.0 - sigmoid))).astype(BF16)
    du_ref[...] = (da * swish).astype(BF16)


def feed_forward(x, pair_w, hidden_grad, tile=256):
    height, depth = x.shape
    width = hidden_grad.shape[1]
    steps = width // tile
    tall = pl.BlockSpec((height, tile), lambda j: (0, j))
    return pl.pallas_call(
        feed_kernel,
        out_shape=(jax.ShapeDtypeStruct((height, width), BF16),) * 3,
        grid=(steps,),
        in_specs=[
            whole(x.shape),
            pl.BlockSpec((depth, tile), lambda j: (0, j)),
            pl.BlockSpec((depth, tile), lambda j: (0, j + steps)),
            tall,
        ],
        out_specs=(tall,) * 3,
        cost_estimate=FREE,
    )(x, pair_w, pair_w, hidden_grad)


def swap_kernel(plan, given, count, *refs):
    weights, outs = refs[:given], refs[given : given + count]
    rest = refs[given + count :]
    held, (send_sem, recv_sem, in_sem, out_sem) = rest[: len(plan)], rest[len(plan) :]
    row = lax.axis_index("row")
    barrier = pltpu.get_barrier_semaphore()
    pl.semaphore_signal(
        barrier, inc=1, device_id={"row": 1 - row}, device_id_type=pl.DeviceIdType.MESH
    )
    remote, local = [], []
    for at, (source, by_rows, out, start, offset, size) in enumerate(plan):
        weight = weights[source]
        height, width = weight.shape

        def part(index):
            if by_rows:
                return weight.at[pl.ds(pl.multiple_of(index * size, size), size), :]
            first = pl.multiple_of(index * (width // 2) + start, 128)
            return weight.at[:, pl.ds(first, size)]

        def place(second):
            if by_rows:
                return outs[out].at[:, pl.ds(second * width, width)]
            return outs[out].at[pl.ds(second * height, height), pl.ds(offset, size)]

        remote.append(
            pltpu.make_async_remote_copy(
                src_ref=part(1 - row),
                dst_ref=place(1),
                send_sem=send_sem.at[at],
                recv_sem=recv_sem.at[at],
                device_id={"row": 1 - row},
                device_id_type=pl.DeviceIdType.MESH,
            )
        )
        local.append(
            (
                pltpu.make_async_copy(part(row), held[at], in_sem.at[at]),
                pltpu.make_async_copy(held[at], place(0), out_sem.at[at]),
            )
        )
    for fetch, _ in local:
        fetch.start()
    pl.semaphore_wait(barrier, 1)
    for copy in remote:
        copy.start()
    for fetch, store in local:
        fetch.wait()
        store.start()
    for _, store in local:
        store.wait()
    for copy in remote:
        copy.wait()


def swap_weights(weights, plan, shapes, identity):
    held = []
    for source, by_rows, _, _, _, size in plan:
        height, width = weights[source].shape
        held.append((size, width) if by_rows else (height, size))
    sems = pltpu.SemaphoreType.DMA((len(plan),))
    return pl.pallas_call(
        lambda *refs: swap_kernel(plan, len(weights), len(shapes), *refs),
        out_shape=[jax.ShapeDtypeStruct(shape, BF16) for shape in shapes],
        in_specs=[pl.BlockSpec(memory_space=pl.ANY)] * len(weights),
        out_specs=[pl.BlockSpec(memory_space=pl.ANY)] * len(shapes),
        scratch_shapes=[pltpu.VMEM(shape, BF16) for shape in held] + [sems] * 4,
        compiler_params=pltpu.CompilerParams(collective_id=identity, has_side_effects=True),
        cost_estimate=FREE,
    )(*weights)


MESH = pl.DeviceIdType.MESH


def greet(*moves):
    barrier = pltpu.get_barrier_semaphore()
    total = 0
    for count, target in moves:
        total = total + count

        @pl.when(count > 0)
        def _():
            pl.semaphore_signal(barrier, inc=1, device_id=target, device_id_type=MESH)

    pl.semaphore_wait(barrier, total)


class ZLine:
    def __init__(self, line, grads, out, stage, came, sems, count, sided):
        self.line, self.grads, self.out, self.stage = line, grads, out, stage
        self.came, self.sems, self.sided = came, sems, sided
        width = grads.shape[1] // count
        self.pieces = [(k, pl.ds(k * width, width)) for k in range(count)]
        self.dp, self.row = lax.axis_index("dp"), lax.axis_index("row")
        self.z = self.dp // 2
        self.last = line - 1
        self.ways = ((0, self.z, 2), (1, self.last - self.z, -2))

    def rows_of(self, dest):
        size = self.grads.shape[0] // self.line
        if self.sided:
            dest = lax.rem(dest + self.line - self.row * (self.line // 2), self.line)
        return pl.ds(pl.multiple_of(dest * size, size), size)

    def copy(self, source, way, step, slot, piece, columns):
        return pltpu.make_async_remote_copy(
            src_ref=source,
            dst_ref=self.came.at[way, slot, :, columns],
            send_sem=self.sems.at[0, way, slot, piece],
            recv_sem=self.sems.at[1, way, slot, piece],
            device_id={"dp": self.dp + step},
            device_id_type=MESH,
        )

    def arrived(self, way, step, slot, piece, columns):
        held = self.came.at[way, slot, :, columns]
        self.copy(held, way, step, slot, piece, columns).wait_recv()
        return held

    def run(self, start, stop):
        def one_step(slot, _):
            for piece, columns in self.pieces:
                for way, place, step in self.ways:
                    far = self.last - slot + place
                    dest = far if step > 0 else self.last - far

                    @pl.when((place == 0) & (place < self.last))
                    def _():
                        source = self.grads.at[self.rows_of(dest), columns]
                        self.copy(source, way, step, slot, piece, columns).start()

                    @pl.when((place > 0) & (place <= slot))
                    def _():
                        held = self.arrived(way, step, slot - 1, piece, columns)

                        @pl.when(place < self.last)
                        def _():
                            held[...] = (
                                held[...].astype(F32)
                                + self.grads[self.rows_of(dest), columns].astype(F32)
                            ).astype(BF16)
                            self.copy(held, way, step, slot, piece, columns).start()

            return 0

        lax.fori_loop(start, stop, one_step, 0)

    def finish(self):
        own = self.rows_of(self.z)
        for piece, columns in self.pieces:
            self.stage[:, columns] = self.grads[own, columns].astype(F32)
            for way, place, step in self.ways:

                @pl.when(place > 0)
                def _():
                    held = self.arrived(way, step, self.last - 1, piece, columns)
                    self.stage[:, columns] += held[...].astype(F32)

        def settle(slot, _):
            for piece, columns in self.pieces:
                for way, place, step in self.ways:

                    @pl.when((place <= slot) & (place < self.last))
                    def _():
                        held = self.came.at[way, slot, :, columns]
                        self.copy(held, way, step, slot, piece, columns).wait_send()

            return 0

        lax.fori_loop(0, self.last, settle, 0)

    def moves(self):
        return (
            (jnp.minimum(self.z, 1), {"dp": self.dp - 2}),
            (jnp.minimum(self.last - self.z, 1), {"dp": self.dp + 2}),
        )


def tiles_loop(width, tile, body):
    def one(j, _):
        body(pl.ds(pl.multiple_of(j * tile, tile), tile), j * tile)
        return 0

    lax.fori_loop(0, width // tile, one, 0)


def tail_kernel(
    line,
    gate_grads,
    up,
    up_row,
    second_mine,
    second_came,
    dqkv,
    dqkv_row,
    first_mine,
    first_came,
    branch,
    mixed_mine,
    mixed_came,
    mixed_row,
    mixed_came_row,
    both,
    pieces,
    gate_out,
    up_out,
    query_out,
    key_out,
    value_out,
    output_out,
    back,
    gains_out,
    gate_z,
    up_z,
    qkv_z,
    output_z,
    up_grads,
    qkv_grads,
    output_grads,
    up_came,
    up_came_row,
    dqkv_came,
    dqkv_came_row,
    branch_came,
    turned_left,
    gate_stage,
    up_stage,
    qkv_stage,
    output_stage,
    gate_sems,
    up_sems,
    qkv_sems,
    output_sems,
    swap_sems,
    out_sems,
    gains,
    back_sems,
    gain_sems,
):
    groups = 2 * line
    dp, row = lax.axis_index("dp"), lax.axis_index("row")
    partner = dp + 1 - 2 * lax.rem(dp, 2)
    gate_line = ZLine(line, gate_grads, gate_out, gate_stage, gate_z, gate_sems, 4, False)
    up_line = ZLine(line, up_grads, up_out, up_stage, up_z, up_sems, 4, False)
    qkv_line = ZLine(line, qkv_grads, None, qkv_stage, qkv_z, qkv_sems, 3, False)
    output_line = ZLine(line, output_grads, output_out, output_stage, output_z, output_sems, 1, True)

    def swap(source, target, at, device):
        return pltpu.make_async_remote_copy(
            src_ref=source,
            dst_ref=target,
            send_sem=swap_sems.at[0, at],
            recv_sem=swap_sems.at[1, at],
            device_id=device,
            device_id_type=MESH,
        )

    up_x = swap(up, up_came, 0, {"dp": partner})
    branch_x = swap(branch, branch_came, 1, {"dp": partner})
    dqkv_x = swap(dqkv, dqkv_came, 2, {"dp": partner})
    up_across = swap(up_came, up_came_row, 3, {"row": 1 - row})
    dqkv_across = swap(dqkv_came, dqkv_came_row, 4, {"row": 1 - row})

    stores = []

    def store(source, target):
        copy = pltpu.make_async_copy(source, target, out_sems.at[len(stores)])
        copy.start()
        stores.append(copy)

    def store_wide(line_of):
        size = line_of.stage.shape[1] // 2
        for part in range(2):
            place = row if part == 0 else 1 - row
            there = pl.ds(pl.multiple_of(place * size, size), size)
            store(line_of.stage.at[:, pl.ds(part * size, size)], line_of.out.at[:, there])

    def store_qkv():
        heads = dqkv.shape[1] // 3
        for part in range(2):
            place = row if part == 0 else 1 - row
            for pair in range(heads // 128):
                for kind, out in enumerate((query_out, key_out, value_out)):
                    here = pl.ds(part * 3 * heads + pair * 384 + kind * 128, 128)
                    there = pl.ds(pl.multiple_of(place * heads + pair * 128, 128), 128)
                    store(qkv_stage.at[:, here], out.at[:, there])

    def returned(step):
        target = lax.rem(dp + step, groups)
        return pltpu.make_async_remote_copy(
            src_ref=both.at[:, target],
            dst_ref=back.at[:, dp],
            send_sem=back_sems.at[0, step],
            recv_sem=back_sems.at[1, step],
            device_id={"dp": target},
            device_id_type=MESH,
        )

    gain_steps = groups.bit_length() - 1

    def gain_copy(step):
        reach = 1 << step
        peer = dp + reach - 2 * reach * lax.rem(dp // reach, 2)
        return pltpu.make_async_remote_copy(
            src_ref=gains.at[0, step],
            dst_ref=gains.at[1, step],
            send_sem=gain_sems.at[0, step],
            recv_sem=gain_sems.at[1, step],
            device_id={"dp": peer},
            device_id_type=MESH,
        )

    def gain_step(step):
        if step >= gain_steps:
            return
        gain_copy(step).wait_recv()
        total = gains[0, step] + gains[1, step]
        if step + 1 == gain_steps:
            gains_out[...] = total
        else:
            gains[0, step + 1] = total
            gain_copy(step + 1).start()

    others = [(jnp.int32(1), {"dp": lax.rem(dp + step, groups)}) for step in range(1, groups)]
    greet(*others, (jnp.int32(1), {"row": 1 - row}))
    gains[0, 0] = pieces[...]
    gain_copy(0).start()
    gate_line.run(0, 1)
    up_x.start()
    branch_x.start()
    dqkv_x.start()

    def send_back(step, _):
        returned(step).start()
        return 0

    lax.fori_loop(1, groups, send_back, 0)
    store(both.at[:, dp], back.at[:, dp])

    depth = second_mine.shape[0]
    turned_left[:, :depth] = second_mine[...].T
    turned_left[:, depth:] = second_came[...].T
    gate_line.run(1, 2)

    def wide(target, shift, mine, came):
        def body(columns, start):
            total = mm(turned_left[:, :depth], mine[:, columns])
            total = total + mm(turned_left[:, depth:], came[:, columns])
            tile = total.shape[1]
            target[:, pl.ds(pl.multiple_of(shift + start, tile), tile)] = total.astype(BF16)

        tiles_loop(mine.shape[1], 512, body)

    up_x.wait_recv()
    up_across.start()
    gain_step(0)
    gate_line.run(2, line - 1)
    wide(up_grads, 0, up, up_came)
    up_across.wait_recv()
    wide(up_grads, up.shape[1], up_row, up_came_row)
    up_line.run(0, 1)
    gate_line.finish()
    store_wide(gate_line)

    turned_left[:, :depth] = first_mine[...].T
    turned_left[:, depth:] = first_came[...].T
    branch_x.wait_recv()

    def side(start, mine, came):
        def body(columns, _):
            total = mm_tn(mine[...], branch[:, columns]) + mm_tn(came[...], branch_came[:, columns])
            output_grads[pl.ds(start, mine.shape[1]), columns] = total.astype(BF16)

        tiles_loop(branch.shape[1], 512, body)

    side(0, mixed_mine, mixed_came)
    side(mixed_mine.shape[1], mixed_row, mixed_came_row)
    output_line.run(0, 1)
    up_line.run(1, 2)
    gain_step(1)
    dqkv_x.wait_recv()
    dqkv_across.start()
    wide(qkv_grads, 0, dqkv, dqkv_came)
    dqkv_across.wait_recv()
    wide(qkv_grads, dqkv.shape[1], dqkv_row, dqkv_came_row)
    qkv_line.run(0, 1)
    output_line.run(1, 2)
    up_line.run(2, line - 1)
    qkv_line.run(1, 2)
    output_line.run(2, line - 1)
    for step in range(2, gain_steps):
        gain_step(step)
    up_line.finish()
    store_wide(up_line)
    qkv_line.run(2, line - 1)
    output_line.finish()
    store(output_stage, output_out)
    qkv_line.finish()
    store_qkv()

    def get_back(step, _):
        returned(step).wait()
        return 0

    lax.fori_loop(1, groups, get_back, 0)
    for step in range(gain_steps):
        gain_copy(step).wait_send()
    for copy in (up_x, branch_x, dqkv_x, up_across, dqkv_across):
        copy.wait_send()
    for copy in stores:
        copy.wait()


def stream(source_of, slots_of, sems, count, body):
    def fetch(j, slot):
        return [
            pltpu.make_async_copy(source, target, sems.at[slot, k])
            for k, (source, target) in enumerate(zip(source_of(j), slots_of(slot)))
        ]

    for copy in fetch(0, 0):
        copy.start()

    def one(j, _):
        slot = lax.rem(j, 2)

        @pl.when(j + 1 < count)
        def _():
            for copy in fetch(j + 1, 1 - slot):
                copy.start()

        for copy in fetch(j, slot):
            copy.wait()
        body(j, slot)
        return 0

    lax.fori_loop(0, count, one, 0)


def rows_loop(body, size=64):
    def one(j, _):
        body(pl.ds(pl.multiple_of(j * size, size), size))
        return 0

    lax.fori_loop(0, ROWS // size, one, 0)


def chain_kernel(
    line,
    hidden,
    gate_grad,
    up_grad,
    second_mine,
    second_theirs,
    top_half,
    top_came,
    mixed_came,
    pair_w,
    down_w,
    qkv_w,
    out_w,
    turned,
    middle,
    inverse_first,
    inverse_second,
    gain_second,
    gain_first,
    x_own,
    key_live,
    cos,
    first,
    second,
    down_out,
    gate_grads,
    second_came,
    up_row,
    dqkv,
    dqkv_row,
    branch,
    mixed_came_row,
    both_out,
    pieces_out,
    gate_row,
    gate_came,
    gate_came_row,
    tiles,
    tall_tiles,
    pair_tiles,
    kept,
    sent,
    row_came,
    summed,
    col_came,
    block_sent,
    block_came,
    hidden_row,
    hidden_came,
    hidden_came_row,
    branch_row,
    dots,
    down_grads,
    down_z,
    middle_own,
    layer_own,
    first_own,
    mixed_grad,
    turned_left,
    feed_sum,
    attention_sum,
    swap_sems,
    piece_sems,
    tile_sems,
    down_sems,
    copy_sems,
):
    dp, row, col = lax.axis_index("dp"), lax.axis_index("row"), lax.axis_index("col")
    x = lax.rem(dp, 2)
    partner = {"dp": dp + 1 - 2 * x}
    across = {"row": 1 - row}
    beside = {"col": 1 - col}
    down_line = ZLine(line, down_grads, down_out, None, down_z, down_sems, 4, True)
    half = D // 2
    block = D // 4
    quarter = hidden.shape[1]
    pending = []

    def swap(source, target, at, device, sems=swap_sems):
        copy = pltpu.make_async_remote_copy(
            src_ref=source,
            dst_ref=target,
            send_sem=sems.at[0, at],
            recv_sem=sems.at[1, at],
            device_id=device,
            device_id_type=MESH,
        )
        return copy

    def begin(copy):
        copy.start()
        pending.append(copy)
        return copy

    greet(
        *down_line.moves(),
        (jnp.int32(1), partner),
        (jnp.int32(1), across),
        (jnp.int32(1), beside),
    )

    per = line // 2
    width = quarter // line

    def hidden_part(index, at):
        return hidden.at[:, pl.ds(pl.multiple_of((2 * at + index) * width, width), width)]

    to_x, to_row, on_row = [], [], []
    for at in range(per):
        there = pl.ds(at * width, width)
        to_x.append(
            begin(swap(hidden_part(1 - x, at), hidden_came.at[:, there], at, partner, piece_sems))
        )
    for at in range(per):
        there = pl.ds(at * width, width)
        to_row.append(
            begin(swap(hidden_part(x, at), hidden_row.at[:, there], per + at, across, piece_sems))
        )
    second_x = begin(swap(second_theirs, second_came, 0, partner))
    gate_x = begin(swap(gate_grad, gate_came, 1, partner))

    def nt_product(w, depth, start, body):
        stream(
            lambda j: [w.at[pl.ds(pl.multiple_of(start + j * 256, 256), 256), :]],
            lambda slot: [tiles.at[slot, :, pl.ds(0, depth)]],
            tile_sems,
            half // 256,
            body,
        )

    def columns_at(j, size=256):
        return pl.ds(pl.multiple_of(j * size, size), size)

    def pair_body(target, dtype):
        def body(j, slot):
            total = mm_nt(gate_grad[...], tiles[slot, :, :quarter])
            total = total + mm_nt(up_grad[...], tiles[slot, :, quarter:])
            target[:, columns_at(j)] = total.astype(dtype)

        return body

    nt_product(pair_w, 2 * quarter, half, pair_body(sent, BF16))
    pair_r = begin(swap(sent, row_came.at[0], 2, across))
    nt_product(pair_w, 2 * quarter, 0, pair_body(kept, F32))
    pair_r.wait_recv()

    def join_pair(rows):
        summed[rows, :] = (kept[rows, :] + row_came[0, rows, :].astype(F32)).astype(BF16)

    rows_loop(join_pair)
    pair_c = begin(swap(summed, col_came, 3, beside))
    gate_r = begin(swap(gate_grad, gate_row, 4, across))
    up_r = begin(swap(up_grad, up_row, 5, across))
    mixed_r = begin(swap(mixed_came, mixed_came_row, 6, across))

    def down_product(start, target, dtype):
        def body(j, slot):
            target[:, columns_at(j)] = mm(hidden[...], tall_tiles[slot]).astype(dtype)

        stream(
            lambda j: [down_w.at[:, pl.ds(pl.multiple_of(start + j * 256, 256), 256)]],
            lambda slot: [tall_tiles.at[slot]],
            tile_sems,
            half // 256,
            body,
        )

    pair_r.wait_send()
    pending[:] = [copy for copy in pending if copy is not pair_r]
    down_product(half, sent, BF16)
    layer_r = begin(swap(sent, row_came.at[1], 7, across))
    down_product(0, kept, F32)
    layer_r.wait_recv()

    def mine_of(value):
        return jnp.where(col == 0, value[:, :block], value[:, block:])

    def theirs_of(value):
        return jnp.where(col == 0, value[:, block:], value[:, :block])

    def join_layer(rows):
        total = kept[rows, :] + row_came[1, rows, :].astype(F32)
        layer_own[rows, :] = mine_of(total)
        block_sent[0, rows, :] = theirs_of(total).astype(BF16)

    rows_loop(join_layer)
    layer_c = begin(swap(block_sent.at[0], block_came.at[0], 8, beside))
    middle_in = pltpu.make_async_copy(middle, kept, copy_sems.at[0])
    middle_in.start()

    for copy in to_x:
        copy.wait_recv()
    for at in range(per):
        there = pl.ds(at * width, width)
        on_row.append(
            begin(
                swap(
                    hidden_came.at[:, there],
                    hidden_came_row.at[:, there],
                    2 * per + at,
                    across,
                    piece_sems,
                )
            )
        )

    def down_grad(part, left_of, came):
        def body(columns, _):
            for at in range(per):
                there = pl.ds(at * width, width)
                total = mm_tn(left_of(at)[...], top_half[:, columns])
                total = total + mm_tn(came[:, there], top_came[:, columns])
                down_grads[pl.ds((part * per + at) * width, width), columns] = total.astype(BF16)

        tiles_loop(half, 512, body)

    down_grad(0, lambda at: hidden_part(x, at), hidden_came)
    for copy in to_row + on_row:
        copy.wait_recv()
    down_grad(1, lambda at: hidden_row.at[:, pl.ds(at * width, width)], hidden_came_row)
    down_line.run(0, 1)

    middle_in.wait()
    pair_c.wait_recv()
    feed_sum[...] = jnp.zeros_like(feed_sum)

    def second_grads(rows):
        grad = summed[rows, :].astype(F32) + col_came[rows, :].astype(F32)
        return grad, grad * gain_second[...]

    def norm_first_pass(rows):
        grad, scaled = second_grads(rows)
        held = kept[rows, :]
        feed_sum[...] += jnp.sum(grad * held * inverse_second[rows, :], axis=0, keepdims=True)
        total = jnp.sum(scaled * held, axis=1, keepdims=True)
        dots[0, rows, :] = jnp.broadcast_to(total, (total.shape[0], 128))

    rows_loop(norm_first_pass)
    dot_r = begin(swap(dots.at[0], dots.at[1], 9, across))
    dot_r.wait_recv()

    def norm_second_pass(rows):
        _, scaled = second_grads(rows)
        held = kept[rows, :]
        inverse = inverse_second[rows, :]
        dot = dots[0, rows, :1] + dots[1, rows, :1]
        grad = (
            top_half[rows, :].astype(F32) + scaled * inverse - held * (inverse**3 * dot / D)
        )
        branch[rows, :] = grad.astype(BF16)
        middle_own[rows, :] = mine_of(grad)
        layer_own[rows, :] += mine_of(held)

    rows_loop(norm_second_pass)
    branch_r = begin(swap(branch, branch_row, 10, across))
    branch_r.wait_recv()

    def mixed_body(j, slot):
        total = mm_nt(branch[...], tiles[slot, :, :half])
        total = total + mm_nt(branch_row[...], tiles[slot, :, half:D])
        mixed_grad[:, columns_at(j)] = total.astype(BF16)

    stream(
        lambda j: [out_w.at[pl.ds(pl.multiple_of(j * 256, 256), 256), :]],
        lambda slot: [tiles.at[slot, :, pl.ds(0, D)]],
        tile_sems,
        out_w.shape[0] // 256,
        mixed_body,
    )
    down_line.run(1, 2)
    pairs = turned.shape[1] // 384
    lower = lax.broadcasted_iota(jnp.int32, (SL, SL), 1) <= lax.broadcasted_iota(
        jnp.int32, (SL, SL), 0
    )

    def attend(at, _):
        micro, pair = at // pairs, lax.rem(at, pairs)
        rows = pl.ds(pl.multiple_of(micro * SL, SL), SL)

        def part(kind):
            return pl.ds(pl.multiple_of(pair * 384 + kind * 128, 128), 128)

        allowed = lower & (key_live[pl.ds(micro, 1), :] > 0.5)
        dq, dk, dv = head_grads(
            turned[rows, part(0)],
            turned[rows, part(1)],
            turned[rows, part(2)],
            mixed_grad[rows, pl.ds(pl.multiple_of(pair * 128, 128), 128)],
            allowed,
            cos[...],
            first[...],
            second[...],
        )
        dqkv[rows, part(0)] = dq
        dqkv[rows, part(1)] = dk
        dqkv[rows, part(2)] = dv
        return 0

    lax.fori_loop(0, MICRO * pairs, attend, 0)

    def first_body(target, dtype):
        def body(j, slot):
            total = mm_nt(dqkv[...], tiles[slot, :, : dqkv.shape[1]])
            target[:, columns_at(j)] = total.astype(dtype)

        return body

    layer_r.wait_send()
    pending[:] = [copy for copy in pending if copy is not layer_r]
    nt_product(qkv_w, dqkv.shape[1], half, first_body(sent, BF16))
    first_r = begin(swap(sent, row_came.at[2], 11, across))
    dqkv_r = begin(swap(dqkv, dqkv_row, 12, across))
    nt_product(qkv_w, dqkv.shape[1], 0, first_body(kept, F32))
    first_r.wait_recv()

    def join_first(rows):
        total = kept[rows, :] + row_came[2, rows, :].astype(F32)
        first_own[rows, :] = mine_of(total)
        block_sent[1, rows, :] = theirs_of(total).astype(BF16)

    rows_loop(join_first)
    first_c = begin(swap(block_sent.at[1], block_came.at[1], 13, beside))
    down_line.run(2, line - 1)

    second_x.wait_recv()
    depth = second_mine.shape[0]
    turned_left[:, :depth] = second_mine[...].T
    turned_left[:, depth:] = second_came[...].T
    gate_x.wait_recv()
    gate_on = begin(swap(gate_came, gate_came_row, 14, across))

    def gate_part(shift, sources, values):
        def body(j, slot):
            mine, came = values(j, slot)
            total = mm(turned_left[:, :depth], mine) + mm(turned_left[:, depth:], came)
            there = pl.ds(pl.multiple_of(shift + j * 512, 512), 512)
            gate_grads[:, there] = total.astype(BF16)

        stream(
            lambda j: [source.at[:, columns_at(j, 512)] for source in sources],
            lambda slot: [pair_tiles.at[slot, k] for k in range(len(sources))],
            tile_sems,
            quarter // 512,
            body,
        )

    gate_part(
        0,
        [gate_came],
        lambda j, slot: (gate_grad[:, columns_at(j, 512)], pair_tiles[slot, 0]),
    )
    gate_r.wait_recv()
    gate_on.wait_recv()
    gate_part(
        quarter,
        [gate_row, gate_came_row],
        lambda j, slot: (pair_tiles[slot, 0], pair_tiles[slot, 1]),
    )

    layer_c.wait_recv()
    first_c.wait_recv()
    attention_sum[...] = jnp.zeros_like(attention_sum)

    def last_first_pass(rows):
        layer = layer_own[rows, :] + block_came[0, rows, :].astype(F32)
        both_out[rows, :] = layer.astype(BF16)
        grad = first_own[rows, :] + block_came[1, rows, :].astype(F32)
        first_own[rows, :] = grad
        held = x_own[rows, :].astype(F32)
        attention_sum[...] += jnp.sum(grad * held * inverse_first[rows, :], axis=0, keepdims=True)
        total = jnp.sum(grad * gain_first[...] * held, axis=1, keepdims=True)
        dots[2, rows, :] = jnp.broadcast_to(total, (total.shape[0], 128))

    rows_loop(last_first_pass)
    dot_r = begin(swap(dots.at[2], dots.at[3], 15, across))
    dot_r.wait_recv()

    def add_dots(rows):
        dots[4, rows, :] = dots[2, rows, :] + dots[3, rows, :]

    rows_loop(add_dots)
    dot_c = begin(swap(dots.at[4], dots.at[5], 16, beside))
    dot_c.wait_recv()

    def last_second_pass(rows):
        inverse = inverse_first[rows, :]
        dot = dots[4, rows, :1] + dots[5, rows, :1]
        scaled = first_own[rows, :] * gain_first[...]
        held = x_own[rows, :].astype(F32)
        grad = middle_own[rows, :] + scaled * inverse - held * (inverse**3 * dot / D)
        below = pl.ds(pl.multiple_of(rows.start + ROWS, rows.size), rows.size)
        both_out[below, :] = grad.astype(BF16)

    rows_loop(last_second_pass)
    pieces_out[0:1, :] = attention_sum[...]
    pieces_out[1:2, :] = mine_of(feed_sum[...])

    down_line.stage = kept.at[pl.ds(0, down_grads.shape[0] // line), :]
    down_line.finish()
    down_store = pltpu.make_async_copy(down_line.stage, down_out, copy_sems.at[1])
    down_store.start()
    for copy in (up_r, mixed_r, dqkv_r):
        copy.wait_recv()
    for copy in pending:
        copy.wait_send()
    down_store.wait()


def chain(line, identity, *values):
    hidden, gate_grad = values[:2]
    quarter = hidden.shape[1]
    narrow = values[3].shape[1]
    mixed_width = values[7].shape[1]
    qkv_width = values[12].shape[1]
    half, block = D // 2, D // 4
    rows = quarter // 2
    vmem = pl.BlockSpec(memory_space=pltpu.VMEM)
    anywhere = pl.BlockSpec(memory_space=pl.ANY)
    outside = {8, 9, 10, 11, 13}

    def array(*shape, dtype=BF16):
        return jax.ShapeDtypeStruct(shape, dtype)

    def buffer(*shape, dtype=BF16):
        return pltpu.VMEM(shape, dtype)

    outs = [
        (array(2 * rows // line, half, dtype=F32), anywhere),
        (array(narrow, 2 * quarter), vmem),
        (array(ROWS, narrow), vmem),
        (array(ROWS, quarter), anywhere),
        (array(ROWS, qkv_width), vmem),
        (array(ROWS, qkv_width), anywhere),
        (array(ROWS, half), vmem),
        (array(ROWS, mixed_width), anywhere),
        (array(2 * ROWS, block), vmem),
        (array(2, block, dtype=F32), vmem),
        (array(ROWS, quarter), anywhere),
        (array(ROWS, quarter), anywhere),
        (array(ROWS, quarter), anywhere),
    ]
    sem = pltpu.SemaphoreType.DMA
    return pl.pallas_call(
        lambda *refs: chain_kernel(line, *refs),
        out_shape=[shape for shape, _ in outs],
        in_specs=[anywhere if k in outside else vmem for k in range(len(values))],
        out_specs=[place for _, place in outs],
        scratch_shapes=[
            buffer(2, 256, 2 * quarter),
            buffer(2, quarter, 256),
            buffer(2, 2, ROWS, 512),
            buffer(ROWS, half, dtype=F32),
            buffer(ROWS, half),
            buffer(3, ROWS, half),
            buffer(ROWS, half),
            buffer(ROWS, half),
            buffer(2, ROWS, block),
            buffer(2, ROWS, block),
            buffer(ROWS, rows),
            buffer(ROWS, rows),
            buffer(ROWS, rows),
            buffer(ROWS, half),
            buffer(6, ROWS, 128, dtype=F32),
            buffer(2 * rows, half),
            buffer(2, line - 1, 2 * rows // line, half),
            buffer(ROWS, block, dtype=F32),
            buffer(ROWS, block, dtype=F32),
            buffer(ROWS, block, dtype=F32),
            buffer(ROWS, qkv_width // 3),
            buffer(narrow, 2 * ROWS),
            buffer(1, half, dtype=F32),
            buffer(1, block, dtype=F32),
            sem((2, 17)),
            sem((2, 3 * (line // 2))),
            sem((2, 2)),
            sem((2, 2, line - 1, 4)),
            sem((2,)),
        ],
        compiler_params=pltpu.CompilerParams(
            collective_id=identity, has_side_effects=True, vmem_limit_bytes=67043328
        ),
        cost_estimate=FREE,
    )(*values)


def tail_sums(line, identity, *values):
    (gate_grads, up, _, _, _, dqkv, _, _, _, branch) = values[:10]
    rows = gate_grads.shape[0]
    side_rows = 2 * values[10].shape[1]
    tokens = up.shape[0]
    widths = (gate_grads.shape[1], gate_grads.shape[1], 2 * dqkv.shape[1], branch.shape[1])
    heights = (rows, rows, rows, side_rows)
    pieces = (4, 4, 3, 1)
    sizes = [(h // line, w) for h, w in zip(heights, widths)]
    vmem = pl.BlockSpec(memory_space=pltpu.VMEM)
    anywhere = pl.BlockSpec(memory_space=pl.ANY)
    both, gains = values[14:]
    height = sizes[0][0]
    gain_steps = both.shape[1].bit_length() - 1

    def buffer(*shape):
        return pltpu.VMEM(shape, BF16)

    def array(*shape):
        return jax.ShapeDtypeStruct(shape, F32)

    return pl.pallas_call(
        lambda *refs: tail_kernel(line, *refs),
        out_shape=[
            array(*sizes[0]),
            array(*sizes[1]),
            array(height, widths[2] // 3),
            array(height, widths[2] // 3),
            array(height, widths[2] // 3),
            array(*sizes[3]),
            jax.ShapeDtypeStruct(both.shape, BF16),
            array(*gains.shape),
        ],
        in_specs=[vmem] * 14 + [anywhere, vmem],
        out_specs=[anywhere] * 7 + [vmem],
        scratch_shapes=[buffer(2, line - 1, *size) for size in sizes]
        + [buffer(h, w) for h, w in zip(heights[1:], widths[1:])]
        + [buffer(*up.shape)] * 2
        + [buffer(*dqkv.shape)] * 2
        + [buffer(*branch.shape)]
        + [buffer(rows, 2 * tokens)]
        + [pltpu.VMEM(size, F32) for size in sizes]
        + [pltpu.SemaphoreType.DMA((2, 2, line - 1, count)) for count in pieces]
        + [pltpu.SemaphoreType.DMA((2, 5)), pltpu.SemaphoreType.DMA((6 + widths[2] // 128,))]
        + [pltpu.VMEM((2, gain_steps, *gains.shape), F32)]
        + [
            pltpu.SemaphoreType.DMA((2, both.shape[1])),
            pltpu.SemaphoreType.DMA((2, gain_steps)),
        ],
        compiler_params=pltpu.CompilerParams(
            collective_id=identity, has_side_effects=True, vmem_limit_bytes=67043328
        ),
        cost_estimate=FREE,
    )(*values)


def put_back_kernel(order_ref, back_ref, layer_ref, grad_ref):
    groups = back_ref.shape[1]

    def one(at, _):
        micro, slot = at // groups, lax.rem(at, groups)
        place = order_ref[micro, slot]
        layer_ref[micro, place] = back_ref[micro, slot]
        grad_ref[micro, place] = back_ref[MICRO + micro, slot]
        return 0

    lax.fori_loop(0, MICRO * groups, one, 0)


def put_back(order, back):
    vmem = pl.BlockSpec(memory_space=pltpu.VMEM)
    shape = jax.ShapeDtypeStruct((MICRO,) + back.shape[1:], BF16)
    return pl.pallas_call(
        put_back_kernel,
        out_shape=(shape, shape),
        in_specs=[pl.BlockSpec(memory_space=pltpu.SMEM), vmem],
        out_specs=(vmem, vmem),
        cost_estimate=FREE,
    )(order, back)


def per_device(
    tokens,
    lengths,
    deal_order,
    attention_gain,
    query_weight,
    key_weight,
    value_weight,
    output_weight,
    feed_gain,
    gate_weight,
    up_weight,
    down_weight,
    cotangent,
):
    groups = lax.axis_size("dp")
    line = groups // 2
    dp = lax.axis_index("dp")
    row = lax.axis_index("row")
    col = lax.axis_index("col")
    z, x = dp // 2, dp % 2
    half = D // 2
    block = D // 4

    def over_row(v):
        return lax.ppermute(v, "row", SWAP)

    def over_col(v):
        return lax.ppermute(v, "col", SWAP)

    def over_x(v):
        return lax.ppermute(v, "dp", [(i, i ^ 1) for i in range(groups)])

    def ordered(own, other, index, axis=-1):
        return jnp.where(
            index == 0,
            jnp.concatenate([own, other], axis=axis),
            jnp.concatenate([other, own], axis=axis),
        )

    def x_parts(v, width):
        even = jnp.concatenate(
            [v[:, s : s + width] for s in range(0, v.shape[1], 2 * width)], axis=1
        )
        odd = jnp.concatenate(
            [v[:, s : s + width] for s in range(width, v.shape[1], 2 * width)], axis=1
        )
        return jnp.where(x == 0, even, odd), jnp.where(x == 0, odd, even)

    token = []

    def ordered_after(*values):
        out = lax.optimization_barrier(tuple(values) + tuple(token))
        return out[: len(values)] if len(values) > 1 else out[0]

    def mark(value):
        token[:] = [value]
        return value

    def arrive(*values):
        out = ordered_after(*values)
        mark(out[0] if len(values) > 1 else out)
        return out

    gathered = jnp.take_along_axis(tokens, deal_order[:, :, None, None], axis=1)
    gathered = mark(lax.optimization_barrier(gathered))
    dealt = lax.all_to_all(gathered, "dp", split_axis=1, concat_axis=2, tiled=True)
    own_order = lax.dynamic_slice_in_dim(deal_order, dp, 1, 1)
    own_lengths = jnp.take_along_axis(lengths, own_order, axis=1)[:, 0]
    tables = rope_tables()
    live = (jnp.arange(SL, dtype=jnp.int32)[None, :] < own_lengths[:, None]).reshape(ROWS, 1)
    key_live = live.reshape(MICRO, SL).astype(F32)
    top_block = jnp.where(live, cotangent.reshape(ROWS, block), 0.0).astype(BF16)

    gains = jnp.stack([attention_gain, feed_gain])
    gains_half = ordered(gains, over_col(gains), col)
    gains_other = over_row(gains_half)
    gains_full = jnp.concatenate([gains_half, gains_other], axis=1)

    top_col = over_col(top_block)
    quarter = gate_weight.shape[1] // 2
    gate_weight, up_weight = ordered_after(gate_weight, up_weight)
    (pair_w,) = swap_weights(
        (gate_weight, up_weight),
        ((0, False, 0, 0, 0, quarter), (1, False, 0, 0, quarter, quarter)),
        ((D, 2 * quarter),),
        0,
    )
    mark(pair_w)
    x_block = arrive(dealt).reshape(ROWS, block)
    x_came = over_col(x_block)
    heads = query_weight.shape[1] // 2
    query_weight, key_weight, value_weight, output_weight = ordered_after(
        query_weight, key_weight, value_weight, output_weight
    )
    plan = [
        (kind, False, 0, at, 3 * at + 128 * kind, 128)
        for kind in range(3)
        for at in range(0, heads, 128)
    ]
    qkv_w, out_w = swap_weights(
        (query_weight, key_weight, value_weight, output_weight),
        tuple(plan) + ((3, True, 1, 0, 0, heads),),
        ((D, 3 * heads), (heads, D)),
        1,
    )
    mark(qkv_w)
    top_half = ordered(top_block, arrive(top_col), col)
    top_half = mark(lax.optimization_barrier(top_half))
    x_half = ordered(x_block, arrive(x_came), col)
    x_half = mark(lax.optimization_barrier(x_half))
    top_came = over_x(top_half)
    top_row = over_row(top_half)

    x_other = arrive(over_row(x_half))
    x_full = jnp.concatenate([x_half, x_other], axis=1).astype(F32)
    inverse_first = lax.rsqrt(jnp.mean(x_full * x_full, axis=1, keepdims=True) + EPSILON)
    normed_first = (x_full * inverse_first * gains_full[0][None, :]).astype(BF16)
    normed_first = mark(lax.optimization_barrier(normed_first))
    qkv = multiply(normed_first, qkv_w, False, 384, F32)
    mixed, turned = attend_forward(own_lengths, qkv, tables)
    kept, sent = split_product([mixed], out_w, False, 512)
    mark(sent)
    came = arrive(over_row(sent))
    summed = (kept + came.astype(F32)).astype(BF16)
    summed = mark(lax.optimization_barrier(summed))
    summed_other = over_col(summed)
    top_row = arrive(top_row)
    narrow = half // groups
    first_mine, first_theirs = x_parts(normed_first[:, :half], narrow)
    top_full = jnp.concatenate([top_half, top_row], axis=1)
    (down_w,) = swap_weights(
        (ordered_after(down_weight),),
        ((0, True, 0, 0, 0, down_weight.shape[0] // 2),),
        ((down_weight.shape[0] // 2, D),),
        2,
    )
    hidden_grad = mark(multiply(top_full, down_w, True, 512, F32))
    top_came = arrive(top_came)
    mixed_mine, mixed_theirs = x_parts(mixed, 2 * mixed.shape[1] // groups)
    first_came = over_x(ordered_after(first_theirs))
    mixed_came = over_x(ordered_after(mixed_theirs))
    mixed_row = over_row(mixed_mine)
    summed_other = arrive(summed_other)
    middle = x_half.astype(F32) + (summed.astype(F32) + summed_other.astype(F32))

    middle_low = middle.astype(BF16)
    middle_low, middle = lax.optimization_barrier((middle_low, middle))
    mark(middle_low)
    middle_other = arrive(over_row(middle_low))
    middle_full = jnp.concatenate([middle_low, middle_other], axis=1).astype(F32)
    inverse_second = lax.rsqrt(
        jnp.mean(middle_full * middle_full, axis=1, keepdims=True) + EPSILON
    )
    normed_second = (middle_full * inverse_second * gains_full[1][None, :]).astype(BF16)
    normed_second = mark(lax.optimization_barrier(normed_second))
    hidden, gate_grad, up_grad = feed_forward(normed_second, pair_w, hidden_grad)
    mark(hidden)
    first_came, mixed_came, mixed_row = arrive(first_came, mixed_came, mixed_row)

    def own_block(v):
        return lax.dynamic_slice_in_dim(v, col * block, block, 1)

    second_mine, second_theirs = x_parts(normed_second[:, :half], narrow)
    (
        down_sum,
        gate_grads,
        second_came,
        up_row,
        dqkv,
        dqkv_row,
        branch,
        mixed_came_row,
        both,
        pieces,
        _,
        _,
        _,
    ) = chain(
        line,
        4,
        *ordered_after(
            hidden,
            gate_grad,
            up_grad,
            second_mine,
            second_theirs,
            top_half,
            top_came,
            mixed_came,
            pair_w,
            down_w,
            qkv_w,
            out_w,
            turned,
            middle,
            inverse_first,
            inverse_second,
            gains_half[1:],
            own_block(gains_half)[:1],
            x_block,
            key_live,
            *tables,
        ),
    )
    mark(both)

    gate_sum, up_sum, query_sum, key_sum, value_sum, output_sum, back, gain_sums = tail_sums(
        line,
        3,
        *ordered_after(
            gate_grads,
            up_grad,
            up_row,
            second_mine,
            second_came,
            dqkv,
            dqkv_row,
            first_mine,
            first_came,
            branch,
            mixed_mine,
            mixed_came,
            mixed_row,
            mixed_came_row,
            both.reshape(2 * MICRO, groups, SL // groups, block),
            pieces,
        ),
    )
    layer_output, tokens_grad = put_back(deal_order, back)
    gain_size = block // groups
    gain_sums = lax.dynamic_slice_in_dim(gain_sums, dp * gain_size, gain_size, 1)

    return (
        layer_output,
        tokens_grad,
        gain_sums[0],
        query_sum,
        key_sum,
        value_sum,
        output_sum,
        gain_sums[1],
        gate_sum,
        up_sum,
        down_sum,
    )


def solution(mesh):
    in_specs = (
        P(None, None, "dp", ("row", "col")),
        P(),
        P(),
        P(("row", "col")),
        P("row", "col"),
        P("row", "col"),
        P("row", "col"),
        P("col", "row"),
        P(("row", "col")),
        P("row", "col"),
        P("row", "col"),
        P("col", "row"),
        P(None, "dp", None, ("row", "col")),
    )
    out_specs = (
        P(None, None, "dp", ("row", "col")),
        P(None, None, "dp", ("row", "col")),
        P(("row", "col", "dp")),
        P(("row", "dp"), "col"),
        P(("row", "dp"), "col"),
        P(("row", "dp"), "col"),
        P(("col", "dp"), "row"),
        P(("row", "col", "dp")),
        P(("row", "dp"), "col"),
        P(("row", "dp"), "col"),
        P(("col", "dp"), "row"),
    )
    return jax.shard_map(
        per_device, mesh=mesh, in_specs=in_specs, out_specs=out_specs, check_vma=False
    )
```

```python
import math

import jax
import jax.numpy as jnp
from jax import lax
from jax.experimental import pallas as pl
from jax.experimental.pallas import tpu as pltpu
from jax.sharding import PartitionSpec as P

D = 2048
HEADS = 32
HEAD_DIM = 64
SL = 256
MICRO = 2
ROWS = MICRO * SL

EPSILON = 1e-05
ROPE_THETA = 130000.0
MASKED_SCORE = -1000000000.0
F32 = jnp.float32
BF16 = jnp.bfloat16
SWAP = [(0, 1), (1, 0)]


def mm(a, b):
    return jnp.dot(a, b, preferred_element_type=F32)


def mm_nt(a, b):
    return lax.dot_general(a, b, (((1,), (1,)), ((), ())), preferred_element_type=F32)


def mm_tn(a, b):
    return lax.dot_general(a, b, (((0,), (0,)), ((), ())), preferred_element_type=F32)


def rope_tables():
    half = HEAD_DIM // 2
    frequency = jnp.exp(
        jnp.arange(half, dtype=F32) * (-2.0 * math.log(ROPE_THETA) / HEAD_DIM)
    )
    angles = jnp.arange(SL, dtype=F32)[:, None] * frequency[None, :]
    cosine = jnp.cos(angles)
    sine = jnp.sin(angles)
    zero = jnp.zeros_like(sine)
    table_cos = jnp.concatenate([cosine] * 4, axis=1)
    table_first = jnp.concatenate([sine, zero] * 2, axis=1)
    table_second = jnp.concatenate([zero, sine] * 2, axis=1)
    return table_cos, table_first, table_second


def turn(v, cos, first, second):
    ahead = pltpu.roll(v, 128 - HEAD_DIM // 2, 1)
    behind = pltpu.roll(v, HEAD_DIM // 2, 1)
    return v * cos - ahead * first + behind * second


def turn_back(v, cos, first, second):
    ahead = pltpu.roll(v, 128 - HEAD_DIM // 2, 1)
    behind = pltpu.roll(v, HEAD_DIM // 2, 1)
    return v * cos + ahead * first - behind * second


def head_mask(head):
    lane = lax.broadcasted_iota(jnp.int32, (SL, 128), 1)
    return (lane // HEAD_DIM) == head


def softmax_of(q, k, allowed):
    scores = mm_nt(q, k) * HEAD_DIM ** (-0.5)
    scores = jnp.where(allowed, scores, MASKED_SCORE)
    exps = jnp.exp(scores - jnp.max(scores, axis=1, keepdims=True))
    return exps / jnp.sum(exps, axis=1, keepdims=True)


FREE = pl.CostEstimate(flops=0, bytes_accessed=0, transcendentals=0)


def whole(shape):
    return pl.BlockSpec(shape, lambda *at: (0,) * len(shape), pipeline_mode=pl.Buffered(1))


def head_outputs(qkv, allowed, cos, first, second):
    qr = turn(qkv[:, :128], cos, first, second).astype(BF16)
    kr = turn(qkv[:, 128:256], cos, first, second).astype(BF16)
    vr = qkv[:, 256:].astype(BF16)
    out = jnp.zeros((SL, 128), F32)
    for head in range(2):
        mask = head_mask(head)
        probs = softmax_of(jnp.where(mask, qr, jnp.zeros_like(qr)), kr, allowed).astype(BF16)
        out = out + mm(probs, jnp.where(mask, vr, jnp.zeros_like(vr)))
    return qr, kr, vr, out.astype(BF16)


def head_grads(qr, kr, vr, od, allowed, cos, first, second):
    dq = jnp.zeros((SL, 128), F32)
    dk = jnp.zeros((SL, 128), F32)
    dv = jnp.zeros((SL, 128), F32)
    zero = jnp.zeros_like(qr)
    for head in range(2):
        mask = head_mask(head)
        q_own = jnp.where(mask, qr, zero)
        k_own = jnp.where(mask, kr, zero)
        od_own = jnp.where(mask, od, zero)
        probs = softmax_of(q_own, kr, allowed)
        d_probs = mm_nt(od_own, vr)
        dv = dv + mm_tn(probs.astype(BF16), od_own)
        inner = jnp.sum(probs * d_probs, axis=1, keepdims=True)
        d_scores = (probs * (d_probs - inner)).astype(BF16)
        dq = dq + mm(d_scores, k_own)
        dk = dk + mm_tn(d_scores, q_own)
    scale = HEAD_DIM ** (-0.5)
    return (
        turn_back(dq * scale, cos, first, second).astype(BF16),
        turn_back(dk * scale, cos, first, second).astype(BF16),
        dv.astype(BF16),
    )


def feed_kernel(x_ref, gate_ref, up_ref, da_ref, hidden_ref, dg_ref, du_ref):
    x = x_ref[...]
    gate = mm(x, gate_ref[...])
    up = mm(x, up_ref[...])
    da = da_ref[...]
    sigmoid = 1.0 / (1.0 + jnp.exp(-gate))
    swish = gate * sigmoid
    hidden_ref[...] = (swish * up).astype(BF16)
    dg_ref[...] = (da * up * sigmoid * (1.0 + gate * (1.0 - sigmoid))).astype(BF16)
    du_ref[...] = (da * swish).astype(BF16)


def feed_forward(x, pair_w, hidden_grad, tile=256):
    height, depth = x.shape
    width = hidden_grad.shape[1]
    steps = width // tile
    tall = pl.BlockSpec((height, tile), lambda j: (0, j))
    return pl.pallas_call(
        feed_kernel,
        out_shape=(jax.ShapeDtypeStruct((height, width), BF16),) * 3,
        grid=(steps,),
        in_specs=[
            whole(x.shape),
            pl.BlockSpec((depth, tile), lambda j: (0, j)),
            pl.BlockSpec((depth, tile), lambda j: (0, j + steps)),
            tall,
        ],
        out_specs=(tall,) * 3,
        cost_estimate=FREE,
    )(x, pair_w, pair_w, hidden_grad)


MESH = pl.DeviceIdType.MESH


def greet(*moves):
    barrier = pltpu.get_barrier_semaphore()
    total = 0
    for count, target in moves:
        total = total + count

        @pl.when(count > 0)
        def _():
            pl.semaphore_signal(barrier, inc=1, device_id=target, device_id_type=MESH)

    pl.semaphore_wait(barrier, total)


class ZLine:
    def __init__(self, line, grads, out, stage, came, sems, count, sided):
        self.line, self.grads, self.out, self.stage = line, grads, out, stage
        self.came, self.sems, self.sided = came, sems, sided
        width = grads.shape[1] // count
        self.pieces = [(k, pl.ds(k * width, width)) for k in range(count)]
        self.dp, self.row = lax.axis_index("dp"), lax.axis_index("row")
        self.z = self.dp // 2
        self.last = line - 1
        self.ways = ((0, self.z, 2), (1, self.last - self.z, -2))

    def rows_of(self, dest):
        size = self.grads.shape[0] // self.line
        if self.sided:
            dest = lax.rem(dest + self.line - self.row * (self.line // 2), self.line)
        return pl.ds(pl.multiple_of(dest * size, size), size)

    def copy(self, source, way, step, slot, piece, columns):
        return pltpu.make_async_remote_copy(
            src_ref=source,
            dst_ref=self.came.at[way, slot, :, columns],
            send_sem=self.sems.at[0, way, slot, piece],
            recv_sem=self.sems.at[1, way, slot, piece],
            device_id={"dp": self.dp + step},
            device_id_type=MESH,
        )

    def arrived(self, way, step, slot, piece, columns):
        held = self.came.at[way, slot, :, columns]
        self.copy(held, way, step, slot, piece, columns).wait_recv()
        return held

    def run(self, start, stop):
        def one_step(slot, _):
            for piece, columns in self.pieces:
                for way, place, step in self.ways:
                    far = self.last - slot + place
                    dest = far if step > 0 else self.last - far

                    @pl.when((place == 0) & (place < self.last))
                    def _():
                        source = self.grads.at[self.rows_of(dest), columns]
                        self.copy(source, way, step, slot, piece, columns).start()

                    @pl.when((place > 0) & (place <= slot))
                    def _():
                        held = self.arrived(way, step, slot - 1, piece, columns)

                        @pl.when(place < self.last)
                        def _():
                            held[...] = (
                                held[...].astype(F32)
                                + self.grads[self.rows_of(dest), columns].astype(F32)
                            ).astype(BF16)
                            self.copy(held, way, step, slot, piece, columns).start()

            return 0

        lax.fori_loop(start, stop, one_step, 0)

    def finish(self):
        own = self.rows_of(self.z)
        for piece, columns in self.pieces:
            self.stage[:, columns] = self.grads[own, columns].astype(F32)
            for way, place, step in self.ways:

                @pl.when(place > 0)
                def _():
                    held = self.arrived(way, step, self.last - 1, piece, columns)
                    self.stage[:, columns] += held[...].astype(F32)

        def settle(slot, _):
            for piece, columns in self.pieces:
                for way, place, step in self.ways:

                    @pl.when((place <= slot) & (place < self.last))
                    def _():
                        held = self.came.at[way, slot, :, columns]
                        self.copy(held, way, step, slot, piece, columns).wait_send()

            return 0

        lax.fori_loop(0, self.last, settle, 0)

    def moves(self):
        return (
            (jnp.minimum(self.z, 1), {"dp": self.dp - 2}),
            (jnp.minimum(self.last - self.z, 1), {"dp": self.dp + 2}),
        )


def tiles_loop(width, tile, body):
    def one(j, _):
        body(pl.ds(pl.multiple_of(j * tile, tile), tile), j * tile)
        return 0

    lax.fori_loop(0, width // tile, one, 0)


def tail_kernel(
    line,
    gate_grads,
    up,
    up_row,
    second_mine,
    second_came,
    dqkv,
    dqkv_row,
    first_mine,
    first_theirs,
    branch,
    mixed_mine,
    mixed_theirs,
    both,
    pieces,
    gate_out,
    up_out,
    query_out,
    key_out,
    value_out,
    output_out,
    back,
    gains_out,
    gate_z,
    up_z,
    qkv_z,
    output_z,
    up_grads,
    qkv_grads,
    output_grads,
    up_came,
    up_came_row,
    dqkv_came,
    dqkv_came_row,
    branch_came,
    first_came,
    mixed_came,
    mixed_row,
    mixed_came_row,
    turned_left,
    gate_stage,
    up_stage,
    qkv_stage,
    output_stage,
    gate_sems,
    up_sems,
    qkv_sems,
    output_sems,
    swap_sems,
    out_sems,
    gains,
    back_sems,
    gain_sems,
):
    groups = 2 * line
    dp, row = lax.axis_index("dp"), lax.axis_index("row")
    partner = dp + 1 - 2 * lax.rem(dp, 2)
    gate_line = ZLine(line, gate_grads, gate_out, gate_stage, gate_z, gate_sems, 4, False)
    up_line = ZLine(line, up_grads, up_out, up_stage, up_z, up_sems, 4, False)
    qkv_line = ZLine(line, qkv_grads, None, qkv_stage, qkv_z, qkv_sems, 3, False)
    output_line = ZLine(line, output_grads, output_out, output_stage, output_z, output_sems, 1, True)

    def swap(source, target, at, device):
        return pltpu.make_async_remote_copy(
            src_ref=source,
            dst_ref=target,
            send_sem=swap_sems.at[0, at],
            recv_sem=swap_sems.at[1, at],
            device_id=device,
            device_id_type=MESH,
        )

    up_x = swap(up, up_came, 0, {"dp": partner})
    branch_x = swap(branch, branch_came, 1, {"dp": partner})
    dqkv_x = swap(dqkv, dqkv_came, 2, {"dp": partner})
    up_across = swap(up_came, up_came_row, 3, {"row": 1 - row})
    dqkv_across = swap(dqkv_came, dqkv_came_row, 4, {"row": 1 - row})
    first_x = swap(first_theirs, first_came, 5, {"dp": partner})
    mixed_x = swap(mixed_theirs, mixed_came, 6, {"dp": partner})
    mixed_r = swap(mixed_mine, mixed_row, 7, {"row": 1 - row})
    mixed_across = swap(mixed_came, mixed_came_row, 8, {"row": 1 - row})

    stores = []

    def store(source, target):
        copy = pltpu.make_async_copy(source, target, out_sems.at[len(stores)])
        copy.start()
        stores.append(copy)

    def store_wide(line_of):
        size = line_of.stage.shape[1] // 2
        for part in range(2):
            place = row if part == 0 else 1 - row
            there = pl.ds(pl.multiple_of(place * size, size), size)
            store(line_of.stage.at[:, pl.ds(part * size, size)], line_of.out.at[:, there])

    def store_qkv():
        heads = dqkv.shape[1] // 3
        for part in range(2):
            place = row if part == 0 else 1 - row
            for pair in range(heads // 128):
                for kind, out in enumerate((query_out, key_out, value_out)):
                    here = pl.ds(part * 3 * heads + pair * 384 + kind * 128, 128)
                    there = pl.ds(pl.multiple_of(place * heads + pair * 128, 128), 128)
                    store(qkv_stage.at[:, here], out.at[:, there])

    def returned(step):
        target = lax.rem(dp + step, groups)
        return pltpu.make_async_remote_copy(
            src_ref=both.at[:, target],
            dst_ref=back.at[:, dp],
            send_sem=back_sems.at[0, step],
            recv_sem=back_sems.at[1, step],
            device_id={"dp": target},
            device_id_type=MESH,
        )

    gain_steps = groups.bit_length() - 1

    def gain_copy(step):
        reach = 1 << step
        peer = dp + reach - 2 * reach * lax.rem(dp // reach, 2)
        return pltpu.make_async_remote_copy(
            src_ref=gains.at[0, step],
            dst_ref=gains.at[1, step],
            send_sem=gain_sems.at[0, step],
            recv_sem=gain_sems.at[1, step],
            device_id={"dp": peer},
            device_id_type=MESH,
        )

    def gain_step(step):
        if step >= gain_steps:
            return
        gain_copy(step).wait_recv()
        total = gains[0, step] + gains[1, step]
        if step + 1 == gain_steps:
            gains_out[...] = total
        else:
            gains[0, step + 1] = total
            gain_copy(step + 1).start()

    others = [(jnp.int32(1), {"dp": lax.rem(dp + step, groups)}) for step in range(1, groups)]
    greet(*others, (jnp.int32(1), {"row": 1 - row}))
    gains[0, 0] = pieces[...]
    gain_copy(0).start()
    gate_line.run(0, 1)
    up_x.start()
    mixed_x.start()
    branch_x.start()
    first_x.start()
    dqkv_x.start()
    mixed_r.start()

    def send_back(step, _):
        returned(step).start()
        return 0

    lax.fori_loop(1, groups, send_back, 0)
    store(both.at[:, dp], back.at[:, dp])

    depth = second_mine.shape[0]
    turned_left[:, :depth] = second_mine[...].T
    turned_left[:, depth:] = second_came[...].T
    gate_line.run(1, 2)

    def wide(target, shift, mine, came):
        def body(columns, start):
            total = mm(turned_left[:, :depth], mine[:, columns])
            total = total + mm(turned_left[:, depth:], came[:, columns])
            tile = total.shape[1]
            target[:, pl.ds(pl.multiple_of(shift + start, tile), tile)] = total.astype(BF16)

        tiles_loop(mine.shape[1], 512, body)

    up_x.wait_recv()
    up_across.start()
    gain_step(0)
    gate_line.run(2, line - 1)
    wide(up_grads, 0, up, up_came)
    up_across.wait_recv()
    wide(up_grads, up.shape[1], up_row, up_came_row)
    up_line.run(0, 1)
    gate_line.finish()
    store_wide(gate_line)

    mixed_x.wait_recv()
    mixed_across.start()
    branch_x.wait_recv()

    def side(start, mine, came):
        def body(columns, _):
            total = mm_tn(mine[...], branch[:, columns]) + mm_tn(came[...], branch_came[:, columns])
            output_grads[pl.ds(start, mine.shape[1]), columns] = total.astype(BF16)

        tiles_loop(branch.shape[1], 512, body)

    side(0, mixed_mine, mixed_came)
    mixed_r.wait_recv()
    mixed_across.wait_recv()
    side(mixed_mine.shape[1], mixed_row, mixed_came_row)
    output_line.run(0, 1)
    up_line.run(1, 2)
    gain_step(1)
    first_x.wait_recv()
    turned_left[:, :depth] = first_mine[...].T
    turned_left[:, depth:] = first_came[...].T
    dqkv_x.wait_recv()
    dqkv_across.start()
    wide(qkv_grads, 0, dqkv, dqkv_came)
    dqkv_across.wait_recv()
    wide(qkv_grads, dqkv.shape[1], dqkv_row, dqkv_came_row)
    qkv_line.run(0, 1)
    output_line.run(1, 2)
    up_line.run(2, line - 1)
    qkv_line.run(1, 2)
    output_line.run(2, line - 1)
    for step in range(2, gain_steps):
        gain_step(step)
    up_line.finish()
    store_wide(up_line)
    qkv_line.run(2, line - 1)
    output_line.finish()
    store(output_stage, output_out)
    qkv_line.finish()
    store_qkv()

    def get_back(step, _):
        returned(step).wait()
        return 0

    lax.fori_loop(1, groups, get_back, 0)
    for step in range(gain_steps):
        gain_copy(step).wait_send()
    copies = (up_x, branch_x, dqkv_x, up_across, dqkv_across)
    for copy in copies + (first_x, mixed_x, mixed_r, mixed_across):
        copy.wait_send()
    for copy in stores:
        copy.wait()


def stream(source_of, slots_of, sems, count, body):
    def fetch(j, slot):
        return [
            pltpu.make_async_copy(source, target, sems.at[slot, k])
            for k, (source, target) in enumerate(zip(source_of(j), slots_of(slot)))
        ]

    for copy in fetch(0, 0):
        copy.start()

    def one(j, _):
        slot = lax.rem(j, 2)

        @pl.when(j + 1 < count)
        def _():
            for copy in fetch(j + 1, 1 - slot):
                copy.start()

        for copy in fetch(j, slot):
            copy.wait()
        body(j, slot)
        return 0

    lax.fori_loop(0, count, one, 0)


def rows_loop(body, size=64):
    def one(j, _):
        body(pl.ds(pl.multiple_of(j * size, size), size))
        return 0

    lax.fori_loop(0, ROWS // size, one, 0)


def deal_kernel(order_ref, tokens_ref, dealt_ref):
    groups = tokens_ref.shape[1]

    def one(at, _):
        micro, slot = at // groups, lax.rem(at, groups)
        dealt_ref[micro, slot] = tokens_ref[micro, order_ref[micro, slot]]
        return 0

    lax.fori_loop(0, MICRO * groups, one, 0)


def deal(order, tokens):
    vmem = pl.BlockSpec(memory_space=pltpu.VMEM)
    return pl.pallas_call(
        deal_kernel,
        out_shape=jax.ShapeDtypeStruct(tokens.shape, BF16),
        in_specs=[pl.BlockSpec(memory_space=pltpu.SMEM), vmem],
        out_specs=vmem,
        cost_estimate=FREE,
    )(order, tokens)


def front_kernel(
    dealt,
    top_block,
    gain_first,
    gain_second,
    key_live,
    cos,
    first,
    second,
    query_weight,
    key_weight,
    value_weight,
    output_weight,
    gate_weight,
    up_weight,
    down_weight,
    pair_out,
    down_out,
    qkv_out,
    out_out,
    x_in,
    top_half,
    top_came,
    normed_first,
    turned,
    mixed,
    middle,
    inverse_first,
    inverse_second,
    normed_second,
    hidden_grad,
    qkv_w,
    out_w,
    pair_held,
    down_held,
    tiles,
    x_came,
    x_half,
    x_other,
    top_col,
    top_row,
    sent,
    row_came,
    kept,
    summed,
    col_came,
    low,
    low_came,
    deal_sems,
    weight_sems,
    local_sems,
    swap_sems,
    tile_sems,
):
    groups = dealt.shape[1]
    dp, row, col = lax.axis_index("dp"), lax.axis_index("row"), lax.axis_index("col")
    partner = {"dp": dp + 1 - 2 * lax.rem(dp, 2)}
    across = {"row": 1 - row}
    beside = {"col": 1 - col}
    half, block = D // 2, D // 4
    heads = query_weight.shape[1] // 2
    quarter = gate_weight.shape[1] // 2
    pending = []

    def remote(source, target, sems, at, device):
        copy = pltpu.make_async_remote_copy(
            src_ref=source,
            dst_ref=target,
            send_sem=sems.at[0, at],
            recv_sem=sems.at[1, at],
            device_id=device,
            device_id_type=MESH,
        )
        copy.start()
        pending.append(copy)
        return copy

    def swap(source, target, at, device):
        return remote(source, target, swap_sems, at, device)

    def columns(w, index, start, size):
        begin = pl.multiple_of(index * (w.shape[1] // 2) + start, 128)
        return w.at[:, pl.ds(begin, size)]

    def rows_half(w, index):
        size = w.shape[0] // 2
        return w.at[pl.ds(pl.multiple_of(index * size, size), size), :]

    locals_started = []

    def local(source, target):
        copy = pltpu.make_async_copy(source, target, local_sems.at[len(locals_started)])
        copy.start()
        locals_started.append(copy)
        return copy

    own_now = []
    for kind, w in enumerate((query_weight, key_weight, value_weight)):
        for at in range(0, heads, 128):
            there = pl.ds(3 * at + 128 * kind, 128)
            own_now.append(local(columns(w, row, at, 128), qkv_w.at[pl.ds(0, half), there]))
    own_now.append(local(rows_half(output_weight, row), out_w.at[:, pl.ds(0, half)]))
    own_gate = local(columns(gate_weight, row, 0, quarter), pair_held.at[0])
    own_up = local(columns(up_weight, row, 0, quarter), pair_held.at[1])
    own_down = local(rows_half(down_weight, row), down_held)
    own_rows = local(dealt.at[:, dp], x_in.at[:, dp])
    others = [(jnp.int32(1), {"dp": lax.rem(dp + step, groups)}) for step in range(1, groups)]
    greet(*others, (jnp.int32(1), across), (jnp.int32(1), beside))

    def dealing(step, micro):
        target = lax.rem(dp + step, groups)
        return pltpu.make_async_remote_copy(
            src_ref=dealt.at[micro, target],
            dst_ref=x_in.at[micro, dp],
            send_sem=deal_sems.at[0, micro, step],
            recv_sem=deal_sems.at[1, micro, step],
            device_id={"dp": target},
            device_id_type=MESH,
        )

    for micro in range(MICRO):

        def send_rows(step, _):
            dealing(step, micro).start()
            return 0

        lax.fori_loop(1, groups, send_rows, 0)
    top_c = swap(top_block, top_col, 0, beside)
    weights_now = []
    for kind, w in enumerate((query_weight, key_weight, value_weight)):
        for at in range(0, heads, 128):
            there = qkv_w.at[pl.ds(half, half), pl.ds(3 * at + 128 * kind, 128)]
            weights_now.append(
                remote(columns(w, 1 - row, at, 128), there, weight_sems, len(weights_now), across)
            )
    weights_now.append(
        remote(
            rows_half(output_weight, 1 - row),
            out_w.at[:, pl.ds(half, half)],
            weight_sems,
            len(weights_now),
            across,
        )
    )
    weights_late = []
    for k, w in enumerate((gate_weight, up_weight)):
        there = pair_out.at[pl.ds(half, half), pl.ds(k * quarter, quarter)]
        weights_late.append(
            remote(
                columns(w, 1 - row, 0, quarter), there, weight_sems, len(weights_now) + k, across
            )
        )
    own_gate.wait()
    own_up.wait()
    store_gate = local(pair_held.at[0], pair_out.at[pl.ds(0, half), pl.ds(0, quarter)])
    store_up = local(pair_held.at[1], pair_out.at[pl.ds(0, half), pl.ds(quarter, quarter)])
    own_down.wait()
    store_down = local(down_held, down_out.at[:, pl.ds(0, half)])

    def half_of(own, came):
        return jnp.where(
            col == 0,
            jnp.concatenate([own, came], axis=1),
            jnp.concatenate([came, own], axis=1),
        )

    own_rows.wait()
    x_c = []
    for micro in range(MICRO):

        def take_rows(step, _):
            dealing(step, micro).wait_recv()
            return 0

        lax.fori_loop(1, groups, take_rows, 0)
        x_c.append(swap(x_in.at[micro], x_came.at[micro], 1 + micro, beside))
    top_c.wait_recv()

    def top_rows(rows):
        top_half[rows, :] = half_of(top_block[rows, :], top_col[rows, :])

    rows_loop(top_rows)
    top_x = swap(top_half, top_came, 3, partner)

    def micro_rows(micro):
        return pl.ds(micro * SL, SL)

    x_r = []
    for micro in range(MICRO):
        x_c[micro].wait_recv()
        own = x_in[micro].reshape(SL, block)
        came = x_came[micro].reshape(SL, block)
        x_half[micro_rows(micro), :] = half_of(own, came)
        rows = micro_rows(micro)
        x_r.append(swap(x_half.at[rows, :], x_other.at[rows, :], 4 + micro, across))
        if micro == 0:
            for copy in own_now:
                copy.wait()
            for copy in weights_now:
                copy.wait_recv()
    top_r = swap(top_half, top_row, 6, across)
    down_there = down_out.at[:, pl.ds(half, half)]
    down_r = remote(
        rows_half(down_weight, 1 - row), down_there, weight_sems, len(weights_now) + 2, across
    )
    store_qkv = local(qkv_w, qkv_out)
    store_out = local(out_w, out_out)

    lower = lax.broadcasted_iota(jnp.int32, (SL, SL), 1) <= lax.broadcasted_iota(
        jnp.int32, (SL, SL), 0
    )

    def norm_rows(own_ref, other_ref, gain, inverse_ref, out_ref, micro):
        def body(j, _):
            rows = pl.ds(pl.multiple_of(micro * SL + j * 64, 64), 64)
            own = own_ref[rows, :].astype(F32)
            other = other_ref[rows, :].astype(F32)
            total = jnp.sum(own * own, axis=1, keepdims=True)
            total = total + jnp.sum(other * other, axis=1, keepdims=True)
            inverse = lax.rsqrt(total / D + EPSILON)
            inverse_ref[rows, :] = inverse
            out_ref[rows, :half] = (own * inverse * gain[:, :half]).astype(BF16)
            out_ref[rows, half:] = (other * inverse * gain[:, half:]).astype(BF16)
            return 0

        lax.fori_loop(0, SL // 64, body, 0)

    sum_c = []
    for micro in range(MICRO):
        rows = micro_rows(micro)
        x_r[micro].wait_recv()
        norm_rows(x_half, x_other, gain_first, inverse_first, normed_first, micro)
        allowed = lower & (key_live[micro : micro + 1, :] > 0.5)

        def attend(at, _):
            there = pl.multiple_of(at * 768, 128)
            qkv = mm(normed_first[rows, :], qkv_w[:, pl.ds(there, 768)])
            for pair in range(2):
                qr, kr, vr, out = head_outputs(
                    qkv[:, pair * 384 : pair * 384 + 384], allowed, cos[...], first[...], second[...]
                )
                begin = there + pair * 384
                for kind, value in enumerate((qr, kr, vr)):
                    turned[rows, pl.ds(pl.multiple_of(begin + kind * 128, 128), 128)] = value
                mixed[rows, pl.ds(pl.multiple_of(at * 256 + pair * 128, 128), 128)] = out
            return 0

        lax.fori_loop(0, heads // 256, attend, 0)
        sent[rows, :] = mm(mixed[rows, :], out_w[:, half:]).astype(BF16)
        sum_r = swap(sent.at[rows, :], row_came.at[rows, :], 7 + micro, across)
        kept[...] = mm(mixed[rows, :], out_w[:, :half])
        sum_r.wait_recv()
        summed[rows, :] = (kept[...] + row_came[rows, :].astype(F32)).astype(BF16)
        sum_c.append(swap(summed.at[rows, :], col_came.at[rows, :], 9 + micro, beside))

    top_r.wait_recv()
    store_down.wait()
    down_r.wait_recv()

    def da_body(j, slot):
        total = mm_nt(top_half[...], tiles[slot, :, :half])
        total = total + mm_nt(top_row[...], tiles[slot, :, half:])
        hidden_grad[:, pl.ds(pl.multiple_of(j * 256, 256), 256)] = total

    stream(
        lambda j: [down_out.at[pl.ds(pl.multiple_of(j * 256, 256), 256), :]],
        lambda slot: [tiles.at[slot]],
        tile_sems,
        quarter // 256,
        da_body,
    )

    low_r = []
    for micro in range(MICRO):
        rows = micro_rows(micro)
        sum_c[micro].wait_recv()

        def middle_rows(j, _):
            here = pl.ds(pl.multiple_of(micro * SL + j * 64, 64), 64)
            total = x_half[here, :].astype(F32) + (
                summed[here, :].astype(F32) + col_came[here, :].astype(F32)
            )
            middle[here, :] = total
            low[here, :] = total.astype(BF16)
            return 0

        lax.fori_loop(0, SL // 64, middle_rows, 0)
        low_r.append(swap(low.at[rows, :], low_came.at[rows, :], 11 + micro, across))
        low_r[micro].wait_recv()
        norm_rows(low, low_came, gain_second, inverse_second, normed_second, micro)

    top_x.wait_recv()
    for copy in weights_late:
        copy.wait_recv()
    for copy in pending:
        copy.wait_send()

    def close(step, _):
        for micro in range(MICRO):
            dealing(step, micro).wait_send()
        return 0

    lax.fori_loop(1, groups, close, 0)
    for copy in (store_gate, store_up, store_qkv, store_out):
        copy.wait()


def front(line, identity, *values):
    dealt, query_weight, gate_weight = values[0], values[8], values[12]
    groups = dealt.shape[1]
    half, block = D // 2, D // 4
    heads = query_weight.shape[1] // 2
    quarter = gate_weight.shape[1] // 2
    vmem = pl.BlockSpec(memory_space=pltpu.VMEM)
    anywhere = pl.BlockSpec(memory_space=pl.ANY)

    def array(*shape, dtype=BF16):
        return jax.ShapeDtypeStruct(shape, dtype)

    def buffer(*shape, dtype=BF16):
        return pltpu.VMEM(shape, dtype)

    sem = pltpu.SemaphoreType.DMA
    now = 3 * (heads // 128) + 1
    return pl.pallas_call(
        front_kernel,
        out_shape=[
            array(D, 2 * quarter),
            array(quarter, D),
            array(D, 3 * heads),
            array(heads, D),
            array(*dealt.shape),
            array(ROWS, half),
            array(ROWS, half),
            array(ROWS, D),
            array(ROWS, 3 * heads),
            array(ROWS, heads),
            array(ROWS, half, dtype=F32),
            array(ROWS, 1, dtype=F32),
            array(ROWS, 1, dtype=F32),
            array(ROWS, D),
            array(ROWS, quarter, dtype=F32),
        ],
        in_specs=[vmem] * 8 + [anywhere] * 7,
        out_specs=[anywhere] * 4 + [vmem] * 11,
        scratch_shapes=[
            buffer(D, 3 * heads),
            buffer(heads, D),
            buffer(2, half, quarter),
            buffer(quarter, half),
            buffer(2, 256, D),
            buffer(*dealt.shape),
            buffer(ROWS, half),
            buffer(ROWS, half),
            buffer(ROWS, block),
            buffer(ROWS, half),
            buffer(ROWS, half),
            buffer(ROWS, half),
            buffer(SL, half, dtype=F32),
            buffer(ROWS, half),
            buffer(ROWS, half),
            buffer(ROWS, half),
            buffer(ROWS, half),
            sem((2, MICRO, groups)),
            sem((2, now + 3)),
            sem((now + 9,)),
            sem((2, 13)),
            sem((2, 2)),
        ],
        compiler_params=pltpu.CompilerParams(
            collective_id=identity, has_side_effects=True, vmem_limit_bytes=67043328
        ),
        cost_estimate=FREE,
    )(*values)


def chain_kernel(
    line,
    hidden,
    gate_grad,
    up_grad,
    second_mine,
    second_theirs,
    top_half,
    top_came,
    pair_w,
    down_w,
    qkv_w,
    out_w,
    turned,
    middle,
    inverse_first,
    inverse_second,
    gain_second,
    gain_first,
    x_own,
    key_live,
    cos,
    first,
    second,
    down_out,
    gate_grads,
    second_came,
    up_row,
    dqkv,
    dqkv_row,
    branch,
    both_out,
    pieces_out,
    gate_row,
    gate_came,
    gate_came_row,
    tiles,
    tall_tiles,
    pair_tiles,
    kept,
    sent,
    row_came,
    summed,
    col_came,
    block_sent,
    block_came,
    hidden_row,
    hidden_came,
    hidden_came_row,
    branch_row,
    dots,
    down_grads,
    down_z,
    middle_own,
    layer_own,
    first_own,
    mixed_grad,
    turned_left,
    feed_sum,
    attention_sum,
    swap_sems,
    piece_sems,
    tile_sems,
    down_sems,
    copy_sems,
):
    dp, row, col = lax.axis_index("dp"), lax.axis_index("row"), lax.axis_index("col")
    x = lax.rem(dp, 2)
    partner = {"dp": dp + 1 - 2 * x}
    across = {"row": 1 - row}
    beside = {"col": 1 - col}
    down_line = ZLine(line, down_grads, down_out, None, down_z, down_sems, 4, True)
    half = D // 2
    block = D // 4
    quarter = hidden.shape[1]
    pending = []

    def swap(source, target, at, device, sems=swap_sems):
        copy = pltpu.make_async_remote_copy(
            src_ref=source,
            dst_ref=target,
            send_sem=sems.at[0, at],
            recv_sem=sems.at[1, at],
            device_id=device,
            device_id_type=MESH,
        )
        return copy

    def begin(copy):
        copy.start()
        pending.append(copy)
        return copy

    greet(
        *down_line.moves(),
        (jnp.int32(1), partner),
        (jnp.int32(1), across),
        (jnp.int32(1), beside),
    )

    per = line // 2
    width = quarter // line

    def hidden_part(index, at):
        return hidden.at[:, pl.ds(pl.multiple_of((2 * at + index) * width, width), width)]

    to_x, to_row, on_row = [], [], []
    for at in range(per):
        there = pl.ds(at * width, width)
        to_x.append(
            begin(swap(hidden_part(1 - x, at), hidden_came.at[:, there], at, partner, piece_sems))
        )
    for at in range(per):
        there = pl.ds(at * width, width)
        to_row.append(
            begin(swap(hidden_part(x, at), hidden_row.at[:, there], per + at, across, piece_sems))
        )
    second_x = begin(swap(second_theirs, second_came, 0, partner))
    gate_x = begin(swap(gate_grad, gate_came, 1, partner))

    def nt_product(w, depth, start, body):
        stream(
            lambda j: [w.at[pl.ds(pl.multiple_of(start + j * 256, 256), 256), :]],
            lambda slot: [tiles.at[slot, :, pl.ds(0, depth)]],
            tile_sems,
            half // 256,
            body,
        )

    def columns_at(j, size=256):
        return pl.ds(pl.multiple_of(j * size, size), size)

    def pair_body(target, dtype):
        def body(j, slot):
            total = mm_nt(gate_grad[...], tiles[slot, :, :quarter])
            total = total + mm_nt(up_grad[...], tiles[slot, :, quarter:])
            target[:, columns_at(j)] = total.astype(dtype)

        return body

    nt_product(pair_w, 2 * quarter, half, pair_body(sent, BF16))
    pair_r = begin(swap(sent, row_came.at[0], 2, across))
    nt_product(pair_w, 2 * quarter, 0, pair_body(kept, F32))
    pair_r.wait_recv()

    def join_pair(rows):
        summed[rows, :] = (kept[rows, :] + row_came[0, rows, :].astype(F32)).astype(BF16)

    rows_loop(join_pair)
    pair_c = begin(swap(summed, col_came, 3, beside))
    gate_r = begin(swap(gate_grad, gate_row, 4, across))
    up_r = begin(swap(up_grad, up_row, 5, across))

    def down_product(start, target, dtype):
        def body(j, slot):
            target[:, columns_at(j)] = mm(hidden[...], tall_tiles[slot]).astype(dtype)

        stream(
            lambda j: [down_w.at[:, pl.ds(pl.multiple_of(start + j * 256, 256), 256)]],
            lambda slot: [tall_tiles.at[slot]],
            tile_sems,
            half // 256,
            body,
        )

    pair_r.wait_send()
    pending[:] = [copy for copy in pending if copy is not pair_r]
    down_product(half, sent, BF16)
    layer_r = begin(swap(sent, row_came.at[1], 7, across))
    down_product(0, kept, F32)
    layer_r.wait_recv()

    def mine_of(value):
        return jnp.where(col == 0, value[:, :block], value[:, block:])

    def theirs_of(value):
        return jnp.where(col == 0, value[:, block:], value[:, :block])

    def join_layer(rows):
        total = kept[rows, :] + row_came[1, rows, :].astype(F32)
        layer_own[rows, :] = mine_of(total)
        block_sent[0, rows, :] = theirs_of(total).astype(BF16)

    rows_loop(join_layer)
    layer_c = begin(swap(block_sent.at[0], block_came.at[0], 8, beside))
    middle_in = pltpu.make_async_copy(middle, kept, copy_sems.at[0])
    middle_in.start()

    for copy in to_x:
        copy.wait_recv()
    for at in range(per):
        there = pl.ds(at * width, width)
        on_row.append(
            begin(
                swap(
                    hidden_came.at[:, there],
                    hidden_came_row.at[:, there],
                    2 * per + at,
                    across,
                    piece_sems,
                )
            )
        )

    def down_grad(part, left_of, came):
        def body(columns, _):
            for at in range(per):
                there = pl.ds(at * width, width)
                total = mm_tn(left_of(at)[...], top_half[:, columns])
                total = total + mm_tn(came[:, there], top_came[:, columns])
                down_grads[pl.ds((part * per + at) * width, width), columns] = total.astype(BF16)

        tiles_loop(half, 512, body)

    down_grad(0, lambda at: hidden_part(x, at), hidden_came)
    for copy in to_row + on_row:
        copy.wait_recv()
    down_grad(1, lambda at: hidden_row.at[:, pl.ds(at * width, width)], hidden_came_row)
    down_line.run(0, 1)

    middle_in.wait()
    pair_c.wait_recv()
    feed_sum[...] = jnp.zeros_like(feed_sum)

    def second_grads(rows):
        grad = summed[rows, :].astype(F32) + col_came[rows, :].astype(F32)
        return grad, grad * gain_second[...]

    def norm_first_pass(rows):
        grad, scaled = second_grads(rows)
        held = kept[rows, :]
        feed_sum[...] += jnp.sum(grad * held * inverse_second[rows, :], axis=0, keepdims=True)
        total = jnp.sum(scaled * held, axis=1, keepdims=True)
        dots[0, rows, :] = jnp.broadcast_to(total, (total.shape[0], 128))

    rows_loop(norm_first_pass)
    dot_r = begin(swap(dots.at[0], dots.at[1], 9, across))
    dot_r.wait_recv()

    def norm_second_pass(rows):
        _, scaled = second_grads(rows)
        held = kept[rows, :]
        inverse = inverse_second[rows, :]
        dot = dots[0, rows, :1] + dots[1, rows, :1]
        grad = (
            top_half[rows, :].astype(F32) + scaled * inverse - held * (inverse**3 * dot / D)
        )
        branch[rows, :] = grad.astype(BF16)
        middle_own[rows, :] = mine_of(grad)
        layer_own[rows, :] += mine_of(held)

    rows_loop(norm_second_pass)
    branch_r = begin(swap(branch, branch_row, 10, across))
    branch_r.wait_recv()

    def mixed_body(j, slot):
        total = mm_nt(branch[...], tiles[slot, :, :half])
        total = total + mm_nt(branch_row[...], tiles[slot, :, half:D])
        mixed_grad[:, columns_at(j)] = total.astype(BF16)

    stream(
        lambda j: [out_w.at[pl.ds(pl.multiple_of(j * 256, 256), 256), :]],
        lambda slot: [tiles.at[slot, :, pl.ds(0, D)]],
        tile_sems,
        out_w.shape[0] // 256,
        mixed_body,
    )
    down_line.run(1, 2)
    pairs = turned.shape[1] // 384
    lower = lax.broadcasted_iota(jnp.int32, (SL, SL), 1) <= lax.broadcasted_iota(
        jnp.int32, (SL, SL), 0
    )

    def attend(at, _):
        micro, pair = at // pairs, lax.rem(at, pairs)
        rows = pl.ds(pl.multiple_of(micro * SL, SL), SL)

        def part(kind):
            return pl.ds(pl.multiple_of(pair * 384 + kind * 128, 128), 128)

        allowed = lower & (key_live[pl.ds(micro, 1), :] > 0.5)
        dq, dk, dv = head_grads(
            turned[rows, part(0)],
            turned[rows, part(1)],
            turned[rows, part(2)],
            mixed_grad[rows, pl.ds(pl.multiple_of(pair * 128, 128), 128)],
            allowed,
            cos[...],
            first[...],
            second[...],
        )
        dqkv[rows, part(0)] = dq
        dqkv[rows, part(1)] = dk
        dqkv[rows, part(2)] = dv
        return 0

    lax.fori_loop(0, MICRO * pairs, attend, 0)

    def first_body(target, dtype):
        def body(j, slot):
            total = mm_nt(dqkv[...], tiles[slot, :, : dqkv.shape[1]])
            target[:, columns_at(j)] = total.astype(dtype)

        return body

    layer_r.wait_send()
    pending[:] = [copy for copy in pending if copy is not layer_r]
    nt_product(qkv_w, dqkv.shape[1], half, first_body(sent, BF16))
    first_r = begin(swap(sent, row_came.at[2], 11, across))
    dqkv_r = begin(swap(dqkv, dqkv_row, 12, across))
    nt_product(qkv_w, dqkv.shape[1], 0, first_body(kept, F32))
    first_r.wait_recv()

    def join_first(rows):
        total = kept[rows, :] + row_came[2, rows, :].astype(F32)
        first_own[rows, :] = mine_of(total)
        block_sent[1, rows, :] = theirs_of(total).astype(BF16)

    rows_loop(join_first)
    first_c = begin(swap(block_sent.at[1], block_came.at[1], 13, beside))
    down_line.run(2, line - 1)

    second_x.wait_recv()
    depth = second_mine.shape[0]
    turned_left[:, :depth] = second_mine[...].T
    turned_left[:, depth:] = second_came[...].T
    gate_x.wait_recv()
    gate_on = begin(swap(gate_came, gate_came_row, 14, across))

    def gate_part(shift, sources, values):
        def body(j, slot):
            mine, came = values(j, slot)
            total = mm(turned_left[:, :depth], mine) + mm(turned_left[:, depth:], came)
            there = pl.ds(pl.multiple_of(shift + j * 512, 512), 512)
            gate_grads[:, there] = total.astype(BF16)

        stream(
            lambda j: [source.at[:, columns_at(j, 512)] for source in sources],
            lambda slot: [pair_tiles.at[slot, k] for k in range(len(sources))],
            tile_sems,
            quarter // 512,
            body,
        )

    gate_part(
        0,
        [gate_came],
        lambda j, slot: (gate_grad[:, columns_at(j, 512)], pair_tiles[slot, 0]),
    )
    gate_r.wait_recv()
    gate_on.wait_recv()
    gate_part(
        quarter,
        [gate_row, gate_came_row],
        lambda j, slot: (pair_tiles[slot, 0], pair_tiles[slot, 1]),
    )

    layer_c.wait_recv()
    first_c.wait_recv()
    attention_sum[...] = jnp.zeros_like(attention_sum)

    def last_first_pass(rows):
        layer = layer_own[rows, :] + block_came[0, rows, :].astype(F32)
        both_out[rows, :] = layer.astype(BF16)
        grad = first_own[rows, :] + block_came[1, rows, :].astype(F32)
        first_own[rows, :] = grad
        held = x_own[rows, :].astype(F32)
        attention_sum[...] += jnp.sum(grad * held * inverse_first[rows, :], axis=0, keepdims=True)
        total = jnp.sum(grad * gain_first[...] * held, axis=1, keepdims=True)
        dots[2, rows, :] = jnp.broadcast_to(total, (total.shape[0], 128))

    rows_loop(last_first_pass)
    dot_r = begin(swap(dots.at[2], dots.at[3], 15, across))
    dot_r.wait_recv()

    def add_dots(rows):
        dots[4, rows, :] = dots[2, rows, :] + dots[3, rows, :]

    rows_loop(add_dots)
    dot_c = begin(swap(dots.at[4], dots.at[5], 16, beside))
    dot_c.wait_recv()

    def last_second_pass(rows):
        inverse = inverse_first[rows, :]
        dot = dots[4, rows, :1] + dots[5, rows, :1]
        scaled = first_own[rows, :] * gain_first[...]
        held = x_own[rows, :].astype(F32)
        grad = middle_own[rows, :] + scaled * inverse - held * (inverse**3 * dot / D)
        below = pl.ds(pl.multiple_of(rows.start + ROWS, rows.size), rows.size)
        both_out[below, :] = grad.astype(BF16)

    rows_loop(last_second_pass)
    pieces_out[0:1, :] = attention_sum[...]
    pieces_out[1:2, :] = mine_of(feed_sum[...])

    down_line.stage = kept.at[pl.ds(0, down_grads.shape[0] // line), :]
    down_line.finish()
    down_store = pltpu.make_async_copy(down_line.stage, down_out, copy_sems.at[1])
    down_store.start()
    for copy in (up_r, dqkv_r):
        copy.wait_recv()
    for copy in pending:
        copy.wait_send()
    down_store.wait()


def chain(line, identity, *values):
    hidden, gate_grad = values[:2]
    quarter = hidden.shape[1]
    narrow = values[3].shape[1]
    qkv_width = values[11].shape[1]
    half, block = D // 2, D // 4
    rows = quarter // 2
    vmem = pl.BlockSpec(memory_space=pltpu.VMEM)
    anywhere = pl.BlockSpec(memory_space=pl.ANY)
    outside = {7, 8, 9, 10, 12}

    def array(*shape, dtype=BF16):
        return jax.ShapeDtypeStruct(shape, dtype)

    def buffer(*shape, dtype=BF16):
        return pltpu.VMEM(shape, dtype)

    outs = [
        (array(2 * rows // line, half, dtype=F32), anywhere),
        (array(narrow, 2 * quarter), vmem),
        (array(ROWS, narrow), vmem),
        (array(ROWS, quarter), anywhere),
        (array(ROWS, qkv_width), vmem),
        (array(ROWS, qkv_width), anywhere),
        (array(ROWS, half), vmem),
        (array(2 * ROWS, block), vmem),
        (array(2, block, dtype=F32), vmem),
        (array(ROWS, quarter), anywhere),
        (array(ROWS, quarter), anywhere),
        (array(ROWS, quarter), anywhere),
    ]
    sem = pltpu.SemaphoreType.DMA
    return pl.pallas_call(
        lambda *refs: chain_kernel(line, *refs),
        out_shape=[shape for shape, _ in outs],
        in_specs=[anywhere if k in outside else vmem for k in range(len(values))],
        out_specs=[place for _, place in outs],
        scratch_shapes=[
            buffer(2, 256, 2 * quarter),
            buffer(2, quarter, 256),
            buffer(2, 2, ROWS, 512),
            buffer(ROWS, half, dtype=F32),
            buffer(ROWS, half),
            buffer(3, ROWS, half),
            buffer(ROWS, half),
            buffer(ROWS, half),
            buffer(2, ROWS, block),
            buffer(2, ROWS, block),
            buffer(ROWS, rows),
            buffer(ROWS, rows),
            buffer(ROWS, rows),
            buffer(ROWS, half),
            buffer(6, ROWS, 128, dtype=F32),
            buffer(2 * rows, half),
            buffer(2, line - 1, 2 * rows // line, half),
            buffer(ROWS, block, dtype=F32),
            buffer(ROWS, block, dtype=F32),
            buffer(ROWS, block, dtype=F32),
            buffer(ROWS, qkv_width // 3),
            buffer(narrow, 2 * ROWS),
            buffer(1, half, dtype=F32),
            buffer(1, block, dtype=F32),
            sem((2, 17)),
            sem((2, 3 * (line // 2))),
            sem((2, 2)),
            sem((2, 2, line - 1, 4)),
            sem((2,)),
        ],
        compiler_params=pltpu.CompilerParams(
            collective_id=identity, has_side_effects=True, vmem_limit_bytes=67043328
        ),
        cost_estimate=FREE,
    )(*values)


def tail_sums(line, identity, *values):
    (gate_grads, up, _, _, _, dqkv, _, _, _, branch) = values[:10]
    rows = gate_grads.shape[0]
    side_rows = 2 * values[10].shape[1]
    tokens = up.shape[0]
    widths = (gate_grads.shape[1], gate_grads.shape[1], 2 * dqkv.shape[1], branch.shape[1])
    heights = (rows, rows, rows, side_rows)
    pieces = (4, 4, 3, 1)
    sizes = [(h // line, w) for h, w in zip(heights, widths)]
    vmem = pl.BlockSpec(memory_space=pltpu.VMEM)
    anywhere = pl.BlockSpec(memory_space=pl.ANY)
    both, gains = values[12:]
    height = sizes[0][0]
    gain_steps = both.shape[1].bit_length() - 1

    def buffer(*shape):
        return pltpu.VMEM(shape, BF16)

    def array(*shape):
        return jax.ShapeDtypeStruct(shape, F32)

    return pl.pallas_call(
        lambda *refs: tail_kernel(line, *refs),
        out_shape=[
            array(*sizes[0]),
            array(*sizes[1]),
            array(height, widths[2] // 3),
            array(height, widths[2] // 3),
            array(height, widths[2] // 3),
            array(*sizes[3]),
            jax.ShapeDtypeStruct(both.shape, BF16),
            array(*gains.shape),
        ],
        in_specs=[vmem] * 12 + [anywhere, vmem],
        out_specs=[anywhere] * 7 + [vmem],
        scratch_shapes=[buffer(2, line - 1, *size) for size in sizes]
        + [buffer(h, w) for h, w in zip(heights[1:], widths[1:])]
        + [buffer(*up.shape)] * 2
        + [buffer(*dqkv.shape)] * 2
        + [buffer(*branch.shape), buffer(*values[7].shape)]
        + [buffer(*values[10].shape)] * 3
        + [buffer(rows, 2 * tokens)]
        + [pltpu.VMEM(size, F32) for size in sizes]
        + [pltpu.SemaphoreType.DMA((2, 2, line - 1, count)) for count in pieces]
        + [pltpu.SemaphoreType.DMA((2, 9)), pltpu.SemaphoreType.DMA((6 + widths[2] // 128,))]
        + [pltpu.VMEM((2, gain_steps, *gains.shape), F32)]
        + [
            pltpu.SemaphoreType.DMA((2, both.shape[1])),
            pltpu.SemaphoreType.DMA((2, gain_steps)),
        ],
        compiler_params=pltpu.CompilerParams(
            collective_id=identity, has_side_effects=True, vmem_limit_bytes=67043328
        ),
        cost_estimate=FREE,
    )(*values)


def put_back_kernel(order_ref, back_ref, layer_ref, grad_ref):
    groups = back_ref.shape[1]

    def one(at, _):
        micro, slot = at // groups, lax.rem(at, groups)
        place = order_ref[micro, slot]
        layer_ref[micro, place] = back_ref[micro, slot]
        grad_ref[micro, place] = back_ref[MICRO + micro, slot]
        return 0

    lax.fori_loop(0, MICRO * groups, one, 0)


def put_back(order, back):
    vmem = pl.BlockSpec(memory_space=pltpu.VMEM)
    shape = jax.ShapeDtypeStruct((MICRO,) + back.shape[1:], BF16)
    return pl.pallas_call(
        put_back_kernel,
        out_shape=(shape, shape),
        in_specs=[pl.BlockSpec(memory_space=pltpu.SMEM), vmem],
        out_specs=(vmem, vmem),
        cost_estimate=FREE,
    )(order, back)


def per_device(
    tokens,
    lengths,
    deal_order,
    attention_gain,
    query_weight,
    key_weight,
    value_weight,
    output_weight,
    feed_gain,
    gate_weight,
    up_weight,
    down_weight,
    cotangent,
):
    groups = lax.axis_size("dp")
    line = groups // 2
    dp = lax.axis_index("dp")
    row = lax.axis_index("row")
    col = lax.axis_index("col")
    z, x = dp // 2, dp % 2
    half = D // 2
    block = D // 4

    def over_row(v):
        return lax.ppermute(v, "row", SWAP)

    def over_col(v):
        return lax.ppermute(v, "col", SWAP)

    def ordered(own, other, index, axis=-1):
        return jnp.where(
            index == 0,
            jnp.concatenate([own, other], axis=axis),
            jnp.concatenate([other, own], axis=axis),
        )

    def x_parts(v, width):
        even = jnp.concatenate(
            [v[:, s : s + width] for s in range(0, v.shape[1], 2 * width)], axis=1
        )
        odd = jnp.concatenate(
            [v[:, s : s + width] for s in range(width, v.shape[1], 2 * width)], axis=1
        )
        return jnp.where(x == 0, even, odd), jnp.where(x == 0, odd, even)

    token = []

    def ordered_after(*values):
        out = lax.optimization_barrier(tuple(values) + tuple(token))
        return out[: len(values)] if len(values) > 1 else out[0]

    def mark(value):
        token[:] = [value]
        return value

    own_order = lax.dynamic_slice_in_dim(deal_order, dp, 1, 1)
    own_lengths = jnp.take_along_axis(lengths, own_order, axis=1)[:, 0]
    tables = rope_tables()
    live = (jnp.arange(SL, dtype=jnp.int32)[None, :] < own_lengths[:, None]).reshape(ROWS, 1)
    key_live = live.reshape(MICRO, SL).astype(F32)
    top_block = jnp.where(live, cotangent.reshape(ROWS, block), 0.0).astype(BF16)
    gains = jnp.stack([attention_gain, feed_gain])
    gains_half = ordered(gains, over_col(gains), col)
    gains_full = jnp.concatenate([gains_half, over_row(gains_half)], axis=1)
    (
        pair_w,
        down_w,
        qkv_w,
        out_w,
        x_block,
        top_half,
        top_came,
        normed_first,
        turned,
        mixed,
        middle,
        inverse_first,
        inverse_second,
        normed_second,
        hidden_grad,
    ) = front(
        line,
        0,
        deal(deal_order, tokens),
        top_block,
        gains_full[:1],
        gains_full[1:],
        key_live,
        *tables,
        query_weight,
        key_weight,
        value_weight,
        output_weight,
        gate_weight,
        up_weight,
        down_weight,
    )
    x_block = x_block.reshape(ROWS, block)
    narrow = half // groups
    hidden, gate_grad, up_grad = feed_forward(normed_second, pair_w, hidden_grad)
    mark(hidden)

    def own_block(v):
        return lax.dynamic_slice_in_dim(v, col * block, block, 1)

    first_mine, first_theirs = x_parts(normed_first[:, :half], narrow)
    mixed_mine, mixed_theirs = x_parts(mixed, 2 * mixed.shape[1] // groups)
    second_mine, second_theirs = x_parts(normed_second[:, :half], narrow)
    (
        down_sum,
        gate_grads,
        second_came,
        up_row,
        dqkv,
        dqkv_row,
        branch,
        both,
        pieces,
        _,
        _,
        _,
    ) = chain(
        line,
        4,
        *ordered_after(
            hidden,
            gate_grad,
            up_grad,
            second_mine,
            second_theirs,
            top_half,
            top_came,
            pair_w,
            down_w,
            qkv_w,
            out_w,
            turned,
            middle,
            inverse_first,
            inverse_second,
            gains_half[1:],
            own_block(gains_half)[:1],
            x_block,
            key_live,
            *tables,
        ),
    )
    mark(both)

    gate_sum, up_sum, query_sum, key_sum, value_sum, output_sum, back, gain_sums = tail_sums(
        line,
        3,
        *ordered_after(
            gate_grads,
            up_grad,
            up_row,
            second_mine,
            second_came,
            dqkv,
            dqkv_row,
            first_mine,
            first_theirs,
            branch,
            mixed_mine,
            mixed_theirs,
            both.reshape(2 * MICRO, groups, SL // groups, block),
            pieces,
        ),
    )
    layer_output, tokens_grad = put_back(deal_order, back)
    gain_size = block // groups
    gain_sums = lax.dynamic_slice_in_dim(gain_sums, dp * gain_size, gain_size, 1)

    return (
        layer_output,
        tokens_grad,
        gain_sums[0],
        query_sum,
        key_sum,
        value_sum,
        output_sum,
        gain_sums[1],
        gate_sum,
        up_sum,
        down_sum,
    )


def solution(mesh):
    in_specs = (
        P(None, None, "dp", ("row", "col")),
        P(),
        P(),
        P(("row", "col")),
        P("row", "col"),
        P("row", "col"),
        P("row", "col"),
        P("col", "row"),
        P(("row", "col")),
        P("row", "col"),
        P("row", "col"),
        P("col", "row"),
        P(None, "dp", None, ("row", "col")),
    )
    out_specs = (
        P(None, None, "dp", ("row", "col")),
        P(None, None, "dp", ("row", "col")),
        P(("row", "col", "dp")),
        P(("row", "dp"), "col"),
        P(("row", "dp"), "col"),
        P(("row", "dp"), "col"),
        P(("col", "dp"), "row"),
        P(("row", "col", "dp")),
        P(("row", "dp"), "col"),
        P(("row", "dp"), "col"),
        P(("col", "dp"), "row"),
    )
    return jax.shard_map(
        per_device, mesh=mesh, in_specs=in_specs, out_specs=out_specs, check_vma=False
    )
```

```python
import math

import jax
import jax.numpy as jnp
from jax import lax
from jax.experimental import pallas as pl
from jax.experimental.pallas import tpu as pltpu
from jax.sharding import PartitionSpec as P

D = 2048
HEADS = 32
HEAD_DIM = 64
SL = 256
MICRO = 2
ROWS = MICRO * SL

EPSILON = 1e-05
ROPE_THETA = 130000.0
MASKED_SCORE = -1000000000.0
F32 = jnp.float32
BF16 = jnp.bfloat16
SWAP = [(0, 1), (1, 0)]


def mm(a, b):
    return jnp.dot(a, b, preferred_element_type=F32)


def mm_nt(a, b):
    return lax.dot_general(a, b, (((1,), (1,)), ((), ())), preferred_element_type=F32)


def mm_tn(a, b):
    return lax.dot_general(a, b, (((0,), (0,)), ((), ())), preferred_element_type=F32)


def rope_tables():
    half = HEAD_DIM // 2
    frequency = jnp.exp(
        jnp.arange(half, dtype=F32) * (-2.0 * math.log(ROPE_THETA) / HEAD_DIM)
    )
    angles = jnp.arange(SL, dtype=F32)[:, None] * frequency[None, :]
    cosine = jnp.cos(angles)
    sine = jnp.sin(angles)
    zero = jnp.zeros_like(sine)
    table_cos = jnp.concatenate([cosine] * 4, axis=1)
    table_first = jnp.concatenate([sine, zero] * 2, axis=1)
    table_second = jnp.concatenate([zero, sine] * 2, axis=1)
    return table_cos, table_first, table_second


def turn(v, cos, first, second):
    ahead = pltpu.roll(v, 128 - HEAD_DIM // 2, 1)
    behind = pltpu.roll(v, HEAD_DIM // 2, 1)
    return v * cos - ahead * first + behind * second


def turn_back(v, cos, first, second):
    ahead = pltpu.roll(v, 128 - HEAD_DIM // 2, 1)
    behind = pltpu.roll(v, HEAD_DIM // 2, 1)
    return v * cos + ahead * first - behind * second


def head_mask(head):
    lane = lax.broadcasted_iota(jnp.int32, (SL, 128), 1)
    return (lane // HEAD_DIM) == head


def softmax_of(q, k, allowed):
    scores = mm_nt(q, k) * HEAD_DIM ** (-0.5)
    scores = jnp.where(allowed, scores, MASKED_SCORE)
    exps = jnp.exp(scores - jnp.max(scores, axis=1, keepdims=True))
    return exps / jnp.sum(exps, axis=1, keepdims=True)


FREE = pl.CostEstimate(flops=0, bytes_accessed=0, transcendentals=0)


def whole(shape):
    return pl.BlockSpec(shape, lambda *at: (0,) * len(shape), pipeline_mode=pl.Buffered(1))


def head_outputs(qkv, allowed, cos, first, second):
    qr = turn(qkv[:, :128], cos, first, second).astype(BF16)
    kr = turn(qkv[:, 128:256], cos, first, second).astype(BF16)
    vr = qkv[:, 256:].astype(BF16)
    out = jnp.zeros((SL, 128), F32)
    for head in range(2):
        mask = head_mask(head)
        probs = softmax_of(jnp.where(mask, qr, jnp.zeros_like(qr)), kr, allowed).astype(BF16)
        out = out + mm(probs, jnp.where(mask, vr, jnp.zeros_like(vr)))
    return qr, kr, vr, out.astype(BF16)


def head_grads(qr, kr, vr, od, allowed, cos, first, second):
    dq = jnp.zeros((SL, 128), F32)
    dk = jnp.zeros((SL, 128), F32)
    dv = jnp.zeros((SL, 128), F32)
    zero = jnp.zeros_like(qr)
    for head in range(2):
        mask = head_mask(head)
        q_own = jnp.where(mask, qr, zero)
        k_own = jnp.where(mask, kr, zero)
        od_own = jnp.where(mask, od, zero)
        probs = softmax_of(q_own, kr, allowed)
        d_probs = mm_nt(od_own, vr)
        dv = dv + mm_tn(probs.astype(BF16), od_own)
        inner = jnp.sum(probs * d_probs, axis=1, keepdims=True)
        d_scores = (probs * (d_probs - inner)).astype(BF16)
        dq = dq + mm(d_scores, k_own)
        dk = dk + mm_tn(d_scores, q_own)
    scale = HEAD_DIM ** (-0.5)
    return (
        turn_back(dq * scale, cos, first, second).astype(BF16),
        turn_back(dk * scale, cos, first, second).astype(BF16),
        dv.astype(BF16),
    )


MESH = pl.DeviceIdType.MESH


def greet(*moves):
    barrier = pltpu.get_barrier_semaphore()
    total = 0
    for count, target in moves:
        total = total + count

        @pl.when(count > 0)
        def _():
            pl.semaphore_signal(barrier, inc=1, device_id=target, device_id_type=MESH)

    pl.semaphore_wait(barrier, total)


class ZLine:
    def __init__(self, line, grads, out, stage, came, sems, count, sided):
        self.line, self.grads, self.out, self.stage = line, grads, out, stage
        self.came, self.sems, self.sided = came, sems, sided
        width = grads.shape[1] // count
        self.pieces = [(k, pl.ds(k * width, width)) for k in range(count)]
        self.dp, self.row = lax.axis_index("dp"), lax.axis_index("row")
        self.z = self.dp // 2
        self.last = line - 1
        self.ways = ((0, self.z, 2), (1, self.last - self.z, -2))

    def rows_of(self, dest):
        size = self.grads.shape[0] // self.line
        if self.sided:
            dest = lax.rem(dest + self.line - self.row * (self.line // 2), self.line)
        return pl.ds(pl.multiple_of(dest * size, size), size)

    def copy(self, source, way, step, slot, piece, columns):
        return pltpu.make_async_remote_copy(
            src_ref=source,
            dst_ref=self.came.at[way, slot, :, columns],
            send_sem=self.sems.at[0, way, slot, piece],
            recv_sem=self.sems.at[1, way, slot, piece],
            device_id={"dp": self.dp + step},
            device_id_type=MESH,
        )

    def arrived(self, way, step, slot, piece, columns):
        held = self.came.at[way, slot, :, columns]
        self.copy(held, way, step, slot, piece, columns).wait_recv()
        return held

    def run(self, start, stop):
        def one_step(slot, _):
            for piece, columns in self.pieces:
                for way, place, step in self.ways:
                    far = self.last - slot + place
                    dest = far if step > 0 else self.last - far

                    @pl.when((place == 0) & (place < self.last))
                    def _():
                        source = self.grads.at[self.rows_of(dest), columns]
                        self.copy(source, way, step, slot, piece, columns).start()

                    @pl.when((place > 0) & (place <= slot))
                    def _():
                        held = self.arrived(way, step, slot - 1, piece, columns)

                        @pl.when(place < self.last)
                        def _():
                            held[...] = (
                                held[...].astype(F32)
                                + self.grads[self.rows_of(dest), columns].astype(F32)
                            ).astype(BF16)
                            self.copy(held, way, step, slot, piece, columns).start()

            return 0

        lax.fori_loop(start, stop, one_step, 0)

    def finish(self):
        own = self.rows_of(self.z)
        for piece, columns in self.pieces:
            self.stage[:, columns] = self.grads[own, columns].astype(F32)
            for way, place, step in self.ways:

                @pl.when(place > 0)
                def _():
                    held = self.arrived(way, step, self.last - 1, piece, columns)
                    self.stage[:, columns] += held[...].astype(F32)

        def settle(slot, _):
            for piece, columns in self.pieces:
                for way, place, step in self.ways:

                    @pl.when((place <= slot) & (place < self.last))
                    def _():
                        held = self.came.at[way, slot, :, columns]
                        self.copy(held, way, step, slot, piece, columns).wait_send()

            return 0

        lax.fori_loop(0, self.last, settle, 0)

    def moves(self):
        return (
            (jnp.minimum(self.z, 1), {"dp": self.dp - 2}),
            (jnp.minimum(self.last - self.z, 1), {"dp": self.dp + 2}),
        )


def tiles_loop(width, tile, body):
    def one(j, _):
        body(pl.ds(pl.multiple_of(j * tile, tile), tile), j * tile)
        return 0

    lax.fori_loop(0, width // tile, one, 0)


def tail_kernel(
    line,
    gate_grads,
    up,
    up_row,
    second_mine,
    second_came,
    dqkv,
    dqkv_row,
    first_mine,
    first_theirs,
    branch,
    mixed_mine,
    mixed_theirs,
    both,
    pieces,
    gate_out,
    up_out,
    query_out,
    key_out,
    value_out,
    output_out,
    back,
    gains_out,
    gate_z,
    up_z,
    qkv_z,
    output_z,
    up_grads,
    qkv_grads,
    output_grads,
    up_came,
    up_came_row,
    dqkv_came,
    dqkv_came_row,
    branch_came,
    first_came,
    mixed_came,
    mixed_row,
    mixed_came_row,
    turned_left,
    gate_stage,
    up_stage,
    qkv_stage,
    output_stage,
    gate_sems,
    up_sems,
    qkv_sems,
    output_sems,
    swap_sems,
    out_sems,
    gains,
    back_sems,
    gain_sems,
):
    groups = 2 * line
    dp, row = lax.axis_index("dp"), lax.axis_index("row")
    partner = dp + 1 - 2 * lax.rem(dp, 2)
    gate_line = ZLine(line, gate_grads, gate_out, gate_stage, gate_z, gate_sems, 4, False)
    up_line = ZLine(line, up_grads, up_out, up_stage, up_z, up_sems, 4, False)
    qkv_line = ZLine(line, qkv_grads, None, qkv_stage, qkv_z, qkv_sems, 3, False)
    output_line = ZLine(line, output_grads, output_out, output_stage, output_z, output_sems, 1, True)

    def swap(source, target, at, device):
        return pltpu.make_async_remote_copy(
            src_ref=source,
            dst_ref=target,
            send_sem=swap_sems.at[0, at],
            recv_sem=swap_sems.at[1, at],
            device_id=device,
            device_id_type=MESH,
        )

    up_x = swap(up, up_came, 0, {"dp": partner})
    branch_x = swap(branch, branch_came, 1, {"dp": partner})
    dqkv_x = swap(dqkv, dqkv_came, 2, {"dp": partner})
    up_across = swap(up_came, up_came_row, 3, {"row": 1 - row})
    dqkv_across = swap(dqkv_came, dqkv_came_row, 4, {"row": 1 - row})
    first_x = swap(first_theirs, first_came, 5, {"dp": partner})
    mixed_x = swap(mixed_theirs, mixed_came, 6, {"dp": partner})
    mixed_r = swap(mixed_mine, mixed_row, 7, {"row": 1 - row})
    mixed_across = swap(mixed_came, mixed_came_row, 8, {"row": 1 - row})

    stores = []

    def store(source, target):
        copy = pltpu.make_async_copy(source, target, out_sems.at[len(stores)])
        copy.start()
        stores.append(copy)

    def store_wide(line_of):
        size = line_of.stage.shape[1] // 2
        for part in range(2):
            place = row if part == 0 else 1 - row
            there = pl.ds(pl.multiple_of(place * size, size), size)
            store(line_of.stage.at[:, pl.ds(part * size, size)], line_of.out.at[:, there])

    def store_qkv():
        heads = dqkv.shape[1] // 3
        for part in range(2):
            place = row if part == 0 else 1 - row
            for pair in range(heads // 128):
                for kind, out in enumerate((query_out, key_out, value_out)):
                    here = pl.ds(part * 3 * heads + pair * 384 + kind * 128, 128)
                    there = pl.ds(pl.multiple_of(place * heads + pair * 128, 128), 128)
                    store(qkv_stage.at[:, here], out.at[:, there])

    def returned(step):
        target = lax.rem(dp + step, groups)
        return pltpu.make_async_remote_copy(
            src_ref=both.at[:, target],
            dst_ref=back.at[:, dp],
            send_sem=back_sems.at[0, step],
            recv_sem=back_sems.at[1, step],
            device_id={"dp": target},
            device_id_type=MESH,
        )

    gain_steps = groups.bit_length() - 1

    def gain_copy(step):
        reach = 1 << step
        peer = dp + reach - 2 * reach * lax.rem(dp // reach, 2)
        return pltpu.make_async_remote_copy(
            src_ref=gains.at[0, step],
            dst_ref=gains.at[1, step],
            send_sem=gain_sems.at[0, step],
            recv_sem=gain_sems.at[1, step],
            device_id={"dp": peer},
            device_id_type=MESH,
        )

    def gain_step(step):
        if step >= gain_steps:
            return
        gain_copy(step).wait_recv()
        total = gains[0, step] + gains[1, step]
        if step + 1 == gain_steps:
            gains_out[...] = total
        else:
            gains[0, step + 1] = total
            gain_copy(step + 1).start()

    others = [(jnp.int32(1), {"dp": lax.rem(dp + step, groups)}) for step in range(1, groups)]
    greet(*others, (jnp.int32(1), {"row": 1 - row}))
    gains[0, 0] = pieces[...]
    gain_copy(0).start()
    gate_line.run(0, 1)
    up_x.start()
    mixed_x.start()
    branch_x.start()
    first_x.start()
    dqkv_x.start()
    mixed_r.start()

    def send_back(step, _):
        returned(step).start()
        return 0

    lax.fori_loop(1, groups, send_back, 0)
    store(both.at[:, dp], back.at[:, dp])

    depth = second_mine.shape[0]
    turned_left[:, :depth] = second_mine[...].T
    turned_left[:, depth:] = second_came[...].T
    gate_line.run(1, 2)

    def wide(target, shift, mine, came):
        def body(columns, start):
            total = mm(turned_left[:, :depth], mine[:, columns])
            total = total + mm(turned_left[:, depth:], came[:, columns])
            tile = total.shape[1]
            target[:, pl.ds(pl.multiple_of(shift + start, tile), tile)] = total.astype(BF16)

        tiles_loop(mine.shape[1], 512, body)

    up_x.wait_recv()
    up_across.start()
    gain_step(0)
    gate_line.run(2, line - 1)
    wide(up_grads, 0, up, up_came)
    up_across.wait_recv()
    wide(up_grads, up.shape[1], up_row, up_came_row)
    up_line.run(0, 1)
    gate_line.finish()
    store_wide(gate_line)

    mixed_x.wait_recv()
    mixed_across.start()
    branch_x.wait_recv()

    def side(start, mine, came):
        def body(columns, _):
            total = mm_tn(mine[...], branch[:, columns]) + mm_tn(came[...], branch_came[:, columns])
            output_grads[pl.ds(start, mine.shape[1]), columns] = total.astype(BF16)

        tiles_loop(branch.shape[1], 512, body)

    side(0, mixed_mine, mixed_came)
    mixed_r.wait_recv()
    mixed_across.wait_recv()
    side(mixed_mine.shape[1], mixed_row, mixed_came_row)
    output_line.run(0, 1)
    up_line.run(1, 2)
    gain_step(1)
    first_x.wait_recv()
    turned_left[:, :depth] = first_mine[...].T
    turned_left[:, depth:] = first_came[...].T
    dqkv_x.wait_recv()
    dqkv_across.start()
    wide(qkv_grads, 0, dqkv, dqkv_came)
    dqkv_across.wait_recv()
    wide(qkv_grads, dqkv.shape[1], dqkv_row, dqkv_came_row)
    qkv_line.run(0, 1)
    output_line.run(1, 2)
    up_line.run(2, line - 1)
    qkv_line.run(1, 2)
    output_line.run(2, line - 1)
    for step in range(2, gain_steps):
        gain_step(step)
    up_line.finish()
    store_wide(up_line)
    qkv_line.run(2, line - 1)
    output_line.finish()
    store(output_stage, output_out)
    qkv_line.finish()
    store_qkv()

    def get_back(step, _):
        returned(step).wait()
        return 0

    lax.fori_loop(1, groups, get_back, 0)
    for step in range(gain_steps):
        gain_copy(step).wait_send()
    copies = (up_x, branch_x, dqkv_x, up_across, dqkv_across)
    for copy in copies + (first_x, mixed_x, mixed_r, mixed_across):
        copy.wait_send()
    for copy in stores:
        copy.wait()


def stream(source_of, slots_of, sems, count, body):
    def fetch(j, slot):
        return [
            pltpu.make_async_copy(source, target, sems.at[slot, k])
            for k, (source, target) in enumerate(zip(source_of(j), slots_of(slot)))
        ]

    for copy in fetch(0, 0):
        copy.start()

    def one(j, _):
        slot = lax.rem(j, 2)

        @pl.when(j + 1 < count)
        def _():
            for copy in fetch(j + 1, 1 - slot):
                copy.start()

        for copy in fetch(j, slot):
            copy.wait()
        body(j, slot)
        return 0

    lax.fori_loop(0, count, one, 0)


def rows_loop(body, size=64):
    def one(j, _):
        body(pl.ds(pl.multiple_of(j * size, size), size))
        return 0

    lax.fori_loop(0, ROWS // size, one, 0)


def prepare_kernel(order_ref, len_ref, tokens_ref, top_ref, dealt_ref, block_ref, live_ref):
    groups = tokens_ref.shape[1]
    dp = lax.axis_index("dp")

    def one(at, _):
        micro, slot = at // groups, lax.rem(at, groups)
        dealt_ref[micro, slot] = tokens_ref[micro, order_ref[micro, slot]]
        return 0

    lax.fori_loop(0, MICRO * groups, one, 0)
    for micro in range(MICRO):
        length = len_ref[micro, order_ref[micro, dp]]
        rows = lax.broadcasted_iota(jnp.int32, top_ref.shape[2:], 0)
        top = top_ref[micro, 0]
        top = jnp.where(rows < length, top.astype(F32), 0.0).astype(BF16)
        block_ref[micro * SL : micro * SL + SL, :] = top
        keys = lax.broadcasted_iota(jnp.int32, (1, SL), 1)
        live_ref[micro : micro + 1, :] = jnp.where(keys < length, 1.0, 0.0)


def prepare(order, lengths, tokens, cotangent):
    vmem = pl.BlockSpec(memory_space=pltpu.VMEM)
    smem = pl.BlockSpec(memory_space=pltpu.SMEM)
    return pl.pallas_call(
        prepare_kernel,
        out_shape=(
            jax.ShapeDtypeStruct(tokens.shape, BF16),
            jax.ShapeDtypeStruct((ROWS, cotangent.shape[3]), BF16),
            jax.ShapeDtypeStruct((MICRO, SL), F32),
        ),
        in_specs=[smem, smem, vmem, vmem],
        out_specs=(vmem,) * 3,
        cost_estimate=FREE,
    )(order, lengths, tokens, cotangent)


def front_kernel(
    dealt,
    top_block,
    gain_first,
    gain_second,
    key_live,
    cos,
    first,
    second,
    query_weight,
    key_weight,
    value_weight,
    output_weight,
    gate_weight,
    up_weight,
    down_weight,
    pair_out,
    down_out,
    qkv_out,
    out_out,
    x_in,
    top_half,
    top_came,
    normed_first,
    turned,
    mixed,
    middle,
    inverse_first,
    inverse_second,
    normed_second,
    hidden_grad,
    gains,
    qkv_w,
    out_w,
    gains_own,
    gains_col,
    gains_row,
    pair_held,
    down_held,
    tiles,
    x_came,
    x_half,
    x_other,
    top_col,
    top_row,
    sent,
    row_came,
    kept,
    summed,
    col_came,
    low,
    low_came,
    deal_sems,
    weight_sems,
    local_sems,
    swap_sems,
    tile_sems,
):
    groups = dealt.shape[1]
    dp, row, col = lax.axis_index("dp"), lax.axis_index("row"), lax.axis_index("col")
    partner = {"dp": dp + 1 - 2 * lax.rem(dp, 2)}
    across = {"row": 1 - row}
    beside = {"col": 1 - col}
    half, block = D // 2, D // 4
    heads = query_weight.shape[1] // 2
    quarter = gate_weight.shape[1] // 2
    pending = []

    def remote(source, target, sems, at, device):
        copy = pltpu.make_async_remote_copy(
            src_ref=source,
            dst_ref=target,
            send_sem=sems.at[0, at],
            recv_sem=sems.at[1, at],
            device_id=device,
            device_id_type=MESH,
        )
        copy.start()
        pending.append(copy)
        return copy

    def swap(source, target, at, device):
        return remote(source, target, swap_sems, at, device)

    def columns(w, index, start, size):
        begin = pl.multiple_of(index * (w.shape[1] // 2) + start, 128)
        return w.at[:, pl.ds(begin, size)]

    def rows_half(w, index):
        size = w.shape[0] // 2
        return w.at[pl.ds(pl.multiple_of(index * size, size), size), :]

    locals_started = []

    def local(source, target):
        copy = pltpu.make_async_copy(source, target, local_sems.at[len(locals_started)])
        copy.start()
        locals_started.append(copy)
        return copy

    own_now = []
    for kind, w in enumerate((query_weight, key_weight, value_weight)):
        for at in range(0, heads, 128):
            there = pl.ds(3 * at + 128 * kind, 128)
            own_now.append(local(columns(w, row, at, 128), qkv_w.at[pl.ds(0, half), there]))
    own_now.append(local(rows_half(output_weight, row), out_w.at[:, pl.ds(0, half)]))
    own_gate = local(columns(gate_weight, row, 0, quarter), pair_held.at[0])
    own_up = local(columns(up_weight, row, 0, quarter), pair_held.at[1])
    own_down = local(rows_half(down_weight, row), down_held)
    own_rows = local(dealt.at[:, dp], x_in.at[:, dp])
    others = [(jnp.int32(1), {"dp": lax.rem(dp + step, groups)}) for step in range(1, groups)]
    greet(*others, (jnp.int32(1), across), (jnp.int32(1), beside))

    def dealing(step, micro):
        target = lax.rem(dp + step, groups)
        return pltpu.make_async_remote_copy(
            src_ref=dealt.at[micro, target],
            dst_ref=x_in.at[micro, dp],
            send_sem=deal_sems.at[0, micro, step],
            recv_sem=deal_sems.at[1, micro, step],
            device_id={"dp": target},
            device_id_type=MESH,
        )

    for micro in range(MICRO):

        def send_rows(step, _):
            dealing(step, micro).start()
            return 0

        lax.fori_loop(1, groups, send_rows, 0)
    gains_own[0:1, :] = gain_first[...]
    gains_own[1:2, :] = gain_second[...]
    gain_c = swap(gains_own, gains_col, 13, beside)
    top_c = swap(top_block, top_col, 0, beside)
    weights_now = []
    for kind, w in enumerate((query_weight, key_weight, value_weight)):
        for at in range(0, heads, 128):
            there = qkv_w.at[pl.ds(half, half), pl.ds(3 * at + 128 * kind, 128)]
            weights_now.append(
                remote(columns(w, 1 - row, at, 128), there, weight_sems, len(weights_now), across)
            )
    weights_now.append(
        remote(
            rows_half(output_weight, 1 - row),
            out_w.at[:, pl.ds(half, half)],
            weight_sems,
            len(weights_now),
            across,
        )
    )
    weights_late = []
    for k, w in enumerate((gate_weight, up_weight)):
        there = pair_out.at[pl.ds(half, half), pl.ds(k * quarter, quarter)]
        weights_late.append(
            remote(
                columns(w, 1 - row, 0, quarter), there, weight_sems, len(weights_now) + k, across
            )
        )
    own_gate.wait()
    own_up.wait()
    store_gate = local(pair_held.at[0], pair_out.at[pl.ds(0, half), pl.ds(0, quarter)])
    store_up = local(pair_held.at[1], pair_out.at[pl.ds(0, half), pl.ds(quarter, quarter)])
    own_down.wait()
    store_down = local(down_held, down_out.at[:, pl.ds(0, half)])

    def half_of(own, came):
        return jnp.where(
            col == 0,
            jnp.concatenate([own, came], axis=1),
            jnp.concatenate([came, own], axis=1),
        )

    own_rows.wait()
    x_c = []
    for micro in range(MICRO):

        def take_rows(step, _):
            dealing(step, micro).wait_recv()
            return 0

        lax.fori_loop(1, groups, take_rows, 0)
        x_c.append(swap(x_in.at[micro], x_came.at[micro], 1 + micro, beside))
    gain_c.wait_recv()
    gains[...] = half_of(gains_own[...], gains_col[...])
    gain_r = swap(gains, gains_row, 14, across)
    top_c.wait_recv()

    def top_rows(rows):
        top_half[rows, :] = half_of(top_block[rows, :], top_col[rows, :])

    rows_loop(top_rows)
    top_x = swap(top_half, top_came, 3, partner)

    def micro_rows(micro):
        return pl.ds(micro * SL, SL)

    x_r = []
    for micro in range(MICRO):
        x_c[micro].wait_recv()
        own = x_in[micro].reshape(SL, block)
        came = x_came[micro].reshape(SL, block)
        x_half[micro_rows(micro), :] = half_of(own, came)
        rows = micro_rows(micro)
        x_r.append(swap(x_half.at[rows, :], x_other.at[rows, :], 4 + micro, across))
        if micro == 0:
            for copy in own_now:
                copy.wait()
            for copy in weights_now:
                copy.wait_recv()
    top_r = swap(top_half, top_row, 6, across)
    down_there = down_out.at[:, pl.ds(half, half)]
    down_r = remote(
        rows_half(down_weight, 1 - row), down_there, weight_sems, len(weights_now) + 2, across
    )
    store_qkv = local(qkv_w, qkv_out)
    store_out = local(out_w, out_out)

    lower = lax.broadcasted_iota(jnp.int32, (SL, SL), 1) <= lax.broadcasted_iota(
        jnp.int32, (SL, SL), 0
    )

    gain_r.wait_recv()

    def norm_rows(own_ref, other_ref, at, inverse_ref, out_ref, micro):
        def body(j, _):
            rows = pl.ds(pl.multiple_of(micro * SL + j * 64, 64), 64)
            own = own_ref[rows, :].astype(F32)
            other = other_ref[rows, :].astype(F32)
            total = jnp.sum(own * own, axis=1, keepdims=True)
            total = total + jnp.sum(other * other, axis=1, keepdims=True)
            inverse = lax.rsqrt(total / D + EPSILON)
            inverse_ref[rows, :] = inverse
            out_ref[rows, :half] = (own * inverse * gains[at : at + 1, :]).astype(BF16)
            out_ref[rows, half:] = (other * inverse * gains_row[at : at + 1, :]).astype(BF16)
            return 0

        lax.fori_loop(0, SL // 64, body, 0)

    sum_c = []
    for micro in range(MICRO):
        rows = micro_rows(micro)
        x_r[micro].wait_recv()
        norm_rows(x_half, x_other, 0, inverse_first, normed_first, micro)
        allowed = lower & (key_live[micro : micro + 1, :] > 0.5)

        def attend(at, _):
            there = pl.multiple_of(at * 768, 128)
            qkv = mm(normed_first[rows, :], qkv_w[:, pl.ds(there, 768)])
            for pair in range(2):
                qr, kr, vr, out = head_outputs(
                    qkv[:, pair * 384 : pair * 384 + 384], allowed, cos[...], first[...], second[...]
                )
                begin = there + pair * 384
                for kind, value in enumerate((qr, kr, vr)):
                    turned[rows, pl.ds(pl.multiple_of(begin + kind * 128, 128), 128)] = value
                mixed[rows, pl.ds(pl.multiple_of(at * 256 + pair * 128, 128), 128)] = out
            return 0

        lax.fori_loop(0, heads // 256, attend, 0)
        sent[rows, :] = mm(mixed[rows, :], out_w[:, half:]).astype(BF16)
        sum_r = swap(sent.at[rows, :], row_came.at[rows, :], 7 + micro, across)
        kept[...] = mm(mixed[rows, :], out_w[:, :half])
        sum_r.wait_recv()
        summed[rows, :] = (kept[...] + row_came[rows, :].astype(F32)).astype(BF16)
        sum_c.append(swap(summed.at[rows, :], col_came.at[rows, :], 9 + micro, beside))

    top_r.wait_recv()
    store_down.wait()
    down_r.wait_recv()

    def da_body(j, slot):
        total = mm_nt(top_half[...], tiles[slot, :, :half])
        total = total + mm_nt(top_row[...], tiles[slot, :, half:])
        hidden_grad[:, pl.ds(pl.multiple_of(j * 256, 256), 256)] = total

    stream(
        lambda j: [down_out.at[pl.ds(pl.multiple_of(j * 256, 256), 256), :]],
        lambda slot: [tiles.at[slot]],
        tile_sems,
        quarter // 256,
        da_body,
    )

    low_r = []
    for micro in range(MICRO):
        rows = micro_rows(micro)
        sum_c[micro].wait_recv()

        def middle_rows(j, _):
            here = pl.ds(pl.multiple_of(micro * SL + j * 64, 64), 64)
            total = x_half[here, :].astype(F32) + (
                summed[here, :].astype(F32) + col_came[here, :].astype(F32)
            )
            middle[here, :] = total
            low[here, :] = total.astype(BF16)
            return 0

        lax.fori_loop(0, SL // 64, middle_rows, 0)
        low_r.append(swap(low.at[rows, :], low_came.at[rows, :], 11 + micro, across))
        low_r[micro].wait_recv()
        norm_rows(low, low_came, 1, inverse_second, normed_second, micro)

    top_x.wait_recv()
    for copy in weights_late:
        copy.wait_recv()
    for copy in pending:
        copy.wait_send()

    def close(step, _):
        for micro in range(MICRO):
            dealing(step, micro).wait_send()
        return 0

    lax.fori_loop(1, groups, close, 0)
    for copy in (store_gate, store_up, store_qkv, store_out):
        copy.wait()


def front(line, identity, *values):
    dealt, query_weight, gate_weight = values[0], values[8], values[12]
    groups = dealt.shape[1]
    half, block = D // 2, D // 4
    heads = query_weight.shape[1] // 2
    quarter = gate_weight.shape[1] // 2
    vmem = pl.BlockSpec(memory_space=pltpu.VMEM)
    anywhere = pl.BlockSpec(memory_space=pl.ANY)

    def array(*shape, dtype=BF16):
        return jax.ShapeDtypeStruct(shape, dtype)

    def buffer(*shape, dtype=BF16):
        return pltpu.VMEM(shape, dtype)

    sem = pltpu.SemaphoreType.DMA
    now = 3 * (heads // 128) + 1
    return pl.pallas_call(
        front_kernel,
        out_shape=[
            array(D, 2 * quarter),
            array(quarter, D),
            array(D, 3 * heads),
            array(heads, D),
            array(*dealt.shape),
            array(ROWS, half),
            array(ROWS, half),
            array(ROWS, D),
            array(ROWS, 3 * heads),
            array(ROWS, heads),
            array(ROWS, half, dtype=F32),
            array(ROWS, 1, dtype=F32),
            array(ROWS, 1, dtype=F32),
            array(ROWS, D),
            array(ROWS, quarter, dtype=F32),
            array(2, half, dtype=F32),
        ],
        in_specs=[vmem] * 8 + [anywhere] * 7,
        out_specs=[anywhere] * 4 + [vmem] * 12,
        scratch_shapes=[
            buffer(D, 3 * heads),
            buffer(heads, D),
            buffer(2, block, dtype=F32),
            buffer(2, block, dtype=F32),
            buffer(2, half, dtype=F32),
            buffer(2, half, quarter),
            buffer(quarter, half),
            buffer(2, 256, D),
            buffer(*dealt.shape),
            buffer(ROWS, half),
            buffer(ROWS, half),
            buffer(ROWS, block),
            buffer(ROWS, half),
            buffer(ROWS, half),
            buffer(ROWS, half),
            buffer(SL, half, dtype=F32),
            buffer(ROWS, half),
            buffer(ROWS, half),
            buffer(ROWS, half),
            buffer(ROWS, half),
            sem((2, MICRO, groups)),
            sem((2, now + 3)),
            sem((now + 9,)),
            sem((2, 15)),
            sem((2, 2)),
        ],
        compiler_params=pltpu.CompilerParams(
            collective_id=identity, has_side_effects=True, vmem_limit_bytes=67043328
        ),
        cost_estimate=FREE,
    )(*values)


def chain_kernel(
    line,
    normed,
    hidden_grad,
    second_mine,
    second_theirs,
    top_half,
    top_came,
    pair_w,
    down_w,
    qkv_w,
    out_w,
    turned,
    middle,
    inverse_first,
    inverse_second,
    gain_second,
    gain_first,
    x_own,
    key_live,
    cos,
    first,
    second,
    down_out,
    gate_grads,
    second_came,
    up_grad,
    up_row,
    dqkv,
    dqkv_row,
    branch,
    both_out,
    pieces_out,
    gate_row,
    gate_came,
    gate_came_row,
    hidden,
    gate_grad,
    tiles,
    tall_tiles,
    da_tiles,
    kept,
    sent,
    row_came,
    summed,
    col_came,
    block_sent,
    block_came,
    hidden_row,
    hidden_came,
    hidden_came_row,
    branch_row,
    dots,
    down_grads,
    down_z,
    middle_own,
    layer_own,
    first_own,
    mixed_grad,
    turned_left,
    feed_sum,
    attention_sum,
    swap_sems,
    piece_sems,
    tile_sems,
    down_sems,
    copy_sems,
):
    dp, row, col = lax.axis_index("dp"), lax.axis_index("row"), lax.axis_index("col")
    x = lax.rem(dp, 2)
    partner = {"dp": dp + 1 - 2 * x}
    across = {"row": 1 - row}
    beside = {"col": 1 - col}
    down_line = ZLine(line, down_grads, down_out, None, down_z, down_sems, 4, True)
    half = D // 2
    block = D // 4
    quarter = normed.shape[1]
    pending = []

    def swap(source, target, at, device, sems=swap_sems):
        copy = pltpu.make_async_remote_copy(
            src_ref=source,
            dst_ref=target,
            send_sem=sems.at[0, at],
            recv_sem=sems.at[1, at],
            device_id=device,
            device_id_type=MESH,
        )
        return copy

    def begin(copy):
        copy.start()
        pending.append(copy)
        return copy

    greet(
        *down_line.moves(),
        (jnp.int32(1), partner),
        (jnp.int32(1), across),
        (jnp.int32(1), beside),
    )

    per = line // 2
    width = quarter // line
    tile = min(width, 256)
    each = width // tile

    def hidden_part(index, at):
        return hidden.at[:, pl.ds(pl.multiple_of((2 * at + index) * width, width), width)]

    def feed_columns(j, shift=0):
        piece = j // each
        index = jnp.where(piece < per, 1 - x, x)
        begin = (2 * lax.rem(piece, per) + index) * width + lax.rem(j, each) * tile
        return pl.ds(pl.multiple_of(shift + begin, tile), tile)

    to_x = [
        swap(
            hidden_part(1 - x, at),
            hidden_came.at[:, pl.ds(at * width, width)],
            at,
            partner,
            piece_sems,
        )
        for at in range(per)
    ]
    pending.extend(to_x)

    def feed_body(j, slot):
        gate = mm(normed[...], tall_tiles[slot, 0, :, :tile])
        up = mm(normed[...], tall_tiles[slot, 1, :, :tile])
        da = da_tiles[slot, :, :tile]
        sigmoid = 1.0 / (1.0 + jnp.exp(-gate))
        swish = gate * sigmoid
        there = feed_columns(j)
        hidden[:, there] = (swish * up).astype(BF16)
        gate_grad[:, there] = (da * up * sigmoid * (1.0 + gate * (1.0 - sigmoid))).astype(BF16)
        up_grad[:, there] = (da * swish).astype(BF16)
        for at in range(per):

            @pl.when(j == (at + 1) * each - 1)
            def _():
                to_x[at].start()

    narrow_tile = pl.ds(0, tile)
    stream(
        lambda j: [
            pair_w.at[:, feed_columns(j)],
            pair_w.at[:, feed_columns(j, quarter)],
            hidden_grad.at[:, feed_columns(j)],
        ],
        lambda slot: [
            tall_tiles.at[slot, 0, :, narrow_tile],
            tall_tiles.at[slot, 1, :, narrow_tile],
            da_tiles.at[slot, :, narrow_tile],
        ],
        tile_sems,
        quarter // tile,
        feed_body,
    )
    to_row, on_row = [], []
    for at in range(per):
        there = pl.ds(at * width, width)
        to_row.append(
            begin(swap(hidden_part(x, at), hidden_row.at[:, there], per + at, across, piece_sems))
        )
    second_x = begin(swap(second_theirs, second_came, 0, partner))
    gate_x = begin(swap(gate_grad, gate_came, 1, partner))

    def nt_product(w, depth, start, body):
        stream(
            lambda j: [w.at[pl.ds(pl.multiple_of(start + j * 256, 256), 256), :]],
            lambda slot: [tiles.at[slot, :, pl.ds(0, depth)]],
            tile_sems,
            half // 256,
            body,
        )

    def columns_at(j, size=256):
        return pl.ds(pl.multiple_of(j * size, size), size)

    def pair_body(target, dtype):
        def body(j, slot):
            total = mm_nt(gate_grad[...], tiles[slot, :, :quarter])
            total = total + mm_nt(up_grad[...], tiles[slot, :, quarter:])
            target[:, columns_at(j)] = total.astype(dtype)

        return body

    nt_product(pair_w, 2 * quarter, half, pair_body(sent, BF16))
    pair_r = begin(swap(sent, row_came.at[0], 2, across))
    nt_product(pair_w, 2 * quarter, 0, pair_body(kept, F32))
    pair_r.wait_recv()

    def join_pair(rows):
        summed[rows, :] = (kept[rows, :] + row_came[0, rows, :].astype(F32)).astype(BF16)

    rows_loop(join_pair)
    pair_c = begin(swap(summed, col_came, 3, beside))
    gate_r = begin(swap(gate_grad, gate_row, 4, across))
    up_r = begin(swap(up_grad, up_row, 5, across))

    def down_product(start, target, dtype):
        def body(j, slot):
            target[:, columns_at(j)] = mm(hidden[...], tall_tiles[slot, 0]).astype(dtype)

        stream(
            lambda j: [down_w.at[:, pl.ds(pl.multiple_of(start + j * 256, 256), 256)]],
            lambda slot: [tall_tiles.at[slot, 0]],
            tile_sems,
            half // 256,
            body,
        )

    pair_r.wait_send()
    pending[:] = [copy for copy in pending if copy is not pair_r]
    down_product(half, sent, BF16)
    layer_r = begin(swap(sent, row_came.at[1], 7, across))
    down_product(0, kept, F32)
    layer_r.wait_recv()

    def mine_of(value):
        return jnp.where(col == 0, value[:, :block], value[:, block:])

    def theirs_of(value):
        return jnp.where(col == 0, value[:, block:], value[:, :block])

    def join_layer(rows):
        total = kept[rows, :] + row_came[1, rows, :].astype(F32)
        layer_own[rows, :] = mine_of(total)
        block_sent[0, rows, :] = theirs_of(total).astype(BF16)

    rows_loop(join_layer)
    layer_c = begin(swap(block_sent.at[0], block_came.at[0], 8, beside))
    middle_in = pltpu.make_async_copy(middle, kept, copy_sems.at[0])
    middle_in.start()

    for copy in to_x:
        copy.wait_recv()
    for at in range(per):
        there = pl.ds(at * width, width)
        on_row.append(
            begin(
                swap(
                    hidden_came.at[:, there],
                    hidden_came_row.at[:, there],
                    2 * per + at,
                    across,
                    piece_sems,
                )
            )
        )

    def down_grad(part, left_of, came):
        def body(columns, _):
            for at in range(per):
                there = pl.ds(at * width, width)
                total = mm_tn(left_of(at)[...], top_half[:, columns])
                total = total + mm_tn(came[:, there], top_came[:, columns])
                down_grads[pl.ds((part * per + at) * width, width), columns] = total.astype(BF16)

        tiles_loop(half, 512, body)

    down_grad(0, lambda at: hidden_part(x, at), hidden_came)
    for copy in to_row + on_row:
        copy.wait_recv()
    down_grad(1, lambda at: hidden_row.at[:, pl.ds(at * width, width)], hidden_came_row)
    down_line.run(0, 1)

    middle_in.wait()
    pair_c.wait_recv()
    feed_sum[...] = jnp.zeros_like(feed_sum)

    def second_grads(rows):
        grad = summed[rows, :].astype(F32) + col_came[rows, :].astype(F32)
        return grad, grad * gain_second[1:2, :]

    def norm_first_pass(rows):
        grad, scaled = second_grads(rows)
        held = kept[rows, :]
        feed_sum[...] += jnp.sum(grad * held * inverse_second[rows, :], axis=0, keepdims=True)
        total = jnp.sum(scaled * held, axis=1, keepdims=True)
        dots[0, rows, :] = jnp.broadcast_to(total, (total.shape[0], 128))

    rows_loop(norm_first_pass)
    dot_r = begin(swap(dots.at[0], dots.at[1], 9, across))
    dot_r.wait_recv()

    def norm_second_pass(rows):
        _, scaled = second_grads(rows)
        held = kept[rows, :]
        inverse = inverse_second[rows, :]
        dot = dots[0, rows, :1] + dots[1, rows, :1]
        grad = (
            top_half[rows, :].astype(F32) + scaled * inverse - held * (inverse**3 * dot / D)
        )
        branch[rows, :] = grad.astype(BF16)
        middle_own[rows, :] = mine_of(grad)
        layer_own[rows, :] += mine_of(held)

    rows_loop(norm_second_pass)
    branch_r = begin(swap(branch, branch_row, 10, across))
    branch_r.wait_recv()

    def mixed_body(j, slot):
        total = mm_nt(branch[...], tiles[slot, :, :half])
        total = total + mm_nt(branch_row[...], tiles[slot, :, half:D])
        mixed_grad[:, columns_at(j)] = total.astype(BF16)

    stream(
        lambda j: [out_w.at[pl.ds(pl.multiple_of(j * 256, 256), 256), :]],
        lambda slot: [tiles.at[slot, :, pl.ds(0, D)]],
        tile_sems,
        out_w.shape[0] // 256,
        mixed_body,
    )
    down_line.run(1, 2)
    pairs = turned.shape[1] // 384
    lower = lax.broadcasted_iota(jnp.int32, (SL, SL), 1) <= lax.broadcasted_iota(
        jnp.int32, (SL, SL), 0
    )

    def attend(at, _):
        micro, pair = at // pairs, lax.rem(at, pairs)
        rows = pl.ds(pl.multiple_of(micro * SL, SL), SL)

        def part(kind):
            return pl.ds(pl.multiple_of(pair * 384 + kind * 128, 128), 128)

        allowed = lower & (key_live[pl.ds(micro, 1), :] > 0.5)
        dq, dk, dv = head_grads(
            turned[rows, part(0)],
            turned[rows, part(1)],
            turned[rows, part(2)],
            mixed_grad[rows, pl.ds(pl.multiple_of(pair * 128, 128), 128)],
            allowed,
            cos[...],
            first[...],
            second[...],
        )
        dqkv[rows, part(0)] = dq
        dqkv[rows, part(1)] = dk
        dqkv[rows, part(2)] = dv
        return 0

    lax.fori_loop(0, MICRO * pairs, attend, 0)

    def first_body(target, dtype):
        def body(j, slot):
            total = mm_nt(dqkv[...], tiles[slot, :, : dqkv.shape[1]])
            target[:, columns_at(j)] = total.astype(dtype)

        return body

    layer_r.wait_send()
    pending[:] = [copy for copy in pending if copy is not layer_r]
    nt_product(qkv_w, dqkv.shape[1], half, first_body(sent, BF16))
    first_r = begin(swap(sent, row_came.at[2], 11, across))
    dqkv_r = begin(swap(dqkv, dqkv_row, 12, across))
    nt_product(qkv_w, dqkv.shape[1], 0, first_body(kept, F32))
    first_r.wait_recv()

    def join_first(rows):
        total = kept[rows, :] + row_came[2, rows, :].astype(F32)
        first_own[rows, :] = mine_of(total)
        block_sent[1, rows, :] = theirs_of(total).astype(BF16)

    rows_loop(join_first)
    first_c = begin(swap(block_sent.at[1], block_came.at[1], 13, beside))
    down_line.run(2, line - 1)

    second_x.wait_recv()
    depth = second_mine.shape[0]
    turned_left[:, :depth] = second_mine[...].T
    turned_left[:, depth:] = second_came[...].T
    gate_x.wait_recv()
    gate_on = begin(swap(gate_came, gate_came_row, 14, across))

    def gate_part(shift, sources, values):
        def body(j, slot):
            mine, came = values(j, slot)
            total = mm(turned_left[:, :depth], mine) + mm(turned_left[:, depth:], came)
            there = pl.ds(pl.multiple_of(shift + j * 256, 256), 256)
            gate_grads[:, there] = total.astype(BF16)

        stream(
            lambda j: [source.at[:, columns_at(j)] for source in sources],
            lambda slot: [tall_tiles.at[slot, k, pl.ds(0, ROWS)] for k in range(len(sources))],
            tile_sems,
            quarter // 256,
            body,
        )

    gate_part(
        0,
        [gate_came],
        lambda j, slot: (gate_grad[:, columns_at(j)], tall_tiles[slot, 0, :ROWS]),
    )
    gate_r.wait_recv()
    gate_on.wait_recv()
    gate_part(
        quarter,
        [gate_row, gate_came_row],
        lambda j, slot: (tall_tiles[slot, 0, :ROWS], tall_tiles[slot, 1, :ROWS]),
    )

    layer_c.wait_recv()
    first_c.wait_recv()
    attention_sum[...] = jnp.zeros_like(attention_sum)

    def last_first_pass(rows):
        layer = layer_own[rows, :] + block_came[0, rows, :].astype(F32)
        both_out[rows, :] = layer.astype(BF16)
        grad = first_own[rows, :] + block_came[1, rows, :].astype(F32)
        first_own[rows, :] = grad
        held = x_own[rows, :].astype(F32)
        attention_sum[...] += jnp.sum(grad * held * inverse_first[rows, :], axis=0, keepdims=True)
        total = jnp.sum(grad * gain_first[...] * held, axis=1, keepdims=True)
        dots[2, rows, :] = jnp.broadcast_to(total, (total.shape[0], 128))

    rows_loop(last_first_pass)
    dot_r = begin(swap(dots.at[2], dots.at[3], 15, across))
    dot_r.wait_recv()

    def add_dots(rows):
        dots[4, rows, :] = dots[2, rows, :] + dots[3, rows, :]

    rows_loop(add_dots)
    dot_c = begin(swap(dots.at[4], dots.at[5], 16, beside))
    dot_c.wait_recv()

    def last_second_pass(rows):
        inverse = inverse_first[rows, :]
        dot = dots[4, rows, :1] + dots[5, rows, :1]
        scaled = first_own[rows, :] * gain_first[...]
        held = x_own[rows, :].astype(F32)
        grad = middle_own[rows, :] + scaled * inverse - held * (inverse**3 * dot / D)
        below = pl.ds(pl.multiple_of(rows.start + ROWS, rows.size), rows.size)
        both_out[below, :] = grad.astype(BF16)

    rows_loop(last_second_pass)
    pieces_out[0:1, :] = attention_sum[...]
    pieces_out[1:2, :] = mine_of(feed_sum[...])

    down_line.stage = kept.at[pl.ds(0, down_grads.shape[0] // line), :]
    down_line.finish()
    down_store = pltpu.make_async_copy(down_line.stage, down_out, copy_sems.at[1])
    down_store.start()
    for copy in (up_r, dqkv_r):
        copy.wait_recv()
    for copy in pending:
        copy.wait_send()
    down_store.wait()


def chain(line, identity, *values):
    quarter = values[1].shape[1]
    narrow = values[2].shape[1]
    qkv_width = values[10].shape[1]
    half, block = D // 2, D // 4
    rows = quarter // 2
    vmem = pl.BlockSpec(memory_space=pltpu.VMEM)
    anywhere = pl.BlockSpec(memory_space=pl.ANY)
    outside = {1, 3, 6, 7, 8, 9, 11}

    def array(*shape, dtype=BF16):
        return jax.ShapeDtypeStruct(shape, dtype)

    def buffer(*shape, dtype=BF16):
        return pltpu.VMEM(shape, dtype)

    outs = [
        (array(2 * rows // line, half, dtype=F32), anywhere),
        (array(narrow, 2 * quarter), vmem),
        (array(ROWS, narrow), vmem),
        (array(ROWS, quarter), vmem),
        (array(ROWS, quarter), anywhere),
        (array(ROWS, qkv_width), vmem),
        (array(ROWS, qkv_width), anywhere),
        (array(ROWS, half), vmem),
        (array(2 * ROWS, block), vmem),
        (array(2, block, dtype=F32), vmem),
        (array(ROWS, quarter), anywhere),
        (array(ROWS, quarter), anywhere),
        (array(ROWS, quarter), anywhere),
    ]
    sem = pltpu.SemaphoreType.DMA
    return pl.pallas_call(
        lambda *refs: chain_kernel(line, *refs),
        out_shape=[shape for shape, _ in outs],
        in_specs=[anywhere if k in outside else vmem for k in range(len(values))],
        out_specs=[place for _, place in outs],
        scratch_shapes=[
            buffer(ROWS, quarter),
            buffer(ROWS, quarter),
            buffer(2, 256, 2 * quarter),
            buffer(2, 2, quarter, 256),
            buffer(2, ROWS, 256, dtype=F32),
            buffer(ROWS, half, dtype=F32),
            buffer(ROWS, half),
            buffer(3, ROWS, half),
            buffer(ROWS, half),
            buffer(ROWS, half),
            buffer(2, ROWS, block),
            buffer(2, ROWS, block),
            buffer(ROWS, rows),
            buffer(ROWS, rows),
            buffer(ROWS, rows),
            buffer(ROWS, half),
            buffer(6, ROWS, 128, dtype=F32),
            buffer(2 * rows, half),
            buffer(2, line - 1, 2 * rows // line, half),
            buffer(ROWS, block, dtype=F32),
            buffer(ROWS, block, dtype=F32),
            buffer(ROWS, block, dtype=F32),
            buffer(ROWS, qkv_width // 3),
            buffer(narrow, 2 * ROWS),
            buffer(1, half, dtype=F32),
            buffer(1, block, dtype=F32),
            sem((2, 17)),
            sem((2, 3 * (line // 2))),
            sem((2, 3)),
            sem((2, 2, line - 1, 4)),
            sem((2,)),
        ],
        compiler_params=pltpu.CompilerParams(
            collective_id=identity, has_side_effects=True, vmem_limit_bytes=67043328
        ),
        cost_estimate=FREE,
    )(*values)


def tail_sums(line, identity, *values):
    (gate_grads, up, _, _, _, dqkv, _, _, _, branch) = values[:10]
    rows = gate_grads.shape[0]
    side_rows = 2 * values[10].shape[1]
    tokens = up.shape[0]
    widths = (gate_grads.shape[1], gate_grads.shape[1], 2 * dqkv.shape[1], branch.shape[1])
    heights = (rows, rows, rows, side_rows)
    pieces = (4, 4, 3, 1)
    sizes = [(h // line, w) for h, w in zip(heights, widths)]
    vmem = pl.BlockSpec(memory_space=pltpu.VMEM)
    anywhere = pl.BlockSpec(memory_space=pl.ANY)
    both, gains = values[12:]
    height = sizes[0][0]
    gain_steps = both.shape[1].bit_length() - 1

    def buffer(*shape):
        return pltpu.VMEM(shape, BF16)

    def array(*shape):
        return jax.ShapeDtypeStruct(shape, F32)

    return pl.pallas_call(
        lambda *refs: tail_kernel(line, *refs),
        out_shape=[
            array(*sizes[0]),
            array(*sizes[1]),
            array(height, widths[2] // 3),
            array(height, widths[2] // 3),
            array(height, widths[2] // 3),
            array(*sizes[3]),
            jax.ShapeDtypeStruct(both.shape, BF16),
            array(*gains.shape),
        ],
        in_specs=[vmem] * 12 + [anywhere, vmem],
        out_specs=[anywhere] * 7 + [vmem],
        scratch_shapes=[buffer(2, line - 1, *size) for size in sizes]
        + [buffer(h, w) for h, w in zip(heights[1:], widths[1:])]
        + [buffer(*up.shape)] * 2
        + [buffer(*dqkv.shape)] * 2
        + [buffer(*branch.shape), buffer(*values[7].shape)]
        + [buffer(*values[10].shape)] * 3
        + [buffer(rows, 2 * tokens)]
        + [pltpu.VMEM(size, F32) for size in sizes]
        + [pltpu.SemaphoreType.DMA((2, 2, line - 1, count)) for count in pieces]
        + [pltpu.SemaphoreType.DMA((2, 9)), pltpu.SemaphoreType.DMA((6 + widths[2] // 128,))]
        + [pltpu.VMEM((2, gain_steps, *gains.shape), F32)]
        + [
            pltpu.SemaphoreType.DMA((2, both.shape[1])),
            pltpu.SemaphoreType.DMA((2, gain_steps)),
        ],
        compiler_params=pltpu.CompilerParams(
            collective_id=identity, has_side_effects=True, vmem_limit_bytes=67043328
        ),
        cost_estimate=FREE,
    )(*values)


def finish_kernel(count, order_ref, back_ref, *refs):
    sums, rest = refs[:count], refs[count:]
    layer_ref, grad_ref = rest[:2]
    outs, held, sems = rest[2 : 2 + count], rest[2 + count : 2 + 2 * count], rest[2 + 2 * count]
    groups = back_ref.shape[1]
    loads = [pltpu.make_async_copy(sums[k], held[k], sems.at[0, k]) for k in range(count)]
    stores = [pltpu.make_async_copy(held[k], outs[k], sems.at[1, k]) for k in range(count)]
    for copy in loads:
        copy.start()

    def one(at, _):
        micro, slot = at // groups, lax.rem(at, groups)
        place = order_ref[micro, slot]
        layer_ref[micro, place] = back_ref[micro, slot]
        grad_ref[micro, place] = back_ref[MICRO + micro, slot]
        return 0

    lax.fori_loop(0, MICRO * groups, one, 0)
    for load, store in zip(loads, stores):
        load.wait()
        store.start()
    for store in stores:
        store.wait()


def finish(order, back, *sums):
    vmem = pl.BlockSpec(memory_space=pltpu.VMEM)
    anywhere = pl.BlockSpec(memory_space=pl.ANY)
    rows = jax.ShapeDtypeStruct((MICRO,) + back.shape[1:], BF16)
    count = len(sums)
    return pl.pallas_call(
        lambda *refs: finish_kernel(count, *refs),
        out_shape=[rows, rows] + [jax.ShapeDtypeStruct(v.shape, F32) for v in sums],
        in_specs=[pl.BlockSpec(memory_space=pltpu.SMEM), vmem] + [anywhere] * count,
        out_specs=[vmem, vmem] + [anywhere] * count,
        scratch_shapes=[pltpu.VMEM(v.shape, F32) for v in sums]
        + [pltpu.SemaphoreType.DMA((2, count))],
        cost_estimate=FREE,
    )(order, back, *sums)


def per_device(
    tokens,
    lengths,
    deal_order,
    attention_gain,
    query_weight,
    key_weight,
    value_weight,
    output_weight,
    feed_gain,
    gate_weight,
    up_weight,
    down_weight,
    cotangent,
):
    groups = lax.axis_size("dp")
    line = groups // 2
    dp = lax.axis_index("dp")
    row = lax.axis_index("row")
    col = lax.axis_index("col")
    z, x = dp // 2, dp % 2
    half = D // 2
    block = D // 4

    def over_row(v):
        return lax.ppermute(v, "row", SWAP)

    def over_col(v):
        return lax.ppermute(v, "col", SWAP)

    def ordered(own, other, index, axis=-1):
        return jnp.where(
            index == 0,
            jnp.concatenate([own, other], axis=axis),
            jnp.concatenate([other, own], axis=axis),
        )

    def x_parts(v, width):
        even = jnp.concatenate(
            [v[:, s : s + width] for s in range(0, v.shape[1], 2 * width)], axis=1
        )
        odd = jnp.concatenate(
            [v[:, s : s + width] for s in range(width, v.shape[1], 2 * width)], axis=1
        )
        return jnp.where(x == 0, even, odd), jnp.where(x == 0, odd, even)

    def plain(*values):
        return values

    dealt, top_block, key_live = prepare(deal_order, lengths, tokens, cotangent)
    tables = rope_tables()
    (
        pair_w,
        down_w,
        qkv_w,
        out_w,
        x_block,
        top_half,
        top_came,
        normed_first,
        turned,
        mixed,
        middle,
        inverse_first,
        inverse_second,
        normed_second,
        hidden_grad,
        gains_half,
    ) = front(
        line,
        0,
        dealt,
        top_block,
        attention_gain.reshape(1, block),
        feed_gain.reshape(1, block),
        key_live,
        *tables,
        query_weight,
        key_weight,
        value_weight,
        output_weight,
        gate_weight,
        up_weight,
        down_weight,
    )
    x_block = x_block.reshape(ROWS, block)
    narrow = half // groups
    first_mine, first_theirs = x_parts(normed_first[:, :half], narrow)
    mixed_mine, mixed_theirs = x_parts(mixed, 2 * mixed.shape[1] // groups)
    second_mine, second_theirs = x_parts(normed_second[:, :half], narrow)
    (
        down_sum,
        gate_grads,
        second_came,
        up_grad,
        up_row,
        dqkv,
        dqkv_row,
        branch,
        both,
        pieces,
        _,
        _,
        _,
    ) = chain(
        line,
        4,
        *plain(
            normed_second,
            hidden_grad,
            second_mine,
            second_theirs,
            top_half,
            top_came,
            pair_w,
            down_w,
            qkv_w,
            out_w,
            turned,
            middle,
            inverse_first,
            inverse_second,
            gains_half,
            attention_gain.reshape(1, block),
            x_block,
            key_live,
            *tables,
        ),
    )

    gate_sum, up_sum, query_sum, key_sum, value_sum, output_sum, back, gain_sums = tail_sums(
        line,
        3,
        *plain(
            gate_grads,
            up_grad,
            up_row,
            second_mine,
            second_came,
            dqkv,
            dqkv_row,
            first_mine,
            first_theirs,
            branch,
            mixed_mine,
            mixed_theirs,
            both.reshape(2 * MICRO, groups, SL // groups, block),
            pieces,
        ),
    )
    (
        layer_output,
        tokens_grad,
        down_sum,
        gate_sum,
        up_sum,
        query_sum,
        key_sum,
        value_sum,
        output_sum,
    ) = finish(
        deal_order,
        back,
        down_sum,
        gate_sum,
        up_sum,
        query_sum,
        key_sum,
        value_sum,
        output_sum,
    )
    gain_size = block // groups
    gain_sums = lax.dynamic_slice_in_dim(gain_sums, dp * gain_size, gain_size, 1)

    return (
        layer_output,
        tokens_grad,
        gain_sums[0],
        query_sum,
        key_sum,
        value_sum,
        output_sum,
        gain_sums[1],
        gate_sum,
        up_sum,
        down_sum,
    )


def solution(mesh):
    in_specs = (
        P(None, None, "dp", ("row", "col")),
        P(),
        P(),
        P(("row", "col")),
        P("row", "col"),
        P("row", "col"),
        P("row", "col"),
        P("col", "row"),
        P(("row", "col")),
        P("row", "col"),
        P("row", "col"),
        P("col", "row"),
        P(None, "dp", None, ("row", "col")),
    )
    out_specs = (
        P(None, None, "dp", ("row", "col")),
        P(None, None, "dp", ("row", "col")),
        P(("row", "col", "dp")),
        P(("row", "dp"), "col"),
        P(("row", "dp"), "col"),
        P(("row", "dp"), "col"),
        P(("col", "dp"), "row"),
        P(("row", "col", "dp")),
        P(("row", "dp"), "col"),
        P(("row", "dp"), "col"),
        P(("col", "dp"), "row"),
    )
    return jax.shard_map(
        per_device, mesh=mesh, in_specs=in_specs, out_specs=out_specs, check_vma=False
    )
```

```python
import math

import jax
import jax.numpy as jnp
from jax import lax
from jax.experimental import pallas as pl
from jax.experimental.pallas import tpu as pltpu
from jax.sharding import PartitionSpec as P

D = 2048
HEADS = 32
HEAD_DIM = 64
SL = 256
MICRO = 2
ROWS = MICRO * SL

EPSILON = 1e-05
ROPE_THETA = 130000.0
MASKED_SCORE = -1000000000.0
F32 = jnp.float32
BF16 = jnp.bfloat16
SWAP = [(0, 1), (1, 0)]


def mm(a, b):
    return jnp.dot(a, b, preferred_element_type=F32)


def mm_nt(a, b):
    return lax.dot_general(a, b, (((1,), (1,)), ((), ())), preferred_element_type=F32)


def mm_tn(a, b):
    return lax.dot_general(a, b, (((0,), (0,)), ((), ())), preferred_element_type=F32)


def rope_tables():
    half = HEAD_DIM // 2
    frequency = jnp.exp(
        jnp.arange(half, dtype=F32) * (-2.0 * math.log(ROPE_THETA) / HEAD_DIM)
    )
    angles = jnp.arange(SL, dtype=F32)[:, None] * frequency[None, :]
    cosine = jnp.cos(angles)
    sine = jnp.sin(angles)
    zero = jnp.zeros_like(sine)
    table_cos = jnp.concatenate([cosine] * 4, axis=1)
    table_first = jnp.concatenate([sine, zero] * 2, axis=1)
    table_second = jnp.concatenate([zero, sine] * 2, axis=1)
    return table_cos, table_first, table_second


def turn(v, cos, first, second):
    ahead = pltpu.roll(v, 128 - HEAD_DIM // 2, 1)
    behind = pltpu.roll(v, HEAD_DIM // 2, 1)
    return v * cos - ahead * first + behind * second


def turn_back(v, cos, first, second):
    ahead = pltpu.roll(v, 128 - HEAD_DIM // 2, 1)
    behind = pltpu.roll(v, HEAD_DIM // 2, 1)
    return v * cos + ahead * first - behind * second


def head_mask(head):
    lane = lax.broadcasted_iota(jnp.int32, (SL, 128), 1)
    return (lane // HEAD_DIM) == head


def softmax_of(q, k, allowed):
    scores = mm_nt(q, k) * HEAD_DIM ** (-0.5)
    scores = jnp.where(allowed, scores, MASKED_SCORE)
    exps = jnp.exp(scores - jnp.max(scores, axis=1, keepdims=True))
    return exps / jnp.sum(exps, axis=1, keepdims=True)


FREE = pl.CostEstimate(flops=0, bytes_accessed=0, transcendentals=0)


def whole(shape):
    return pl.BlockSpec(shape, lambda *at: (0,) * len(shape), pipeline_mode=pl.Buffered(1))


def head_outputs(qkv, allowed, cos, first, second):
    qr = turn(qkv[:, :128], cos, first, second).astype(BF16)
    kr = turn(qkv[:, 128:256], cos, first, second).astype(BF16)
    vr = qkv[:, 256:].astype(BF16)
    out = jnp.zeros((SL, 128), F32)
    for head in range(2):
        mask = head_mask(head)
        probs = softmax_of(jnp.where(mask, qr, jnp.zeros_like(qr)), kr, allowed).astype(BF16)
        out = out + mm(probs, jnp.where(mask, vr, jnp.zeros_like(vr)))
    return qr, kr, vr, out.astype(BF16)


def head_grads(qr, kr, vr, od, allowed, cos, first, second):
    dq = jnp.zeros((SL, 128), F32)
    dk = jnp.zeros((SL, 128), F32)
    dv = jnp.zeros((SL, 128), F32)
    zero = jnp.zeros_like(qr)
    for head in range(2):
        mask = head_mask(head)
        q_own = jnp.where(mask, qr, zero)
        k_own = jnp.where(mask, kr, zero)
        od_own = jnp.where(mask, od, zero)
        probs = softmax_of(q_own, kr, allowed)
        d_probs = mm_nt(od_own, vr)
        dv = dv + mm_tn(probs.astype(BF16), od_own)
        inner = jnp.sum(probs * d_probs, axis=1, keepdims=True)
        d_scores = (probs * (d_probs - inner)).astype(BF16)
        dq = dq + mm(d_scores, k_own)
        dk = dk + mm_tn(d_scores, q_own)
    scale = HEAD_DIM ** (-0.5)
    return (
        turn_back(dq * scale, cos, first, second).astype(BF16),
        turn_back(dk * scale, cos, first, second).astype(BF16),
        dv.astype(BF16),
    )


MESH = pl.DeviceIdType.MESH


def greet(*moves):
    barrier = pltpu.get_barrier_semaphore()
    total = 0
    for count, target in moves:
        total = total + count

        @pl.when(count > 0)
        def _():
            pl.semaphore_signal(barrier, inc=1, device_id=target, device_id_type=MESH)

    pl.semaphore_wait(barrier, total)


class ZLine:
    def __init__(self, line, grads, out, stage, came, sems, count, sided):
        self.line, self.grads, self.out, self.stage = line, grads, out, stage
        self.came, self.sems, self.sided = came, sems, sided
        width = grads.shape[1] // count
        self.pieces = [(k, pl.ds(k * width, width)) for k in range(count)]
        self.dp, self.row = lax.axis_index("dp"), lax.axis_index("row")
        self.z = self.dp // 2
        self.last = line - 1
        self.ways = ((0, self.z, 2), (1, self.last - self.z, -2))

    def rows_of(self, dest):
        size = self.grads.shape[0] // self.line
        if self.sided:
            dest = lax.rem(dest + self.line - self.row * (self.line // 2), self.line)
        return pl.ds(pl.multiple_of(dest * size, size), size)

    def copy(self, source, way, step, slot, piece, columns):
        return pltpu.make_async_remote_copy(
            src_ref=source,
            dst_ref=self.came.at[way, slot, :, columns],
            send_sem=self.sems.at[0, way, slot, piece],
            recv_sem=self.sems.at[1, way, slot, piece],
            device_id={"dp": self.dp + step},
            device_id_type=MESH,
        )

    def arrived(self, way, step, slot, piece, columns):
        held = self.came.at[way, slot, :, columns]
        self.copy(held, way, step, slot, piece, columns).wait_recv()
        return held

    def run(self, start, stop):
        def one_step(slot, _):
            for piece, columns in self.pieces:
                for way, place, step in self.ways:
                    far = self.last - slot + place
                    dest = far if step > 0 else self.last - far

                    @pl.when((place == 0) & (place < self.last))
                    def _():
                        source = self.grads.at[self.rows_of(dest), columns]
                        self.copy(source, way, step, slot, piece, columns).start()

                    @pl.when((place > 0) & (place <= slot))
                    def _():
                        held = self.arrived(way, step, slot - 1, piece, columns)

                        @pl.when(place < self.last)
                        def _():
                            held[...] = (
                                held[...].astype(F32)
                                + self.grads[self.rows_of(dest), columns].astype(F32)
                            ).astype(BF16)
                            self.copy(held, way, step, slot, piece, columns).start()

            return 0

        lax.fori_loop(start, stop, one_step, 0)

    def finish(self):
        own = self.rows_of(self.z)
        for piece, columns in self.pieces:
            self.stage[:, columns] = self.grads[own, columns].astype(F32)
            for way, place, step in self.ways:

                @pl.when(place > 0)
                def _():
                    held = self.arrived(way, step, self.last - 1, piece, columns)
                    self.stage[:, columns] += held[...].astype(F32)

        def settle(slot, _):
            for piece, columns in self.pieces:
                for way, place, step in self.ways:

                    @pl.when((place <= slot) & (place < self.last))
                    def _():
                        held = self.came.at[way, slot, :, columns]
                        self.copy(held, way, step, slot, piece, columns).wait_send()

            return 0

        lax.fori_loop(0, self.last, settle, 0)

    def moves(self):
        return (
            (jnp.minimum(self.z, 1), {"dp": self.dp - 2}),
            (jnp.minimum(self.last - self.z, 1), {"dp": self.dp + 2}),
        )


def tiles_loop(width, tile, body):
    def one(j, _):
        body(pl.ds(pl.multiple_of(j * tile, tile), tile), j * tile)
        return 0

    lax.fori_loop(0, width // tile, one, 0)


def tail_kernel(
    line,
    gate_grads,
    up_in,
    up_row_in,
    second_mine_in,
    second_came_in,
    dqkv_in,
    dqkv_row_in,
    first_mine_in,
    first_theirs,
    branch_in,
    mixed_mine_in,
    mixed_theirs,
    both,
    pieces,
    gate_out,
    up_out,
    query_out,
    key_out,
    value_out,
    output_out,
    back,
    gains_out,
    up,
    up_row,
    second_mine,
    second_came,
    dqkv,
    dqkv_row,
    first_mine,
    branch,
    mixed_mine,
    gate_z,
    up_z,
    qkv_z,
    output_z,
    up_grads,
    qkv_grads,
    output_grads,
    up_came,
    up_came_row,
    dqkv_came,
    dqkv_came_row,
    branch_came,
    first_came,
    mixed_came,
    mixed_row,
    mixed_came_row,
    turned_left,
    gate_stage,
    up_stage,
    qkv_stage,
    output_stage,
    gate_sems,
    up_sems,
    qkv_sems,
    output_sems,
    swap_sems,
    out_sems,
    gains,
    back_sems,
    gain_sems,
    fetch_sems,
):
    groups = 2 * line
    dp, row = lax.axis_index("dp"), lax.axis_index("row")
    partner = dp + 1 - 2 * lax.rem(dp, 2)
    gate_line = ZLine(line, gate_grads, gate_out, gate_stage, gate_z, gate_sems, 4, False)
    up_line = ZLine(line, up_grads, up_out, up_stage, up_z, up_sems, 4, False)
    qkv_line = ZLine(line, qkv_grads, None, qkv_stage, qkv_z, qkv_sems, 3, False)
    output_line = ZLine(line, output_grads, output_out, output_stage, output_z, output_sems, 1, True)

    def swap(source, target, at, device):
        return pltpu.make_async_remote_copy(
            src_ref=source,
            dst_ref=target,
            send_sem=swap_sems.at[0, at],
            recv_sem=swap_sems.at[1, at],
            device_id=device,
            device_id_type=MESH,
        )

    fetches = {}
    order = (
        (second_mine_in, second_mine),
        (second_came_in, second_came),
        (up_in, up),
        (up_row_in, up_row),
        (mixed_mine_in, mixed_mine),
        (branch_in, branch),
        (first_mine_in, first_mine),
        (dqkv_in, dqkv),
        (dqkv_row_in, dqkv_row),
    )
    for at, (source, target) in enumerate(order):
        fetches[at] = pltpu.make_async_copy(source, target, fetch_sems.at[at])
        fetches[at].start()
    up_x = swap(up_in, up_came, 0, {"dp": partner})
    branch_x = swap(branch_in, branch_came, 1, {"dp": partner})
    dqkv_x = swap(dqkv_in, dqkv_came, 2, {"dp": partner})
    up_across = swap(up_came, up_came_row, 3, {"row": 1 - row})
    dqkv_across = swap(dqkv_came, dqkv_came_row, 4, {"row": 1 - row})
    first_x = swap(first_theirs, first_came, 5, {"dp": partner})
    mixed_x = swap(mixed_theirs, mixed_came, 6, {"dp": partner})
    mixed_r = swap(mixed_mine_in, mixed_row, 7, {"row": 1 - row})
    mixed_across = swap(mixed_came, mixed_came_row, 8, {"row": 1 - row})

    stores = []

    def store(source, target):
        copy = pltpu.make_async_copy(source, target, out_sems.at[len(stores)])
        copy.start()
        stores.append(copy)

    def store_wide(line_of):
        size = line_of.stage.shape[1] // 2
        for part in range(2):
            place = row if part == 0 else 1 - row
            there = pl.ds(pl.multiple_of(place * size, size), size)
            store(line_of.stage.at[:, pl.ds(part * size, size)], line_of.out.at[:, there])

    def store_qkv():
        heads = dqkv.shape[1] // 3
        for part in range(2):
            place = row if part == 0 else 1 - row
            for pair in range(heads // 128):
                for kind, out in enumerate((query_out, key_out, value_out)):
                    here = pl.ds(part * 3 * heads + pair * 384 + kind * 128, 128)
                    there = pl.ds(pl.multiple_of(place * heads + pair * 128, 128), 128)
                    store(qkv_stage.at[:, here], out.at[:, there])

    def returned(step):
        target = lax.rem(dp + step, groups)
        return pltpu.make_async_remote_copy(
            src_ref=both.at[:, target],
            dst_ref=back.at[:, dp],
            send_sem=back_sems.at[0, step],
            recv_sem=back_sems.at[1, step],
            device_id={"dp": target},
            device_id_type=MESH,
        )

    gain_steps = groups.bit_length() - 1

    def gain_copy(step):
        reach = 1 << step
        peer = dp + reach - 2 * reach * lax.rem(dp // reach, 2)
        return pltpu.make_async_remote_copy(
            src_ref=gains.at[0, step],
            dst_ref=gains.at[1, step],
            send_sem=gain_sems.at[0, step],
            recv_sem=gain_sems.at[1, step],
            device_id={"dp": peer},
            device_id_type=MESH,
        )

    def gain_step(step):
        if step >= gain_steps:
            return
        gain_copy(step).wait_recv()
        total = gains[0, step] + gains[1, step]
        if step + 1 == gain_steps:
            gains_out[...] = total
        else:
            gains[0, step + 1] = total
            gain_copy(step + 1).start()

    others = [(jnp.int32(1), {"dp": lax.rem(dp + step, groups)}) for step in range(1, groups)]
    greet(*others, (jnp.int32(1), {"row": 1 - row}))
    gains[0, 0] = pieces[...]
    gain_copy(0).start()
    gate_line.run(0, 1)
    up_x.start()
    mixed_x.start()
    branch_x.start()
    first_x.start()
    dqkv_x.start()
    mixed_r.start()

    def send_back(step, _):
        returned(step).start()
        return 0

    lax.fori_loop(1, groups, send_back, 0)
    store(both.at[:, dp], back.at[:, dp])

    fetches[0].wait()
    fetches[1].wait()
    depth = second_mine.shape[0]
    turned_left[:, :depth] = second_mine[...].T
    turned_left[:, depth:] = second_came[...].T
    gate_line.run(1, 2)

    def wide(target, shift, mine, came):
        def body(columns, start):
            total = mm(turned_left[:, :depth], mine[:, columns])
            total = total + mm(turned_left[:, depth:], came[:, columns])
            tile = total.shape[1]
            target[:, pl.ds(pl.multiple_of(shift + start, tile), tile)] = total.astype(BF16)

        tiles_loop(mine.shape[1], 512, body)

    up_x.wait_recv()
    up_across.start()
    gain_step(0)
    gate_line.run(2, line - 1)
    fetches[2].wait()
    fetches[3].wait()
    wide(up_grads, 0, up, up_came)
    up_across.wait_recv()
    wide(up_grads, up.shape[1], up_row, up_came_row)
    up_line.run(0, 1)
    gate_line.finish()
    store_wide(gate_line)

    mixed_x.wait_recv()
    mixed_across.start()
    branch_x.wait_recv()

    def side(start, mine, came):
        def body(columns, _):
            total = mm_tn(mine[...], branch[:, columns]) + mm_tn(came[...], branch_came[:, columns])
            output_grads[pl.ds(start, mine.shape[1]), columns] = total.astype(BF16)

        tiles_loop(branch.shape[1], 512, body)

    fetches[4].wait()
    fetches[5].wait()
    side(0, mixed_mine, mixed_came)
    mixed_r.wait_recv()
    mixed_across.wait_recv()
    side(mixed_mine.shape[1], mixed_row, mixed_came_row)
    output_line.run(0, 1)
    up_line.run(1, 2)
    gain_step(1)
    for at in (6, 7, 8):
        fetches[at].wait()
    first_x.wait_recv()
    turned_left[:, :depth] = first_mine[...].T
    turned_left[:, depth:] = first_came[...].T
    dqkv_x.wait_recv()
    dqkv_across.start()
    wide(qkv_grads, 0, dqkv, dqkv_came)
    dqkv_across.wait_recv()
    wide(qkv_grads, dqkv.shape[1], dqkv_row, dqkv_came_row)
    qkv_line.run(0, 1)
    output_line.run(1, 2)
    up_line.run(2, line - 1)
    qkv_line.run(1, 2)
    output_line.run(2, line - 1)
    for step in range(2, gain_steps):
        gain_step(step)
    up_line.finish()
    store_wide(up_line)
    qkv_line.run(2, line - 1)
    output_line.finish()
    store(output_stage, output_out)
    qkv_line.finish()
    store_qkv()

    def get_back(step, _):
        returned(step).wait()
        return 0

    lax.fori_loop(1, groups, get_back, 0)
    for step in range(gain_steps):
        gain_copy(step).wait_send()
    copies = (up_x, branch_x, dqkv_x, up_across, dqkv_across)
    for copy in copies + (first_x, mixed_x, mixed_r, mixed_across):
        copy.wait_send()
    for copy in stores:
        copy.wait()


def stream(source_of, slots_of, sems, count, body):
    def fetch(j, slot):
        return [
            pltpu.make_async_copy(source, target, sems.at[slot, k])
            for k, (source, target) in enumerate(zip(source_of(j), slots_of(slot)))
        ]

    for copy in fetch(0, 0):
        copy.start()

    def one(j, _):
        slot = lax.rem(j, 2)

        @pl.when(j + 1 < count)
        def _():
            for copy in fetch(j + 1, 1 - slot):
                copy.start()

        for copy in fetch(j, slot):
            copy.wait()
        body(j, slot)
        return 0

    lax.fori_loop(0, count, one, 0)


def rows_loop(body, size=64):
    def one(j, _):
        body(pl.ds(pl.multiple_of(j * size, size), size))
        return 0

    lax.fori_loop(0, ROWS // size, one, 0)


def prepare_kernel(order_ref, len_ref, tokens_ref, top_ref, dealt_ref, block_ref, live_ref):
    groups = tokens_ref.shape[1]
    dp = lax.axis_index("dp")

    def one(at, _):
        micro, slot = at // groups, lax.rem(at, groups)
        dealt_ref[micro, slot] = tokens_ref[micro, order_ref[micro, slot]]
        return 0

    lax.fori_loop(0, MICRO * groups, one, 0)
    for micro in range(MICRO):
        length = len_ref[micro, order_ref[micro, dp]]
        rows = lax.broadcasted_iota(jnp.int32, top_ref.shape[2:], 0)
        top = top_ref[micro, 0]
        top = jnp.where(rows < length, top.astype(F32), 0.0).astype(BF16)
        block_ref[micro * SL : micro * SL + SL, :] = top
        keys = lax.broadcasted_iota(jnp.int32, (1, SL), 1)
        live_ref[micro : micro + 1, :] = jnp.where(keys < length, 1.0, 0.0)


def prepare(order, lengths, tokens, cotangent):
    vmem = pl.BlockSpec(memory_space=pltpu.VMEM)
    smem = pl.BlockSpec(memory_space=pltpu.SMEM)
    return pl.pallas_call(
        prepare_kernel,
        out_shape=(
            jax.ShapeDtypeStruct(tokens.shape, BF16),
            jax.ShapeDtypeStruct((ROWS, cotangent.shape[3]), BF16),
            jax.ShapeDtypeStruct((MICRO, SL), F32),
        ),
        in_specs=[smem, smem, vmem, vmem],
        out_specs=(vmem,) * 3,
        cost_estimate=FREE,
    )(order, lengths, tokens, cotangent)


def front_kernel(
    dealt,
    top_block,
    gain_first,
    gain_second,
    key_live,
    cos,
    first,
    second,
    query_weight,
    key_weight,
    value_weight,
    output_weight,
    gate_weight,
    up_weight,
    down_weight,
    pair_out,
    down_out,
    qkv_out,
    out_out,
    x_out,
    top_half_out,
    top_came_out,
    first_mine_out,
    first_theirs_out,
    turned_out,
    mixed_mine_out,
    mixed_theirs_out,
    middle_out,
    second_mine_out,
    second_theirs_out,
    normed_second_out,
    hidden_grad_out,
    inverse_first,
    inverse_second,
    gains,
    x_in,
    top_half,
    top_came,
    normed_first,
    first_mine,
    first_theirs,
    turned,
    mixed,
    mixed_mine,
    mixed_theirs,
    middle,
    second_mine,
    second_theirs,
    normed_second,
    hidden_grad,
    qkv_w,
    out_w,
    gains_own,
    gains_col,
    gains_row,
    pair_held,
    down_held,
    tiles,
    x_came,
    x_half,
    x_other,
    top_col,
    top_row,
    sent,
    row_came,
    kept,
    summed,
    col_came,
    low,
    low_came,
    deal_sems,
    weight_sems,
    local_sems,
    swap_sems,
    tile_sems,
):
    groups = dealt.shape[1]
    dp, row, col = lax.axis_index("dp"), lax.axis_index("row"), lax.axis_index("col")
    x = lax.rem(dp, 2)
    partner = {"dp": dp + 1 - 2 * x}
    across = {"row": 1 - row}
    beside = {"col": 1 - col}
    half, block = D // 2, D // 4
    heads = query_weight.shape[1] // 2
    quarter = gate_weight.shape[1] // 2
    pending = []

    def remote(source, target, sems, at, device):
        copy = pltpu.make_async_remote_copy(
            src_ref=source,
            dst_ref=target,
            send_sem=sems.at[0, at],
            recv_sem=sems.at[1, at],
            device_id=device,
            device_id_type=MESH,
        )
        copy.start()
        pending.append(copy)
        return copy

    def swap(source, target, at, device):
        return remote(source, target, swap_sems, at, device)

    def columns(w, index, start, size):
        begin = pl.multiple_of(index * (w.shape[1] // 2) + start, 128)
        return w.at[:, pl.ds(begin, size)]

    def rows_half(w, index):
        size = w.shape[0] // 2
        return w.at[pl.ds(pl.multiple_of(index * size, size), size), :]

    locals_started = []

    def local(source, target):
        copy = pltpu.make_async_copy(source, target, local_sems.at[len(locals_started)])
        copy.start()
        locals_started.append(copy)
        return copy

    own_now = []
    for kind, w in enumerate((query_weight, key_weight, value_weight)):
        for at in range(0, heads, 128):
            there = pl.ds(3 * at + 128 * kind, 128)
            own_now.append(local(columns(w, row, at, 128), qkv_w.at[pl.ds(0, half), there]))
    own_now.append(local(rows_half(output_weight, row), out_w.at[:, pl.ds(0, half)]))
    own_gate = local(columns(gate_weight, row, 0, quarter), pair_held.at[0])
    own_up = local(columns(up_weight, row, 0, quarter), pair_held.at[1])
    own_down = local(rows_half(down_weight, row), down_held)
    own_rows = local(dealt.at[:, dp], x_in.at[:, dp])
    others = [(jnp.int32(1), {"dp": lax.rem(dp + step, groups)}) for step in range(1, groups)]
    greet(*others, (jnp.int32(1), across), (jnp.int32(1), beside))

    def dealing(step, micro):
        target = lax.rem(dp + step, groups)
        return pltpu.make_async_remote_copy(
            src_ref=dealt.at[micro, target],
            dst_ref=x_in.at[micro, dp],
            send_sem=deal_sems.at[0, micro, step],
            recv_sem=deal_sems.at[1, micro, step],
            device_id={"dp": target},
            device_id_type=MESH,
        )

    for micro in range(MICRO):

        def send_rows(step, _):
            dealing(step, micro).start()
            return 0

        lax.fori_loop(1, groups, send_rows, 0)
    gains_own[0:1, :] = gain_first[...]
    gains_own[1:2, :] = gain_second[...]
    gain_c = swap(gains_own, gains_col, 13, beside)
    top_c = swap(top_block, top_col, 0, beside)
    weights_now = []
    for kind, w in enumerate((query_weight, key_weight, value_weight)):
        for at in range(0, heads, 128):
            there = qkv_w.at[pl.ds(half, half), pl.ds(3 * at + 128 * kind, 128)]
            weights_now.append(
                remote(columns(w, 1 - row, at, 128), there, weight_sems, len(weights_now), across)
            )
    weights_now.append(
        remote(
            rows_half(output_weight, 1 - row),
            out_w.at[:, pl.ds(half, half)],
            weight_sems,
            len(weights_now),
            across,
        )
    )
    weights_late = []
    for k, w in enumerate((gate_weight, up_weight)):
        there = pair_out.at[pl.ds(half, half), pl.ds(k * quarter, quarter)]
        weights_late.append(
            remote(
                columns(w, 1 - row, 0, quarter), there, weight_sems, len(weights_now) + k, across
            )
        )
    own_gate.wait()
    own_up.wait()
    store_gate = local(pair_held.at[0], pair_out.at[pl.ds(0, half), pl.ds(0, quarter)])
    store_up = local(pair_held.at[1], pair_out.at[pl.ds(0, half), pl.ds(quarter, quarter)])
    own_down.wait()
    store_down = local(down_held, down_out.at[:, pl.ds(0, half)])

    def half_of(own, came):
        return jnp.where(
            col == 0,
            jnp.concatenate([own, came], axis=1),
            jnp.concatenate([came, own], axis=1),
        )

    own_rows.wait()
    x_c = []
    for micro in range(MICRO):

        def take_rows(step, _):
            dealing(step, micro).wait_recv()
            return 0

        lax.fori_loop(1, groups, take_rows, 0)
        x_c.append(swap(x_in.at[micro], x_came.at[micro], 1 + micro, beside))
    gain_c.wait_recv()
    gains[...] = half_of(gains_own[...], gains_col[...])
    gain_r = swap(gains, gains_row, 14, across)
    top_c.wait_recv()

    def top_rows(rows):
        top_half[rows, :] = half_of(top_block[rows, :], top_col[rows, :])

    rows_loop(top_rows)
    results = [local(x_in, x_out), local(top_half, top_half_out)]
    top_x = swap(top_half, top_came, 3, partner)

    def micro_rows(micro):
        return pl.ds(micro * SL, SL)

    x_r = []
    for micro in range(MICRO):
        x_c[micro].wait_recv()
        own = x_in[micro].reshape(SL, block)
        came = x_came[micro].reshape(SL, block)
        x_half[micro_rows(micro), :] = half_of(own, came)
        rows = micro_rows(micro)
        x_r.append(swap(x_half.at[rows, :], x_other.at[rows, :], 4 + micro, across))
        if micro == 0:
            for copy in own_now:
                copy.wait()
            for copy in weights_now:
                copy.wait_recv()
    top_r = swap(top_half, top_row, 6, across)
    down_there = down_out.at[:, pl.ds(half, half)]
    down_r = remote(
        rows_half(down_weight, 1 - row), down_there, weight_sems, len(weights_now) + 2, across
    )
    store_qkv = local(qkv_w, qkv_out)
    store_out = local(out_w, out_out)

    lower = lax.broadcasted_iota(jnp.int32, (SL, SL), 1) <= lax.broadcasted_iota(
        jnp.int32, (SL, SL), 0
    )

    gain_r.wait_recv()

    def norm_rows(own_ref, other_ref, at, inverse_ref, out_ref, micro):
        def body(j, _):
            rows = pl.ds(pl.multiple_of(micro * SL + j * 64, 64), 64)
            own = own_ref[rows, :].astype(F32)
            other = other_ref[rows, :].astype(F32)
            total = jnp.sum(own * own, axis=1, keepdims=True)
            total = total + jnp.sum(other * other, axis=1, keepdims=True)
            inverse = lax.rsqrt(total / D + EPSILON)
            inverse_ref[rows, :] = inverse
            out_ref[rows, :half] = (own * inverse * gains[at : at + 1, :]).astype(BF16)
            out_ref[rows, half:] = (other * inverse * gains_row[at : at + 1, :]).astype(BF16)
            return 0

        lax.fori_loop(0, SL // 64, body, 0)

    sum_c = []
    for micro in range(MICRO):
        rows = micro_rows(micro)
        x_r[micro].wait_recv()
        norm_rows(x_half, x_other, 0, inverse_first, normed_first, micro)
        allowed = lower & (key_live[micro : micro + 1, :] > 0.5)

        def attend(at, _):
            there = pl.multiple_of(at * 768, 128)
            qkv = mm(normed_first[rows, :], qkv_w[:, pl.ds(there, 768)])
            for pair in range(2):
                qr, kr, vr, out = head_outputs(
                    qkv[:, pair * 384 : pair * 384 + 384], allowed, cos[...], first[...], second[...]
                )
                begin = there + pair * 384
                for kind, value in enumerate((qr, kr, vr)):
                    turned[rows, pl.ds(pl.multiple_of(begin + kind * 128, 128), 128)] = value
                mixed[rows, pl.ds(pl.multiple_of(at * 256 + pair * 128, 128), 128)] = out
            return 0

        lax.fori_loop(0, heads // 256, attend, 0)
        sent[rows, :] = mm(mixed[rows, :], out_w[:, half:]).astype(BF16)
        sum_r = swap(sent.at[rows, :], row_came.at[rows, :], 7 + micro, across)
        kept[...] = mm(mixed[rows, :], out_w[:, :half])
        sum_r.wait_recv()
        summed[rows, :] = (kept[...] + row_came[rows, :].astype(F32)).astype(BF16)
        sum_c.append(swap(summed.at[rows, :], col_came.at[rows, :], 9 + micro, beside))

    results.append(local(turned, turned_out))

    def by_x(source, mine, theirs, rows, width):
        value = source[rows, : 2 * mine.shape[1]]
        even = [value[:, at : at + width] for at in range(0, value.shape[1], 2 * width)]
        odd = [value[:, at : at + width] for at in range(width, value.shape[1], 2 * width)]
        even, odd = jnp.concatenate(even, axis=1), jnp.concatenate(odd, axis=1)
        mine[rows, :] = jnp.where(x == 0, even, odd)
        theirs[rows, :] = jnp.where(x == 0, odd, even)

    top_r.wait_recv()
    store_down.wait()
    down_r.wait_recv()

    def da_body(j, slot):
        total = mm_nt(top_half[...], tiles[slot, :, :half])
        total = total + mm_nt(top_row[...], tiles[slot, :, half:])
        hidden_grad[:, pl.ds(pl.multiple_of(j * 256, 256), 256)] = total

    stream(
        lambda j: [down_out.at[pl.ds(pl.multiple_of(j * 256, 256), 256), :]],
        lambda slot: [tiles.at[slot]],
        tile_sems,
        quarter // 256,
        da_body,
    )

    results.append(local(hidden_grad, hidden_grad_out))

    def select_rows(rows):
        by_x(normed_first, first_mine, first_theirs, rows, half // groups)
        by_x(mixed, mixed_mine, mixed_theirs, rows, 2 * heads // groups)

    rows_loop(select_rows)
    results.append(local(first_mine, first_mine_out))
    results.append(local(first_theirs, first_theirs_out))
    results.append(local(mixed_mine, mixed_mine_out))
    results.append(local(mixed_theirs, mixed_theirs_out))

    low_r = []
    for micro in range(MICRO):
        rows = micro_rows(micro)
        sum_c[micro].wait_recv()

        def middle_rows(j, _):
            here = pl.ds(pl.multiple_of(micro * SL + j * 64, 64), 64)
            total = x_half[here, :].astype(F32) + (
                summed[here, :].astype(F32) + col_came[here, :].astype(F32)
            )
            middle[here, :] = total
            low[here, :] = total.astype(BF16)
            return 0

        lax.fori_loop(0, SL // 64, middle_rows, 0)
        results.append(local(middle.at[rows, :], middle_out.at[rows, :]))
        low_r.append(swap(low.at[rows, :], low_came.at[rows, :], 11 + micro, across))
        low_r[micro].wait_recv()
        norm_rows(low, low_came, 1, inverse_second, normed_second, micro)
        results.append(local(normed_second.at[rows, :], normed_second_out.at[rows, :]))

        def second_rows(j, _):
            here = pl.ds(pl.multiple_of(micro * SL + j * 64, 64), 64)
            by_x(normed_second, second_mine, second_theirs, here, half // groups)
            return 0

        lax.fori_loop(0, SL // 64, second_rows, 0)
        results.append(local(second_mine.at[rows, :], second_mine_out.at[rows, :]))
        results.append(local(second_theirs.at[rows, :], second_theirs_out.at[rows, :]))

    top_x.wait_recv()
    results.append(local(top_came, top_came_out))
    for copy in weights_late:
        copy.wait_recv()
    for copy in pending:
        copy.wait_send()

    def close(step, _):
        for micro in range(MICRO):
            dealing(step, micro).wait_send()
        return 0

    lax.fori_loop(1, groups, close, 0)
    for copy in [store_gate, store_up, store_qkv, store_out] + results:
        copy.wait()


def front(line, identity, *values):
    dealt, query_weight, gate_weight = values[0], values[8], values[12]
    groups = dealt.shape[1]
    half, block = D // 2, D // 4
    heads = query_weight.shape[1] // 2
    quarter = gate_weight.shape[1] // 2
    vmem = pl.BlockSpec(memory_space=pltpu.VMEM)
    anywhere = pl.BlockSpec(memory_space=pl.ANY)

    def array(*shape, dtype=BF16):
        return jax.ShapeDtypeStruct(shape, dtype)

    def buffer(*shape, dtype=BF16):
        return pltpu.VMEM(shape, dtype)

    sem = pltpu.SemaphoreType.DMA
    now = 3 * (heads // 128) + 1
    held = [
        (dealt.shape, BF16),
        ((ROWS, half), BF16),
        ((ROWS, half), BF16),
        ((ROWS, block), BF16),
        ((ROWS, block), BF16),
        ((ROWS, 3 * heads), BF16),
        ((ROWS, heads // 2), BF16),
        ((ROWS, heads // 2), BF16),
        ((ROWS, half), F32),
        ((ROWS, block), BF16),
        ((ROWS, block), BF16),
        ((ROWS, D), BF16),
        ((ROWS, quarter), F32),
    ]
    normed_first, mixed = ((ROWS, D), BF16), ((ROWS, heads), BF16)
    inside = held[:3] + [normed_first] + held[3:6] + [mixed] + held[6:]
    return pl.pallas_call(
        front_kernel,
        out_shape=[
            array(D, 2 * quarter),
            array(quarter, D),
            array(D, 3 * heads),
            array(heads, D),
            *[array(*shape, dtype=kind) for shape, kind in held],
            array(ROWS, 1, dtype=F32),
            array(ROWS, 1, dtype=F32),
            array(2, half, dtype=F32),
        ],
        in_specs=[vmem] * 8 + [anywhere] * 7,
        out_specs=[anywhere] * (4 + len(held)) + [vmem] * 3,
        scratch_shapes=[
            *[buffer(*shape, dtype=kind) for shape, kind in inside],
            buffer(D, 3 * heads),
            buffer(heads, D),
            buffer(2, block, dtype=F32),
            buffer(2, block, dtype=F32),
            buffer(2, half, dtype=F32),
            buffer(2, half, quarter),
            buffer(quarter, half),
            buffer(2, 256, D),
            buffer(*dealt.shape),
            buffer(ROWS, half),
            buffer(ROWS, half),
            buffer(ROWS, block),
            buffer(ROWS, half),
            buffer(ROWS, half),
            buffer(ROWS, half),
            buffer(SL, half, dtype=F32),
            buffer(ROWS, half),
            buffer(ROWS, half),
            buffer(ROWS, half),
            buffer(ROWS, half),
            sem((2, MICRO, groups)),
            sem((2, now + 3)),
            sem((now + 28,)),
            sem((2, 15)),
            sem((2, 2)),
        ],
        compiler_params=pltpu.CompilerParams(
            collective_id=identity, has_side_effects=True, vmem_limit_bytes=67043328
        ),
        cost_estimate=FREE,
    )(*values)


def chain_kernel(
    line,
    normed,
    hidden_grad,
    second_mine,
    second_theirs,
    top_half,
    top_came,
    pair_w,
    down_w,
    qkv_w,
    out_w,
    turned,
    middle,
    inverse_first,
    inverse_second,
    gain_second,
    gain_first,
    x_own,
    key_live,
    cos,
    first,
    second,
    down_out,
    gate_grads_out,
    second_came_out,
    up_grad_out,
    up_row,
    dqkv_out,
    dqkv_row,
    branch_out,
    both_out,
    pieces_out,
    gate_row,
    gate_came,
    gate_came_row,
    gate_grads,
    second_came,
    up_grad,
    dqkv,
    branch,
    hidden,
    gate_grad,
    tiles,
    tall_tiles,
    da_tiles,
    kept,
    sent,
    row_came,
    summed,
    col_came,
    block_sent,
    block_came,
    hidden_row,
    hidden_came,
    hidden_came_row,
    branch_row,
    dots,
    down_grads,
    down_z,
    middle_own,
    layer_own,
    first_own,
    mixed_grad,
    turned_left,
    feed_sum,
    attention_sum,
    swap_sems,
    piece_sems,
    tile_sems,
    down_sems,
    copy_sems,
):
    dp, row, col = lax.axis_index("dp"), lax.axis_index("row"), lax.axis_index("col")
    x = lax.rem(dp, 2)
    partner = {"dp": dp + 1 - 2 * x}
    across = {"row": 1 - row}
    beside = {"col": 1 - col}
    down_line = ZLine(line, down_grads, down_out, None, down_z, down_sems, 4, True)
    half = D // 2
    block = D // 4
    quarter = normed.shape[1]
    pending, results = [], []

    def result(source, target):
        copy = pltpu.make_async_copy(source, target, copy_sems.at[2 + len(results)])
        copy.start()
        results.append(copy)

    def swap(source, target, at, device, sems=swap_sems):
        copy = pltpu.make_async_remote_copy(
            src_ref=source,
            dst_ref=target,
            send_sem=sems.at[0, at],
            recv_sem=sems.at[1, at],
            device_id=device,
            device_id_type=MESH,
        )
        return copy

    def begin(copy):
        copy.start()
        pending.append(copy)
        return copy

    greet(
        *down_line.moves(),
        (jnp.int32(1), partner),
        (jnp.int32(1), across),
        (jnp.int32(1), beside),
    )

    per = line // 2
    width = quarter // line
    tile = min(width, 256)
    each = width // tile

    def hidden_part(index, at):
        return hidden.at[:, pl.ds(pl.multiple_of((2 * at + index) * width, width), width)]

    def feed_columns(j, shift=0):
        piece = j // each
        index = jnp.where(piece < per, 1 - x, x)
        begin = (2 * lax.rem(piece, per) + index) * width + lax.rem(j, each) * tile
        return pl.ds(pl.multiple_of(shift + begin, tile), tile)

    to_x = [
        swap(
            hidden_part(1 - x, at),
            hidden_came.at[:, pl.ds(at * width, width)],
            at,
            partner,
            piece_sems,
        )
        for at in range(per)
    ]
    pending.extend(to_x)

    def feed_body(j, slot):
        gate = mm(normed[...], tall_tiles[slot, 0, :, :tile])
        up = mm(normed[...], tall_tiles[slot, 1, :, :tile])
        da = da_tiles[slot, :, :tile]
        sigmoid = 1.0 / (1.0 + jnp.exp(-gate))
        swish = gate * sigmoid
        there = feed_columns(j)
        hidden[:, there] = (swish * up).astype(BF16)
        gate_grad[:, there] = (da * up * sigmoid * (1.0 + gate * (1.0 - sigmoid))).astype(BF16)
        up_grad[:, there] = (da * swish).astype(BF16)
        for at in range(per):

            @pl.when(j == (at + 1) * each - 1)
            def _():
                to_x[at].start()

    narrow_tile = pl.ds(0, tile)
    stream(
        lambda j: [
            pair_w.at[:, feed_columns(j)],
            pair_w.at[:, feed_columns(j, quarter)],
            hidden_grad.at[:, feed_columns(j)],
        ],
        lambda slot: [
            tall_tiles.at[slot, 0, :, narrow_tile],
            tall_tiles.at[slot, 1, :, narrow_tile],
            da_tiles.at[slot, :, narrow_tile],
        ],
        tile_sems,
        quarter // tile,
        feed_body,
    )
    to_row, on_row = [], []
    for at in range(per):
        there = pl.ds(at * width, width)
        to_row.append(
            begin(swap(hidden_part(x, at), hidden_row.at[:, there], per + at, across, piece_sems))
        )
    result(up_grad, up_grad_out)
    second_x = begin(swap(second_theirs, second_came, 0, partner))
    gate_x = begin(swap(gate_grad, gate_came, 1, partner))

    def nt_product(w, depth, start, body):
        stream(
            lambda j: [w.at[pl.ds(pl.multiple_of(start + j * 256, 256), 256), :]],
            lambda slot: [tiles.at[slot, :, pl.ds(0, depth)]],
            tile_sems,
            half // 256,
            body,
        )

    def columns_at(j, size=256):
        return pl.ds(pl.multiple_of(j * size, size), size)

    def pair_body(target, dtype):
        def body(j, slot):
            total = mm_nt(gate_grad[...], tiles[slot, :, :quarter])
            total = total + mm_nt(up_grad[...], tiles[slot, :, quarter:])
            target[:, columns_at(j)] = total.astype(dtype)

        return body

    nt_product(pair_w, 2 * quarter, half, pair_body(sent, BF16))
    pair_r = begin(swap(sent, row_came.at[0], 2, across))
    nt_product(pair_w, 2 * quarter, 0, pair_body(kept, F32))
    pair_r.wait_recv()

    def join_pair(rows):
        summed[rows, :] = (kept[rows, :] + row_came[0, rows, :].astype(F32)).astype(BF16)

    rows_loop(join_pair)
    pair_c = begin(swap(summed, col_came, 3, beside))
    gate_r = begin(swap(gate_grad, gate_row, 4, across))
    up_r = begin(swap(up_grad, up_row, 5, across))

    for copy in to_x:
        copy.wait_recv()
    for at in range(per):
        there = pl.ds(at * width, width)
        on_row.append(
            begin(
                swap(
                    hidden_came.at[:, there],
                    hidden_came_row.at[:, there],
                    2 * per + at,
                    across,
                    piece_sems,
                )
            )
        )

    def down_grad(part, left_of, came):
        def body(columns, _):
            for at in range(per):
                there = pl.ds(at * width, width)
                total = mm_tn(left_of(at)[...], top_half[:, columns])
                total = total + mm_tn(came[:, there], top_came[:, columns])
                down_grads[pl.ds((part * per + at) * width, width), columns] = total.astype(BF16)

        tiles_loop(half, 512, body)

    down_grad(0, lambda at: hidden_part(x, at), hidden_came)
    for copy in to_row + on_row:
        copy.wait_recv()
    down_grad(1, lambda at: hidden_row.at[:, pl.ds(at * width, width)], hidden_came_row)
    down_line.run(0, 1)

    def down_product(start, target, dtype):
        def body(j, slot):
            target[:, columns_at(j)] = mm(hidden[...], tall_tiles[slot, 0]).astype(dtype)

        stream(
            lambda j: [down_w.at[:, pl.ds(pl.multiple_of(start + j * 256, 256), 256)]],
            lambda slot: [tall_tiles.at[slot, 0]],
            tile_sems,
            half // 256,
            body,
        )

    pair_r.wait_send()
    pending[:] = [copy for copy in pending if copy is not pair_r]
    down_product(half, sent, BF16)
    layer_r = begin(swap(sent, row_came.at[1], 7, across))
    down_product(0, kept, F32)
    layer_r.wait_recv()

    def mine_of(value):
        return jnp.where(col == 0, value[:, :block], value[:, block:])

    def theirs_of(value):
        return jnp.where(col == 0, value[:, block:], value[:, :block])

    def join_layer(rows):
        total = kept[rows, :] + row_came[1, rows, :].astype(F32)
        layer_own[rows, :] = mine_of(total)
        block_sent[0, rows, :] = theirs_of(total).astype(BF16)

    rows_loop(join_layer)
    layer_c = begin(swap(block_sent.at[0], block_came.at[0], 8, beside))
    middle_in = pltpu.make_async_copy(middle, kept, copy_sems.at[0])
    middle_in.start()

    middle_in.wait()
    pair_c.wait_recv()
    feed_sum[...] = jnp.zeros_like(feed_sum)

    def second_grads(rows):
        grad = summed[rows, :].astype(F32) + col_came[rows, :].astype(F32)
        return grad, grad * gain_second[1:2, :]

    def norm_first_pass(rows):
        grad, scaled = second_grads(rows)
        held = kept[rows, :]
        feed_sum[...] += jnp.sum(grad * held * inverse_second[rows, :], axis=0, keepdims=True)
        total = jnp.sum(scaled * held, axis=1, keepdims=True)
        dots[0, rows, :] = jnp.broadcast_to(total, (total.shape[0], 128))

    rows_loop(norm_first_pass)
    dot_r = begin(swap(dots.at[0], dots.at[1], 9, across))
    dot_r.wait_recv()

    def norm_second_pass(rows):
        _, scaled = second_grads(rows)
        held = kept[rows, :]
        inverse = inverse_second[rows, :]
        dot = dots[0, rows, :1] + dots[1, rows, :1]
        grad = (
            top_half[rows, :].astype(F32) + scaled * inverse - held * (inverse**3 * dot / D)
        )
        branch[rows, :] = grad.astype(BF16)
        middle_own[rows, :] = mine_of(grad)
        layer_own[rows, :] += mine_of(held)

    rows_loop(norm_second_pass)
    result(branch, branch_out)
    branch_r = begin(swap(branch, branch_row, 10, across))
    branch_r.wait_recv()

    down_line.run(1, 2)

    def mixed_body(j, slot):
        total = mm_nt(branch[...], tiles[slot, :, :half])
        total = total + mm_nt(branch_row[...], tiles[slot, :, half:D])
        mixed_grad[:, columns_at(j)] = total.astype(BF16)

    stream(
        lambda j: [out_w.at[pl.ds(pl.multiple_of(j * 256, 256), 256), :]],
        lambda slot: [tiles.at[slot, :, pl.ds(0, D)]],
        tile_sems,
        out_w.shape[0] // 256,
        mixed_body,
    )
    pairs = turned.shape[1] // 384
    lower = lax.broadcasted_iota(jnp.int32, (SL, SL), 1) <= lax.broadcasted_iota(
        jnp.int32, (SL, SL), 0
    )

    def attend(at, _):
        micro, pair = at // pairs, lax.rem(at, pairs)
        rows = pl.ds(pl.multiple_of(micro * SL, SL), SL)

        def part(kind):
            return pl.ds(pl.multiple_of(pair * 384 + kind * 128, 128), 128)

        allowed = lower & (key_live[pl.ds(micro, 1), :] > 0.5)
        dq, dk, dv = head_grads(
            turned[rows, part(0)],
            turned[rows, part(1)],
            turned[rows, part(2)],
            mixed_grad[rows, pl.ds(pl.multiple_of(pair * 128, 128), 128)],
            allowed,
            cos[...],
            first[...],
            second[...],
        )
        dqkv[rows, part(0)] = dq
        dqkv[rows, part(1)] = dk
        dqkv[rows, part(2)] = dv
        return 0

    lax.fori_loop(0, MICRO * pairs, attend, 0)
    result(dqkv, dqkv_out)

    def first_body(target, dtype):
        def body(j, slot):
            total = mm_nt(dqkv[...], tiles[slot, :, : dqkv.shape[1]])
            target[:, columns_at(j)] = total.astype(dtype)

        return body

    layer_r.wait_send()
    pending[:] = [copy for copy in pending if copy is not layer_r]
    nt_product(qkv_w, dqkv.shape[1], half, first_body(sent, BF16))
    first_r = begin(swap(sent, row_came.at[2], 11, across))
    dqkv_r = begin(swap(dqkv, dqkv_row, 12, across))
    nt_product(qkv_w, dqkv.shape[1], 0, first_body(kept, F32))
    down_line.run(2, line - 1)
    first_r.wait_recv()

    def join_first(rows):
        total = kept[rows, :] + row_came[2, rows, :].astype(F32)
        first_own[rows, :] = mine_of(total)
        block_sent[1, rows, :] = theirs_of(total).astype(BF16)

    rows_loop(join_first)
    first_c = begin(swap(block_sent.at[1], block_came.at[1], 13, beside))

    second_x.wait_recv()
    result(second_came, second_came_out)
    depth = second_mine.shape[0]
    turned_left[:, :depth] = second_mine[...].T
    turned_left[:, depth:] = second_came[...].T
    gate_x.wait_recv()
    gate_on = begin(swap(gate_came, gate_came_row, 14, across))

    def gate_part(shift, sources, values):
        def body(j, slot):
            mine, came = values(j, slot)
            total = mm(turned_left[:, :depth], mine) + mm(turned_left[:, depth:], came)
            there = pl.ds(pl.multiple_of(shift + j * 256, 256), 256)
            gate_grads[:, there] = total.astype(BF16)

        stream(
            lambda j: [source.at[:, columns_at(j)] for source in sources],
            lambda slot: [tall_tiles.at[slot, k, pl.ds(0, ROWS)] for k in range(len(sources))],
            tile_sems,
            quarter // 256,
            body,
        )

    gate_part(
        0,
        [gate_came],
        lambda j, slot: (gate_grad[:, columns_at(j)], tall_tiles[slot, 0, :ROWS]),
    )
    gate_r.wait_recv()
    gate_on.wait_recv()
    gate_part(
        quarter,
        [gate_row, gate_came_row],
        lambda j, slot: (tall_tiles[slot, 0, :ROWS], tall_tiles[slot, 1, :ROWS]),
    )

    result(gate_grads, gate_grads_out)
    layer_c.wait_recv()
    first_c.wait_recv()
    attention_sum[...] = jnp.zeros_like(attention_sum)

    def last_first_pass(rows):
        layer = layer_own[rows, :] + block_came[0, rows, :].astype(F32)
        both_out[rows, :] = layer.astype(BF16)
        grad = first_own[rows, :] + block_came[1, rows, :].astype(F32)
        first_own[rows, :] = grad
        held = x_own[rows, :].astype(F32)
        attention_sum[...] += jnp.sum(grad * held * inverse_first[rows, :], axis=0, keepdims=True)
        total = jnp.sum(grad * gain_first[...] * held, axis=1, keepdims=True)
        dots[2, rows, :] = jnp.broadcast_to(total, (total.shape[0], 128))

    rows_loop(last_first_pass)
    dot_r = begin(swap(dots.at[2], dots.at[3], 15, across))
    dot_r.wait_recv()

    def add_dots(rows):
        dots[4, rows, :] = dots[2, rows, :] + dots[3, rows, :]

    rows_loop(add_dots)
    dot_c = begin(swap(dots.at[4], dots.at[5], 16, beside))
    dot_c.wait_recv()

    def last_second_pass(rows):
        inverse = inverse_first[rows, :]
        dot = dots[4, rows, :1] + dots[5, rows, :1]
        scaled = first_own[rows, :] * gain_first[...]
        held = x_own[rows, :].astype(F32)
        grad = middle_own[rows, :] + scaled * inverse - held * (inverse**3 * dot / D)
        below = pl.ds(pl.multiple_of(rows.start + ROWS, rows.size), rows.size)
        both_out[below, :] = grad.astype(BF16)

    rows_loop(last_second_pass)
    pieces_out[0:1, :] = attention_sum[...]
    pieces_out[1:2, :] = mine_of(feed_sum[...])

    down_line.stage = kept.at[pl.ds(0, down_grads.shape[0] // line), :]
    down_line.finish()
    down_store = pltpu.make_async_copy(down_line.stage, down_out, copy_sems.at[1])
    down_store.start()
    for copy in (up_r, dqkv_r):
        copy.wait_recv()
    for copy in pending:
        copy.wait_send()
    down_store.wait()
    for copy in results:
        copy.wait()


def chain(line, identity, *values):
    quarter = values[1].shape[1]
    narrow = values[2].shape[1]
    qkv_width = values[10].shape[1]
    half, block = D // 2, D // 4
    rows = quarter // 2
    vmem = pl.BlockSpec(memory_space=pltpu.VMEM)
    anywhere = pl.BlockSpec(memory_space=pl.ANY)
    outside = {1, 3, 6, 7, 8, 9, 11}

    def array(*shape, dtype=BF16):
        return jax.ShapeDtypeStruct(shape, dtype)

    def buffer(*shape, dtype=BF16):
        return pltpu.VMEM(shape, dtype)

    outs = [
        (array(2 * rows // line, half, dtype=F32), anywhere),
        (array(narrow, 2 * quarter), anywhere),
        (array(ROWS, narrow), anywhere),
        (array(ROWS, quarter), anywhere),
        (array(ROWS, quarter), anywhere),
        (array(ROWS, qkv_width), anywhere),
        (array(ROWS, qkv_width), anywhere),
        (array(ROWS, half), anywhere),
        (array(2 * ROWS, block), vmem),
        (array(2, block, dtype=F32), vmem),
        (array(ROWS, quarter), anywhere),
        (array(ROWS, quarter), anywhere),
        (array(ROWS, quarter), anywhere),
    ]
    sem = pltpu.SemaphoreType.DMA
    return pl.pallas_call(
        lambda *refs: chain_kernel(line, *refs),
        out_shape=[shape for shape, _ in outs],
        in_specs=[anywhere if k in outside else vmem for k in range(len(values))],
        out_specs=[place for _, place in outs],
        scratch_shapes=[
            buffer(narrow, 2 * quarter),
            buffer(ROWS, narrow),
            buffer(ROWS, quarter),
            buffer(ROWS, qkv_width),
            buffer(ROWS, half),
            buffer(ROWS, quarter),
            buffer(ROWS, quarter),
            buffer(2, 256, 2 * quarter),
            buffer(2, 2, quarter, 256),
            buffer(2, ROWS, 256, dtype=F32),
            buffer(ROWS, half, dtype=F32),
            buffer(ROWS, half),
            buffer(3, ROWS, half),
            buffer(ROWS, half),
            buffer(ROWS, half),
            buffer(2, ROWS, block),
            buffer(2, ROWS, block),
            buffer(ROWS, rows),
            buffer(ROWS, rows),
            buffer(ROWS, rows),
            buffer(ROWS, half),
            buffer(6, ROWS, 128, dtype=F32),
            buffer(2 * rows, half),
            buffer(2, line - 1, 2 * rows // line, half),
            buffer(ROWS, block, dtype=F32),
            buffer(ROWS, block, dtype=F32),
            buffer(ROWS, block, dtype=F32),
            buffer(ROWS, qkv_width // 3),
            buffer(narrow, 2 * ROWS),
            buffer(1, half, dtype=F32),
            buffer(1, block, dtype=F32),
            sem((2, 17)),
            sem((2, 3 * (line // 2))),
            sem((2, 3)),
            sem((2, 2, line - 1, 4)),
            sem((7,)),
        ],
        compiler_params=pltpu.CompilerParams(
            collective_id=identity, has_side_effects=True, vmem_limit_bytes=67043328
        ),
        cost_estimate=FREE,
    )(*values)


def tail_sums(line, identity, *values):
    (gate_grads, up, _, _, _, dqkv, _, _, _, branch) = values[:10]
    rows = gate_grads.shape[0]
    side_rows = 2 * values[10].shape[1]
    tokens = up.shape[0]
    widths = (gate_grads.shape[1], gate_grads.shape[1], 2 * dqkv.shape[1], branch.shape[1])
    heights = (rows, rows, rows, side_rows)
    pieces = (4, 4, 3, 1)
    sizes = [(h // line, w) for h, w in zip(heights, widths)]
    vmem = pl.BlockSpec(memory_space=pltpu.VMEM)
    anywhere = pl.BlockSpec(memory_space=pl.ANY)
    both, gains = values[12:]
    height = sizes[0][0]
    gain_steps = both.shape[1].bit_length() - 1

    def buffer(*shape):
        return pltpu.VMEM(shape, BF16)

    def array(*shape):
        return jax.ShapeDtypeStruct(shape, F32)

    return pl.pallas_call(
        lambda *refs: tail_kernel(line, *refs),
        out_shape=[
            array(*sizes[0]),
            array(*sizes[1]),
            array(height, widths[2] // 3),
            array(height, widths[2] // 3),
            array(height, widths[2] // 3),
            array(*sizes[3]),
            jax.ShapeDtypeStruct(both.shape, BF16),
            array(*gains.shape),
        ],
        in_specs=[vmem] + [anywhere] * 12 + [vmem],
        out_specs=[anywhere] * 7 + [vmem],
        scratch_shapes=[buffer(*values[at].shape) for at in (1, 2, 3, 4, 5, 6, 7, 9, 10)]
        + [buffer(2, line - 1, *size) for size in sizes]
        + [buffer(h, w) for h, w in zip(heights[1:], widths[1:])]
        + [buffer(*up.shape)] * 2
        + [buffer(*dqkv.shape)] * 2
        + [buffer(*branch.shape), buffer(*values[7].shape)]
        + [buffer(*values[10].shape)] * 3
        + [buffer(rows, 2 * tokens)]
        + [pltpu.VMEM(size, F32) for size in sizes]
        + [pltpu.SemaphoreType.DMA((2, 2, line - 1, count)) for count in pieces]
        + [pltpu.SemaphoreType.DMA((2, 9)), pltpu.SemaphoreType.DMA((6 + widths[2] // 128,))]
        + [pltpu.VMEM((2, gain_steps, *gains.shape), F32)]
        + [
            pltpu.SemaphoreType.DMA((2, both.shape[1])),
            pltpu.SemaphoreType.DMA((2, gain_steps)),
            pltpu.SemaphoreType.DMA((9,)),
        ],
        compiler_params=pltpu.CompilerParams(
            collective_id=identity, has_side_effects=True, vmem_limit_bytes=67043328
        ),
        cost_estimate=FREE,
    )(*values)


def finish_kernel(count, order_ref, back_ref, *refs):
    sums, rest = refs[:count], refs[count:]
    layer_ref, grad_ref = rest[:2]
    outs, held, sems = rest[2 : 2 + count], rest[2 + count : 2 + 2 * count], rest[2 + 2 * count]
    groups = back_ref.shape[1]
    loads = [pltpu.make_async_copy(sums[k], held[k], sems.at[0, k]) for k in range(count)]
    stores = [pltpu.make_async_copy(held[k], outs[k], sems.at[1, k]) for k in range(count)]
    for copy in loads:
        copy.start()

    def one(at, _):
        micro, slot = at // groups, lax.rem(at, groups)
        place = order_ref[micro, slot]
        layer_ref[micro, place] = back_ref[micro, slot]
        grad_ref[micro, place] = back_ref[MICRO + micro, slot]
        return 0

    lax.fori_loop(0, MICRO * groups, one, 0)
    for load, store in zip(loads, stores):
        load.wait()
        store.start()
    for store in stores:
        store.wait()


def finish(order, back, *sums):
    vmem = pl.BlockSpec(memory_space=pltpu.VMEM)
    anywhere = pl.BlockSpec(memory_space=pl.ANY)
    rows = jax.ShapeDtypeStruct((MICRO,) + back.shape[1:], BF16)
    count = len(sums)
    return pl.pallas_call(
        lambda *refs: finish_kernel(count, *refs),
        out_shape=[rows, rows] + [jax.ShapeDtypeStruct(v.shape, F32) for v in sums],
        in_specs=[pl.BlockSpec(memory_space=pltpu.SMEM), vmem] + [anywhere] * count,
        out_specs=[vmem, vmem] + [anywhere] * count,
        scratch_shapes=[pltpu.VMEM(v.shape, F32) for v in sums]
        + [pltpu.SemaphoreType.DMA((2, count))],
        cost_estimate=FREE,
    )(order, back, *sums)


def per_device(
    tokens,
    lengths,
    deal_order,
    attention_gain,
    query_weight,
    key_weight,
    value_weight,
    output_weight,
    feed_gain,
    gate_weight,
    up_weight,
    down_weight,
    cotangent,
):
    groups = lax.axis_size("dp")
    line = groups // 2
    dp = lax.axis_index("dp")
    row = lax.axis_index("row")
    col = lax.axis_index("col")
    z, x = dp // 2, dp % 2
    half = D // 2
    block = D // 4

    def over_row(v):
        return lax.ppermute(v, "row", SWAP)

    def over_col(v):
        return lax.ppermute(v, "col", SWAP)

    def ordered(own, other, index, axis=-1):
        return jnp.where(
            index == 0,
            jnp.concatenate([own, other], axis=axis),
            jnp.concatenate([other, own], axis=axis),
        )

    def x_parts(v, width):
        even = jnp.concatenate(
            [v[:, s : s + width] for s in range(0, v.shape[1], 2 * width)], axis=1
        )
        odd = jnp.concatenate(
            [v[:, s : s + width] for s in range(width, v.shape[1], 2 * width)], axis=1
        )
        return jnp.where(x == 0, even, odd), jnp.where(x == 0, odd, even)

    def plain(*values):
        return values

    dealt, top_block, key_live = prepare(deal_order, lengths, tokens, cotangent)
    tables = rope_tables()
    (
        pair_w,
        down_w,
        qkv_w,
        out_w,
        x_block,
        top_half,
        top_came,
        first_mine,
        first_theirs,
        turned,
        mixed_mine,
        mixed_theirs,
        middle,
        second_mine,
        second_theirs,
        normed_second,
        hidden_grad,
        inverse_first,
        inverse_second,
        gains_half,
    ) = front(
        line,
        0,
        dealt,
        top_block,
        attention_gain.reshape(1, block),
        feed_gain.reshape(1, block),
        key_live,
        *tables,
        query_weight,
        key_weight,
        value_weight,
        output_weight,
        gate_weight,
        up_weight,
        down_weight,
    )
    x_block = x_block.reshape(ROWS, block)
    narrow = half // groups
    (
        down_sum,
        gate_grads,
        second_came,
        up_grad,
        up_row,
        dqkv,
        dqkv_row,
        branch,
        both,
        pieces,
        _,
        _,
        _,
    ) = chain(
        line,
        4,
        *plain(
            normed_second,
            hidden_grad,
            second_mine,
            second_theirs,
            top_half,
            top_came,
            pair_w,
            down_w,
            qkv_w,
            out_w,
            turned,
            middle,
            inverse_first,
            inverse_second,
            gains_half,
            attention_gain.reshape(1, block),
            x_block,
            key_live,
            *tables,
        ),
    )

    gate_sum, up_sum, query_sum, key_sum, value_sum, output_sum, back, gain_sums = tail_sums(
        line,
        3,
        *plain(
            gate_grads,
            up_grad,
            up_row,
            second_mine,
            second_came,
            dqkv,
            dqkv_row,
            first_mine,
            first_theirs,
            branch,
            mixed_mine,
            mixed_theirs,
            both.reshape(2 * MICRO, groups, SL // groups, block),
            pieces,
        ),
    )
    (
        layer_output,
        tokens_grad,
        down_sum,
        gate_sum,
        up_sum,
        query_sum,
        key_sum,
        value_sum,
        output_sum,
    ) = finish(
        deal_order,
        back,
        down_sum,
        gate_sum,
        up_sum,
        query_sum,
        key_sum,
        value_sum,
        output_sum,
    )
    gain_size = block // groups
    gain_sums = lax.dynamic_slice_in_dim(gain_sums, dp * gain_size, gain_size, 1)

    return (
        layer_output,
        tokens_grad,
        gain_sums[0],
        query_sum,
        key_sum,
        value_sum,
        output_sum,
        gain_sums[1],
        gate_sum,
        up_sum,
        down_sum,
    )


def solution(mesh):
    in_specs = (
        P(None, None, "dp", ("row", "col")),
        P(),
        P(),
        P(("row", "col")),
        P("row", "col"),
        P("row", "col"),
        P("row", "col"),
        P("col", "row"),
        P(("row", "col")),
        P("row", "col"),
        P("row", "col"),
        P("col", "row"),
        P(None, "dp", None, ("row", "col")),
    )
    out_specs = (
        P(None, None, "dp", ("row", "col")),
        P(None, None, "dp", ("row", "col")),
        P(("row", "col", "dp")),
        P(("row", "dp"), "col"),
        P(("row", "dp"), "col"),
        P(("row", "dp"), "col"),
        P(("col", "dp"), "row"),
        P(("row", "col", "dp")),
        P(("row", "dp"), "col"),
        P(("row", "dp"), "col"),
        P(("col", "dp"), "row"),
    )
    return jax.shard_map(
        per_device, mesh=mesh, in_specs=in_specs, out_specs=out_specs, check_vma=False
    )
```

```python
import math

import jax
import jax.numpy as jnp
import numpy as np
from jax import lax
from jax.experimental import pallas as pl
from jax.experimental.pallas import tpu as pltpu
from jax.sharding import PartitionSpec as P

D = 2048
HEADS = 32
HEAD_DIM = 64
SL = 256
MICRO = 2
ROWS = MICRO * SL

EPSILON = 1e-05
ROPE_THETA = 130000.0
MASKED_SCORE = -1000000000.0
F32 = jnp.float32
BF16 = jnp.bfloat16
SWAP = [(0, 1), (1, 0)]


def mm(a, b):
    return jnp.dot(a, b, preferred_element_type=F32)


def mm_nt(a, b):
    return lax.dot_general(a, b, (((1,), (1,)), ((), ())), preferred_element_type=F32)


def mm_tn(a, b):
    return lax.dot_general(a, b, (((0,), (0,)), ((), ())), preferred_element_type=F32)


def rope_tables():
    half = HEAD_DIM // 2
    frequency = np.exp(np.arange(half, dtype=np.float32) * np.float32(-2.0 * math.log(ROPE_THETA) / HEAD_DIM))
    angles = np.arange(SL, dtype=np.float32)[:, None] * frequency[None, :]
    cosine, sine = np.cos(angles), np.sin(angles)
    zero = np.zeros_like(sine)
    table_cos = np.concatenate([cosine] * 4, axis=1)
    table_first = np.concatenate([sine, zero] * 2, axis=1)
    table_second = np.concatenate([zero, sine] * 2, axis=1)
    return jnp.asarray(table_cos), jnp.asarray(table_first), jnp.asarray(table_second)


def turn(v, cos, first, second):
    ahead = pltpu.roll(v, 128 - HEAD_DIM // 2, 1)
    behind = pltpu.roll(v, HEAD_DIM // 2, 1)
    return v * cos - ahead * first + behind * second


def turn_back(v, cos, first, second):
    ahead = pltpu.roll(v, 128 - HEAD_DIM // 2, 1)
    behind = pltpu.roll(v, HEAD_DIM // 2, 1)
    return v * cos + ahead * first - behind * second


def head_mask(head):
    lane = lax.broadcasted_iota(jnp.int32, (SL, 128), 1)
    return (lane // HEAD_DIM) == head


def softmax_of(q, k, allowed):
    scores = jnp.where(allowed, mm_nt(q, k), MASKED_SCORE)
    exps = jnp.exp(scores - jnp.max(scores, axis=1, keepdims=True))
    return exps * (1.0 / jnp.sum(exps, axis=1, keepdims=True))


def scaled_down(q):
    return (q.astype(F32) * HEAD_DIM ** (-0.5)).astype(BF16)


BLOCKS = ((slice(0, SL), SL),)


FREE = pl.CostEstimate(flops=0, bytes_accessed=0, transcendentals=0)


def whole(shape):
    return pl.BlockSpec(shape, lambda *at: (0,) * len(shape), pipeline_mode=pl.Buffered(1))


def head_outputs(qkv, allowed, cos, first, second):
    qr = turn(qkv[:, :128], cos, first, second).astype(BF16)
    kr = turn(qkv[:, 128:256], cos, first, second).astype(BF16)
    vr = qkv[:, 256:].astype(BF16)
    zero = jnp.zeros_like(vr)
    outs = [jnp.zeros((SL, 128), F32)]
    scaled = scaled_down(qr)
    for head in range(2):
        mask = head_mask(head)
        q_own = jnp.where(mask, scaled, zero)
        v_own = jnp.where(mask, vr, zero)
        for at, (rows, keys) in enumerate(BLOCKS):
            probs = softmax_of(q_own[rows], kr[:keys], allowed[rows, :keys]).astype(BF16)
            outs[at] = outs[at] + mm(probs, v_own[:keys])
    return qr, kr, vr, jnp.concatenate(outs, axis=0).astype(BF16)


def head_grads(qr, kr, vr, od, allowed, cos, first, second):
    dq = [jnp.zeros((SL, 128), F32)]
    dk = [jnp.zeros((SL, 128), F32)]
    dv = [jnp.zeros((SL, 128), F32)]
    zero = jnp.zeros_like(qr)
    scaled = scaled_down(qr)
    for head in range(2):
        mask = head_mask(head)
        q_own = jnp.where(mask, scaled, zero)
        k_own = jnp.where(mask, kr, zero)
        od_own = jnp.where(mask, od, zero)
        for at, (rows, keys) in enumerate(BLOCKS):
            probs = softmax_of(q_own[rows], kr[:keys], allowed[rows, :keys])
            d_probs = mm_nt(od_own[rows], vr[:keys])
            dv[at] = dv[at] + mm_tn(probs.astype(BF16), od_own[rows])
            inner = jnp.sum(probs * d_probs, axis=1, keepdims=True)
            d_scores = (probs * (d_probs - inner)).astype(BF16)
            dq[at] = dq[at] + mm(d_scores, k_own[:keys])
            dk[at] = dk[at] + mm_tn(d_scores, q_own[rows])

    def keys_sum(parts):
        return parts[0]

    dq = jnp.concatenate(dq, axis=0) * HEAD_DIM ** (-0.5)
    return (
        turn_back(dq, cos, first, second).astype(BF16),
        turn_back(keys_sum(dk), cos, first, second).astype(BF16),
        keys_sum(dv).astype(BF16),
    )


MESH = pl.DeviceIdType.MESH


def greet(*moves):
    barrier = pltpu.get_barrier_semaphore()
    total = 0
    for count, target in moves:
        total = total + count

        @pl.when(count > 0)
        def _():
            pl.semaphore_signal(barrier, inc=1, device_id=target, device_id_type=MESH)

    pl.semaphore_wait(barrier, total)


class ZLine:
    def __init__(self, line, grads, out, stage, came, sems, count, sided):
        self.line, self.grads, self.out, self.stage = line, grads, out, stage
        self.came, self.sems, self.sided = came, sems, sided
        width = grads.shape[1] // count
        self.pieces = [(k, pl.ds(k * width, width)) for k in range(count)]
        self.dp, self.row = lax.axis_index("dp"), lax.axis_index("row")
        self.z = self.dp // 2
        self.last = line - 1
        self.ways = ((0, self.z, 2), (1, self.last - self.z, -2))

    def rows_of(self, dest):
        size = self.grads.shape[0] // self.line
        if self.sided:
            dest = lax.rem(dest + self.line - self.row * (self.line // 2), self.line)
        return pl.ds(pl.multiple_of(dest * size, size), size)

    def copy(self, source, way, step, slot, piece, columns):
        return pltpu.make_async_remote_copy(
            src_ref=source,
            dst_ref=self.came.at[way, slot, :, columns],
            send_sem=self.sems.at[0, way, slot, piece],
            recv_sem=self.sems.at[1, way, slot, piece],
            device_id={"dp": self.dp + step},
            device_id_type=MESH,
        )

    def arrived(self, way, step, slot, piece, columns):
        held = self.came.at[way, slot, :, columns]
        self.copy(held, way, step, slot, piece, columns).wait_recv()
        return held

    def run(self, start, stop):
        def one_step(slot, _):
            for piece, columns in self.pieces:
                for way, place, step in self.ways:
                    far = self.last - slot + place
                    dest = far if step > 0 else self.last - far

                    @pl.when((place == 0) & (place < self.last))
                    def _():
                        source = self.grads.at[self.rows_of(dest), columns]
                        self.copy(source, way, step, slot, piece, columns).start()

                    @pl.when((place > 0) & (place <= slot))
                    def _():
                        held = self.arrived(way, step, slot - 1, piece, columns)

                        @pl.when(place < self.last)
                        def _():
                            held[...] = (
                                held[...].astype(F32)
                                + self.grads[self.rows_of(dest), columns].astype(F32)
                            ).astype(BF16)
                            self.copy(held, way, step, slot, piece, columns).start()

            return 0

        lax.fori_loop(start, stop, one_step, 0)

    def finish(self):
        own = self.rows_of(self.z)
        for piece, columns in self.pieces:
            self.stage[:, columns] = self.grads[own, columns].astype(F32)
            for way, place, step in self.ways:

                @pl.when(place > 0)
                def _():
                    held = self.arrived(way, step, self.last - 1, piece, columns)
                    self.stage[:, columns] += held[...].astype(F32)

        def settle(slot, _):
            for piece, columns in self.pieces:
                for way, place, step in self.ways:

                    @pl.when((place <= slot) & (place < self.last))
                    def _():
                        held = self.came.at[way, slot, :, columns]
                        self.copy(held, way, step, slot, piece, columns).wait_send()

            return 0

        lax.fori_loop(0, self.last, settle, 0)

    def moves(self):
        return (
            (jnp.minimum(self.z, 1), {"dp": self.dp - 2}),
            (jnp.minimum(self.last - self.z, 1), {"dp": self.dp + 2}),
        )


def tiles_loop(width, tile, body):
    def one(j, _):
        body(pl.ds(pl.multiple_of(j * tile, tile), tile), j * tile)
        return 0

    lax.fori_loop(0, width // tile, one, 0)


def tail_kernel(
    line,
    gate_grads,
    up_in,
    up_row_in,
    second_mine_in,
    second_came_in,
    dqkv_in,
    dqkv_row_in,
    first_mine_in,
    first_theirs,
    branch_in,
    mixed_mine_in,
    mixed_theirs,
    both,
    pieces,
    gate_out,
    up_out,
    query_out,
    key_out,
    value_out,
    output_out,
    back,
    gains_out,
    up,
    up_row,
    second_mine,
    second_came,
    dqkv,
    dqkv_row,
    first_mine,
    branch,
    mixed_mine,
    gate_z,
    up_z,
    qkv_z,
    output_z,
    up_grads,
    qkv_grads,
    output_grads,
    up_came,
    up_came_row,
    dqkv_came,
    dqkv_came_row,
    branch_came,
    first_came,
    mixed_came,
    mixed_row,
    mixed_came_row,
    turned_left,
    gate_stage,
    up_stage,
    qkv_stage,
    output_stage,
    gate_sems,
    up_sems,
    qkv_sems,
    output_sems,
    swap_sems,
    out_sems,
    gains,
    back_sems,
    gain_sems,
    fetch_sems,
):
    groups = 2 * line
    dp, row = lax.axis_index("dp"), lax.axis_index("row")
    partner = dp + 1 - 2 * lax.rem(dp, 2)
    gate_line = ZLine(line, gate_grads, gate_out, gate_stage, gate_z, gate_sems, 4, False)
    up_line = ZLine(line, up_grads, up_out, up_stage, up_z, up_sems, 4, False)
    qkv_line = ZLine(line, qkv_grads, None, qkv_stage, qkv_z, qkv_sems, 3, False)
    output_line = ZLine(line, output_grads, output_out, output_stage, output_z, output_sems, 1, True)

    def swap(source, target, at, device):
        return pltpu.make_async_remote_copy(
            src_ref=source,
            dst_ref=target,
            send_sem=swap_sems.at[0, at],
            recv_sem=swap_sems.at[1, at],
            device_id=device,
            device_id_type=MESH,
        )

    fetches = {}
    order = (
        (second_mine_in, second_mine),
        (second_came_in, second_came),
        (up_in, up),
        (up_row_in, up_row),
        (mixed_mine_in, mixed_mine),
        (branch_in, branch),
        (first_mine_in, first_mine),
        (dqkv_in, dqkv),
        (dqkv_row_in, dqkv_row),
    )
    for at, (source, target) in enumerate(order):
        fetches[at] = pltpu.make_async_copy(source, target, fetch_sems.at[at])
        fetches[at].start()
    up_x = swap(up_in, up_came, 0, {"dp": partner})
    branch_x = swap(branch_in, branch_came, 1, {"dp": partner})
    dqkv_x = swap(dqkv_in, dqkv_came, 2, {"dp": partner})
    up_across = swap(up_came, up_came_row, 3, {"row": 1 - row})
    dqkv_across = swap(dqkv_came, dqkv_came_row, 4, {"row": 1 - row})
    first_x = swap(first_theirs, first_came, 5, {"dp": partner})
    mixed_x = swap(mixed_theirs, mixed_came, 6, {"dp": partner})
    mixed_r = swap(mixed_mine_in, mixed_row, 7, {"row": 1 - row})
    mixed_across = swap(mixed_came, mixed_came_row, 8, {"row": 1 - row})

    stores = []

    def store(source, target):
        copy = pltpu.make_async_copy(source, target, out_sems.at[len(stores)])
        copy.start()
        stores.append(copy)

    def store_wide(line_of):
        size = line_of.stage.shape[1] // 2
        for part in range(2):
            place = row if part == 0 else 1 - row
            there = pl.ds(pl.multiple_of(place * size, size), size)
            store(line_of.stage.at[:, pl.ds(part * size, size)], line_of.out.at[:, there])

    def store_qkv():
        heads = dqkv.shape[1] // 3
        for part in range(2):
            place = row if part == 0 else 1 - row
            for pair in range(heads // 128):
                for kind, out in enumerate((query_out, key_out, value_out)):
                    here = pl.ds(part * 3 * heads + pair * 384 + kind * 128, 128)
                    there = pl.ds(pl.multiple_of(place * heads + pair * 128, 128), 128)
                    store(qkv_stage.at[:, here], out.at[:, there])

    def returned(step):
        target = lax.rem(dp + step, groups)
        return pltpu.make_async_remote_copy(
            src_ref=both.at[:, target],
            dst_ref=back.at[:, dp],
            send_sem=back_sems.at[0, step],
            recv_sem=back_sems.at[1, step],
            device_id={"dp": target},
            device_id_type=MESH,
        )

    gain_steps = groups.bit_length() - 1

    def gain_copy(step):
        reach = 1 << step
        peer = dp + reach - 2 * reach * lax.rem(dp // reach, 2)
        return pltpu.make_async_remote_copy(
            src_ref=gains.at[0, step],
            dst_ref=gains.at[1, step],
            send_sem=gain_sems.at[0, step],
            recv_sem=gain_sems.at[1, step],
            device_id={"dp": peer},
            device_id_type=MESH,
        )

    def gain_step(step):
        if step >= gain_steps:
            return
        gain_copy(step).wait_recv()
        total = gains[0, step] + gains[1, step]
        if step + 1 == gain_steps:
            gains_out[...] = total
        else:
            gains[0, step + 1] = total
            gain_copy(step + 1).start()

    others = [(jnp.int32(1), {"dp": lax.rem(dp + step, groups)}) for step in range(1, groups)]
    greet(*others, (jnp.int32(1), {"row": 1 - row}))
    gains[0, 0] = pieces[...]
    gain_copy(0).start()
    gate_line.run(0, 1)
    up_x.start()
    mixed_x.start()
    branch_x.start()
    first_x.start()
    dqkv_x.start()
    mixed_r.start()

    def send_back(step, _):
        returned(step).start()
        return 0

    lax.fori_loop(1, groups, send_back, 0)
    store(both.at[:, dp], back.at[:, dp])

    fetches[0].wait()
    fetches[1].wait()
    depth = second_mine.shape[0]
    turned_left[:, :depth] = second_mine[...].T
    turned_left[:, depth:] = second_came[...].T
    gate_line.run(1, 2)

    def wide(target, shift, mine, came):
        def body(columns, start):
            total = mm(turned_left[:, :depth], mine[:, columns])
            total = total + mm(turned_left[:, depth:], came[:, columns])
            tile = total.shape[1]
            target[:, pl.ds(pl.multiple_of(shift + start, tile), tile)] = total.astype(BF16)

        tiles_loop(mine.shape[1], 512, body)

    up_x.wait_recv()
    up_across.start()
    gain_step(0)
    gate_line.run(2, line - 1)
    fetches[2].wait()
    fetches[3].wait()
    wide(up_grads, 0, up, up_came)
    up_across.wait_recv()
    wide(up_grads, up.shape[1], up_row, up_came_row)
    up_line.run(0, 1)
    gate_line.finish()
    store_wide(gate_line)

    mixed_x.wait_recv()
    mixed_across.start()
    branch_x.wait_recv()

    def side(start, mine, came):
        def body(columns, _):
            total = mm_tn(mine[...], branch[:, columns]) + mm_tn(came[...], branch_came[:, columns])
            output_grads[pl.ds(start, mine.shape[1]), columns] = total.astype(BF16)

        tiles_loop(branch.shape[1], 512, body)

    fetches[4].wait()
    fetches[5].wait()
    side(0, mixed_mine, mixed_came)
    mixed_r.wait_recv()
    mixed_across.wait_recv()
    side(mixed_mine.shape[1], mixed_row, mixed_came_row)
    output_line.run(0, 1)
    up_line.run(1, 2)
    gain_step(1)
    for at in (6, 7, 8):
        fetches[at].wait()
    first_x.wait_recv()
    turned_left[:, :depth] = first_mine[...].T
    turned_left[:, depth:] = first_came[...].T
    dqkv_x.wait_recv()
    dqkv_across.start()
    wide(qkv_grads, 0, dqkv, dqkv_came)
    dqkv_across.wait_recv()
    wide(qkv_grads, dqkv.shape[1], dqkv_row, dqkv_came_row)
    qkv_line.run(0, 1)
    output_line.run(1, 2)
    up_line.run(2, line - 1)
    qkv_line.run(1, 2)
    output_line.run(2, line - 1)
    for step in range(2, gain_steps):
        gain_step(step)
    up_line.finish()
    store_wide(up_line)
    qkv_line.run(2, line - 1)
    output_line.finish()
    store(output_stage, output_out)
    qkv_line.finish()
    store_qkv()

    def get_back(step, _):
        returned(step).wait()
        return 0

    lax.fori_loop(1, groups, get_back, 0)
    for step in range(gain_steps):
        gain_copy(step).wait_send()
    copies = (up_x, branch_x, dqkv_x, up_across, dqkv_across)
    for copy in copies + (first_x, mixed_x, mixed_r, mixed_across):
        copy.wait_send()
    for copy in stores:
        copy.wait()


def stream(source_of, slots_of, sems, count, body):
    def fetch(j, slot):
        return [
            pltpu.make_async_copy(source, target, sems.at[slot, k])
            for k, (source, target) in enumerate(zip(source_of(j), slots_of(slot)))
        ]

    for copy in fetch(0, 0):
        copy.start()

    def one(j, _):
        slot = lax.rem(j, 2)

        @pl.when(j + 1 < count)
        def _():
            for copy in fetch(j + 1, 1 - slot):
                copy.start()

        for copy in fetch(j, slot):
            copy.wait()
        body(j, slot)
        return 0

    lax.fori_loop(0, count, one, 0)


def rows_loop(body, size=64):
    def one(j, _):
        body(pl.ds(pl.multiple_of(j * size, size), size))
        return 0

    lax.fori_loop(0, ROWS // size, one, 0)


def prepare_kernel(order_ref, len_ref, tokens_ref, top_ref, dealt_ref, block_ref, live_ref):
    groups = tokens_ref.shape[1]
    dp = lax.axis_index("dp")

    def one(at, _):
        micro, slot = at // groups, lax.rem(at, groups)
        dealt_ref[micro, slot] = tokens_ref[micro, order_ref[micro, slot]]
        return 0

    lax.fori_loop(0, MICRO * groups, one, 0)
    for micro in range(MICRO):
        length = len_ref[micro, order_ref[micro, dp]]
        rows = lax.broadcasted_iota(jnp.int32, top_ref.shape[2:], 0)
        top = top_ref[micro, 0]
        top = jnp.where(rows < length, top.astype(F32), 0.0).astype(BF16)
        block_ref[micro * SL : micro * SL + SL, :] = top
        keys = lax.broadcasted_iota(jnp.int32, (1, SL), 1)
        live_ref[micro : micro + 1, :] = jnp.where(keys < length, 1.0, 0.0)


def prepare(order, lengths, tokens, cotangent):
    vmem = pl.BlockSpec(memory_space=pltpu.VMEM)
    smem = pl.BlockSpec(memory_space=pltpu.SMEM)
    return pl.pallas_call(
        prepare_kernel,
        out_shape=(
            jax.ShapeDtypeStruct(tokens.shape, BF16),
            jax.ShapeDtypeStruct((ROWS, cotangent.shape[3]), BF16),
            jax.ShapeDtypeStruct((MICRO, SL), F32),
        ),
        in_specs=[smem, smem, vmem, vmem],
        out_specs=(vmem,) * 3,
        cost_estimate=FREE,
    )(order, lengths, tokens, cotangent)


def front_kernel(
    dealt,
    top_block,
    gain_first,
    gain_second,
    key_live,
    cos,
    first,
    second,
    query_weight,
    key_weight,
    value_weight,
    output_weight,
    gate_weight,
    up_weight,
    down_weight,
    pair_out,
    down_out,
    qkv_out,
    out_out,
    x_out,
    top_half_out,
    top_came_out,
    first_mine_out,
    first_theirs_out,
    turned_out,
    mixed_mine_out,
    mixed_theirs_out,
    middle_out,
    second_mine_out,
    second_theirs_out,
    normed_second_out,
    hidden_grad_out,
    inverse_first,
    inverse_second,
    gains,
    x_in,
    top_half,
    top_came,
    normed_first,
    first_mine,
    first_theirs,
    turned,
    mixed,
    mixed_mine,
    mixed_theirs,
    middle,
    second_mine,
    second_theirs,
    normed_second,
    hidden_grad,
    qkv_w,
    out_w,
    gains_own,
    gains_col,
    gains_row,
    pair_held,
    down_held,
    tiles,
    x_came,
    x_half,
    x_other,
    top_col,
    top_row,
    sent,
    row_came,
    kept,
    summed,
    col_came,
    low,
    low_came,
    deal_sems,
    weight_sems,
    local_sems,
    swap_sems,
    tile_sems,
):
    groups = dealt.shape[1]
    dp, row, col = lax.axis_index("dp"), lax.axis_index("row"), lax.axis_index("col")
    x = lax.rem(dp, 2)
    partner = {"dp": dp + 1 - 2 * x}
    across = {"row": 1 - row}
    beside = {"col": 1 - col}
    half, block = D // 2, D // 4
    heads = query_weight.shape[1] // 2
    quarter = gate_weight.shape[1] // 2
    pending = []

    def remote(source, target, sems, at, device):
        copy = pltpu.make_async_remote_copy(
            src_ref=source,
            dst_ref=target,
            send_sem=sems.at[0, at],
            recv_sem=sems.at[1, at],
            device_id=device,
            device_id_type=MESH,
        )
        copy.start()
        pending.append(copy)
        return copy

    def swap(source, target, at, device):
        return remote(source, target, swap_sems, at, device)

    def columns(w, index, start, size):
        begin = pl.multiple_of(index * (w.shape[1] // 2) + start, 128)
        return w.at[:, pl.ds(begin, size)]

    def rows_half(w, index):
        size = w.shape[0] // 2
        return w.at[pl.ds(pl.multiple_of(index * size, size), size), :]

    locals_started = []

    def local(source, target):
        copy = pltpu.make_async_copy(source, target, local_sems.at[len(locals_started)])
        copy.start()
        locals_started.append(copy)
        return copy

    own_now = []
    for kind, w in enumerate((query_weight, key_weight, value_weight)):
        for at in range(0, heads, 128):
            there = pl.ds(3 * at + 128 * kind, 128)
            own_now.append(local(columns(w, row, at, 128), qkv_w.at[pl.ds(0, half), there]))
    own_now.append(local(rows_half(output_weight, row), out_w.at[:, pl.ds(0, half)]))
    own_gate = local(columns(gate_weight, row, 0, quarter), pair_held.at[0])
    own_up = local(columns(up_weight, row, 0, quarter), pair_held.at[1])
    own_down = local(rows_half(down_weight, row), down_held)
    own_rows = local(dealt.at[:, dp], x_in.at[:, dp])
    others = [(jnp.int32(1), {"dp": lax.rem(dp + step, groups)}) for step in range(1, groups)]
    greet(*others, (jnp.int32(1), across), (jnp.int32(1), beside))

    def dealing(step, micro):
        target = lax.rem(dp + step, groups)
        return pltpu.make_async_remote_copy(
            src_ref=dealt.at[micro, target],
            dst_ref=x_in.at[micro, dp],
            send_sem=deal_sems.at[0, micro, step],
            recv_sem=deal_sems.at[1, micro, step],
            device_id={"dp": target},
            device_id_type=MESH,
        )

    for micro in range(MICRO):

        def send_rows(step, _):
            dealing(step, micro).start()
            return 0

        lax.fori_loop(1, groups, send_rows, 0)
    gains_own[0:1, :] = gain_first[...]
    gains_own[1:2, :] = gain_second[...]
    gain_c = swap(gains_own, gains_col, 13, beside)
    top_c = swap(top_block, top_col, 0, beside)
    weights_now = []
    for kind, w in enumerate((query_weight, key_weight, value_weight)):
        for at in range(0, heads, 128):
            there = qkv_w.at[pl.ds(half, half), pl.ds(3 * at + 128 * kind, 128)]
            weights_now.append(
                remote(columns(w, 1 - row, at, 128), there, weight_sems, len(weights_now), across)
            )
    weights_now.append(
        remote(
            rows_half(output_weight, 1 - row),
            out_w.at[:, pl.ds(half, half)],
            weight_sems,
            len(weights_now),
            across,
        )
    )
    weights_late = []
    for k, w in enumerate((gate_weight, up_weight)):
        there = pair_out.at[pl.ds(half, half), pl.ds(k * quarter, quarter)]
        weights_late.append(
            remote(
                columns(w, 1 - row, 0, quarter), there, weight_sems, len(weights_now) + k, across
            )
        )
    own_gate.wait()
    own_up.wait()
    store_gate = local(pair_held.at[0], pair_out.at[pl.ds(0, half), pl.ds(0, quarter)])
    store_up = local(pair_held.at[1], pair_out.at[pl.ds(0, half), pl.ds(quarter, quarter)])
    own_down.wait()
    store_down = local(down_held, down_out.at[:, pl.ds(0, half)])

    def half_of(own, came):
        return jnp.where(
            col == 0,
            jnp.concatenate([own, came], axis=1),
            jnp.concatenate([came, own], axis=1),
        )

    own_rows.wait()
    x_c = []
    for micro in range(MICRO):

        def take_rows(step, _):
            dealing(step, micro).wait_recv()
            return 0

        lax.fori_loop(1, groups, take_rows, 0)
        x_c.append(swap(x_in.at[micro], x_came.at[micro], 1 + micro, beside))
    gain_c.wait_recv()
    gains[...] = half_of(gains_own[...], gains_col[...])
    gain_r = swap(gains, gains_row, 14, across)
    top_c.wait_recv()

    def top_rows(rows):
        top_half[rows, :] = half_of(top_block[rows, :], top_col[rows, :])

    rows_loop(top_rows)
    results = [local(x_in, x_out), local(top_half, top_half_out)]
    top_x = swap(top_half, top_came, 3, partner)

    def micro_rows(micro):
        return pl.ds(micro * SL, SL)

    x_r = []
    for micro in range(MICRO):
        x_c[micro].wait_recv()
        own = x_in[micro].reshape(SL, block)
        came = x_came[micro].reshape(SL, block)
        x_half[micro_rows(micro), :] = half_of(own, came)
        rows = micro_rows(micro)
        x_r.append(swap(x_half.at[rows, :], x_other.at[rows, :], 4 + micro, across))
        if micro == 0:
            for copy in own_now:
                copy.wait()
            for copy in weights_now:
                copy.wait_recv()
    top_r = swap(top_half, top_row, 6, across)
    down_there = down_out.at[:, pl.ds(half, half)]
    down_r = remote(
        rows_half(down_weight, 1 - row), down_there, weight_sems, len(weights_now) + 2, across
    )
    store_qkv = local(qkv_w, qkv_out)
    store_out = local(out_w, out_out)

    lower = lax.broadcasted_iota(jnp.int32, (SL, SL), 1) <= lax.broadcasted_iota(
        jnp.int32, (SL, SL), 0
    )

    gain_r.wait_recv()

    def norm_rows(own_ref, other_ref, at, inverse_ref, out_ref, micro):
        def body(j, _):
            rows = pl.ds(pl.multiple_of(micro * SL + j * 64, 64), 64)
            own = own_ref[rows, :].astype(F32)
            other = other_ref[rows, :].astype(F32)
            total = jnp.sum(own * own, axis=1, keepdims=True)
            total = total + jnp.sum(other * other, axis=1, keepdims=True)
            inverse = lax.rsqrt(total / D + EPSILON)
            inverse_ref[rows, :] = inverse
            out_ref[rows, :half] = (own * inverse * gains[at : at + 1, :]).astype(BF16)
            out_ref[rows, half:] = (other * inverse * gains_row[at : at + 1, :]).astype(BF16)
            return 0

        lax.fori_loop(0, SL // 64, body, 0)

    sum_c = []
    for micro in range(MICRO):
        rows = micro_rows(micro)
        x_r[micro].wait_recv()
        norm_rows(x_half, x_other, 0, inverse_first, normed_first, micro)
        allowed = lower & (key_live[micro : micro + 1, :] > 0.5)

        def attend(at, _):
            there = pl.multiple_of(at * 768, 128)
            qkv = mm(normed_first[rows, :], qkv_w[:, pl.ds(there, 768)])
            for pair in range(2):
                qr, kr, vr, out = head_outputs(
                    qkv[:, pair * 384 : pair * 384 + 384], allowed, cos[...], first[...], second[...]
                )
                begin = there + pair * 384
                for kind, value in enumerate((qr, kr, vr)):
                    turned[rows, pl.ds(pl.multiple_of(begin + kind * 128, 128), 128)] = value
                mixed[rows, pl.ds(pl.multiple_of(at * 256 + pair * 128, 128), 128)] = out
            return 0

        lax.fori_loop(0, heads // 256, attend, 0)
        sent[rows, :] = mm(mixed[rows, :], out_w[:, half:]).astype(BF16)
        sum_r = swap(sent.at[rows, :], row_came.at[rows, :], 7 + micro, across)
        kept[...] = mm(mixed[rows, :], out_w[:, :half])
        sum_r.wait_recv()
        summed[rows, :] = (kept[...] + row_came[rows, :].astype(F32)).astype(BF16)
        sum_c.append(swap(summed.at[rows, :], col_came.at[rows, :], 9 + micro, beside))

    results.append(local(turned, turned_out))

    def by_x(source, mine, theirs, rows, width):
        value = source[rows, : 2 * mine.shape[1]]
        even = [value[:, at : at + width] for at in range(0, value.shape[1], 2 * width)]
        odd = [value[:, at : at + width] for at in range(width, value.shape[1], 2 * width)]
        even, odd = jnp.concatenate(even, axis=1), jnp.concatenate(odd, axis=1)
        mine[rows, :] = jnp.where(x == 0, even, odd)
        theirs[rows, :] = jnp.where(x == 0, odd, even)

    top_r.wait_recv()
    store_down.wait()
    down_r.wait_recv()

    def da_body(j, slot):
        total = mm_nt(top_half[...], tiles[slot, :, :half])
        total = total + mm_nt(top_row[...], tiles[slot, :, half:])
        hidden_grad[:, pl.ds(pl.multiple_of(j * 256, 256), 256)] = total

    stream(
        lambda j: [down_out.at[pl.ds(pl.multiple_of(j * 256, 256), 256), :]],
        lambda slot: [tiles.at[slot]],
        tile_sems,
        quarter // 256,
        da_body,
    )

    results.append(local(hidden_grad, hidden_grad_out))

    def select_rows(rows):
        by_x(normed_first, first_mine, first_theirs, rows, half // groups)
        by_x(mixed, mixed_mine, mixed_theirs, rows, 2 * heads // groups)

    rows_loop(select_rows)
    results.append(local(first_mine, first_mine_out))
    results.append(local(first_theirs, first_theirs_out))
    results.append(local(mixed_mine, mixed_mine_out))
    results.append(local(mixed_theirs, mixed_theirs_out))

    low_r = []
    for micro in range(MICRO):
        rows = micro_rows(micro)
        sum_c[micro].wait_recv()

        def middle_rows(j, _):
            here = pl.ds(pl.multiple_of(micro * SL + j * 64, 64), 64)
            total = x_half[here, :].astype(F32) + (
                summed[here, :].astype(F32) + col_came[here, :].astype(F32)
            )
            middle[here, :] = total
            low[here, :] = total.astype(BF16)
            return 0

        lax.fori_loop(0, SL // 64, middle_rows, 0)
        results.append(local(middle.at[rows, :], middle_out.at[rows, :]))
        low_r.append(swap(low.at[rows, :], low_came.at[rows, :], 11 + micro, across))
        low_r[micro].wait_recv()
        norm_rows(low, low_came, 1, inverse_second, normed_second, micro)
        results.append(local(normed_second.at[rows, :], normed_second_out.at[rows, :]))

        def second_rows(j, _):
            here = pl.ds(pl.multiple_of(micro * SL + j * 64, 64), 64)
            by_x(normed_second, second_mine, second_theirs, here, half // groups)
            return 0

        lax.fori_loop(0, SL // 64, second_rows, 0)
        results.append(local(second_mine.at[rows, :], second_mine_out.at[rows, :]))
        results.append(local(second_theirs.at[rows, :], second_theirs_out.at[rows, :]))

    top_x.wait_recv()
    results.append(local(top_came, top_came_out))
    for copy in weights_late:
        copy.wait_recv()
    for copy in pending:
        copy.wait_send()

    def close(step, _):
        for micro in range(MICRO):
            dealing(step, micro).wait_send()
        return 0

    lax.fori_loop(1, groups, close, 0)
    for copy in [store_gate, store_up, store_qkv, store_out] + results:
        copy.wait()


def front(line, identity, *values):
    dealt, query_weight, gate_weight = values[0], values[8], values[12]
    groups = dealt.shape[1]
    half, block = D // 2, D // 4
    heads = query_weight.shape[1] // 2
    quarter = gate_weight.shape[1] // 2
    vmem = pl.BlockSpec(memory_space=pltpu.VMEM)
    anywhere = pl.BlockSpec(memory_space=pl.ANY)

    def array(*shape, dtype=BF16):
        return jax.ShapeDtypeStruct(shape, dtype)

    def buffer(*shape, dtype=BF16):
        return pltpu.VMEM(shape, dtype)

    sem = pltpu.SemaphoreType.DMA
    now = 3 * (heads // 128) + 1
    held = [
        (dealt.shape, BF16),
        ((ROWS, half), BF16),
        ((ROWS, half), BF16),
        ((ROWS, block), BF16),
        ((ROWS, block), BF16),
        ((ROWS, 3 * heads), BF16),
        ((ROWS, heads // 2), BF16),
        ((ROWS, heads // 2), BF16),
        ((ROWS, half), F32),
        ((ROWS, block), BF16),
        ((ROWS, block), BF16),
        ((ROWS, D), BF16),
        ((ROWS, quarter), F32),
    ]
    normed_first, mixed = ((ROWS, D), BF16), ((ROWS, heads), BF16)
    inside = held[:3] + [normed_first] + held[3:6] + [mixed] + held[6:]
    return pl.pallas_call(
        front_kernel,
        out_shape=[
            array(D, 2 * quarter),
            array(quarter, D),
            array(D, 3 * heads),
            array(heads, D),
            *[array(*shape, dtype=kind) for shape, kind in held],
            array(ROWS, 1, dtype=F32),
            array(ROWS, 1, dtype=F32),
            array(2, half, dtype=F32),
        ],
        in_specs=[vmem] * 8 + [anywhere] * 7,
        out_specs=[anywhere] * (4 + len(held)) + [vmem] * 3,
        scratch_shapes=[
            *[buffer(*shape, dtype=kind) for shape, kind in inside],
            buffer(D, 3 * heads),
            buffer(heads, D),
            buffer(2, block, dtype=F32),
            buffer(2, block, dtype=F32),
            buffer(2, half, dtype=F32),
            buffer(2, half, quarter),
            buffer(quarter, half),
            buffer(2, 256, D),
            buffer(*dealt.shape),
            buffer(ROWS, half),
            buffer(ROWS, half),
            buffer(ROWS, block),
            buffer(ROWS, half),
            buffer(ROWS, half),
            buffer(ROWS, half),
            buffer(SL, half, dtype=F32),
            buffer(ROWS, half),
            buffer(ROWS, half),
            buffer(ROWS, half),
            buffer(ROWS, half),
            sem((2, MICRO, groups)),
            sem((2, now + 3)),
            sem((now + 28,)),
            sem((2, 15)),
            sem((2, 2)),
        ],
        compiler_params=pltpu.CompilerParams(
            collective_id=identity, has_side_effects=True, vmem_limit_bytes=67043328
        ),
        cost_estimate=FREE,
    )(*values)


def chain_kernel(
    line,
    normed,
    hidden_grad,
    second_mine,
    second_theirs,
    top_half,
    top_came,
    pair_w,
    down_w,
    qkv_w,
    out_w,
    turned,
    middle,
    inverse_first,
    inverse_second,
    gain_second,
    gain_first,
    x_own,
    key_live,
    cos,
    first,
    second,
    down_out,
    gate_grads_out,
    second_came_out,
    up_grad_out,
    up_row,
    dqkv_out,
    dqkv_row,
    branch_out,
    both_out,
    pieces_out,
    gate_row,
    gate_came,
    gate_came_row,
    gate_grads,
    second_came,
    up_grad,
    dqkv,
    branch,
    hidden,
    gate_grad,
    tiles,
    tall_tiles,
    da_tiles,
    kept,
    sent,
    row_came,
    summed,
    col_came,
    block_sent,
    block_came,
    hidden_row,
    hidden_came,
    hidden_came_row,
    branch_row,
    dots,
    down_grads,
    down_z,
    middle_own,
    layer_own,
    first_own,
    mixed_grad,
    turned_left,
    feed_sum,
    attention_sum,
    swap_sems,
    piece_sems,
    tile_sems,
    down_sems,
    copy_sems,
):
    dp, row, col = lax.axis_index("dp"), lax.axis_index("row"), lax.axis_index("col")
    x = lax.rem(dp, 2)
    partner = {"dp": dp + 1 - 2 * x}
    across = {"row": 1 - row}
    beside = {"col": 1 - col}
    down_line = ZLine(line, down_grads, down_out, None, down_z, down_sems, 4, True)
    half = D // 2
    block = D // 4
    quarter = normed.shape[1]
    pending, results = [], []

    def result(source, target):
        copy = pltpu.make_async_copy(source, target, copy_sems.at[2 + len(results)])
        copy.start()
        results.append(copy)

    def swap(source, target, at, device, sems=swap_sems):
        copy = pltpu.make_async_remote_copy(
            src_ref=source,
            dst_ref=target,
            send_sem=sems.at[0, at],
            recv_sem=sems.at[1, at],
            device_id=device,
            device_id_type=MESH,
        )
        return copy

    def begin(copy):
        copy.start()
        pending.append(copy)
        return copy

    greet(
        *down_line.moves(),
        (jnp.int32(1), partner),
        (jnp.int32(1), across),
        (jnp.int32(1), beside),
    )

    per = line // 2
    width = quarter // line
    tile = min(width, 256)
    each = width // tile

    def hidden_part(index, at):
        return hidden.at[:, pl.ds(pl.multiple_of((2 * at + index) * width, width), width)]

    def feed_columns(j, shift=0):
        piece = j // each
        index = jnp.where(piece < per, 1 - x, x)
        begin = (2 * lax.rem(piece, per) + index) * width + lax.rem(j, each) * tile
        return pl.ds(pl.multiple_of(shift + begin, tile), tile)

    to_x = [
        swap(
            hidden_part(1 - x, at),
            hidden_came.at[:, pl.ds(at * width, width)],
            at,
            partner,
            piece_sems,
        )
        for at in range(per)
    ]
    pending.extend(to_x)

    def feed_body(j, slot):
        gate = mm(normed[...], tall_tiles[slot, 0, :, :tile])
        up = mm(normed[...], tall_tiles[slot, 1, :, :tile])
        da = da_tiles[slot, :, :tile]
        sigmoid = 1.0 / (1.0 + jnp.exp(-gate))
        swish = gate * sigmoid
        there = feed_columns(j)
        hidden[:, there] = (swish * up).astype(BF16)
        gate_grad[:, there] = (da * up * sigmoid * (1.0 + gate * (1.0 - sigmoid))).astype(BF16)
        up_grad[:, there] = (da * swish).astype(BF16)
        for at in range(per):

            @pl.when(j == (at + 1) * each - 1)
            def _():
                to_x[at].start()

    narrow_tile = pl.ds(0, tile)
    stream(
        lambda j: [
            pair_w.at[:, feed_columns(j)],
            pair_w.at[:, feed_columns(j, quarter)],
            hidden_grad.at[:, feed_columns(j)],
        ],
        lambda slot: [
            tall_tiles.at[slot, 0, :, narrow_tile],
            tall_tiles.at[slot, 1, :, narrow_tile],
            da_tiles.at[slot, :, narrow_tile],
        ],
        tile_sems,
        quarter // tile,
        feed_body,
    )
    to_row, on_row = [], []
    for at in range(per):
        there = pl.ds(at * width, width)
        to_row.append(
            begin(swap(hidden_part(x, at), hidden_row.at[:, there], per + at, across, piece_sems))
        )
    result(up_grad, up_grad_out)
    second_x = begin(swap(second_theirs, second_came, 0, partner))
    gate_x = begin(swap(gate_grad, gate_came, 1, partner))

    def nt_product(w, depth, start, body):
        stream(
            lambda j: [w.at[pl.ds(pl.multiple_of(start + j * 256, 256), 256), :]],
            lambda slot: [tiles.at[slot, :, pl.ds(0, depth)]],
            tile_sems,
            half // 256,
            body,
        )

    def columns_at(j, size=256):
        return pl.ds(pl.multiple_of(j * size, size), size)

    def pair_body(target, dtype):
        def body(j, slot):
            total = mm_nt(gate_grad[...], tiles[slot, :, :quarter])
            total = total + mm_nt(up_grad[...], tiles[slot, :, quarter:])
            target[:, columns_at(j)] = total.astype(dtype)

        return body

    nt_product(pair_w, 2 * quarter, half, pair_body(sent, BF16))
    pair_r = begin(swap(sent, row_came.at[0], 2, across))
    nt_product(pair_w, 2 * quarter, 0, pair_body(kept, F32))
    pair_r.wait_recv()

    def join_pair(rows):
        summed[rows, :] = (kept[rows, :] + row_came[0, rows, :].astype(F32)).astype(BF16)

    rows_loop(join_pair)
    pair_c = begin(swap(summed, col_came, 3, beside))
    gate_r = begin(swap(gate_grad, gate_row, 4, across))
    up_r = begin(swap(up_grad, up_row, 5, across))

    for copy in to_x:
        copy.wait_recv()
    for at in range(per):
        there = pl.ds(at * width, width)
        on_row.append(
            begin(
                swap(
                    hidden_came.at[:, there],
                    hidden_came_row.at[:, there],
                    2 * per + at,
                    across,
                    piece_sems,
                )
            )
        )

    def down_grad(part, left_of, came):
        def body(columns, _):
            for at in range(per):
                there = pl.ds(at * width, width)
                total = mm_tn(left_of(at)[...], top_half[:, columns])
                total = total + mm_tn(came[:, there], top_came[:, columns])
                down_grads[pl.ds((part * per + at) * width, width), columns] = total.astype(BF16)

        tiles_loop(half, 512, body)

    down_grad(0, lambda at: hidden_part(x, at), hidden_came)
    for copy in to_row + on_row:
        copy.wait_recv()
    down_grad(1, lambda at: hidden_row.at[:, pl.ds(at * width, width)], hidden_came_row)
    down_line.run(0, 1)

    def down_product(start, target, dtype):
        def body(j, slot):
            target[:, columns_at(j)] = mm(hidden[...], tall_tiles[slot, 0]).astype(dtype)

        stream(
            lambda j: [down_w.at[:, pl.ds(pl.multiple_of(start + j * 256, 256), 256)]],
            lambda slot: [tall_tiles.at[slot, 0]],
            tile_sems,
            half // 256,
            body,
        )

    pair_r.wait_send()
    pending[:] = [copy for copy in pending if copy is not pair_r]
    down_product(half, sent, BF16)
    layer_r = begin(swap(sent, row_came.at[1], 7, across))
    down_product(0, kept, F32)
    layer_r.wait_recv()

    def mine_of(value):
        return jnp.where(col == 0, value[:, :block], value[:, block:])

    def theirs_of(value):
        return jnp.where(col == 0, value[:, block:], value[:, :block])

    def join_layer(rows):
        total = kept[rows, :] + row_came[1, rows, :].astype(F32)
        layer_own[rows, :] = mine_of(total)
        block_sent[0, rows, :] = theirs_of(total).astype(BF16)

    rows_loop(join_layer)
    layer_c = begin(swap(block_sent.at[0], block_came.at[0], 8, beside))
    middle_in = pltpu.make_async_copy(middle, kept, copy_sems.at[0])
    middle_in.start()

    middle_in.wait()
    pair_c.wait_recv()
    feed_sum[...] = jnp.zeros_like(feed_sum)

    def second_grads(rows):
        grad = summed[rows, :].astype(F32) + col_came[rows, :].astype(F32)
        return grad, grad * gain_second[1:2, :]

    def norm_first_pass(rows):
        grad, scaled = second_grads(rows)
        held = kept[rows, :]
        feed_sum[...] += jnp.sum(grad * held * inverse_second[rows, :], axis=0, keepdims=True)
        total = jnp.sum(scaled * held, axis=1, keepdims=True)
        dots[0, rows, :] = jnp.broadcast_to(total, (total.shape[0], 128))

    rows_loop(norm_first_pass)
    dot_r = begin(swap(dots.at[0], dots.at[1], 9, across))
    dot_r.wait_recv()

    def norm_second_pass(rows):
        _, scaled = second_grads(rows)
        held = kept[rows, :]
        inverse = inverse_second[rows, :]
        dot = dots[0, rows, :1] + dots[1, rows, :1]
        grad = (
            top_half[rows, :].astype(F32) + scaled * inverse - held * (inverse**3 * dot / D)
        )
        branch[rows, :] = grad.astype(BF16)
        middle_own[rows, :] = mine_of(grad)
        layer_own[rows, :] += mine_of(held)

    rows_loop(norm_second_pass)
    result(branch, branch_out)
    branch_r = begin(swap(branch, branch_row, 10, across))
    branch_r.wait_recv()

    down_line.run(1, 2)

    def mixed_body(j, slot):
        total = mm_nt(branch[...], tiles[slot, :, :half])
        total = total + mm_nt(branch_row[...], tiles[slot, :, half:D])
        mixed_grad[:, columns_at(j)] = total.astype(BF16)

    stream(
        lambda j: [out_w.at[pl.ds(pl.multiple_of(j * 256, 256), 256), :]],
        lambda slot: [tiles.at[slot, :, pl.ds(0, D)]],
        tile_sems,
        out_w.shape[0] // 256,
        mixed_body,
    )
    pairs = turned.shape[1] // 384
    lower = lax.broadcasted_iota(jnp.int32, (SL, SL), 1) <= lax.broadcasted_iota(
        jnp.int32, (SL, SL), 0
    )

    def attend(at, _):
        micro, pair = at // pairs, lax.rem(at, pairs)
        rows = pl.ds(pl.multiple_of(micro * SL, SL), SL)

        def part(kind):
            return pl.ds(pl.multiple_of(pair * 384 + kind * 128, 128), 128)

        allowed = lower & (key_live[pl.ds(micro, 1), :] > 0.5)
        dq, dk, dv = head_grads(
            turned[rows, part(0)],
            turned[rows, part(1)],
            turned[rows, part(2)],
            mixed_grad[rows, pl.ds(pl.multiple_of(pair * 128, 128), 128)],
            allowed,
            cos[...],
            first[...],
            second[...],
        )
        dqkv[rows, part(0)] = dq
        dqkv[rows, part(1)] = dk
        dqkv[rows, part(2)] = dv
        return 0

    lax.fori_loop(0, MICRO * pairs, attend, 0)
    result(dqkv, dqkv_out)

    def first_body(target, dtype):
        def body(j, slot):
            total = mm_nt(dqkv[...], tiles[slot, :, : dqkv.shape[1]])
            target[:, columns_at(j)] = total.astype(dtype)

        return body

    layer_r.wait_send()
    pending[:] = [copy for copy in pending if copy is not layer_r]
    nt_product(qkv_w, dqkv.shape[1], half, first_body(sent, BF16))
    first_r = begin(swap(sent, row_came.at[2], 11, across))
    dqkv_r = begin(swap(dqkv, dqkv_row, 12, across))
    nt_product(qkv_w, dqkv.shape[1], 0, first_body(kept, F32))
    down_line.run(2, line - 1)
    first_r.wait_recv()

    def join_first(rows):
        total = kept[rows, :] + row_came[2, rows, :].astype(F32)
        first_own[rows, :] = mine_of(total)
        block_sent[1, rows, :] = theirs_of(total).astype(BF16)

    rows_loop(join_first)
    first_c = begin(swap(block_sent.at[1], block_came.at[1], 13, beside))

    second_x.wait_recv()
    result(second_came, second_came_out)
    depth = second_mine.shape[0]
    turned_left[:, :depth] = second_mine[...].T
    turned_left[:, depth:] = second_came[...].T
    gate_x.wait_recv()
    gate_on = begin(swap(gate_came, gate_came_row, 14, across))

    def gate_part(shift, sources, values):
        def body(j, slot):
            mine, came = values(j, slot)
            total = mm(turned_left[:, :depth], mine) + mm(turned_left[:, depth:], came)
            there = pl.ds(pl.multiple_of(shift + j * 256, 256), 256)
            gate_grads[:, there] = total.astype(BF16)

        stream(
            lambda j: [source.at[:, columns_at(j)] for source in sources],
            lambda slot: [tall_tiles.at[slot, k, pl.ds(0, ROWS)] for k in range(len(sources))],
            tile_sems,
            quarter // 256,
            body,
        )

    gate_part(
        0,
        [gate_came],
        lambda j, slot: (gate_grad[:, columns_at(j)], tall_tiles[slot, 0, :ROWS]),
    )
    gate_r.wait_recv()
    gate_on.wait_recv()
    gate_part(
        quarter,
        [gate_row, gate_came_row],
        lambda j, slot: (tall_tiles[slot, 0, :ROWS], tall_tiles[slot, 1, :ROWS]),
    )

    result(gate_grads, gate_grads_out)
    layer_c.wait_recv()
    first_c.wait_recv()
    attention_sum[...] = jnp.zeros_like(attention_sum)

    def last_first_pass(rows):
        layer = layer_own[rows, :] + block_came[0, rows, :].astype(F32)
        both_out[rows, :] = layer.astype(BF16)
        grad = first_own[rows, :] + block_came[1, rows, :].astype(F32)
        first_own[rows, :] = grad
        held = x_own[rows, :].astype(F32)
        attention_sum[...] += jnp.sum(grad * held * inverse_first[rows, :], axis=0, keepdims=True)
        total = jnp.sum(grad * gain_first[...] * held, axis=1, keepdims=True)
        dots[2, rows, :] = jnp.broadcast_to(total, (total.shape[0], 128))

    rows_loop(last_first_pass)
    dot_r = begin(swap(dots.at[2], dots.at[3], 15, across))
    dot_r.wait_recv()

    def add_dots(rows):
        dots[4, rows, :] = dots[2, rows, :] + dots[3, rows, :]

    rows_loop(add_dots)
    dot_c = begin(swap(dots.at[4], dots.at[5], 16, beside))
    dot_c.wait_recv()

    def last_second_pass(rows):
        inverse = inverse_first[rows, :]
        dot = dots[4, rows, :1] + dots[5, rows, :1]
        scaled = first_own[rows, :] * gain_first[...]
        held = x_own[rows, :].astype(F32)
        grad = middle_own[rows, :] + scaled * inverse - held * (inverse**3 * dot / D)
        below = pl.ds(pl.multiple_of(rows.start + ROWS, rows.size), rows.size)
        both_out[below, :] = grad.astype(BF16)

    rows_loop(last_second_pass)
    pieces_out[0:1, :] = attention_sum[...]
    pieces_out[1:2, :] = mine_of(feed_sum[...])

    down_line.stage = kept.at[pl.ds(0, down_grads.shape[0] // line), :]
    down_line.finish()
    down_store = pltpu.make_async_copy(down_line.stage, down_out, copy_sems.at[1])
    down_store.start()
    for copy in (up_r, dqkv_r):
        copy.wait_recv()
    for copy in pending:
        copy.wait_send()
    down_store.wait()
    for copy in results:
        copy.wait()


def chain(line, identity, *values):
    quarter = values[1].shape[1]
    narrow = values[2].shape[1]
    qkv_width = values[10].shape[1]
    half, block = D // 2, D // 4
    rows = quarter // 2
    vmem = pl.BlockSpec(memory_space=pltpu.VMEM)
    anywhere = pl.BlockSpec(memory_space=pl.ANY)
    outside = {1, 3, 6, 7, 8, 9, 11}

    def array(*shape, dtype=BF16):
        return jax.ShapeDtypeStruct(shape, dtype)

    def buffer(*shape, dtype=BF16):
        return pltpu.VMEM(shape, dtype)

    outs = [
        (array(2 * rows // line, half, dtype=F32), anywhere),
        (array(narrow, 2 * quarter), anywhere),
        (array(ROWS, narrow), anywhere),
        (array(ROWS, quarter), anywhere),
        (array(ROWS, quarter), anywhere),
        (array(ROWS, qkv_width), anywhere),
        (array(ROWS, qkv_width), anywhere),
        (array(ROWS, half), anywhere),
        (array(2 * ROWS, block), vmem),
        (array(2, block, dtype=F32), vmem),
        (array(ROWS, quarter), anywhere),
        (array(ROWS, quarter), anywhere),
        (array(ROWS, quarter), anywhere),
    ]
    sem = pltpu.SemaphoreType.DMA
    return pl.pallas_call(
        lambda *refs: chain_kernel(line, *refs),
        out_shape=[shape for shape, _ in outs],
        in_specs=[anywhere if k in outside else vmem for k in range(len(values))],
        out_specs=[place for _, place in outs],
        scratch_shapes=[
            buffer(narrow, 2 * quarter),
            buffer(ROWS, narrow),
            buffer(ROWS, quarter),
            buffer(ROWS, qkv_width),
            buffer(ROWS, half),
            buffer(ROWS, quarter),
            buffer(ROWS, quarter),
            buffer(2, 256, 2 * quarter),
            buffer(2, 2, quarter, 256),
            buffer(2, ROWS, 256, dtype=F32),
            buffer(ROWS, half, dtype=F32),
            buffer(ROWS, half),
            buffer(3, ROWS, half),
            buffer(ROWS, half),
            buffer(ROWS, half),
            buffer(2, ROWS, block),
            buffer(2, ROWS, block),
            buffer(ROWS, rows),
            buffer(ROWS, rows),
            buffer(ROWS, rows),
            buffer(ROWS, half),
            buffer(6, ROWS, 128, dtype=F32),
            buffer(2 * rows, half),
            buffer(2, line - 1, 2 * rows // line, half),
            buffer(ROWS, block, dtype=F32),
            buffer(ROWS, block, dtype=F32),
            buffer(ROWS, block, dtype=F32),
            buffer(ROWS, qkv_width // 3),
            buffer(narrow, 2 * ROWS),
            buffer(1, half, dtype=F32),
            buffer(1, block, dtype=F32),
            sem((2, 17)),
            sem((2, 3 * (line // 2))),
            sem((2, 3)),
            sem((2, 2, line - 1, 4)),
            sem((7,)),
        ],
        compiler_params=pltpu.CompilerParams(
            collective_id=identity, has_side_effects=True, vmem_limit_bytes=67043328
        ),
        cost_estimate=FREE,
    )(*values)


def tail_sums(line, identity, *values):
    (gate_grads, up, _, _, _, dqkv, _, _, _, branch) = values[:10]
    rows = gate_grads.shape[0]
    side_rows = 2 * values[10].shape[1]
    tokens = up.shape[0]
    widths = (gate_grads.shape[1], gate_grads.shape[1], 2 * dqkv.shape[1], branch.shape[1])
    heights = (rows, rows, rows, side_rows)
    pieces = (4, 4, 3, 1)
    sizes = [(h // line, w) for h, w in zip(heights, widths)]
    vmem = pl.BlockSpec(memory_space=pltpu.VMEM)
    anywhere = pl.BlockSpec(memory_space=pl.ANY)
    both, gains = values[12:]
    height = sizes[0][0]
    gain_steps = both.shape[1].bit_length() - 1

    def buffer(*shape):
        return pltpu.VMEM(shape, BF16)

    def array(*shape):
        return jax.ShapeDtypeStruct(shape, F32)

    return pl.pallas_call(
        lambda *refs: tail_kernel(line, *refs),
        out_shape=[
            array(*sizes[0]),
            array(*sizes[1]),
            array(height, widths[2] // 3),
            array(height, widths[2] // 3),
            array(height, widths[2] // 3),
            array(*sizes[3]),
            jax.ShapeDtypeStruct(both.shape, BF16),
            array(*gains.shape),
        ],
        in_specs=[vmem] + [anywhere] * 12 + [vmem],
        out_specs=[anywhere] * 7 + [vmem],
        scratch_shapes=[buffer(*values[at].shape) for at in (1, 2, 3, 4, 5, 6, 7, 9, 10)]
        + [buffer(2, line - 1, *size) for size in sizes]
        + [buffer(h, w) for h, w in zip(heights[1:], widths[1:])]
        + [buffer(*up.shape)] * 2
        + [buffer(*dqkv.shape)] * 2
        + [buffer(*branch.shape), buffer(*values[7].shape)]
        + [buffer(*values[10].shape)] * 3
        + [buffer(rows, 2 * tokens)]
        + [pltpu.VMEM(size, F32) for size in sizes]
        + [pltpu.SemaphoreType.DMA((2, 2, line - 1, count)) for count in pieces]
        + [pltpu.SemaphoreType.DMA((2, 9)), pltpu.SemaphoreType.DMA((6 + widths[2] // 128,))]
        + [pltpu.VMEM((2, gain_steps, *gains.shape), F32)]
        + [
            pltpu.SemaphoreType.DMA((2, both.shape[1])),
            pltpu.SemaphoreType.DMA((2, gain_steps)),
            pltpu.SemaphoreType.DMA((9,)),
        ],
        compiler_params=pltpu.CompilerParams(
            collective_id=identity, has_side_effects=True, vmem_limit_bytes=67043328
        ),
        cost_estimate=FREE,
    )(*values)


def finish_kernel(count, order_ref, back_ref, *refs):
    sums, rest = refs[:count], refs[count:]
    layer_ref, grad_ref = rest[:2]
    outs, held, sems = rest[2 : 2 + count], rest[2 + count : 2 + 2 * count], rest[2 + 2 * count]
    groups = back_ref.shape[1]
    loads = [pltpu.make_async_copy(sums[k], held[k], sems.at[0, k]) for k in range(count)]
    stores = [pltpu.make_async_copy(held[k], outs[k], sems.at[1, k]) for k in range(count)]
    for copy in loads:
        copy.start()

    def one(at, _):
        micro, slot = at // groups, lax.rem(at, groups)
        place = order_ref[micro, slot]
        layer_ref[micro, place] = back_ref[micro, slot]
        grad_ref[micro, place] = back_ref[MICRO + micro, slot]
        return 0

    lax.fori_loop(0, MICRO * groups, one, 0)
    for load, store in zip(loads, stores):
        load.wait()
        store.start()
    for store in stores:
        store.wait()


def finish(order, back, *sums):
    vmem = pl.BlockSpec(memory_space=pltpu.VMEM)
    anywhere = pl.BlockSpec(memory_space=pl.ANY)
    rows = jax.ShapeDtypeStruct((MICRO,) + back.shape[1:], BF16)
    count = len(sums)
    return pl.pallas_call(
        lambda *refs: finish_kernel(count, *refs),
        out_shape=[rows, rows] + [jax.ShapeDtypeStruct(v.shape, F32) for v in sums],
        in_specs=[pl.BlockSpec(memory_space=pltpu.SMEM), vmem] + [anywhere] * count,
        out_specs=[vmem, vmem] + [anywhere] * count,
        scratch_shapes=[pltpu.VMEM(v.shape, F32) for v in sums]
        + [pltpu.SemaphoreType.DMA((2, count))],
        cost_estimate=FREE,
    )(order, back, *sums)


def per_device(
    tokens,
    lengths,
    deal_order,
    attention_gain,
    query_weight,
    key_weight,
    value_weight,
    output_weight,
    feed_gain,
    gate_weight,
    up_weight,
    down_weight,
    cotangent,
):
    groups = lax.axis_size("dp")
    line = groups // 2
    dp = lax.axis_index("dp")
    row = lax.axis_index("row")
    col = lax.axis_index("col")
    z, x = dp // 2, dp % 2
    half = D // 2
    block = D // 4

    def over_row(v):
        return lax.ppermute(v, "row", SWAP)

    def over_col(v):
        return lax.ppermute(v, "col", SWAP)

    def ordered(own, other, index, axis=-1):
        return jnp.where(
            index == 0,
            jnp.concatenate([own, other], axis=axis),
            jnp.concatenate([other, own], axis=axis),
        )

    def x_parts(v, width):
        even = jnp.concatenate(
            [v[:, s : s + width] for s in range(0, v.shape[1], 2 * width)], axis=1
        )
        odd = jnp.concatenate(
            [v[:, s : s + width] for s in range(width, v.shape[1], 2 * width)], axis=1
        )
        return jnp.where(x == 0, even, odd), jnp.where(x == 0, odd, even)

    def plain(*values):
        return values

    dealt, top_block, key_live = prepare(deal_order, lengths, tokens, cotangent)
    tables = rope_tables()
    (
        pair_w,
        down_w,
        qkv_w,
        out_w,
        x_block,
        top_half,
        top_came,
        first_mine,
        first_theirs,
        turned,
        mixed_mine,
        mixed_theirs,
        middle,
        second_mine,
        second_theirs,
        normed_second,
        hidden_grad,
        inverse_first,
        inverse_second,
        gains_half,
    ) = front(
        line,
        0,
        dealt,
        top_block,
        attention_gain.reshape(1, block),
        feed_gain.reshape(1, block),
        key_live,
        *tables,
        query_weight,
        key_weight,
        value_weight,
        output_weight,
        gate_weight,
        up_weight,
        down_weight,
    )
    x_block = x_block.reshape(ROWS, block)
    narrow = half // groups
    (
        down_sum,
        gate_grads,
        second_came,
        up_grad,
        up_row,
        dqkv,
        dqkv_row,
        branch,
        both,
        pieces,
        _,
        _,
        _,
    ) = chain(
        line,
        4,
        *plain(
            normed_second,
            hidden_grad,
            second_mine,
            second_theirs,
            top_half,
            top_came,
            pair_w,
            down_w,
            qkv_w,
            out_w,
            turned,
            middle,
            inverse_first,
            inverse_second,
            gains_half,
            attention_gain.reshape(1, block),
            x_block,
            key_live,
            *tables,
        ),
    )

    gate_sum, up_sum, query_sum, key_sum, value_sum, output_sum, back, gain_sums = tail_sums(
        line,
        3,
        *plain(
            gate_grads,
            up_grad,
            up_row,
            second_mine,
            second_came,
            dqkv,
            dqkv_row,
            first_mine,
            first_theirs,
            branch,
            mixed_mine,
            mixed_theirs,
            both.reshape(2 * MICRO, groups, SL // groups, block),
            pieces,
        ),
    )
    (
        layer_output,
        tokens_grad,
        down_sum,
        gate_sum,
        up_sum,
        query_sum,
        key_sum,
        value_sum,
        output_sum,
    ) = finish(
        deal_order,
        back,
        down_sum,
        gate_sum,
        up_sum,
        query_sum,
        key_sum,
        value_sum,
        output_sum,
    )
    gain_size = block // groups
    gain_sums = lax.dynamic_slice_in_dim(gain_sums, dp * gain_size, gain_size, 1)

    return (
        layer_output,
        tokens_grad,
        gain_sums[0],
        query_sum,
        key_sum,
        value_sum,
        output_sum,
        gain_sums[1],
        gate_sum,
        up_sum,
        down_sum,
    )


def solution(mesh):
    in_specs = (
        P(None, None, "dp", ("row", "col")),
        P(),
        P(),
        P(("row", "col")),
        P("row", "col"),
        P("row", "col"),
        P("row", "col"),
        P("col", "row"),
        P(("row", "col")),
        P("row", "col"),
        P("row", "col"),
        P("col", "row"),
        P(None, "dp", None, ("row", "col")),
    )
    out_specs = (
        P(None, None, "dp", ("row", "col")),
        P(None, None, "dp", ("row", "col")),
        P(("row", "col", "dp")),
        P(("row", "dp"), "col"),
        P(("row", "dp"), "col"),
        P(("row", "dp"), "col"),
        P(("col", "dp"), "row"),
        P(("row", "col", "dp")),
        P(("row", "dp"), "col"),
        P(("row", "dp"), "col"),
        P(("col", "dp"), "row"),
    )
    return jax.shard_map(
        per_device, mesh=mesh, in_specs=in_specs, out_specs=out_specs, check_vma=False
    )
```

```python
import math

import jax
import jax.numpy as jnp
import numpy as np
from jax import lax
from jax.experimental import pallas as pl
from jax.experimental.pallas import tpu as pltpu
from jax.sharding import PartitionSpec as P

D = 2048
HEADS = 32
HEAD_DIM = 64
SL = 256
MICRO = 2
ROWS = MICRO * SL

EPSILON = 1e-05
ROPE_THETA = 130000.0
MASKED_SCORE = -1000000000.0
F32 = jnp.float32
BF16 = jnp.bfloat16
SWAP = [(0, 1), (1, 0)]


def mm(a, b):
    return jnp.dot(a, b, preferred_element_type=F32)


def mm_nt(a, b):
    return lax.dot_general(a, b, (((1,), (1,)), ((), ())), preferred_element_type=F32)


def mm_tn(a, b):
    return lax.dot_general(a, b, (((0,), (0,)), ((), ())), preferred_element_type=F32)


def rope_tables():
    half = HEAD_DIM // 2
    frequency = np.exp(np.arange(half, dtype=np.float32) * np.float32(-2.0 * math.log(ROPE_THETA) / HEAD_DIM))
    angles = np.arange(SL, dtype=np.float32)[:, None] * frequency[None, :]
    cosine, sine = np.cos(angles), np.sin(angles)
    zero = np.zeros_like(sine)
    table_cos = np.concatenate([cosine] * 4, axis=1)
    table_first = np.concatenate([sine, zero] * 2, axis=1)
    table_second = np.concatenate([zero, sine] * 2, axis=1)
    return jnp.asarray(table_cos), jnp.asarray(table_first), jnp.asarray(table_second)


def turn(v, cos, first, second):
    ahead = pltpu.roll(v, 128 - HEAD_DIM // 2, 1)
    behind = pltpu.roll(v, HEAD_DIM // 2, 1)
    return v * cos - ahead * first + behind * second


def turn_back(v, cos, first, second):
    ahead = pltpu.roll(v, 128 - HEAD_DIM // 2, 1)
    behind = pltpu.roll(v, HEAD_DIM // 2, 1)
    return v * cos + ahead * first - behind * second


def head_mask(head):
    lane = lax.broadcasted_iota(jnp.int32, (SL, 128), 1)
    return (lane // HEAD_DIM) == head


def softmax_of(q, k, allowed):
    scores = jnp.where(allowed, mm_nt(q, k), MASKED_SCORE)
    exps = jnp.exp(scores - jnp.max(scores, axis=1, keepdims=True))
    return exps * (1.0 / jnp.sum(exps, axis=1, keepdims=True))


def scaled_down(q):
    return (q.astype(F32) * HEAD_DIM ** (-0.5)).astype(BF16)


BLOCKS = ((slice(0, SL), SL),)


FREE = pl.CostEstimate(flops=0, bytes_accessed=0, transcendentals=0)


def whole(shape):
    return pl.BlockSpec(shape, lambda *at: (0,) * len(shape), pipeline_mode=pl.Buffered(1))


def head_outputs(qkv, allowed, cos, first, second):
    qr = turn(qkv[:, :128], cos, first, second).astype(BF16)
    kr = turn(qkv[:, 128:256], cos, first, second).astype(BF16)
    vr = qkv[:, 256:].astype(BF16)
    zero = jnp.zeros_like(vr)
    outs = [jnp.zeros((SL, 128), F32)]
    scaled = scaled_down(qr)
    for head in range(2):
        mask = head_mask(head)
        q_own = jnp.where(mask, scaled, zero)
        v_own = jnp.where(mask, vr, zero)
        for at, (rows, keys) in enumerate(BLOCKS):
            probs = softmax_of(q_own[rows], kr[:keys], allowed[rows, :keys]).astype(BF16)
            outs[at] = outs[at] + mm(probs, v_own[:keys])
    return qr, kr, vr, jnp.concatenate(outs, axis=0).astype(BF16)


def head_grads(qr, kr, vr, od, allowed, cos, first, second):
    dq = [jnp.zeros((SL, 128), F32)]
    dk = [jnp.zeros((SL, 128), F32)]
    dv = [jnp.zeros((SL, 128), F32)]
    zero = jnp.zeros_like(qr)
    scaled = scaled_down(qr)
    for head in range(2):
        mask = head_mask(head)
        q_own = jnp.where(mask, scaled, zero)
        k_own = jnp.where(mask, kr, zero)
        od_own = jnp.where(mask, od, zero)
        for at, (rows, keys) in enumerate(BLOCKS):
            probs = softmax_of(q_own[rows], kr[:keys], allowed[rows, :keys])
            d_probs = mm_nt(od_own[rows], vr[:keys])
            dv[at] = dv[at] + mm_tn(probs.astype(BF16), od_own[rows])
            inner = jnp.sum(probs * d_probs, axis=1, keepdims=True)
            d_scores = (probs * (d_probs - inner)).astype(BF16)
            dq[at] = dq[at] + mm(d_scores, k_own[:keys])
            dk[at] = dk[at] + mm_tn(d_scores, q_own[rows])

    def keys_sum(parts):
        return parts[0]

    dq = jnp.concatenate(dq, axis=0) * HEAD_DIM ** (-0.5)
    return (
        turn_back(dq, cos, first, second).astype(BF16),
        turn_back(keys_sum(dk), cos, first, second).astype(BF16),
        keys_sum(dv).astype(BF16),
    )


MESH = pl.DeviceIdType.MESH


def greet(*moves):
    barrier = pltpu.get_barrier_semaphore()
    total = 0
    for count, target in moves:
        total = total + count

        @pl.when(count > 0)
        def _():
            pl.semaphore_signal(barrier, inc=1, device_id=target, device_id_type=MESH)

    pl.semaphore_wait(barrier, total)


class ZLine:
    def __init__(self, line, grads, out, stage, came, sems, count, sided):
        self.line, self.grads, self.out, self.stage = line, grads, out, stage
        self.came, self.sems, self.sided = came, sems, sided
        width = grads.shape[1] // count
        self.pieces = [(k, pl.ds(k * width, width)) for k in range(count)]
        self.dp, self.row = lax.axis_index("dp"), lax.axis_index("row")
        self.z = self.dp // 2
        self.last = line - 1
        self.ways = ((0, self.z, 2), (1, self.last - self.z, -2))

    def rows_of(self, dest):
        size = self.grads.shape[0] // self.line
        if self.sided:
            dest = lax.rem(dest + self.line - self.row * (self.line // 2), self.line)
        return pl.ds(pl.multiple_of(dest * size, size), size)

    def copy(self, source, way, step, slot, piece, columns):
        return pltpu.make_async_remote_copy(
            src_ref=source,
            dst_ref=self.came.at[way, slot, :, columns],
            send_sem=self.sems.at[0, way, slot, piece],
            recv_sem=self.sems.at[1, way, slot, piece],
            device_id={"dp": self.dp + step},
            device_id_type=MESH,
        )

    def arrived(self, way, step, slot, piece, columns):
        held = self.came.at[way, slot, :, columns]
        self.copy(held, way, step, slot, piece, columns).wait_recv()
        return held

    def run(self, start, stop):
        def one_step(slot, _):
            for piece, columns in self.pieces:
                for way, place, step in self.ways:
                    far = self.last - slot + place
                    dest = far if step > 0 else self.last - far

                    @pl.when((place == 0) & (place < self.last))
                    def _():
                        source = self.grads.at[self.rows_of(dest), columns]
                        self.copy(source, way, step, slot, piece, columns).start()

                    @pl.when((place > 0) & (place <= slot))
                    def _():
                        held = self.arrived(way, step, slot - 1, piece, columns)

                        @pl.when(place < self.last)
                        def _():
                            held[...] = (
                                held[...].astype(F32)
                                + self.grads[self.rows_of(dest), columns].astype(F32)
                            ).astype(BF16)
                            self.copy(held, way, step, slot, piece, columns).start()

            return 0

        lax.fori_loop(start, stop, one_step, 0)

    def finish(self):
        own = self.rows_of(self.z)
        for piece, columns in self.pieces:
            self.stage[:, columns] = self.grads[own, columns].astype(F32)
            for way, place, step in self.ways:

                @pl.when(place > 0)
                def _():
                    held = self.arrived(way, step, self.last - 1, piece, columns)
                    self.stage[:, columns] += held[...].astype(F32)

        def settle(slot, _):
            for piece, columns in self.pieces:
                for way, place, step in self.ways:

                    @pl.when((place <= slot) & (place < self.last))
                    def _():
                        held = self.came.at[way, slot, :, columns]
                        self.copy(held, way, step, slot, piece, columns).wait_send()

            return 0

        lax.fori_loop(0, self.last, settle, 0)

    def moves(self):
        return (
            (jnp.minimum(self.z, 1), {"dp": self.dp - 2}),
            (jnp.minimum(self.last - self.z, 1), {"dp": self.dp + 2}),
        )


def tiles_loop(width, tile, body):
    def one(j, _):
        body(pl.ds(pl.multiple_of(j * tile, tile), tile), j * tile)
        return 0

    lax.fori_loop(0, width // tile, one, 0)


def tail_kernel(
    line,
    gate_grads,
    up_in,
    up_row_in,
    second_mine_in,
    second_came_in,
    dqkv_in,
    dqkv_row_in,
    first_mine_in,
    first_theirs,
    branch_in,
    mixed_mine_in,
    mixed_theirs,
    both,
    pieces,
    gate_out,
    up_out,
    query_out,
    key_out,
    value_out,
    output_out,
    back,
    gains_out,
    up,
    up_row,
    second_mine,
    second_came,
    dqkv,
    dqkv_row,
    first_mine,
    branch,
    mixed_mine,
    gate_z,
    up_z,
    qkv_z,
    output_z,
    up_grads,
    qkv_grads,
    output_grads,
    up_came,
    up_came_row,
    dqkv_came,
    dqkv_came_row,
    branch_came,
    first_came,
    mixed_came,
    mixed_row,
    mixed_came_row,
    turned_left,
    gate_stage,
    up_stage,
    qkv_stage,
    output_stage,
    gate_sems,
    up_sems,
    qkv_sems,
    output_sems,
    swap_sems,
    out_sems,
    gains,
    back_sems,
    gain_sems,
    fetch_sems,
):
    groups = 2 * line
    dp, row = lax.axis_index("dp"), lax.axis_index("row")
    partner = dp + 1 - 2 * lax.rem(dp, 2)
    gate_line = ZLine(line, gate_grads, gate_out, gate_stage, gate_z, gate_sems, 4, False)
    up_line = ZLine(line, up_grads, up_out, up_stage, up_z, up_sems, 4, False)
    qkv_line = ZLine(line, qkv_grads, None, qkv_stage, qkv_z, qkv_sems, 3, False)
    output_line = ZLine(line, output_grads, output_out, output_stage, output_z, output_sems, 1, True)

    def swap(source, target, at, device):
        return pltpu.make_async_remote_copy(
            src_ref=source,
            dst_ref=target,
            send_sem=swap_sems.at[0, at],
            recv_sem=swap_sems.at[1, at],
            device_id=device,
            device_id_type=MESH,
        )

    fetches = {}
    order = (
        (second_mine_in, second_mine),
        (second_came_in, second_came),
        (up_in, up),
        (up_row_in, up_row),
        (mixed_mine_in, mixed_mine),
        (branch_in, branch),
        (first_mine_in, first_mine),
        (dqkv_in, dqkv),
        (dqkv_row_in, dqkv_row),
    )
    for at, (source, target) in enumerate(order):
        fetches[at] = pltpu.make_async_copy(source, target, fetch_sems.at[at])
        fetches[at].start()
    up_x = swap(up_in, up_came, 0, {"dp": partner})
    branch_x = swap(branch_in, branch_came, 1, {"dp": partner})
    dqkv_x = swap(dqkv_in, dqkv_came, 2, {"dp": partner})
    up_across = swap(up_came, up_came_row, 3, {"row": 1 - row})
    dqkv_across = swap(dqkv_came, dqkv_came_row, 4, {"row": 1 - row})
    first_x = swap(first_theirs, first_came, 5, {"dp": partner})
    mixed_x = swap(mixed_theirs, mixed_came, 6, {"dp": partner})
    mixed_r = swap(mixed_mine_in, mixed_row, 7, {"row": 1 - row})
    mixed_across = swap(mixed_came, mixed_came_row, 8, {"row": 1 - row})

    stores = []

    def store(source, target):
        copy = pltpu.make_async_copy(source, target, out_sems.at[len(stores)])
        copy.start()
        stores.append(copy)

    def store_wide(line_of):
        size = line_of.stage.shape[1] // 2
        for part in range(2):
            place = row if part == 0 else 1 - row
            there = pl.ds(pl.multiple_of(place * size, size), size)
            store(line_of.stage.at[:, pl.ds(part * size, size)], line_of.out.at[:, there])

    def store_qkv():
        heads = dqkv.shape[1] // 3
        for part in range(2):
            place = row if part == 0 else 1 - row
            for pair in range(heads // 128):
                for kind, out in enumerate((query_out, key_out, value_out)):
                    here = pl.ds(part * 3 * heads + pair * 384 + kind * 128, 128)
                    there = pl.ds(pl.multiple_of(place * heads + pair * 128, 128), 128)
                    store(qkv_stage.at[:, here], out.at[:, there])

    def returned(step):
        target = lax.rem(dp + step, groups)
        return pltpu.make_async_remote_copy(
            src_ref=both.at[:, target],
            dst_ref=back.at[:, dp],
            send_sem=back_sems.at[0, step],
            recv_sem=back_sems.at[1, step],
            device_id={"dp": target},
            device_id_type=MESH,
        )

    gain_steps = groups.bit_length() - 1

    def gain_copy(step):
        reach = 1 << step
        peer = dp + reach - 2 * reach * lax.rem(dp // reach, 2)
        return pltpu.make_async_remote_copy(
            src_ref=gains.at[0, step],
            dst_ref=gains.at[1, step],
            send_sem=gain_sems.at[0, step],
            recv_sem=gain_sems.at[1, step],
            device_id={"dp": peer},
            device_id_type=MESH,
        )

    def gain_step(step):
        if step >= gain_steps:
            return
        gain_copy(step).wait_recv()
        total = gains[0, step] + gains[1, step]
        if step + 1 == gain_steps:
            gains_out[...] = total
        else:
            gains[0, step + 1] = total
            gain_copy(step + 1).start()

    others = [(jnp.int32(1), {"dp": lax.rem(dp + step, groups)}) for step in range(1, groups)]
    greet(*others, (jnp.int32(1), {"row": 1 - row}))
    gains[0, 0] = pieces[...]
    gain_copy(0).start()
    gate_line.run(0, 1)
    up_x.start()
    mixed_x.start()
    branch_x.start()
    first_x.start()
    dqkv_x.start()
    mixed_r.start()

    def send_back(step, _):
        returned(step).start()
        return 0

    lax.fori_loop(1, groups, send_back, 0)
    store(both.at[:, dp], back.at[:, dp])

    fetches[0].wait()
    fetches[1].wait()
    depth = second_mine.shape[0]
    turned_left[:, :depth] = second_mine[...].T
    turned_left[:, depth:] = second_came[...].T
    gate_line.run(1, 2)

    def wide(target, shift, mine, came):
        def body(columns, start):
            total = mm(turned_left[:, :depth], mine[:, columns])
            total = total + mm(turned_left[:, depth:], came[:, columns])
            tile = total.shape[1]
            target[:, pl.ds(pl.multiple_of(shift + start, tile), tile)] = total.astype(BF16)

        tiles_loop(mine.shape[1], 512, body)

    up_x.wait_recv()
    up_across.start()
    gain_step(0)
    gate_line.run(2, line - 1)
    fetches[2].wait()
    fetches[3].wait()
    wide(up_grads, 0, up, up_came)
    up_across.wait_recv()
    wide(up_grads, up.shape[1], up_row, up_came_row)
    up_line.run(0, 1)
    gate_line.finish()
    store_wide(gate_line)

    mixed_x.wait_recv()
    mixed_across.start()
    branch_x.wait_recv()

    def side(start, mine, came):
        def body(columns, _):
            total = mm_tn(mine[...], branch[:, columns]) + mm_tn(came[...], branch_came[:, columns])
            output_grads[pl.ds(start, mine.shape[1]), columns] = total.astype(BF16)

        tiles_loop(branch.shape[1], 512, body)

    fetches[4].wait()
    fetches[5].wait()
    side(0, mixed_mine, mixed_came)
    mixed_r.wait_recv()
    mixed_across.wait_recv()
    side(mixed_mine.shape[1], mixed_row, mixed_came_row)
    output_line.run(0, 1)
    up_line.run(1, 2)
    gain_step(1)
    for at in (6, 7, 8):
        fetches[at].wait()
    first_x.wait_recv()
    turned_left[:, :depth] = first_mine[...].T
    turned_left[:, depth:] = first_came[...].T
    dqkv_x.wait_recv()
    dqkv_across.start()
    wide(qkv_grads, 0, dqkv, dqkv_came)
    dqkv_across.wait_recv()
    wide(qkv_grads, dqkv.shape[1], dqkv_row, dqkv_came_row)
    qkv_line.run(0, 1)
    output_line.run(1, 2)
    up_line.run(2, line - 1)
    qkv_line.run(1, 2)
    output_line.run(2, line - 1)
    for step in range(2, gain_steps):
        gain_step(step)
    up_line.finish()
    store_wide(up_line)
    qkv_line.run(2, line - 1)
    output_line.finish()
    store(output_stage, output_out)
    qkv_line.finish()
    store_qkv()

    def get_back(step, _):
        returned(step).wait()
        return 0

    lax.fori_loop(1, groups, get_back, 0)
    for step in range(gain_steps):
        gain_copy(step).wait_send()
    copies = (up_x, branch_x, dqkv_x, up_across, dqkv_across)
    for copy in copies + (first_x, mixed_x, mixed_r, mixed_across):
        copy.wait_send()
    for copy in stores:
        copy.wait()


def stream(source_of, slots_of, sems, count, body):
    def fetch(j, slot):
        return [
            pltpu.make_async_copy(source, target, sems.at[slot, k])
            for k, (source, target) in enumerate(zip(source_of(j), slots_of(slot)))
        ]

    for copy in fetch(0, 0):
        copy.start()

    def one(j, _):
        slot = lax.rem(j, 2)

        @pl.when(j + 1 < count)
        def _():
            for copy in fetch(j + 1, 1 - slot):
                copy.start()

        for copy in fetch(j, slot):
            copy.wait()
        body(j, slot)
        return 0

    lax.fori_loop(0, count, one, 0)


def rows_loop(body, size=64):
    def one(j, _):
        body(pl.ds(pl.multiple_of(j * size, size), size))
        return 0

    lax.fori_loop(0, ROWS // size, one, 0)


def prepare_kernel(order_ref, len_ref, tokens_ref, top_ref, dealt_ref, block_ref, live_ref):
    groups = tokens_ref.shape[1]
    dp = lax.axis_index("dp")

    def one(at, _):
        micro, slot = at // groups, lax.rem(at, groups)
        dealt_ref[micro, slot] = tokens_ref[micro, order_ref[micro, slot]]
        return 0

    lax.fori_loop(0, MICRO * groups, one, 0)
    for micro in range(MICRO):
        length = len_ref[micro, order_ref[micro, dp]]
        rows = lax.broadcasted_iota(jnp.int32, top_ref.shape[2:], 0)
        top = top_ref[micro, 0]
        top = jnp.where(rows < length, top.astype(F32), 0.0).astype(BF16)
        block_ref[micro * SL : micro * SL + SL, :] = top
        keys = lax.broadcasted_iota(jnp.int32, (1, SL), 1)
        live_ref[micro : micro + 1, :] = jnp.where(keys < length, 1.0, 0.0)


def prepare(order, lengths, tokens, cotangent):
    vmem = pl.BlockSpec(memory_space=pltpu.VMEM)
    smem = pl.BlockSpec(memory_space=pltpu.SMEM)
    return pl.pallas_call(
        prepare_kernel,
        out_shape=(
            jax.ShapeDtypeStruct(tokens.shape, BF16),
            jax.ShapeDtypeStruct((ROWS, cotangent.shape[3]), BF16),
            jax.ShapeDtypeStruct((MICRO, SL), F32),
        ),
        in_specs=[smem, smem, vmem, vmem],
        out_specs=(vmem,) * 3,
        cost_estimate=FREE,
    )(order, lengths, tokens, cotangent)


def front_kernel(
    dealt,
    top_block,
    gain_first,
    gain_second,
    key_live,
    cos,
    first,
    second,
    query_weight,
    key_weight,
    value_weight,
    output_weight,
    gate_weight,
    up_weight,
    down_weight,
    pair_out,
    down_out,
    qkv_out,
    out_out,
    x_out,
    top_half_out,
    top_came_out,
    first_mine_out,
    first_theirs_out,
    turned_out,
    mixed_mine_out,
    mixed_theirs_out,
    middle_out,
    second_mine_out,
    second_theirs_out,
    normed_second_out,
    hidden_grad_out,
    inverse_first,
    inverse_second,
    gains,
    x_in,
    top_half,
    top_came,
    normed_first,
    first_mine,
    first_theirs,
    turned,
    mixed,
    mixed_mine,
    mixed_theirs,
    middle,
    second_mine,
    second_theirs,
    normed_second,
    hidden_grad,
    qkv_w,
    out_w,
    gains_own,
    gains_col,
    gains_row,
    pair_held,
    down_held,
    tiles,
    x_came,
    x_half,
    x_other,
    top_col,
    top_row,
    sent,
    row_came,
    kept,
    summed,
    col_came,
    low,
    low_came,
    deal_sems,
    weight_sems,
    local_sems,
    swap_sems,
    tile_sems,
):
    groups = dealt.shape[1]
    dp, row, col = lax.axis_index("dp"), lax.axis_index("row"), lax.axis_index("col")
    x = lax.rem(dp, 2)
    partner = {"dp": dp + 1 - 2 * x}
    across = {"row": 1 - row}
    beside = {"col": 1 - col}
    half, block = D // 2, D // 4
    heads = query_weight.shape[1] // 2
    quarter = gate_weight.shape[1] // 2
    pending = []

    def remote(source, target, sems, at, device):
        copy = pltpu.make_async_remote_copy(
            src_ref=source,
            dst_ref=target,
            send_sem=sems.at[0, at],
            recv_sem=sems.at[1, at],
            device_id=device,
            device_id_type=MESH,
        )
        copy.start()
        pending.append(copy)
        return copy

    def swap(source, target, at, device):
        return remote(source, target, swap_sems, at, device)

    def columns(w, index, start, size):
        begin = pl.multiple_of(index * (w.shape[1] // 2) + start, 128)
        return w.at[:, pl.ds(begin, size)]

    def rows_half(w, index):
        size = w.shape[0] // 2
        return w.at[pl.ds(pl.multiple_of(index * size, size), size), :]

    locals_started = []

    def local(source, target):
        copy = pltpu.make_async_copy(source, target, local_sems.at[len(locals_started)])
        copy.start()
        locals_started.append(copy)
        return copy

    own_now = []
    for kind, w in enumerate((query_weight, key_weight, value_weight)):
        for at in range(0, heads, 128):
            there = pl.ds(3 * at + 128 * kind, 128)
            own_now.append(local(columns(w, row, at, 128), qkv_w.at[pl.ds(0, half), there]))
    own_now.append(local(rows_half(output_weight, row), out_w.at[:, pl.ds(0, half)]))
    own_gate = local(columns(gate_weight, row, 0, quarter), pair_held.at[0])
    own_up = local(columns(up_weight, row, 0, quarter), pair_held.at[1])
    own_down = local(rows_half(down_weight, row), down_held)
    own_rows = local(dealt.at[:, dp], x_in.at[:, dp])
    others = [(jnp.int32(1), {"dp": lax.rem(dp + step, groups)}) for step in range(1, groups)]
    greet(*others, (jnp.int32(1), across), (jnp.int32(1), beside))

    def dealing(step, micro):
        target = lax.rem(dp + step, groups)
        return pltpu.make_async_remote_copy(
            src_ref=dealt.at[micro, target],
            dst_ref=x_in.at[micro, dp],
            send_sem=deal_sems.at[0, micro, step],
            recv_sem=deal_sems.at[1, micro, step],
            device_id={"dp": target},
            device_id_type=MESH,
        )

    for micro in range(MICRO):

        def send_rows(step, _):
            dealing(step, micro).start()
            return 0

        lax.fori_loop(1, groups, send_rows, 0)
    gains_own[0:1, :] = gain_first[...]
    gains_own[1:2, :] = gain_second[...]
    gain_c = swap(gains_own, gains_col, 13, beside)
    top_c = swap(top_block, top_col, 0, beside)
    weights_now = []
    for kind, w in enumerate((query_weight, key_weight, value_weight)):
        for at in range(0, heads, 128):
            there = qkv_w.at[pl.ds(half, half), pl.ds(3 * at + 128 * kind, 128)]
            weights_now.append(
                remote(columns(w, 1 - row, at, 128), there, weight_sems, len(weights_now), across)
            )
    weights_now.append(
        remote(
            rows_half(output_weight, 1 - row),
            out_w.at[:, pl.ds(half, half)],
            weight_sems,
            len(weights_now),
            across,
        )
    )
    weights_late = []
    for k, w in enumerate((gate_weight, up_weight)):
        there = pair_out.at[pl.ds(half, half), pl.ds(k * quarter, quarter)]
        weights_late.append(
            remote(
                columns(w, 1 - row, 0, quarter), there, weight_sems, len(weights_now) + k, across
            )
        )
    own_gate.wait()
    own_up.wait()
    store_gate = local(pair_held.at[0], pair_out.at[pl.ds(0, half), pl.ds(0, quarter)])
    store_up = local(pair_held.at[1], pair_out.at[pl.ds(0, half), pl.ds(quarter, quarter)])
    own_down.wait()
    store_down = local(down_held, down_out.at[:, pl.ds(0, half)])

    def half_of(own, came):
        return jnp.where(
            col == 0,
            jnp.concatenate([own, came], axis=1),
            jnp.concatenate([came, own], axis=1),
        )

    own_rows.wait()
    x_c = []
    for micro in range(MICRO):

        def take_rows(step, _):
            dealing(step, micro).wait_recv()
            return 0

        lax.fori_loop(1, groups, take_rows, 0)
        x_c.append(swap(x_in.at[micro], x_came.at[micro], 1 + micro, beside))
    gain_c.wait_recv()
    gains[...] = half_of(gains_own[...], gains_col[...])
    gain_r = swap(gains, gains_row, 14, across)
    top_c.wait_recv()

    def top_rows(rows):
        top_half[rows, :] = half_of(top_block[rows, :], top_col[rows, :])

    rows_loop(top_rows)
    results = [local(x_in, x_out), local(top_half, top_half_out)]
    top_x = swap(top_half, top_came, 3, partner)

    def micro_rows(micro):
        return pl.ds(micro * SL, SL)

    x_r = []
    for micro in range(MICRO):
        x_c[micro].wait_recv()
        own = x_in[micro].reshape(SL, block)
        came = x_came[micro].reshape(SL, block)
        x_half[micro_rows(micro), :] = half_of(own, came)
        rows = micro_rows(micro)
        x_r.append(swap(x_half.at[rows, :], x_other.at[rows, :], 4 + micro, across))
        if micro == 0:
            for copy in own_now:
                copy.wait()
            for copy in weights_now:
                copy.wait_recv()
    top_r = swap(top_half, top_row, 6, across)
    down_there = down_out.at[:, pl.ds(half, half)]
    down_r = remote(
        rows_half(down_weight, 1 - row), down_there, weight_sems, len(weights_now) + 2, across
    )
    store_qkv = local(qkv_w, qkv_out)
    store_out = local(out_w, out_out)

    lower = lax.broadcasted_iota(jnp.int32, (SL, SL), 1) <= lax.broadcasted_iota(
        jnp.int32, (SL, SL), 0
    )

    gain_r.wait_recv()

    def norm_rows(own_ref, other_ref, at, inverse_ref, out_ref, micro):
        def body(j, _):
            rows = pl.ds(pl.multiple_of(micro * SL + j * 64, 64), 64)
            own = own_ref[rows, :].astype(F32)
            other = other_ref[rows, :].astype(F32)
            total = jnp.sum(own * own, axis=1, keepdims=True)
            total = total + jnp.sum(other * other, axis=1, keepdims=True)
            inverse = lax.rsqrt(total / D + EPSILON)
            inverse_ref[rows, :] = inverse
            out_ref[rows, :half] = (own * inverse * gains[at : at + 1, :]).astype(BF16)
            out_ref[rows, half:] = (other * inverse * gains_row[at : at + 1, :]).astype(BF16)
            return 0

        lax.fori_loop(0, SL // 64, body, 0)

    sum_c = []
    for micro in range(MICRO):
        rows = micro_rows(micro)
        x_r[micro].wait_recv()
        norm_rows(x_half, x_other, 0, inverse_first, normed_first, micro)
        allowed = lower & (key_live[micro : micro + 1, :] > 0.5)

        def attend(at, _):
            there = pl.multiple_of(at * 768, 128)
            qkv = mm(normed_first[rows, :], qkv_w[:, pl.ds(there, 768)])
            for pair in range(2):
                qr, kr, vr, out = head_outputs(
                    qkv[:, pair * 384 : pair * 384 + 384], allowed, cos[...], first[...], second[...]
                )
                begin = there + pair * 384
                for kind, value in enumerate((qr, kr, vr)):
                    turned[rows, pl.ds(pl.multiple_of(begin + kind * 128, 128), 128)] = value
                mixed[rows, pl.ds(pl.multiple_of(at * 256 + pair * 128, 128), 128)] = out
            return 0

        lax.fori_loop(0, heads // 256, attend, 0)
        sent[rows, :] = mm(mixed[rows, :], out_w[:, half:]).astype(BF16)
        sum_r = swap(sent.at[rows, :], row_came.at[rows, :], 7 + micro, across)
        kept[...] = mm(mixed[rows, :], out_w[:, :half])
        sum_r.wait_recv()
        summed[rows, :] = (kept[...] + row_came[rows, :].astype(F32)).astype(BF16)
        sum_c.append(swap(summed.at[rows, :], col_came.at[rows, :], 9 + micro, beside))

    results.append(local(turned, turned_out))

    def by_x(source, mine, theirs, rows, width):
        value = source[rows, : 2 * mine.shape[1]]
        even = [value[:, at : at + width] for at in range(0, value.shape[1], 2 * width)]
        odd = [value[:, at : at + width] for at in range(width, value.shape[1], 2 * width)]
        even, odd = jnp.concatenate(even, axis=1), jnp.concatenate(odd, axis=1)
        mine[rows, :] = jnp.where(x == 0, even, odd)
        theirs[rows, :] = jnp.where(x == 0, odd, even)

    top_r.wait_recv()
    store_down.wait()
    down_r.wait_recv()

    def da_body(j, slot):
        total = mm_nt(top_half[...], tiles[slot, :, :half])
        total = total + mm_nt(top_row[...], tiles[slot, :, half:])
        hidden_grad[:, pl.ds(pl.multiple_of(j * 256, 256), 256)] = total

    stream(
        lambda j: [down_out.at[pl.ds(pl.multiple_of(j * 256, 256), 256), :]],
        lambda slot: [tiles.at[slot]],
        tile_sems,
        quarter // 256,
        da_body,
    )

    results.append(local(hidden_grad, hidden_grad_out))

    def select_rows(rows):
        by_x(normed_first, first_mine, first_theirs, rows, half // groups)
        by_x(mixed, mixed_mine, mixed_theirs, rows, 2 * heads // groups)

    rows_loop(select_rows)
    results.append(local(first_mine, first_mine_out))
    results.append(local(first_theirs, first_theirs_out))
    results.append(local(mixed_mine, mixed_mine_out))
    results.append(local(mixed_theirs, mixed_theirs_out))

    low_r = []
    for micro in range(MICRO):
        rows = micro_rows(micro)
        sum_c[micro].wait_recv()

        def middle_rows(j, _):
            here = pl.ds(pl.multiple_of(micro * SL + j * 64, 64), 64)
            total = x_half[here, :].astype(F32) + (
                summed[here, :].astype(F32) + col_came[here, :].astype(F32)
            )
            middle[here, :] = total
            low[here, :] = total.astype(BF16)
            return 0

        lax.fori_loop(0, SL // 64, middle_rows, 0)
        results.append(local(middle.at[rows, :], middle_out.at[rows, :]))
        low_r.append(swap(low.at[rows, :], low_came.at[rows, :], 11 + micro, across))
        low_r[micro].wait_recv()
        norm_rows(low, low_came, 1, inverse_second, normed_second, micro)
        results.append(local(normed_second.at[rows, :], normed_second_out.at[rows, :]))

        def second_rows(j, _):
            here = pl.ds(pl.multiple_of(micro * SL + j * 64, 64), 64)
            by_x(normed_second, second_mine, second_theirs, here, half // groups)
            return 0

        lax.fori_loop(0, SL // 64, second_rows, 0)
        results.append(local(second_mine.at[rows, :], second_mine_out.at[rows, :]))
        results.append(local(second_theirs.at[rows, :], second_theirs_out.at[rows, :]))

    top_x.wait_recv()
    results.append(local(top_came, top_came_out))
    for copy in weights_late:
        copy.wait_recv()
    for copy in pending:
        copy.wait_send()

    def close(step, _):
        for micro in range(MICRO):
            dealing(step, micro).wait_send()
        return 0

    lax.fori_loop(1, groups, close, 0)
    for copy in [store_gate, store_up, store_qkv, store_out] + results:
        copy.wait()


def front(line, identity, *values):
    dealt, query_weight, gate_weight = values[0], values[8], values[12]
    groups = dealt.shape[1]
    half, block = D // 2, D // 4
    heads = query_weight.shape[1] // 2
    quarter = gate_weight.shape[1] // 2
    vmem = pl.BlockSpec(memory_space=pltpu.VMEM)
    anywhere = pl.BlockSpec(memory_space=pl.ANY)

    def array(*shape, dtype=BF16):
        return jax.ShapeDtypeStruct(shape, dtype)

    def buffer(*shape, dtype=BF16):
        return pltpu.VMEM(shape, dtype)

    sem = pltpu.SemaphoreType.DMA
    now = 3 * (heads // 128) + 1
    held = [
        (dealt.shape, BF16),
        ((ROWS, half), BF16),
        ((ROWS, half), BF16),
        ((ROWS, block), BF16),
        ((ROWS, block), BF16),
        ((ROWS, 3 * heads), BF16),
        ((ROWS, heads // 2), BF16),
        ((ROWS, heads // 2), BF16),
        ((ROWS, half), F32),
        ((ROWS, block), BF16),
        ((ROWS, block), BF16),
        ((ROWS, D), BF16),
        ((ROWS, quarter), F32),
    ]
    normed_first, mixed = ((ROWS, D), BF16), ((ROWS, heads), BF16)
    inside = held[:3] + [normed_first] + held[3:6] + [mixed] + held[6:]
    return pl.pallas_call(
        front_kernel,
        out_shape=[
            array(D, 2 * quarter),
            array(quarter, D),
            array(D, 3 * heads),
            array(heads, D),
            *[array(*shape, dtype=kind) for shape, kind in held],
            array(ROWS, 1, dtype=F32),
            array(ROWS, 1, dtype=F32),
            array(2, half, dtype=F32),
        ],
        in_specs=[vmem] * 8 + [anywhere] * 7,
        out_specs=[anywhere] * (4 + len(held)) + [vmem] * 3,
        scratch_shapes=[
            *[buffer(*shape, dtype=kind) for shape, kind in inside],
            buffer(D, 3 * heads),
            buffer(heads, D),
            buffer(2, block, dtype=F32),
            buffer(2, block, dtype=F32),
            buffer(2, half, dtype=F32),
            buffer(2, half, quarter),
            buffer(quarter, half),
            buffer(2, 256, D),
            buffer(*dealt.shape),
            buffer(ROWS, half),
            buffer(ROWS, half),
            buffer(ROWS, block),
            buffer(ROWS, half),
            buffer(ROWS, half),
            buffer(ROWS, half),
            buffer(SL, half, dtype=F32),
            buffer(ROWS, half),
            buffer(ROWS, half),
            buffer(ROWS, half),
            buffer(ROWS, half),
            sem((2, MICRO, groups)),
            sem((2, now + 3)),
            sem((now + 28,)),
            sem((2, 15)),
            sem((2, 2)),
        ],
        compiler_params=pltpu.CompilerParams(
            collective_id=identity, has_side_effects=True, vmem_limit_bytes=67043328
        ),
        cost_estimate=FREE,
    )(*values)


def chain_kernel(
    line,
    normed,
    hidden_grad,
    second_mine,
    second_theirs,
    top_half,
    top_came,
    pair_w,
    down_w,
    qkv_w,
    out_w,
    turned,
    middle,
    inverse_first,
    inverse_second,
    gain_second,
    gain_first,
    x_own,
    key_live,
    cos,
    first,
    second,
    down_out,
    gate_grads_out,
    second_came_out,
    up_grad_out,
    up_row,
    dqkv_out,
    dqkv_row,
    branch_out,
    both_out,
    pieces_out,
    gate_row,
    gate_came,
    gate_came_row,
    gate_grads,
    second_came,
    up_grad,
    dqkv,
    branch,
    hidden,
    gate_grad,
    tiles,
    tall_tiles,
    da_tiles,
    kept,
    sent,
    row_came,
    summed,
    col_came,
    block_sent,
    block_came,
    hidden_row,
    hidden_came,
    hidden_came_row,
    branch_row,
    dots,
    down_grads,
    down_z,
    middle_own,
    layer_own,
    first_own,
    mixed_grad,
    turned_left,
    feed_sum,
    attention_sum,
    swap_sems,
    piece_sems,
    tile_sems,
    down_sems,
    copy_sems,
):
    dp, row, col = lax.axis_index("dp"), lax.axis_index("row"), lax.axis_index("col")
    x = lax.rem(dp, 2)
    partner = {"dp": dp + 1 - 2 * x}
    across = {"row": 1 - row}
    beside = {"col": 1 - col}
    down_line = ZLine(line, down_grads, down_out, None, down_z, down_sems, 4, True)
    half = D // 2
    block = D // 4
    quarter = normed.shape[1]
    pending, results = [], []

    def result(source, target):
        copy = pltpu.make_async_copy(source, target, copy_sems.at[2 + len(results)])
        copy.start()
        results.append(copy)

    def swap(source, target, at, device, sems=swap_sems):
        copy = pltpu.make_async_remote_copy(
            src_ref=source,
            dst_ref=target,
            send_sem=sems.at[0, at],
            recv_sem=sems.at[1, at],
            device_id=device,
            device_id_type=MESH,
        )
        return copy

    def begin(copy):
        copy.start()
        pending.append(copy)
        return copy

    greet(
        *down_line.moves(),
        (jnp.int32(1), partner),
        (jnp.int32(1), across),
        (jnp.int32(1), beside),
    )

    per = line // 2
    width = quarter // line
    tile = min(width, 256)
    each = width // tile

    def hidden_part(index, at):
        return hidden.at[:, pl.ds(pl.multiple_of((2 * at + index) * width, width), width)]

    def feed_columns(j, shift=0):
        piece = j // each
        index = jnp.where(piece < per, 1 - x, x)
        begin = (2 * lax.rem(piece, per) + index) * width + lax.rem(j, each) * tile
        return pl.ds(pl.multiple_of(shift + begin, tile), tile)

    to_x = [
        swap(
            hidden_part(1 - x, at),
            hidden_came.at[:, pl.ds(at * width, width)],
            at,
            partner,
            piece_sems,
        )
        for at in range(per)
    ]
    pending.extend(to_x)

    def feed_body(j, slot):
        gate = mm(normed[...], tall_tiles[slot, 0, :, :tile])
        up = mm(normed[...], tall_tiles[slot, 1, :, :tile])
        da = da_tiles[slot, :, :tile]
        sigmoid = 1.0 / (1.0 + jnp.exp(-gate))
        swish = gate * sigmoid
        there = feed_columns(j)
        hidden[:, there] = (swish * up).astype(BF16)
        gate_grad[:, there] = (da * up * sigmoid * (1.0 + gate * (1.0 - sigmoid))).astype(BF16)
        up_grad[:, there] = (da * swish).astype(BF16)
        for at in range(per):

            @pl.when(j == (at + 1) * each - 1)
            def _():
                to_x[at].start()

    narrow_tile = pl.ds(0, tile)
    stream(
        lambda j: [
            pair_w.at[:, feed_columns(j)],
            pair_w.at[:, feed_columns(j, quarter)],
            hidden_grad.at[:, feed_columns(j)],
        ],
        lambda slot: [
            tall_tiles.at[slot, 0, :, narrow_tile],
            tall_tiles.at[slot, 1, :, narrow_tile],
            da_tiles.at[slot, :, narrow_tile],
        ],
        tile_sems,
        quarter // tile,
        feed_body,
    )
    to_row, on_row = [], []
    for at in range(per):
        there = pl.ds(at * width, width)
        to_row.append(
            begin(swap(hidden_part(x, at), hidden_row.at[:, there], per + at, across, piece_sems))
        )
    result(up_grad, up_grad_out)
    second_x = begin(swap(second_theirs, second_came, 0, partner))
    gate_x = begin(swap(gate_grad, gate_came, 1, partner))

    def nt_product(w, depth, start, body):
        stream(
            lambda j: [w.at[pl.ds(pl.multiple_of(start + j * 256, 256), 256), :]],
            lambda slot: [tiles.at[slot, :, pl.ds(0, depth)]],
            tile_sems,
            half // 256,
            body,
        )

    def columns_at(j, size=256):
        return pl.ds(pl.multiple_of(j * size, size), size)

    def pair_body(target, dtype):
        def body(j, slot):
            total = mm_nt(gate_grad[...], tiles[slot, :, :quarter])
            total = total + mm_nt(up_grad[...], tiles[slot, :, quarter:])
            target[:, columns_at(j)] = total.astype(dtype)

        return body

    nt_product(pair_w, 2 * quarter, half, pair_body(sent, BF16))
    pair_r = begin(swap(sent, row_came.at[0], 2, across))
    nt_product(pair_w, 2 * quarter, 0, pair_body(kept, F32))
    pair_r.wait_recv()

    def join_pair(rows):
        summed[rows, :] = (kept[rows, :] + row_came[0, rows, :].astype(F32)).astype(BF16)

    rows_loop(join_pair)
    pair_c = begin(swap(summed, col_came, 3, beside))
    gate_r = begin(swap(gate_grad, gate_row, 4, across))
    up_r = begin(swap(up_grad, up_row, 5, across))

    for copy in to_x:
        copy.wait_recv()
    for at in range(per):
        there = pl.ds(at * width, width)
        on_row.append(
            begin(
                swap(
                    hidden_came.at[:, there],
                    hidden_came_row.at[:, there],
                    2 * per + at,
                    across,
                    piece_sems,
                )
            )
        )

    def down_grad(part, left_of, came):
        def body(columns, _):
            for at in range(per):
                there = pl.ds(at * width, width)
                total = mm_tn(left_of(at)[...], top_half[:, columns])
                total = total + mm_tn(came[:, there], top_came[:, columns])
                down_grads[pl.ds((part * per + at) * width, width), columns] = total.astype(BF16)

        tiles_loop(half, 512, body)

    down_grad(0, lambda at: hidden_part(x, at), hidden_came)
    for copy in to_row + on_row:
        copy.wait_recv()
    down_grad(1, lambda at: hidden_row.at[:, pl.ds(at * width, width)], hidden_came_row)
    down_line.run(0, 1)

    def down_product(start, target, dtype):
        def body(j, slot):
            target[:, columns_at(j)] = mm(hidden[...], tall_tiles[slot, 0]).astype(dtype)

        stream(
            lambda j: [down_w.at[:, pl.ds(pl.multiple_of(start + j * 256, 256), 256)]],
            lambda slot: [tall_tiles.at[slot, 0]],
            tile_sems,
            half // 256,
            body,
        )

    pair_r.wait_send()
    pending[:] = [copy for copy in pending if copy is not pair_r]
    down_product(half, sent, BF16)
    layer_r = begin(swap(sent, row_came.at[1], 7, across))
    down_product(0, kept, F32)
    layer_r.wait_recv()

    def mine_of(value):
        return jnp.where(col == 0, value[:, :block], value[:, block:])

    def theirs_of(value):
        return jnp.where(col == 0, value[:, block:], value[:, :block])

    def join_layer(rows):
        total = kept[rows, :] + row_came[1, rows, :].astype(F32)
        layer_own[rows, :] = mine_of(total)
        block_sent[0, rows, :] = theirs_of(total).astype(BF16)

    rows_loop(join_layer)
    layer_c = begin(swap(block_sent.at[0], block_came.at[0], 8, beside))
    middle_in = pltpu.make_async_copy(middle, kept, copy_sems.at[0])
    middle_in.start()

    middle_in.wait()
    pair_c.wait_recv()
    feed_sum[...] = jnp.zeros_like(feed_sum)

    def second_grads(rows):
        grad = summed[rows, :].astype(F32) + col_came[rows, :].astype(F32)
        return grad, grad * gain_second[1:2, :]

    def norm_first_pass(rows):
        grad, scaled = second_grads(rows)
        held = kept[rows, :]
        feed_sum[...] += jnp.sum(grad * held * inverse_second[rows, :], axis=0, keepdims=True)
        total = jnp.sum(scaled * held, axis=1, keepdims=True)
        dots[0, rows, :] = jnp.broadcast_to(total, (total.shape[0], 128))

    rows_loop(norm_first_pass)
    dot_r = begin(swap(dots.at[0], dots.at[1], 9, across))
    dot_r.wait_recv()

    def norm_second_pass(rows):
        _, scaled = second_grads(rows)
        held = kept[rows, :]
        inverse = inverse_second[rows, :]
        dot = dots[0, rows, :1] + dots[1, rows, :1]
        grad = (
            top_half[rows, :].astype(F32) + scaled * inverse - held * (inverse**3 * dot / D)
        )
        branch[rows, :] = grad.astype(BF16)
        middle_own[rows, :] = mine_of(grad)
        layer_own[rows, :] += mine_of(held)

    rows_loop(norm_second_pass)
    result(branch, branch_out)
    branch_r = begin(swap(branch, branch_row, 10, across))
    branch_r.wait_recv()

    down_line.run(1, 2)

    def mixed_body(j, slot):
        total = mm_nt(branch[...], tiles[slot, :, :half])
        total = total + mm_nt(branch_row[...], tiles[slot, :, half:D])
        mixed_grad[:, columns_at(j)] = total.astype(BF16)

    stream(
        lambda j: [out_w.at[pl.ds(pl.multiple_of(j * 256, 256), 256), :]],
        lambda slot: [tiles.at[slot, :, pl.ds(0, D)]],
        tile_sems,
        out_w.shape[0] // 256,
        mixed_body,
    )
    pairs = turned.shape[1] // 384
    lower = lax.broadcasted_iota(jnp.int32, (SL, SL), 1) <= lax.broadcasted_iota(
        jnp.int32, (SL, SL), 0
    )

    def attend(at, _):
        micro, pair = at // pairs, lax.rem(at, pairs)
        rows = pl.ds(pl.multiple_of(micro * SL, SL), SL)

        def part(kind):
            return pl.ds(pl.multiple_of(pair * 384 + kind * 128, 128), 128)

        allowed = lower & (key_live[pl.ds(micro, 1), :] > 0.5)
        dq, dk, dv = head_grads(
            turned[rows, part(0)],
            turned[rows, part(1)],
            turned[rows, part(2)],
            mixed_grad[rows, pl.ds(pl.multiple_of(pair * 128, 128), 128)],
            allowed,
            cos[...],
            first[...],
            second[...],
        )
        dqkv[rows, part(0)] = dq
        dqkv[rows, part(1)] = dk
        dqkv[rows, part(2)] = dv
        return 0

    lax.fori_loop(0, MICRO * pairs, attend, 0)
    result(dqkv, dqkv_out)

    def first_body(target, dtype):
        def body(j, slot):
            total = mm_nt(dqkv[...], tiles[slot, :, : dqkv.shape[1]])
            target[:, columns_at(j)] = total.astype(dtype)

        return body

    layer_r.wait_send()
    pending[:] = [copy for copy in pending if copy is not layer_r]
    nt_product(qkv_w, dqkv.shape[1], half, first_body(sent, BF16))
    first_r = begin(swap(sent, row_came.at[2], 11, across))
    dqkv_r = begin(swap(dqkv, dqkv_row, 12, across))
    nt_product(qkv_w, dqkv.shape[1], 0, first_body(kept, F32))
    down_line.run(2, line - 1)
    first_r.wait_recv()

    def join_first(rows):
        total = kept[rows, :] + row_came[2, rows, :].astype(F32)
        first_own[rows, :] = mine_of(total)
        block_sent[1, rows, :] = theirs_of(total).astype(BF16)

    rows_loop(join_first)
    first_c = begin(swap(block_sent.at[1], block_came.at[1], 13, beside))

    second_x.wait_recv()
    result(second_came, second_came_out)
    depth = second_mine.shape[0]
    turned_left[:, :depth] = second_mine[...].T
    turned_left[:, depth:] = second_came[...].T
    gate_x.wait_recv()
    gate_on = begin(swap(gate_came, gate_came_row, 14, across))

    def gate_part(shift, sources, values):
        def body(j, slot):
            mine, came = values(j, slot)
            total = mm(turned_left[:, :depth], mine) + mm(turned_left[:, depth:], came)
            there = pl.ds(pl.multiple_of(shift + j * 256, 256), 256)
            gate_grads[:, there] = total.astype(BF16)

        stream(
            lambda j: [source.at[:, columns_at(j)] for source in sources],
            lambda slot: [tall_tiles.at[slot, k, pl.ds(0, ROWS)] for k in range(len(sources))],
            tile_sems,
            quarter // 256,
            body,
        )

    gate_part(
        0,
        [gate_came],
        lambda j, slot: (gate_grad[:, columns_at(j)], tall_tiles[slot, 0, :ROWS]),
    )
    gate_r.wait_recv()
    gate_on.wait_recv()
    gate_part(
        quarter,
        [gate_row, gate_came_row],
        lambda j, slot: (tall_tiles[slot, 0, :ROWS], tall_tiles[slot, 1, :ROWS]),
    )

    result(gate_grads, gate_grads_out)
    layer_c.wait_recv()
    first_c.wait_recv()
    attention_sum[...] = jnp.zeros_like(attention_sum)

    def last_first_pass(rows):
        layer = layer_own[rows, :] + block_came[0, rows, :].astype(F32)
        both_out[rows, :] = layer.astype(BF16)
        grad = first_own[rows, :] + block_came[1, rows, :].astype(F32)
        first_own[rows, :] = grad
        held = x_own[rows, :].astype(F32)
        attention_sum[...] += jnp.sum(grad * held * inverse_first[rows, :], axis=0, keepdims=True)
        total = jnp.sum(grad * gain_first[...] * held, axis=1, keepdims=True)
        dots[2, rows, :] = jnp.broadcast_to(total, (total.shape[0], 128))

    rows_loop(last_first_pass)
    dot_r = begin(swap(dots.at[2], dots.at[3], 15, across))
    dot_r.wait_recv()

    def add_dots(rows):
        dots[4, rows, :] = dots[2, rows, :] + dots[3, rows, :]

    rows_loop(add_dots)
    dot_c = begin(swap(dots.at[4], dots.at[5], 16, beside))
    dot_c.wait_recv()

    def last_second_pass(rows):
        inverse = inverse_first[rows, :]
        dot = dots[4, rows, :1] + dots[5, rows, :1]
        scaled = first_own[rows, :] * gain_first[...]
        held = x_own[rows, :].astype(F32)
        grad = middle_own[rows, :] + scaled * inverse - held * (inverse**3 * dot / D)
        below = pl.ds(pl.multiple_of(rows.start + ROWS, rows.size), rows.size)
        both_out[below, :] = grad.astype(BF16)

    rows_loop(last_second_pass)
    pieces_out[0:1, :] = attention_sum[...]
    pieces_out[1:2, :] = mine_of(feed_sum[...])

    down_line.stage = kept.at[pl.ds(0, down_grads.shape[0] // line), :]
    down_line.finish()
    down_store = pltpu.make_async_copy(down_line.stage, down_out, copy_sems.at[1])
    down_store.start()
    for copy in (up_r, dqkv_r):
        copy.wait_recv()
    for copy in pending:
        copy.wait_send()
    down_store.wait()
    for copy in results:
        copy.wait()


def chain(line, identity, *values):
    quarter = values[1].shape[1]
    narrow = values[2].shape[1]
    qkv_width = values[10].shape[1]
    half, block = D // 2, D // 4
    rows = quarter // 2
    vmem = pl.BlockSpec(memory_space=pltpu.VMEM)
    anywhere = pl.BlockSpec(memory_space=pl.ANY)
    outside = {1, 3, 6, 7, 8, 9, 11}

    def array(*shape, dtype=BF16):
        return jax.ShapeDtypeStruct(shape, dtype)

    def buffer(*shape, dtype=BF16):
        return pltpu.VMEM(shape, dtype)

    outs = [
        (array(2 * rows // line, half, dtype=F32), anywhere),
        (array(narrow, 2 * quarter), anywhere),
        (array(ROWS, narrow), anywhere),
        (array(ROWS, quarter), anywhere),
        (array(ROWS, quarter), anywhere),
        (array(ROWS, qkv_width), anywhere),
        (array(ROWS, qkv_width), anywhere),
        (array(ROWS, half), anywhere),
        (array(2 * ROWS, block), vmem),
        (array(2, block, dtype=F32), vmem),
        (array(ROWS, quarter), anywhere),
        (array(ROWS, quarter), anywhere),
        (array(ROWS, quarter), anywhere),
    ]
    sem = pltpu.SemaphoreType.DMA
    return pl.pallas_call(
        lambda *refs: chain_kernel(line, *refs),
        out_shape=[shape for shape, _ in outs],
        in_specs=[anywhere if k in outside else vmem for k in range(len(values))],
        out_specs=[place for _, place in outs],
        scratch_shapes=[
            buffer(narrow, 2 * quarter),
            buffer(ROWS, narrow),
            buffer(ROWS, quarter),
            buffer(ROWS, qkv_width),
            buffer(ROWS, half),
            buffer(ROWS, quarter),
            buffer(ROWS, quarter),
            buffer(2, 256, 2 * quarter),
            buffer(2, 2, quarter, 256),
            buffer(2, ROWS, 256, dtype=F32),
            buffer(ROWS, half, dtype=F32),
            buffer(ROWS, half),
            buffer(3, ROWS, half),
            buffer(ROWS, half),
            buffer(ROWS, half),
            buffer(2, ROWS, block),
            buffer(2, ROWS, block),
            buffer(ROWS, rows),
            buffer(ROWS, rows),
            buffer(ROWS, rows),
            buffer(ROWS, half),
            buffer(6, ROWS, 128, dtype=F32),
            buffer(2 * rows, half),
            buffer(2, line - 1, 2 * rows // line, half),
            buffer(ROWS, block, dtype=F32),
            buffer(ROWS, block, dtype=F32),
            buffer(ROWS, block, dtype=F32),
            buffer(ROWS, qkv_width // 3),
            buffer(narrow, 2 * ROWS),
            buffer(1, half, dtype=F32),
            buffer(1, block, dtype=F32),
            sem((2, 17)),
            sem((2, 3 * (line // 2))),
            sem((2, 3)),
            sem((2, 2, line - 1, 4)),
            sem((7,)),
        ],
        compiler_params=pltpu.CompilerParams(
            collective_id=identity, has_side_effects=True, vmem_limit_bytes=67043328
        ),
        cost_estimate=FREE,
    )(*values)


def tail_sums(line, identity, *values):
    (gate_grads, up, _, _, _, dqkv, _, _, _, branch) = values[:10]
    rows = gate_grads.shape[0]
    side_rows = 2 * values[10].shape[1]
    tokens = up.shape[0]
    widths = (gate_grads.shape[1], gate_grads.shape[1], 2 * dqkv.shape[1], branch.shape[1])
    heights = (rows, rows, rows, side_rows)
    pieces = (4, 4, 3, 1)
    sizes = [(h // line, w) for h, w in zip(heights, widths)]
    vmem = pl.BlockSpec(memory_space=pltpu.VMEM)
    anywhere = pl.BlockSpec(memory_space=pl.ANY)
    both, gains = values[12:]
    height = sizes[0][0]
    gain_steps = both.shape[1].bit_length() - 1

    def buffer(*shape):
        return pltpu.VMEM(shape, BF16)

    def array(*shape):
        return jax.ShapeDtypeStruct(shape, F32)

    return pl.pallas_call(
        lambda *refs: tail_kernel(line, *refs),
        out_shape=[
            array(*sizes[0]),
            array(*sizes[1]),
            array(height, widths[2] // 3),
            array(height, widths[2] // 3),
            array(height, widths[2] // 3),
            array(*sizes[3]),
            jax.ShapeDtypeStruct(both.shape, BF16),
            array(*gains.shape),
        ],
        in_specs=[vmem] + [anywhere] * 12 + [vmem],
        out_specs=[anywhere] * 7 + [vmem],
        scratch_shapes=[buffer(*values[at].shape) for at in (1, 2, 3, 4, 5, 6, 7, 9, 10)]
        + [buffer(2, line - 1, *size) for size in sizes]
        + [buffer(h, w) for h, w in zip(heights[1:], widths[1:])]
        + [buffer(*up.shape)] * 2
        + [buffer(*dqkv.shape)] * 2
        + [buffer(*branch.shape), buffer(*values[7].shape)]
        + [buffer(*values[10].shape)] * 3
        + [buffer(rows, 2 * tokens)]
        + [pltpu.VMEM(size, F32) for size in sizes]
        + [pltpu.SemaphoreType.DMA((2, 2, line - 1, count)) for count in pieces]
        + [pltpu.SemaphoreType.DMA((2, 9)), pltpu.SemaphoreType.DMA((6 + widths[2] // 128,))]
        + [pltpu.VMEM((2, gain_steps, *gains.shape), F32)]
        + [
            pltpu.SemaphoreType.DMA((2, both.shape[1])),
            pltpu.SemaphoreType.DMA((2, gain_steps)),
            pltpu.SemaphoreType.DMA((9,)),
        ],
        compiler_params=pltpu.CompilerParams(
            collective_id=identity, has_side_effects=True, vmem_limit_bytes=67043328
        ),
        cost_estimate=FREE,
    )(*values)


def finish_kernel(count, order_ref, back_ref, gains_ref, *refs):
    sums, rest = refs[:count], refs[count:]
    layer_ref, grad_ref, attention_ref, feed_ref = rest[:4]
    outs, held, sems = rest[4 : 4 + count], rest[4 + count : 4 + 2 * count], rest[4 + 2 * count]
    groups = back_ref.shape[1]
    loads = [pltpu.make_async_copy(sums[k], held[k], sems.at[0, k]) for k in range(count)]
    stores = [pltpu.make_async_copy(held[k], outs[k], sems.at[1, k]) for k in range(count)]
    for copy in loads:
        copy.start()

    def one(at, _):
        micro, slot = at // groups, lax.rem(at, groups)
        place = order_ref[micro, slot]
        layer_ref[micro, place] = back_ref[micro, slot]
        grad_ref[micro, place] = back_ref[MICRO + micro, slot]
        return 0

    lax.fori_loop(0, MICRO * groups, one, 0)
    size = attention_ref.shape[1]
    width = gains_ref.shape[1]
    at = lax.broadcasted_iota(jnp.int32, (width, size), 0)
    wanted = lax.broadcasted_iota(jnp.int32, (width, size), 1) + lax.axis_index("dp") * size
    picked = jnp.dot(
        gains_ref[...],
        jnp.where(at == wanted, 1.0, 0.0),
        preferred_element_type=F32,
        precision=lax.Precision.HIGHEST,
    )
    attention_ref[...] = picked[0:1, :]
    feed_ref[...] = picked[1:2, :]
    for load, store in zip(loads, stores):
        load.wait()
        store.start()
    for store in stores:
        store.wait()


def finish(order, back, gains, *sums):
    vmem = pl.BlockSpec(memory_space=pltpu.VMEM)
    anywhere = pl.BlockSpec(memory_space=pl.ANY)
    rows = jax.ShapeDtypeStruct((MICRO,) + back.shape[1:], BF16)
    part = jax.ShapeDtypeStruct((1, gains.shape[1] // back.shape[1]), F32)
    count = len(sums)
    return pl.pallas_call(
        lambda *refs: finish_kernel(count, *refs),
        out_shape=[rows, rows, part, part] + [jax.ShapeDtypeStruct(v.shape, F32) for v in sums],
        in_specs=[pl.BlockSpec(memory_space=pltpu.SMEM), vmem, vmem] + [anywhere] * count,
        out_specs=[vmem] * 4 + [anywhere] * count,
        scratch_shapes=[pltpu.VMEM(v.shape, F32) for v in sums]
        + [pltpu.SemaphoreType.DMA((2, count))],
        cost_estimate=FREE,
    )(order, back, gains, *sums)


def per_device(
    tokens,
    lengths,
    deal_order,
    attention_gain,
    query_weight,
    key_weight,
    value_weight,
    output_weight,
    feed_gain,
    gate_weight,
    up_weight,
    down_weight,
    cotangent,
):
    groups = lax.axis_size("dp")
    line = groups // 2
    dp = lax.axis_index("dp")
    row = lax.axis_index("row")
    col = lax.axis_index("col")
    z, x = dp // 2, dp % 2
    half = D // 2
    block = D // 4

    def over_row(v):
        return lax.ppermute(v, "row", SWAP)

    def over_col(v):
        return lax.ppermute(v, "col", SWAP)

    def ordered(own, other, index, axis=-1):
        return jnp.where(
            index == 0,
            jnp.concatenate([own, other], axis=axis),
            jnp.concatenate([other, own], axis=axis),
        )

    def x_parts(v, width):
        even = jnp.concatenate(
            [v[:, s : s + width] for s in range(0, v.shape[1], 2 * width)], axis=1
        )
        odd = jnp.concatenate(
            [v[:, s : s + width] for s in range(width, v.shape[1], 2 * width)], axis=1
        )
        return jnp.where(x == 0, even, odd), jnp.where(x == 0, odd, even)

    def plain(*values):
        return values

    dealt, top_block, key_live = prepare(deal_order, lengths, tokens, cotangent)
    tables = rope_tables()
    (
        pair_w,
        down_w,
        qkv_w,
        out_w,
        x_block,
        top_half,
        top_came,
        first_mine,
        first_theirs,
        turned,
        mixed_mine,
        mixed_theirs,
        middle,
        second_mine,
        second_theirs,
        normed_second,
        hidden_grad,
        inverse_first,
        inverse_second,
        gains_half,
    ) = front(
        line,
        0,
        dealt,
        top_block,
        attention_gain.reshape(1, block),
        feed_gain.reshape(1, block),
        key_live,
        *tables,
        query_weight,
        key_weight,
        value_weight,
        output_weight,
        gate_weight,
        up_weight,
        down_weight,
    )
    x_block = x_block.reshape(ROWS, block)
    narrow = half // groups
    (
        down_sum,
        gate_grads,
        second_came,
        up_grad,
        up_row,
        dqkv,
        dqkv_row,
        branch,
        both,
        pieces,
        _,
        _,
        _,
    ) = chain(
        line,
        4,
        *plain(
            normed_second,
            hidden_grad,
            second_mine,
            second_theirs,
            top_half,
            top_came,
            pair_w,
            down_w,
            qkv_w,
            out_w,
            turned,
            middle,
            inverse_first,
            inverse_second,
            gains_half,
            attention_gain.reshape(1, block),
            x_block,
            key_live,
            *tables,
        ),
    )

    gate_sum, up_sum, query_sum, key_sum, value_sum, output_sum, back, gain_sums = tail_sums(
        line,
        3,
        *plain(
            gate_grads,
            up_grad,
            up_row,
            second_mine,
            second_came,
            dqkv,
            dqkv_row,
            first_mine,
            first_theirs,
            branch,
            mixed_mine,
            mixed_theirs,
            both.reshape(2 * MICRO, groups, SL // groups, block),
            pieces,
        ),
    )
    (
        layer_output,
        tokens_grad,
        attention_sum,
        feed_sum,
        down_sum,
        gate_sum,
        up_sum,
        query_sum,
        key_sum,
        value_sum,
        output_sum,
    ) = finish(
        deal_order,
        back,
        gain_sums,
        down_sum,
        gate_sum,
        up_sum,
        query_sum,
        key_sum,
        value_sum,
        output_sum,
    )
    return (
        layer_output,
        tokens_grad,
        attention_sum.reshape(-1),
        query_sum,
        key_sum,
        value_sum,
        output_sum,
        feed_sum.reshape(-1),
        gate_sum,
        up_sum,
        down_sum,
    )


def solution(mesh):
    in_specs = (
        P(None, None, "dp", ("row", "col")),
        P(),
        P(),
        P(("row", "col")),
        P("row", "col"),
        P("row", "col"),
        P("row", "col"),
        P("col", "row"),
        P(("row", "col")),
        P("row", "col"),
        P("row", "col"),
        P("col", "row"),
        P(None, "dp", None, ("row", "col")),
    )
    out_specs = (
        P(None, None, "dp", ("row", "col")),
        P(None, None, "dp", ("row", "col")),
        P(("row", "col", "dp")),
        P(("row", "dp"), "col"),
        P(("row", "dp"), "col"),
        P(("row", "dp"), "col"),
        P(("col", "dp"), "row"),
        P(("row", "col", "dp")),
        P(("row", "dp"), "col"),
        P(("row", "dp"), "col"),
        P(("col", "dp"), "row"),
    )
    return jax.shard_map(
        per_device, mesh=mesh, in_specs=in_specs, out_specs=out_specs, check_vma=False
    )
```

```python
import math

import jax
import jax.numpy as jnp
import numpy as np
from jax import lax
from jax.experimental import pallas as pl
from jax.experimental.pallas import tpu as pltpu
from jax.sharding import PartitionSpec as P

D = 2048
HEADS = 32
HEAD_DIM = 64
SL = 256
MICRO = 2
ROWS = MICRO * SL

EPSILON = 1e-05
ROPE_THETA = 130000.0
MASKED_SCORE = -1000000000.0
F32 = jnp.float32
BF16 = jnp.bfloat16
SWAP = [(0, 1), (1, 0)]


def mm(a, b):
    return jnp.dot(a, b, preferred_element_type=F32)


def mm_nt(a, b):
    return lax.dot_general(a, b, (((1,), (1,)), ((), ())), preferred_element_type=F32)


def mm_tn(a, b):
    return lax.dot_general(a, b, (((0,), (0,)), ((), ())), preferred_element_type=F32)


def rope_tables():
    half = HEAD_DIM // 2
    frequency = np.exp(np.arange(half, dtype=np.float32) * np.float32(-2.0 * math.log(ROPE_THETA) / HEAD_DIM))
    angles = np.arange(SL, dtype=np.float32)[:, None] * frequency[None, :]
    cosine, sine = np.cos(angles), np.sin(angles)
    zero = np.zeros_like(sine)
    table_cos = np.concatenate([cosine] * 4, axis=1)
    table_first = np.concatenate([sine, zero] * 2, axis=1)
    table_second = np.concatenate([zero, sine] * 2, axis=1)
    return jnp.asarray(table_cos), jnp.asarray(table_first), jnp.asarray(table_second)


def turn(v, cos, first, second):
    ahead = pltpu.roll(v, 128 - HEAD_DIM // 2, 1)
    behind = pltpu.roll(v, HEAD_DIM // 2, 1)
    return v * cos - ahead * first + behind * second


def turn_back(v, cos, first, second):
    ahead = pltpu.roll(v, 128 - HEAD_DIM // 2, 1)
    behind = pltpu.roll(v, HEAD_DIM // 2, 1)
    return v * cos + ahead * first - behind * second


def head_mask(head):
    lane = lax.broadcasted_iota(jnp.int32, (SL, 128), 1)
    return (lane // HEAD_DIM) == head


def softmax_of(q, k, allowed):
    scores = jnp.where(allowed, mm_nt(q, k), MASKED_SCORE)
    exps = jnp.exp(scores - jnp.max(scores, axis=1, keepdims=True))
    return exps * (1.0 / jnp.sum(exps, axis=1, keepdims=True))


def scaled_down(q):
    return (q.astype(F32) * HEAD_DIM ** (-0.5)).astype(BF16)


BLOCKS = ((slice(0, SL), SL),)


FREE = pl.CostEstimate(flops=0, bytes_accessed=0, transcendentals=0)


def whole(shape):
    return pl.BlockSpec(shape, lambda *at: (0,) * len(shape), pipeline_mode=pl.Buffered(1))


def head_outputs(qkv, allowed, cos, first, second):
    qr = turn(qkv[:, :128], cos, first, second).astype(BF16)
    kr = turn(qkv[:, 128:256], cos, first, second).astype(BF16)
    vr = qkv[:, 256:].astype(BF16)
    zero = jnp.zeros_like(vr)
    outs = [jnp.zeros((SL, 128), F32)]
    scaled = scaled_down(qr)
    for head in range(2):
        mask = head_mask(head)
        q_own = jnp.where(mask, scaled, zero)
        v_own = jnp.where(mask, vr, zero)
        for at, (rows, keys) in enumerate(BLOCKS):
            probs = softmax_of(q_own[rows], kr[:keys], allowed[rows, :keys]).astype(BF16)
            outs[at] = outs[at] + mm(probs, v_own[:keys])
    return qr, kr, vr, jnp.concatenate(outs, axis=0).astype(BF16)


def head_grads(qr, kr, vr, od, allowed, cos, first, second):
    dq = [jnp.zeros((SL, 128), F32)]
    dk = [jnp.zeros((SL, 128), F32)]
    dv = [jnp.zeros((SL, 128), F32)]
    zero = jnp.zeros_like(qr)
    scaled = scaled_down(qr)
    for head in range(2):
        mask = head_mask(head)
        q_own = jnp.where(mask, scaled, zero)
        k_own = jnp.where(mask, kr, zero)
        od_own = jnp.where(mask, od, zero)
        for at, (rows, keys) in enumerate(BLOCKS):
            probs = softmax_of(q_own[rows], kr[:keys], allowed[rows, :keys])
            d_probs = mm_nt(od_own[rows], vr[:keys])
            dv[at] = dv[at] + mm_tn(probs.astype(BF16), od_own[rows])
            inner = jnp.sum(probs * d_probs, axis=1, keepdims=True)
            d_scores = (probs * (d_probs - inner)).astype(BF16)
            dq[at] = dq[at] + mm(d_scores, k_own[:keys])
            dk[at] = dk[at] + mm_tn(d_scores, q_own[rows])

    def keys_sum(parts):
        return parts[0]

    dq = jnp.concatenate(dq, axis=0) * HEAD_DIM ** (-0.5)
    return (
        turn_back(dq, cos, first, second).astype(BF16),
        turn_back(keys_sum(dk), cos, first, second).astype(BF16),
        keys_sum(dv).astype(BF16),
    )


MESH = pl.DeviceIdType.MESH


def greet(*moves):
    barrier = pltpu.get_barrier_semaphore()
    total = 0
    for count, target in moves:
        total = total + count

        @pl.when(count > 0)
        def _():
            pl.semaphore_signal(barrier, inc=1, device_id=target, device_id_type=MESH)

    pl.semaphore_wait(barrier, total)


class ZLine:
    def __init__(self, line, grads, out, stage, came, sems, count, sided):
        self.line, self.grads, self.out, self.stage = line, grads, out, stage
        self.came, self.sems, self.sided = came, sems, sided
        width = grads.shape[1] // count
        self.pieces = [(k, pl.ds(k * width, width)) for k in range(count)]
        self.dp, self.row = lax.axis_index("dp"), lax.axis_index("row")
        self.z = self.dp // 2
        self.last = line - 1
        self.ways = ((0, self.z, 2), (1, self.last - self.z, -2))

    def rows_of(self, dest):
        size = self.grads.shape[0] // self.line
        if self.sided:
            dest = lax.rem(dest + self.line - self.row * (self.line // 2), self.line)
        return pl.ds(pl.multiple_of(dest * size, size), size)

    def copy(self, source, way, step, slot, piece, columns):
        return pltpu.make_async_remote_copy(
            src_ref=source,
            dst_ref=self.came.at[way, slot, :, columns],
            send_sem=self.sems.at[0, way, slot, piece],
            recv_sem=self.sems.at[1, way, slot, piece],
            device_id={"dp": self.dp + step},
            device_id_type=MESH,
        )

    def arrived(self, way, step, slot, piece, columns):
        held = self.came.at[way, slot, :, columns]
        self.copy(held, way, step, slot, piece, columns).wait_recv()
        return held

    def run(self, start, stop):
        def one_step(slot, _):
            for piece, columns in self.pieces:
                for way, place, step in self.ways:
                    far = self.last - slot + place
                    dest = far if step > 0 else self.last - far

                    @pl.when((place == 0) & (place < self.last))
                    def _():
                        source = self.grads.at[self.rows_of(dest), columns]
                        self.copy(source, way, step, slot, piece, columns).start()

                    @pl.when((place > 0) & (place <= slot))
                    def _():
                        held = self.arrived(way, step, slot - 1, piece, columns)

                        @pl.when(place < self.last)
                        def _():
                            held[...] = (
                                held[...].astype(F32)
                                + self.grads[self.rows_of(dest), columns].astype(F32)
                            ).astype(BF16)
                            self.copy(held, way, step, slot, piece, columns).start()

            return 0

        lax.fori_loop(start, stop, one_step, 0)

    def finish(self):
        own = self.rows_of(self.z)
        for piece, columns in self.pieces:
            self.stage[:, columns] = self.grads[own, columns].astype(F32)
            for way, place, step in self.ways:

                @pl.when(place > 0)
                def _():
                    held = self.arrived(way, step, self.last - 1, piece, columns)
                    self.stage[:, columns] += held[...].astype(F32)

        def settle(slot, _):
            for piece, columns in self.pieces:
                for way, place, step in self.ways:

                    @pl.when((place <= slot) & (place < self.last))
                    def _():
                        held = self.came.at[way, slot, :, columns]
                        self.copy(held, way, step, slot, piece, columns).wait_send()

            return 0

        lax.fori_loop(0, self.last, settle, 0)

    def moves(self):
        return (
            (jnp.minimum(self.z, 1), {"dp": self.dp - 2}),
            (jnp.minimum(self.last - self.z, 1), {"dp": self.dp + 2}),
        )


def tiles_loop(width, tile, body):
    def one(j, _):
        body(pl.ds(pl.multiple_of(j * tile, tile), tile), j * tile)
        return 0

    lax.fori_loop(0, width // tile, one, 0)


def tail_kernel(
    line,
    gate_grads,
    up_in,
    up_row_in,
    second_mine_in,
    second_came_in,
    dqkv_in,
    dqkv_row_in,
    first_mine_in,
    first_theirs,
    branch_in,
    mixed_mine_in,
    mixed_theirs,
    both,
    pieces,
    gate_out,
    up_out,
    query_out,
    key_out,
    value_out,
    output_out,
    back,
    gains_out,
    up,
    up_row,
    second_mine,
    second_came,
    dqkv,
    dqkv_row,
    first_mine,
    branch,
    mixed_mine,
    gate_z,
    up_z,
    qkv_z,
    output_z,
    up_grads,
    qkv_grads,
    output_grads,
    up_came,
    up_came_row,
    dqkv_came,
    dqkv_came_row,
    branch_came,
    first_came,
    mixed_came,
    mixed_row,
    mixed_came_row,
    turned_left,
    gate_stage,
    up_stage,
    qkv_stage,
    output_stage,
    gate_sems,
    up_sems,
    qkv_sems,
    output_sems,
    swap_sems,
    out_sems,
    gains,
    back_sems,
    gain_sems,
    fetch_sems,
):
    groups = 2 * line
    dp, row = lax.axis_index("dp"), lax.axis_index("row")
    partner = dp + 1 - 2 * lax.rem(dp, 2)
    gate_line = ZLine(line, gate_grads, gate_out, gate_stage, gate_z, gate_sems, 4, False)
    up_line = ZLine(line, up_grads, up_out, up_stage, up_z, up_sems, 4, False)
    qkv_line = ZLine(line, qkv_grads, None, qkv_stage, qkv_z, qkv_sems, 3, False)
    output_line = ZLine(line, output_grads, output_out, output_stage, output_z, output_sems, 1, True)

    def swap(source, target, at, device):
        return pltpu.make_async_remote_copy(
            src_ref=source,
            dst_ref=target,
            send_sem=swap_sems.at[0, at],
            recv_sem=swap_sems.at[1, at],
            device_id=device,
            device_id_type=MESH,
        )

    fetches = {}
    order = (
        (second_mine_in, second_mine),
        (second_came_in, second_came),
        (up_in, up),
        (up_row_in, up_row),
        (mixed_mine_in, mixed_mine),
        (branch_in, branch),
        (first_mine_in, first_mine),
        (dqkv_in, dqkv),
        (dqkv_row_in, dqkv_row),
    )
    for at, (source, target) in enumerate(order):
        fetches[at] = pltpu.make_async_copy(source, target, fetch_sems.at[at])
        fetches[at].start()
    up_x = swap(up_in, up_came, 0, {"dp": partner})
    branch_x = swap(branch_in, branch_came, 1, {"dp": partner})
    dqkv_x = swap(dqkv_in, dqkv_came, 2, {"dp": partner})
    up_across = swap(up_came, up_came_row, 3, {"row": 1 - row})
    dqkv_across = swap(dqkv_came, dqkv_came_row, 4, {"row": 1 - row})
    first_x = swap(first_theirs, first_came, 5, {"dp": partner})
    mixed_x = swap(mixed_theirs, mixed_came, 6, {"dp": partner})
    mixed_r = swap(mixed_mine_in, mixed_row, 7, {"row": 1 - row})
    mixed_across = swap(mixed_came, mixed_came_row, 8, {"row": 1 - row})

    stores = []

    def store(source, target):
        copy = pltpu.make_async_copy(source, target, out_sems.at[len(stores)])
        copy.start()
        stores.append(copy)

    def store_wide(line_of):
        size = line_of.stage.shape[1] // 2
        for part in range(2):
            place = row if part == 0 else 1 - row
            there = pl.ds(pl.multiple_of(place * size, size), size)
            store(line_of.stage.at[:, pl.ds(part * size, size)], line_of.out.at[:, there])

    def store_qkv():
        heads = dqkv.shape[1] // 3
        for part in range(2):
            place = row if part == 0 else 1 - row
            for pair in range(heads // 128):
                for kind, out in enumerate((query_out, key_out, value_out)):
                    here = pl.ds(part * 3 * heads + pair * 384 + kind * 128, 128)
                    there = pl.ds(pl.multiple_of(place * heads + pair * 128, 128), 128)
                    store(qkv_stage.at[:, here], out.at[:, there])

    def returned(step):
        target = lax.rem(dp + step, groups)
        return pltpu.make_async_remote_copy(
            src_ref=both.at[:, target],
            dst_ref=back.at[:, dp],
            send_sem=back_sems.at[0, step],
            recv_sem=back_sems.at[1, step],
            device_id={"dp": target},
            device_id_type=MESH,
        )

    gain_steps = groups.bit_length() - 1

    def gain_copy(step):
        reach = 1 << step
        peer = dp + reach - 2 * reach * lax.rem(dp // reach, 2)
        return pltpu.make_async_remote_copy(
            src_ref=gains.at[0, step],
            dst_ref=gains.at[1, step],
            send_sem=gain_sems.at[0, step],
            recv_sem=gain_sems.at[1, step],
            device_id={"dp": peer},
            device_id_type=MESH,
        )

    def gain_step(step):
        if step >= gain_steps:
            return
        gain_copy(step).wait_recv()
        total = gains[0, step] + gains[1, step]
        if step + 1 == gain_steps:
            gains_out[...] = total
        else:
            gains[0, step + 1] = total
            gain_copy(step + 1).start()

    others = [(jnp.int32(1), {"dp": lax.rem(dp + step, groups)}) for step in range(1, groups)]
    greet(*others, (jnp.int32(1), {"row": 1 - row}))
    gains[0, 0] = pieces[...]
    gain_copy(0).start()
    gate_line.run(0, 1)
    up_x.start()
    mixed_x.start()
    branch_x.start()
    first_x.start()
    dqkv_x.start()
    mixed_r.start()

    def send_back(step, _):
        returned(step).start()
        return 0

    store(both.at[:, dp], back.at[:, dp])

    fetches[0].wait()
    fetches[1].wait()
    depth = second_mine.shape[0]
    turned_left[:, :depth] = second_mine[...].T
    turned_left[:, depth:] = second_came[...].T
    gate_line.run(1, 2)
    lax.fori_loop(1, groups, send_back, 0)

    def wide(target, shift, mine, came):
        def body(columns, start):
            total = mm(turned_left[:, :depth], mine[:, columns])
            total = total + mm(turned_left[:, depth:], came[:, columns])
            tile = total.shape[1]
            target[:, pl.ds(pl.multiple_of(shift + start, tile), tile)] = total.astype(BF16)

        tiles_loop(mine.shape[1], 512, body)

    up_x.wait_recv()
    up_across.start()
    gain_step(0)
    gate_line.run(2, line - 1)
    fetches[2].wait()
    fetches[3].wait()
    wide(up_grads, 0, up, up_came)
    up_across.wait_recv()
    wide(up_grads, up.shape[1], up_row, up_came_row)
    up_line.run(0, 1)
    gate_line.finish()
    store_wide(gate_line)

    mixed_x.wait_recv()
    mixed_across.start()
    branch_x.wait_recv()

    def side(start, mine, came):
        def body(columns, _):
            total = mm_tn(mine[...], branch[:, columns]) + mm_tn(came[...], branch_came[:, columns])
            output_grads[pl.ds(start, mine.shape[1]), columns] = total.astype(BF16)

        tiles_loop(branch.shape[1], 512, body)

    fetches[4].wait()
    fetches[5].wait()
    side(0, mixed_mine, mixed_came)
    mixed_r.wait_recv()
    mixed_across.wait_recv()
    side(mixed_mine.shape[1], mixed_row, mixed_came_row)
    output_line.run(0, 1)
    up_line.run(1, 2)
    gain_step(1)
    for at in (6, 7, 8):
        fetches[at].wait()
    first_x.wait_recv()
    turned_left[:, :depth] = first_mine[...].T
    turned_left[:, depth:] = first_came[...].T
    dqkv_x.wait_recv()
    dqkv_across.start()
    wide(qkv_grads, 0, dqkv, dqkv_came)
    dqkv_across.wait_recv()
    wide(qkv_grads, dqkv.shape[1], dqkv_row, dqkv_came_row)
    qkv_line.run(0, 1)
    output_line.run(1, 2)
    up_line.run(2, line - 1)
    qkv_line.run(1, 2)
    output_line.run(2, line - 1)
    for step in range(2, gain_steps):
        gain_step(step)
    up_line.finish()
    store_wide(up_line)
    qkv_line.run(2, line - 1)
    output_line.finish()
    store(output_stage, output_out)
    qkv_line.finish()
    store_qkv()

    def get_back(step, _):
        returned(step).wait()
        return 0

    lax.fori_loop(1, groups, get_back, 0)
    for step in range(gain_steps):
        gain_copy(step).wait_send()
    copies = (up_x, branch_x, dqkv_x, up_across, dqkv_across)
    for copy in copies + (first_x, mixed_x, mixed_r, mixed_across):
        copy.wait_send()
    for copy in stores:
        copy.wait()


def stream(source_of, slots_of, sems, count, body):
    def fetch(j, slot):
        return [
            pltpu.make_async_copy(source, target, sems.at[slot, k])
            for k, (source, target) in enumerate(zip(source_of(j), slots_of(slot)))
        ]

    for copy in fetch(0, 0):
        copy.start()

    def one(j, _):
        slot = lax.rem(j, 2)

        @pl.when(j + 1 < count)
        def _():
            for copy in fetch(j + 1, 1 - slot):
                copy.start()

        for copy in fetch(j, slot):
            copy.wait()
        body(j, slot)
        return 0

    lax.fori_loop(0, count, one, 0)


def rows_loop(body, size=64):
    def one(j, _):
        body(pl.ds(pl.multiple_of(j * size, size), size))
        return 0

    lax.fori_loop(0, ROWS // size, one, 0)


def prepare_kernel(order_ref, len_ref, tokens_ref, top_ref, dealt_ref, block_ref, live_ref):
    groups = tokens_ref.shape[1]
    dp = lax.axis_index("dp")

    def one(at, _):
        micro, slot = at // groups, lax.rem(at, groups)
        dealt_ref[micro, slot] = tokens_ref[micro, order_ref[micro, slot]]
        return 0

    lax.fori_loop(0, MICRO * groups, one, 0)
    for micro in range(MICRO):
        length = len_ref[micro, order_ref[micro, dp]]
        rows = lax.broadcasted_iota(jnp.int32, top_ref.shape[2:], 0)
        top = top_ref[micro, 0]
        top = jnp.where(rows < length, top.astype(F32), 0.0).astype(BF16)
        block_ref[micro * SL : micro * SL + SL, :] = top
        keys = lax.broadcasted_iota(jnp.int32, (1, SL), 1)
        live_ref[micro : micro + 1, :] = jnp.where(keys < length, 1.0, 0.0)


def prepare(order, lengths, tokens, cotangent):
    vmem = pl.BlockSpec(memory_space=pltpu.VMEM)
    smem = pl.BlockSpec(memory_space=pltpu.SMEM)
    return pl.pallas_call(
        prepare_kernel,
        out_shape=(
            jax.ShapeDtypeStruct(tokens.shape, BF16),
            jax.ShapeDtypeStruct((ROWS, cotangent.shape[3]), BF16),
            jax.ShapeDtypeStruct((MICRO, SL), F32),
        ),
        in_specs=[smem, smem, vmem, vmem],
        out_specs=(vmem,) * 3,
        cost_estimate=FREE,
    )(order, lengths, tokens, cotangent)


def front_kernel(
    dealt,
    top_block,
    gain_first,
    gain_second,
    key_live,
    cos,
    first,
    second,
    query_weight,
    key_weight,
    value_weight,
    output_weight,
    gate_weight,
    up_weight,
    down_weight,
    pair_out,
    down_out,
    qkv_out,
    out_out,
    x_out,
    top_half_out,
    top_came_out,
    first_mine_out,
    first_theirs_out,
    turned_out,
    mixed_mine_out,
    mixed_theirs_out,
    middle_out,
    second_mine_out,
    second_theirs_out,
    normed_second_out,
    hidden_grad_out,
    inverse_first,
    inverse_second,
    gains,
    x_in,
    top_half,
    top_came,
    normed_first,
    first_mine,
    first_theirs,
    turned,
    mixed,
    mixed_mine,
    mixed_theirs,
    middle,
    second_mine,
    second_theirs,
    normed_second,
    hidden_grad,
    qkv_w,
    out_w,
    gains_own,
    gains_col,
    gains_row,
    pair_held,
    down_held,
    tiles,
    x_came,
    x_half,
    x_other,
    top_col,
    top_row,
    sent,
    row_came,
    kept,
    summed,
    col_came,
    low,
    low_came,
    deal_sems,
    weight_sems,
    local_sems,
    swap_sems,
    tile_sems,
):
    groups = dealt.shape[1]
    dp, row, col = lax.axis_index("dp"), lax.axis_index("row"), lax.axis_index("col")
    x = lax.rem(dp, 2)
    partner = {"dp": dp + 1 - 2 * x}
    across = {"row": 1 - row}
    beside = {"col": 1 - col}
    half, block = D // 2, D // 4
    heads = query_weight.shape[1] // 2
    quarter = gate_weight.shape[1] // 2
    pending = []

    def remote(source, target, sems, at, device):
        copy = pltpu.make_async_remote_copy(
            src_ref=source,
            dst_ref=target,
            send_sem=sems.at[0, at],
            recv_sem=sems.at[1, at],
            device_id=device,
            device_id_type=MESH,
        )
        copy.start()
        pending.append(copy)
        return copy

    def swap(source, target, at, device):
        return remote(source, target, swap_sems, at, device)

    def columns(w, index, start, size):
        begin = pl.multiple_of(index * (w.shape[1] // 2) + start, 128)
        return w.at[:, pl.ds(begin, size)]

    def rows_half(w, index):
        size = w.shape[0] // 2
        return w.at[pl.ds(pl.multiple_of(index * size, size), size), :]

    locals_started = []

    def local(source, target):
        copy = pltpu.make_async_copy(source, target, local_sems.at[len(locals_started)])
        copy.start()
        locals_started.append(copy)
        return copy

    own_now = []
    for kind, w in enumerate((query_weight, key_weight, value_weight)):
        for at in range(0, heads, 128):
            there = pl.ds(3 * at + 128 * kind, 128)
            own_now.append(local(columns(w, row, at, 128), qkv_w.at[pl.ds(0, half), there]))
    own_now.append(local(rows_half(output_weight, row), out_w.at[:, pl.ds(0, half)]))
    own_gate = local(columns(gate_weight, row, 0, quarter), pair_held.at[0])
    own_up = local(columns(up_weight, row, 0, quarter), pair_held.at[1])
    own_down = local(rows_half(down_weight, row), down_held)
    own_rows = local(dealt.at[:, dp], x_in.at[:, dp])
    others = [(jnp.int32(1), {"dp": lax.rem(dp + step, groups)}) for step in range(1, groups)]
    greet(*others, (jnp.int32(1), across), (jnp.int32(1), beside))

    def dealing(step, micro):
        target = lax.rem(dp + step, groups)
        return pltpu.make_async_remote_copy(
            src_ref=dealt.at[micro, target],
            dst_ref=x_in.at[micro, dp],
            send_sem=deal_sems.at[0, micro, step],
            recv_sem=deal_sems.at[1, micro, step],
            device_id={"dp": target},
            device_id_type=MESH,
        )

    for micro in range(MICRO):

        def send_rows(step, _):
            dealing(step, micro).start()
            return 0

        lax.fori_loop(1, groups, send_rows, 0)
    gains_own[0:1, :] = gain_first[...]
    gains_own[1:2, :] = gain_second[...]
    gain_c = swap(gains_own, gains_col, 13, beside)
    top_c = swap(top_block, top_col, 0, beside)
    weights_now = []
    for kind, w in enumerate((query_weight, key_weight, value_weight)):
        for at in range(0, heads, 128):
            there = qkv_w.at[pl.ds(half, half), pl.ds(3 * at + 128 * kind, 128)]
            weights_now.append(
                remote(columns(w, 1 - row, at, 128), there, weight_sems, len(weights_now), across)
            )
    weights_now.append(
        remote(
            rows_half(output_weight, 1 - row),
            out_w.at[:, pl.ds(half, half)],
            weight_sems,
            len(weights_now),
            across,
        )
    )
    weights_late = []
    for k, w in enumerate((gate_weight, up_weight)):
        there = pair_out.at[pl.ds(half, half), pl.ds(k * quarter, quarter)]
        weights_late.append(
            remote(
                columns(w, 1 - row, 0, quarter), there, weight_sems, len(weights_now) + k, across
            )
        )
    own_gate.wait()
    own_up.wait()
    store_gate = local(pair_held.at[0], pair_out.at[pl.ds(0, half), pl.ds(0, quarter)])
    store_up = local(pair_held.at[1], pair_out.at[pl.ds(0, half), pl.ds(quarter, quarter)])
    own_down.wait()
    store_down = local(down_held, down_out.at[:, pl.ds(0, half)])

    def half_of(own, came):
        return jnp.where(
            col == 0,
            jnp.concatenate([own, came], axis=1),
            jnp.concatenate([came, own], axis=1),
        )

    own_rows.wait()
    x_c = []
    for micro in range(MICRO):

        def take_rows(step, _):
            dealing(step, micro).wait_recv()
            return 0

        lax.fori_loop(1, groups, take_rows, 0)
        x_c.append(swap(x_in.at[micro], x_came.at[micro], 1 + micro, beside))
    gain_c.wait_recv()
    gains[...] = half_of(gains_own[...], gains_col[...])
    gain_r = swap(gains, gains_row, 14, across)
    top_c.wait_recv()

    def top_rows(rows):
        top_half[rows, :] = half_of(top_block[rows, :], top_col[rows, :])

    rows_loop(top_rows)
    results = [local(x_in, x_out), local(top_half, top_half_out)]
    top_x = swap(top_half, top_came, 3, partner)

    def micro_rows(micro):
        return pl.ds(micro * SL, SL)

    x_r = []
    for micro in range(MICRO):
        x_c[micro].wait_recv()
        own = x_in[micro].reshape(SL, block)
        came = x_came[micro].reshape(SL, block)
        x_half[micro_rows(micro), :] = half_of(own, came)
        rows = micro_rows(micro)
        x_r.append(swap(x_half.at[rows, :], x_other.at[rows, :], 4 + micro, across))
        if micro == 0:
            for copy in own_now:
                copy.wait()
            for copy in weights_now:
                copy.wait_recv()
    top_r = swap(top_half, top_row, 6, across)
    down_there = down_out.at[:, pl.ds(half, half)]
    down_r = remote(
        rows_half(down_weight, 1 - row), down_there, weight_sems, len(weights_now) + 2, across
    )
    store_qkv = local(qkv_w, qkv_out)
    store_out = local(out_w, out_out)

    lower = lax.broadcasted_iota(jnp.int32, (SL, SL), 1) <= lax.broadcasted_iota(
        jnp.int32, (SL, SL), 0
    )

    gain_r.wait_recv()

    def norm_rows(own_ref, other_ref, at, inverse_ref, out_ref, micro):
        def body(j, _):
            rows = pl.ds(pl.multiple_of(micro * SL + j * 64, 64), 64)
            own = own_ref[rows, :].astype(F32)
            other = other_ref[rows, :].astype(F32)
            total = jnp.sum(own * own, axis=1, keepdims=True)
            total = total + jnp.sum(other * other, axis=1, keepdims=True)
            inverse = lax.rsqrt(total / D + EPSILON)
            inverse_ref[rows, :] = inverse
            out_ref[rows, :half] = (own * inverse * gains[at : at + 1, :]).astype(BF16)
            out_ref[rows, half:] = (other * inverse * gains_row[at : at + 1, :]).astype(BF16)
            return 0

        lax.fori_loop(0, SL // 64, body, 0)

    sum_c = []
    for micro in range(MICRO):
        rows = micro_rows(micro)
        x_r[micro].wait_recv()
        norm_rows(x_half, x_other, 0, inverse_first, normed_first, micro)
        allowed = lower & (key_live[micro : micro + 1, :] > 0.5)

        def attend(at, _):
            there = pl.multiple_of(at * 768, 128)
            qkv = mm(normed_first[rows, :], qkv_w[:, pl.ds(there, 768)])
            for pair in range(2):
                qr, kr, vr, out = head_outputs(
                    qkv[:, pair * 384 : pair * 384 + 384], allowed, cos[...], first[...], second[...]
                )
                begin = there + pair * 384
                for kind, value in enumerate((qr, kr, vr)):
                    turned[rows, pl.ds(pl.multiple_of(begin + kind * 128, 128), 128)] = value
                mixed[rows, pl.ds(pl.multiple_of(at * 256 + pair * 128, 128), 128)] = out
            return 0

        lax.fori_loop(0, heads // 256, attend, 0)
        sent[rows, :] = mm(mixed[rows, :], out_w[:, half:]).astype(BF16)
        sum_r = swap(sent.at[rows, :], row_came.at[rows, :], 7 + micro, across)
        kept[...] = mm(mixed[rows, :], out_w[:, :half])
        sum_r.wait_recv()
        summed[rows, :] = (kept[...] + row_came[rows, :].astype(F32)).astype(BF16)
        sum_c.append(swap(summed.at[rows, :], col_came.at[rows, :], 9 + micro, beside))

    results.append(local(turned, turned_out))

    def by_x(source, mine, theirs, rows, width):
        value = source[rows, : 2 * mine.shape[1]]
        even = [value[:, at : at + width] for at in range(0, value.shape[1], 2 * width)]
        odd = [value[:, at : at + width] for at in range(width, value.shape[1], 2 * width)]
        even, odd = jnp.concatenate(even, axis=1), jnp.concatenate(odd, axis=1)
        mine[rows, :] = jnp.where(x == 0, even, odd)
        theirs[rows, :] = jnp.where(x == 0, odd, even)

    top_r.wait_recv()
    store_down.wait()
    down_r.wait_recv()

    def da_body(j, slot):
        total = mm_nt(top_half[...], tiles[slot, :, :half])
        total = total + mm_nt(top_row[...], tiles[slot, :, half:])
        hidden_grad[:, pl.ds(pl.multiple_of(j * 256, 256), 256)] = total

    stream(
        lambda j: [down_out.at[pl.ds(pl.multiple_of(j * 256, 256), 256), :]],
        lambda slot: [tiles.at[slot]],
        tile_sems,
        quarter // 256,
        da_body,
    )

    results.append(local(hidden_grad, hidden_grad_out))

    def select_rows(rows):
        by_x(normed_first, first_mine, first_theirs, rows, half // groups)
        by_x(mixed, mixed_mine, mixed_theirs, rows, 2 * heads // groups)

    rows_loop(select_rows)
    results.append(local(first_mine, first_mine_out))
    results.append(local(first_theirs, first_theirs_out))
    results.append(local(mixed_mine, mixed_mine_out))
    results.append(local(mixed_theirs, mixed_theirs_out))

    low_r = []
    for micro in range(MICRO):
        rows = micro_rows(micro)
        sum_c[micro].wait_recv()

        def middle_rows(j, _):
            here = pl.ds(pl.multiple_of(micro * SL + j * 64, 64), 64)
            total = x_half[here, :].astype(F32) + (
                summed[here, :].astype(F32) + col_came[here, :].astype(F32)
            )
            middle[here, :] = total
            low[here, :] = total.astype(BF16)
            return 0

        lax.fori_loop(0, SL // 64, middle_rows, 0)
        results.append(local(middle.at[rows, :], middle_out.at[rows, :]))
        low_r.append(swap(low.at[rows, :], low_came.at[rows, :], 11 + micro, across))
        low_r[micro].wait_recv()
        norm_rows(low, low_came, 1, inverse_second, normed_second, micro)
        results.append(local(normed_second.at[rows, :], normed_second_out.at[rows, :]))

        def second_rows(j, _):
            here = pl.ds(pl.multiple_of(micro * SL + j * 64, 64), 64)
            by_x(normed_second, second_mine, second_theirs, here, half // groups)
            return 0

        lax.fori_loop(0, SL // 64, second_rows, 0)
        results.append(local(second_mine.at[rows, :], second_mine_out.at[rows, :]))
        results.append(local(second_theirs.at[rows, :], second_theirs_out.at[rows, :]))

    top_x.wait_recv()
    results.append(local(top_came, top_came_out))
    for copy in weights_late:
        copy.wait_recv()
    for copy in pending:
        copy.wait_send()

    def close(step, _):
        for micro in range(MICRO):
            dealing(step, micro).wait_send()
        return 0

    lax.fori_loop(1, groups, close, 0)
    for copy in [store_gate, store_up, store_qkv, store_out] + results:
        copy.wait()


def front(line, identity, *values):
    dealt, query_weight, gate_weight = values[0], values[8], values[12]
    groups = dealt.shape[1]
    half, block = D // 2, D // 4
    heads = query_weight.shape[1] // 2
    quarter = gate_weight.shape[1] // 2
    vmem = pl.BlockSpec(memory_space=pltpu.VMEM)
    anywhere = pl.BlockSpec(memory_space=pl.ANY)

    def array(*shape, dtype=BF16):
        return jax.ShapeDtypeStruct(shape, dtype)

    def buffer(*shape, dtype=BF16):
        return pltpu.VMEM(shape, dtype)

    sem = pltpu.SemaphoreType.DMA
    now = 3 * (heads // 128) + 1
    held = [
        (dealt.shape, BF16),
        ((ROWS, half), BF16),
        ((ROWS, half), BF16),
        ((ROWS, block), BF16),
        ((ROWS, block), BF16),
        ((ROWS, 3 * heads), BF16),
        ((ROWS, heads // 2), BF16),
        ((ROWS, heads // 2), BF16),
        ((ROWS, half), F32),
        ((ROWS, block), BF16),
        ((ROWS, block), BF16),
        ((ROWS, D), BF16),
        ((ROWS, quarter), F32),
    ]
    normed_first, mixed = ((ROWS, D), BF16), ((ROWS, heads), BF16)
    inside = held[:3] + [normed_first] + held[3:6] + [mixed] + held[6:]
    return pl.pallas_call(
        front_kernel,
        out_shape=[
            array(D, 2 * quarter),
            array(quarter, D),
            array(D, 3 * heads),
            array(heads, D),
            *[array(*shape, dtype=kind) for shape, kind in held],
            array(ROWS, 1, dtype=F32),
            array(ROWS, 1, dtype=F32),
            array(2, half, dtype=F32),
        ],
        in_specs=[vmem] * 8 + [anywhere] * 7,
        out_specs=[anywhere] * (4 + len(held)) + [vmem] * 3,
        scratch_shapes=[
            *[buffer(*shape, dtype=kind) for shape, kind in inside],
            buffer(D, 3 * heads),
            buffer(heads, D),
            buffer(2, block, dtype=F32),
            buffer(2, block, dtype=F32),
            buffer(2, half, dtype=F32),
            buffer(2, half, quarter),
            buffer(quarter, half),
            buffer(2, 256, D),
            buffer(*dealt.shape),
            buffer(ROWS, half),
            buffer(ROWS, half),
            buffer(ROWS, block),
            buffer(ROWS, half),
            buffer(ROWS, half),
            buffer(ROWS, half),
            buffer(SL, half, dtype=F32),
            buffer(ROWS, half),
            buffer(ROWS, half),
            buffer(ROWS, half),
            buffer(ROWS, half),
            sem((2, MICRO, groups)),
            sem((2, now + 3)),
            sem((now + 28,)),
            sem((2, 15)),
            sem((2, 2)),
        ],
        compiler_params=pltpu.CompilerParams(
            collective_id=identity, has_side_effects=True, vmem_limit_bytes=67043328
        ),
        cost_estimate=FREE,
    )(*values)


def chain_kernel(
    line,
    normed,
    hidden_grad,
    second_mine,
    second_theirs,
    top_half,
    top_came,
    pair_w,
    down_w,
    qkv_w,
    out_w,
    turned,
    middle,
    inverse_first,
    inverse_second,
    gain_second,
    gain_first,
    x_own,
    key_live,
    cos,
    first,
    second,
    down_out,
    gate_grads_out,
    second_came_out,
    up_grad_out,
    up_row,
    dqkv_out,
    dqkv_row,
    branch_out,
    both_out,
    pieces_out,
    gate_row,
    gate_came,
    gate_came_row,
    gate_grads,
    second_came,
    up_grad,
    dqkv,
    branch,
    hidden,
    gate_grad,
    tiles,
    tall_tiles,
    da_tiles,
    kept,
    sent,
    row_came,
    summed,
    col_came,
    block_sent,
    block_came,
    hidden_row,
    hidden_came,
    hidden_came_row,
    branch_row,
    dots,
    down_grads,
    down_z,
    middle_own,
    layer_own,
    first_own,
    mixed_grad,
    turned_left,
    feed_sum,
    attention_sum,
    swap_sems,
    piece_sems,
    tile_sems,
    down_sems,
    copy_sems,
):
    dp, row, col = lax.axis_index("dp"), lax.axis_index("row"), lax.axis_index("col")
    x = lax.rem(dp, 2)
    partner = {"dp": dp + 1 - 2 * x}
    across = {"row": 1 - row}
    beside = {"col": 1 - col}
    down_line = ZLine(line, down_grads, down_out, None, down_z, down_sems, 4, True)
    half = D // 2
    block = D // 4
    quarter = normed.shape[1]
    pending, results = [], []

    def result(source, target):
        copy = pltpu.make_async_copy(source, target, copy_sems.at[2 + len(results)])
        copy.start()
        results.append(copy)

    def swap(source, target, at, device, sems=swap_sems):
        copy = pltpu.make_async_remote_copy(
            src_ref=source,
            dst_ref=target,
            send_sem=sems.at[0, at],
            recv_sem=sems.at[1, at],
            device_id=device,
            device_id_type=MESH,
        )
        return copy

    def begin(copy):
        copy.start()
        pending.append(copy)
        return copy

    greet(
        *down_line.moves(),
        (jnp.int32(1), partner),
        (jnp.int32(1), across),
        (jnp.int32(1), beside),
    )

    per = line // 2
    width = quarter // line
    tile = min(width, 256)
    each = width // tile

    def hidden_part(index, at):
        return hidden.at[:, pl.ds(pl.multiple_of((2 * at + index) * width, width), width)]

    def feed_columns(j, shift=0):
        piece = j // each
        index = jnp.where(piece < per, 1 - x, x)
        begin = (2 * lax.rem(piece, per) + index) * width + lax.rem(j, each) * tile
        return pl.ds(pl.multiple_of(shift + begin, tile), tile)

    to_x = [
        swap(
            hidden_part(1 - x, at),
            hidden_came.at[:, pl.ds(at * width, width)],
            at,
            partner,
            piece_sems,
        )
        for at in range(per)
    ]
    pending.extend(to_x)

    def feed_body(j, slot):
        gate = mm(normed[...], tall_tiles[slot, 0, :, :tile])
        up = mm(normed[...], tall_tiles[slot, 1, :, :tile])
        da = da_tiles[slot, :, :tile]
        sigmoid = 1.0 / (1.0 + jnp.exp(-gate))
        swish = gate * sigmoid
        there = feed_columns(j)
        hidden[:, there] = (swish * up).astype(BF16)
        gate_grad[:, there] = (da * up * sigmoid * (1.0 + gate * (1.0 - sigmoid))).astype(BF16)
        up_grad[:, there] = (da * swish).astype(BF16)
        for at in range(per):

            @pl.when(j == (at + 1) * each - 1)
            def _():
                to_x[at].start()

    narrow_tile = pl.ds(0, tile)
    stream(
        lambda j: [
            pair_w.at[:, feed_columns(j)],
            pair_w.at[:, feed_columns(j, quarter)],
            hidden_grad.at[:, feed_columns(j)],
        ],
        lambda slot: [
            tall_tiles.at[slot, 0, :, narrow_tile],
            tall_tiles.at[slot, 1, :, narrow_tile],
            da_tiles.at[slot, :, narrow_tile],
        ],
        tile_sems,
        quarter // tile,
        feed_body,
    )
    to_row, on_row = [], []
    for at in range(per):
        there = pl.ds(at * width, width)
        to_row.append(
            begin(swap(hidden_part(x, at), hidden_row.at[:, there], per + at, across, piece_sems))
        )
    result(up_grad, up_grad_out)
    second_x = begin(swap(second_theirs, second_came, 0, partner))
    gate_x = begin(swap(gate_grad, gate_came, 1, partner))

    def nt_product(w, depth, start, body):
        stream(
            lambda j: [w.at[pl.ds(pl.multiple_of(start + j * 256, 256), 256), :]],
            lambda slot: [tiles.at[slot, :, pl.ds(0, depth)]],
            tile_sems,
            half // 256,
            body,
        )

    def columns_at(j, size=256):
        return pl.ds(pl.multiple_of(j * size, size), size)

    def pair_body(target, dtype):
        def body(j, slot):
            total = mm_nt(gate_grad[...], tiles[slot, :, :quarter])
            total = total + mm_nt(up_grad[...], tiles[slot, :, quarter:])
            target[:, columns_at(j)] = total.astype(dtype)

        return body

    nt_product(pair_w, 2 * quarter, half, pair_body(sent, BF16))
    pair_r = begin(swap(sent, row_came.at[0], 2, across))
    nt_product(pair_w, 2 * quarter, 0, pair_body(kept, F32))
    pair_r.wait_recv()

    def join_pair(rows):
        summed[rows, :] = (kept[rows, :] + row_came[0, rows, :].astype(F32)).astype(BF16)

    rows_loop(join_pair)
    pair_c = begin(swap(summed, col_came, 3, beside))
    gate_r = begin(swap(gate_grad, gate_row, 4, across))
    up_r = begin(swap(up_grad, up_row, 5, across))

    for copy in to_x:
        copy.wait_recv()
    for at in range(per):
        there = pl.ds(at * width, width)
        on_row.append(
            begin(
                swap(
                    hidden_came.at[:, there],
                    hidden_came_row.at[:, there],
                    2 * per + at,
                    across,
                    piece_sems,
                )
            )
        )

    def down_grad(part, left_of, came):
        def body(columns, _):
            for at in range(per):
                there = pl.ds(at * width, width)
                total = mm_tn(left_of(at)[...], top_half[:, columns])
                total = total + mm_tn(came[:, there], top_came[:, columns])
                down_grads[pl.ds((part * per + at) * width, width), columns] = total.astype(BF16)

        tiles_loop(half, 512, body)

    down_grad(0, lambda at: hidden_part(x, at), hidden_came)
    for copy in to_row + on_row:
        copy.wait_recv()
    down_grad(1, lambda at: hidden_row.at[:, pl.ds(at * width, width)], hidden_came_row)
    down_line.run(0, 1)

    def down_product(start, target, dtype):
        def body(j, slot):
            target[:, columns_at(j)] = mm(hidden[...], tall_tiles[slot, 0]).astype(dtype)

        stream(
            lambda j: [down_w.at[:, pl.ds(pl.multiple_of(start + j * 256, 256), 256)]],
            lambda slot: [tall_tiles.at[slot, 0]],
            tile_sems,
            half // 256,
            body,
        )

    pair_r.wait_send()
    pending[:] = [copy for copy in pending if copy is not pair_r]
    down_product(half, sent, BF16)
    layer_r = begin(swap(sent, row_came.at[1], 7, across))
    down_product(0, kept, F32)
    layer_r.wait_recv()

    def mine_of(value):
        return jnp.where(col == 0, value[:, :block], value[:, block:])

    def theirs_of(value):
        return jnp.where(col == 0, value[:, block:], value[:, :block])

    def join_layer(rows):
        total = kept[rows, :] + row_came[1, rows, :].astype(F32)
        layer_own[rows, :] = mine_of(total)
        block_sent[0, rows, :] = theirs_of(total).astype(BF16)

    rows_loop(join_layer)
    layer_c = begin(swap(block_sent.at[0], block_came.at[0], 8, beside))
    middle_in = pltpu.make_async_copy(middle, kept, copy_sems.at[0])
    middle_in.start()

    middle_in.wait()
    pair_c.wait_recv()
    feed_sum[...] = jnp.zeros_like(feed_sum)

    def second_grads(rows):
        grad = summed[rows, :].astype(F32) + col_came[rows, :].astype(F32)
        return grad, grad * gain_second[1:2, :]

    def norm_first_pass(rows):
        grad, scaled = second_grads(rows)
        held = kept[rows, :]
        feed_sum[...] += jnp.sum(grad * held * inverse_second[rows, :], axis=0, keepdims=True)
        total = jnp.sum(scaled * held, axis=1, keepdims=True)
        dots[0, rows, :] = jnp.broadcast_to(total, (total.shape[0], 128))

    rows_loop(norm_first_pass)
    dot_r = begin(swap(dots.at[0], dots.at[1], 9, across))
    dot_r.wait_recv()

    def norm_second_pass(rows):
        _, scaled = second_grads(rows)
        held = kept[rows, :]
        inverse = inverse_second[rows, :]
        dot = dots[0, rows, :1] + dots[1, rows, :1]
        grad = (
            top_half[rows, :].astype(F32) + scaled * inverse - held * (inverse**3 * dot / D)
        )
        branch[rows, :] = grad.astype(BF16)
        middle_own[rows, :] = mine_of(grad)
        layer_own[rows, :] += mine_of(held)

    rows_loop(norm_second_pass)
    result(branch, branch_out)
    branch_r = begin(swap(branch, branch_row, 10, across))
    branch_r.wait_recv()

    down_line.run(1, 2)

    def mixed_body(j, slot):
        total = mm_nt(branch[...], tiles[slot, :, :half])
        total = total + mm_nt(branch_row[...], tiles[slot, :, half:D])
        mixed_grad[:, columns_at(j)] = total.astype(BF16)

    stream(
        lambda j: [out_w.at[pl.ds(pl.multiple_of(j * 256, 256), 256), :]],
        lambda slot: [tiles.at[slot, :, pl.ds(0, D)]],
        tile_sems,
        out_w.shape[0] // 256,
        mixed_body,
    )
    pairs = turned.shape[1] // 384
    lower = lax.broadcasted_iota(jnp.int32, (SL, SL), 1) <= lax.broadcasted_iota(
        jnp.int32, (SL, SL), 0
    )

    def attend(at, _):
        micro, pair = at // pairs, lax.rem(at, pairs)
        rows = pl.ds(pl.multiple_of(micro * SL, SL), SL)

        def part(kind):
            return pl.ds(pl.multiple_of(pair * 384 + kind * 128, 128), 128)

        allowed = lower & (key_live[pl.ds(micro, 1), :] > 0.5)
        dq, dk, dv = head_grads(
            turned[rows, part(0)],
            turned[rows, part(1)],
            turned[rows, part(2)],
            mixed_grad[rows, pl.ds(pl.multiple_of(pair * 128, 128), 128)],
            allowed,
            cos[...],
            first[...],
            second[...],
        )
        dqkv[rows, part(0)] = dq
        dqkv[rows, part(1)] = dk
        dqkv[rows, part(2)] = dv
        return 0

    lax.fori_loop(0, MICRO * pairs, attend, 0)
    result(dqkv, dqkv_out)

    def first_body(target, dtype):
        def body(j, slot):
            total = mm_nt(dqkv[...], tiles[slot, :, : dqkv.shape[1]])
            target[:, columns_at(j)] = total.astype(dtype)

        return body

    layer_r.wait_send()
    pending[:] = [copy for copy in pending if copy is not layer_r]
    nt_product(qkv_w, dqkv.shape[1], half, first_body(sent, BF16))
    first_r = begin(swap(sent, row_came.at[2], 11, across))
    dqkv_r = begin(swap(dqkv, dqkv_row, 12, across))
    nt_product(qkv_w, dqkv.shape[1], 0, first_body(kept, F32))
    down_line.run(2, line - 1)
    first_r.wait_recv()

    def join_first(rows):
        total = kept[rows, :] + row_came[2, rows, :].astype(F32)
        first_own[rows, :] = mine_of(total)
        block_sent[1, rows, :] = theirs_of(total).astype(BF16)

    rows_loop(join_first)
    first_c = begin(swap(block_sent.at[1], block_came.at[1], 13, beside))

    second_x.wait_recv()
    result(second_came, second_came_out)
    depth = second_mine.shape[0]
    turned_left[:, :depth] = second_mine[...].T
    turned_left[:, depth:] = second_came[...].T
    gate_x.wait_recv()
    gate_on = begin(swap(gate_came, gate_came_row, 14, across))

    def gate_part(shift, sources, values):
        def body(j, slot):
            mine, came = values(j, slot)
            total = mm(turned_left[:, :depth], mine) + mm(turned_left[:, depth:], came)
            there = pl.ds(pl.multiple_of(shift + j * 256, 256), 256)
            gate_grads[:, there] = total.astype(BF16)

        stream(
            lambda j: [source.at[:, columns_at(j)] for source in sources],
            lambda slot: [tall_tiles.at[slot, k, pl.ds(0, ROWS)] for k in range(len(sources))],
            tile_sems,
            quarter // 256,
            body,
        )

    gate_part(
        0,
        [gate_came],
        lambda j, slot: (gate_grad[:, columns_at(j)], tall_tiles[slot, 0, :ROWS]),
    )
    gate_r.wait_recv()
    gate_on.wait_recv()
    gate_part(
        quarter,
        [gate_row, gate_came_row],
        lambda j, slot: (tall_tiles[slot, 0, :ROWS], tall_tiles[slot, 1, :ROWS]),
    )

    result(gate_grads, gate_grads_out)
    layer_c.wait_recv()
    first_c.wait_recv()
    attention_sum[...] = jnp.zeros_like(attention_sum)

    def last_first_pass(rows):
        layer = layer_own[rows, :] + block_came[0, rows, :].astype(F32)
        both_out[rows, :] = layer.astype(BF16)
        grad = first_own[rows, :] + block_came[1, rows, :].astype(F32)
        first_own[rows, :] = grad
        held = x_own[rows, :].astype(F32)
        attention_sum[...] += jnp.sum(grad * held * inverse_first[rows, :], axis=0, keepdims=True)
        total = jnp.sum(grad * gain_first[...] * held, axis=1, keepdims=True)
        dots[2, rows, :] = jnp.broadcast_to(total, (total.shape[0], 128))

    rows_loop(last_first_pass)
    dot_r = begin(swap(dots.at[2], dots.at[3], 15, across))
    dot_r.wait_recv()

    def add_dots(rows):
        dots[4, rows, :] = dots[2, rows, :] + dots[3, rows, :]

    rows_loop(add_dots)
    dot_c = begin(swap(dots.at[4], dots.at[5], 16, beside))
    dot_c.wait_recv()

    def last_second_pass(rows):
        inverse = inverse_first[rows, :]
        dot = dots[4, rows, :1] + dots[5, rows, :1]
        scaled = first_own[rows, :] * gain_first[...]
        held = x_own[rows, :].astype(F32)
        grad = middle_own[rows, :] + scaled * inverse - held * (inverse**3 * dot / D)
        below = pl.ds(pl.multiple_of(rows.start + ROWS, rows.size), rows.size)
        both_out[below, :] = grad.astype(BF16)

    rows_loop(last_second_pass)
    pieces_out[0:1, :] = attention_sum[...]
    pieces_out[1:2, :] = mine_of(feed_sum[...])

    down_line.stage = kept.at[pl.ds(0, down_grads.shape[0] // line), :]
    down_line.finish()
    down_store = pltpu.make_async_copy(down_line.stage, down_out, copy_sems.at[1])
    down_store.start()
    for copy in (up_r, dqkv_r):
        copy.wait_recv()
    for copy in pending:
        copy.wait_send()
    down_store.wait()
    for copy in results:
        copy.wait()


def chain(line, identity, *values):
    quarter = values[1].shape[1]
    narrow = values[2].shape[1]
    qkv_width = values[10].shape[1]
    half, block = D // 2, D // 4
    rows = quarter // 2
    vmem = pl.BlockSpec(memory_space=pltpu.VMEM)
    anywhere = pl.BlockSpec(memory_space=pl.ANY)
    outside = {1, 3, 6, 7, 8, 9, 11}

    def array(*shape, dtype=BF16):
        return jax.ShapeDtypeStruct(shape, dtype)

    def buffer(*shape, dtype=BF16):
        return pltpu.VMEM(shape, dtype)

    outs = [
        (array(2 * rows // line, half, dtype=F32), anywhere),
        (array(narrow, 2 * quarter), anywhere),
        (array(ROWS, narrow), anywhere),
        (array(ROWS, quarter), anywhere),
        (array(ROWS, quarter), anywhere),
        (array(ROWS, qkv_width), anywhere),
        (array(ROWS, qkv_width), anywhere),
        (array(ROWS, half), anywhere),
        (array(2 * ROWS, block), vmem),
        (array(2, block, dtype=F32), vmem),
        (array(ROWS, quarter), anywhere),
        (array(ROWS, quarter), anywhere),
        (array(ROWS, quarter), anywhere),
    ]
    sem = pltpu.SemaphoreType.DMA
    return pl.pallas_call(
        lambda *refs: chain_kernel(line, *refs),
        out_shape=[shape for shape, _ in outs],
        in_specs=[anywhere if k in outside else vmem for k in range(len(values))],
        out_specs=[place for _, place in outs],
        scratch_shapes=[
            buffer(narrow, 2 * quarter),
            buffer(ROWS, narrow),
            buffer(ROWS, quarter),
            buffer(ROWS, qkv_width),
            buffer(ROWS, half),
            buffer(ROWS, quarter),
            buffer(ROWS, quarter),
            buffer(2, 256, 2 * quarter),
            buffer(2, 2, quarter, 256),
            buffer(2, ROWS, 256, dtype=F32),
            buffer(ROWS, half, dtype=F32),
            buffer(ROWS, half),
            buffer(3, ROWS, half),
            buffer(ROWS, half),
            buffer(ROWS, half),
            buffer(2, ROWS, block),
            buffer(2, ROWS, block),
            buffer(ROWS, rows),
            buffer(ROWS, rows),
            buffer(ROWS, rows),
            buffer(ROWS, half),
            buffer(6, ROWS, 128, dtype=F32),
            buffer(2 * rows, half),
            buffer(2, line - 1, 2 * rows // line, half),
            buffer(ROWS, block, dtype=F32),
            buffer(ROWS, block, dtype=F32),
            buffer(ROWS, block, dtype=F32),
            buffer(ROWS, qkv_width // 3),
            buffer(narrow, 2 * ROWS),
            buffer(1, half, dtype=F32),
            buffer(1, block, dtype=F32),
            sem((2, 17)),
            sem((2, 3 * (line // 2))),
            sem((2, 3)),
            sem((2, 2, line - 1, 4)),
            sem((7,)),
        ],
        compiler_params=pltpu.CompilerParams(
            collective_id=identity, has_side_effects=True, vmem_limit_bytes=67043328
        ),
        cost_estimate=FREE,
    )(*values)


def tail_sums(line, identity, *values):
    (gate_grads, up, _, _, _, dqkv, _, _, _, branch) = values[:10]
    rows = gate_grads.shape[0]
    side_rows = 2 * values[10].shape[1]
    tokens = up.shape[0]
    widths = (gate_grads.shape[1], gate_grads.shape[1], 2 * dqkv.shape[1], branch.shape[1])
    heights = (rows, rows, rows, side_rows)
    pieces = (4, 4, 3, 1)
    sizes = [(h // line, w) for h, w in zip(heights, widths)]
    vmem = pl.BlockSpec(memory_space=pltpu.VMEM)
    anywhere = pl.BlockSpec(memory_space=pl.ANY)
    both, gains = values[12:]
    height = sizes[0][0]
    gain_steps = both.shape[1].bit_length() - 1

    def buffer(*shape):
        return pltpu.VMEM(shape, BF16)

    def array(*shape):
        return jax.ShapeDtypeStruct(shape, F32)

    return pl.pallas_call(
        lambda *refs: tail_kernel(line, *refs),
        out_shape=[
            array(*sizes[0]),
            array(*sizes[1]),
            array(height, widths[2] // 3),
            array(height, widths[2] // 3),
            array(height, widths[2] // 3),
            array(*sizes[3]),
            jax.ShapeDtypeStruct(both.shape, BF16),
            array(*gains.shape),
        ],
        in_specs=[vmem] + [anywhere] * 12 + [vmem],
        out_specs=[anywhere] * 7 + [vmem],
        scratch_shapes=[buffer(*values[at].shape) for at in (1, 2, 3, 4, 5, 6, 7, 9, 10)]
        + [buffer(2, line - 1, *size) for size in sizes]
        + [buffer(h, w) for h, w in zip(heights[1:], widths[1:])]
        + [buffer(*up.shape)] * 2
        + [buffer(*dqkv.shape)] * 2
        + [buffer(*branch.shape), buffer(*values[7].shape)]
        + [buffer(*values[10].shape)] * 3
        + [buffer(rows, 2 * tokens)]
        + [pltpu.VMEM(size, F32) for size in sizes]
        + [pltpu.SemaphoreType.DMA((2, 2, line - 1, count)) for count in pieces]
        + [pltpu.SemaphoreType.DMA((2, 9)), pltpu.SemaphoreType.DMA((6 + widths[2] // 128,))]
        + [pltpu.VMEM((2, gain_steps, *gains.shape), F32)]
        + [
            pltpu.SemaphoreType.DMA((2, both.shape[1])),
            pltpu.SemaphoreType.DMA((2, gain_steps)),
            pltpu.SemaphoreType.DMA((9,)),
        ],
        compiler_params=pltpu.CompilerParams(
            collective_id=identity, has_side_effects=True, vmem_limit_bytes=67043328
        ),
        cost_estimate=FREE,
    )(*values)


def finish_kernel(count, order_ref, back_ref, gains_ref, *refs):
    sums, rest = refs[:count], refs[count:]
    layer_ref, grad_ref, attention_ref, feed_ref = rest[:4]
    outs, held, sems = rest[4 : 4 + count], rest[4 + count : 4 + 2 * count], rest[4 + 2 * count]
    groups = back_ref.shape[1]
    loads = [pltpu.make_async_copy(sums[k], held[k], sems.at[0, k]) for k in range(count)]
    stores = [pltpu.make_async_copy(held[k], outs[k], sems.at[1, k]) for k in range(count)]
    for copy in loads:
        copy.start()

    def one(at, _):
        micro, slot = at // groups, lax.rem(at, groups)
        place = order_ref[micro, slot]
        layer_ref[micro, place] = back_ref[micro, slot]
        grad_ref[micro, place] = back_ref[MICRO + micro, slot]
        return 0

    lax.fori_loop(0, MICRO * groups, one, 0)
    size = attention_ref.shape[1]
    width = gains_ref.shape[1]
    at = lax.broadcasted_iota(jnp.int32, (width, size), 0)
    wanted = lax.broadcasted_iota(jnp.int32, (width, size), 1) + lax.axis_index("dp") * size
    picked = jnp.dot(
        gains_ref[...],
        jnp.where(at == wanted, 1.0, 0.0),
        preferred_element_type=F32,
        precision=lax.Precision.HIGHEST,
    )
    attention_ref[...] = picked[0:1, :]
    feed_ref[...] = picked[1:2, :]
    for load, store in zip(loads, stores):
        load.wait()
        store.start()
    for store in stores:
        store.wait()


def finish(order, back, gains, *sums):
    vmem = pl.BlockSpec(memory_space=pltpu.VMEM)
    anywhere = pl.BlockSpec(memory_space=pl.ANY)
    rows = jax.ShapeDtypeStruct((MICRO,) + back.shape[1:], BF16)
    part = jax.ShapeDtypeStruct((1, gains.shape[1] // back.shape[1]), F32)
    count = len(sums)
    return pl.pallas_call(
        lambda *refs: finish_kernel(count, *refs),
        out_shape=[rows, rows, part, part] + [jax.ShapeDtypeStruct(v.shape, F32) for v in sums],
        in_specs=[pl.BlockSpec(memory_space=pltpu.SMEM), vmem, vmem] + [anywhere] * count,
        out_specs=[vmem] * 4 + [anywhere] * count,
        scratch_shapes=[pltpu.VMEM(v.shape, F32) for v in sums]
        + [pltpu.SemaphoreType.DMA((2, count))],
        cost_estimate=FREE,
    )(order, back, gains, *sums)


def per_device(
    tokens,
    lengths,
    deal_order,
    attention_gain,
    query_weight,
    key_weight,
    value_weight,
    output_weight,
    feed_gain,
    gate_weight,
    up_weight,
    down_weight,
    cotangent,
):
    groups = lax.axis_size("dp")
    line = groups // 2
    dp = lax.axis_index("dp")
    row = lax.axis_index("row")
    col = lax.axis_index("col")
    z, x = dp // 2, dp % 2
    half = D // 2
    block = D // 4

    def over_row(v):
        return lax.ppermute(v, "row", SWAP)

    def over_col(v):
        return lax.ppermute(v, "col", SWAP)

    def ordered(own, other, index, axis=-1):
        return jnp.where(
            index == 0,
            jnp.concatenate([own, other], axis=axis),
            jnp.concatenate([other, own], axis=axis),
        )

    def x_parts(v, width):
        even = jnp.concatenate(
            [v[:, s : s + width] for s in range(0, v.shape[1], 2 * width)], axis=1
        )
        odd = jnp.concatenate(
            [v[:, s : s + width] for s in range(width, v.shape[1], 2 * width)], axis=1
        )
        return jnp.where(x == 0, even, odd), jnp.where(x == 0, odd, even)

    def plain(*values):
        return values

    dealt, top_block, key_live = prepare(deal_order, lengths, tokens, cotangent)
    tables = rope_tables()
    (
        pair_w,
        down_w,
        qkv_w,
        out_w,
        x_block,
        top_half,
        top_came,
        first_mine,
        first_theirs,
        turned,
        mixed_mine,
        mixed_theirs,
        middle,
        second_mine,
        second_theirs,
        normed_second,
        hidden_grad,
        inverse_first,
        inverse_second,
        gains_half,
    ) = front(
        line,
        0,
        dealt,
        top_block,
        attention_gain.reshape(1, block),
        feed_gain.reshape(1, block),
        key_live,
        *tables,
        query_weight,
        key_weight,
        value_weight,
        output_weight,
        gate_weight,
        up_weight,
        down_weight,
    )
    x_block = x_block.reshape(ROWS, block)
    narrow = half // groups
    (
        down_sum,
        gate_grads,
        second_came,
        up_grad,
        up_row,
        dqkv,
        dqkv_row,
        branch,
        both,
        pieces,
        _,
        _,
        _,
    ) = chain(
        line,
        4,
        *plain(
            normed_second,
            hidden_grad,
            second_mine,
            second_theirs,
            top_half,
            top_came,
            pair_w,
            down_w,
            qkv_w,
            out_w,
            turned,
            middle,
            inverse_first,
            inverse_second,
            gains_half,
            attention_gain.reshape(1, block),
            x_block,
            key_live,
            *tables,
        ),
    )

    gate_sum, up_sum, query_sum, key_sum, value_sum, output_sum, back, gain_sums = tail_sums(
        line,
        3,
        *plain(
            gate_grads,
            up_grad,
            up_row,
            second_mine,
            second_came,
            dqkv,
            dqkv_row,
            first_mine,
            first_theirs,
            branch,
            mixed_mine,
            mixed_theirs,
            both.reshape(2 * MICRO, groups, SL // groups, block),
            pieces,
        ),
    )
    (
        layer_output,
        tokens_grad,
        attention_sum,
        feed_sum,
        down_sum,
        gate_sum,
        up_sum,
        query_sum,
        key_sum,
        value_sum,
        output_sum,
    ) = finish(
        deal_order,
        back,
        gain_sums,
        down_sum,
        gate_sum,
        up_sum,
        query_sum,
        key_sum,
        value_sum,
        output_sum,
    )
    return (
        layer_output,
        tokens_grad,
        attention_sum.reshape(-1),
        query_sum,
        key_sum,
        value_sum,
        output_sum,
        feed_sum.reshape(-1),
        gate_sum,
        up_sum,
        down_sum,
    )


def solution(mesh):
    in_specs = (
        P(None, None, "dp", ("row", "col")),
        P(),
        P(),
        P(("row", "col")),
        P("row", "col"),
        P("row", "col"),
        P("row", "col"),
        P("col", "row"),
        P(("row", "col")),
        P("row", "col"),
        P("row", "col"),
        P("col", "row"),
        P(None, "dp", None, ("row", "col")),
    )
    out_specs = (
        P(None, None, "dp", ("row", "col")),
        P(None, None, "dp", ("row", "col")),
        P(("row", "col", "dp")),
        P(("row", "dp"), "col"),
        P(("row", "dp"), "col"),
        P(("row", "dp"), "col"),
        P(("col", "dp"), "row"),
        P(("row", "col", "dp")),
        P(("row", "dp"), "col"),
        P(("row", "dp"), "col"),
        P(("col", "dp"), "row"),
    )
    return jax.shard_map(
        per_device, mesh=mesh, in_specs=in_specs, out_specs=out_specs, check_vma=False
    )
```
